32 devices in a mesh: dp: 8 (over y, x, core), tensor: 4 (over z).
Axes of the slice: x: 2, y: 2, z: 4, core: 2. Of those that a mesh axis runs over, the one named last changes fastest.
Arguments:
- hidden_in: bfloat16 [16384, 1024], P(('dp', 'tensor')), may hold values from -6 to 6
- cotangent: bfloat16 [16384, 1024], P(('dp', 'tensor')), may hold values from -6 to 6
- segments: int32 [16384], P('dp'), may hold values from 0 to 63, as said below
- attn_weight: float32 [4, 1024, 1024], P(None, 'dp', 'tensor'), may hold values from -0.1875 to 0.1875
- mlp_weight: float32 [3, 1024, 4096], P(None, 'dp', 'tensor'), may hold values from -0.1875 to 0.1875
- rates: float32 [2, 1024], replicated, may hold values from 0.2 to 0.6
- qk_scale: float32 [1024], P('tensor'), may hold values from 0.9 to 1.5
- mlp_scales: float32 [2, 4096], P(None, 'tensor'), may hold values from 0.5 to 1.5
- attn_moment_one: float32 [4, 1024, 1024], P(None, 'dp', 'tensor'), may hold values from -112 to 112
- attn_moment_two: float32 [4, 1024, 1024], P(None, 'dp', 'tensor'), may hold values from 163 to 1638
- mlp_moment_one: float32 [3, 1024, 4096], P(None, 'dp', 'tensor'), may hold values from -48 to 48
- mlp_moment_two: float32 [3, 1024, 4096], P(None, 'dp', 'tensor'), may hold values from 25 to 256
Outputs:
- hidden_out: bfloat16 [16384, 1024], P(('dp', 'tensor'))
- input_grad: bfloat16 [16384, 1024], P(('dp', 'tensor'))
- attn_weight_grad: float32 [4, 1024, 1024], P(None, 'dp', 'tensor')
- mlp_weight_grad: float32 [3, 1024, 4096], P(None, 'dp', 'tensor')
- rates_grad: float32 [2, 1024], replicated
- qk_scale_grad: float32 [1024], replicated
- mlp_scales_grad: float32 [2, 4096], replicated
- attn_moment_one_new: float32 [4, 1024, 1024], P(None, 'dp', 'tensor')
- attn_moment_two_new: float32 [4, 1024, 1024], P(None, 'dp', 'tensor')
- mlp_moment_one_new: float32 [3, 1024, 4096], P(None, 'dp', 'tensor')
- mlp_moment_two_new: float32 [3, 1024, 4096], P(None, 'dp', 'tensor')
- attn_weight_new: float32 [4, 1024, 1024], P(None, 'dp', 'tensor')
- mlp_weight_new: float32 [3, 1024, 4096], P(None, 'dp', 'tensor')
The draws below stay inside these ranges and needn't reach their ends.
Inputs may be any that keep to these rules, and one draw needn't show every extreme that they name: `segments`: each index of dp holds one packed row of 2048 tokens: whole documents in order, numbered 0, 1, 2, ... from the row's start, each 2048 // 32 times a power of two tokens long (short ones far more common), then padding with id 63 where the row is not full. The first row is a single document of 2048 tokens; the last row ends with padding.
All inputs are finite; a program needn't handle non-finite values.
Results may differ from the reference program's by a relative error of at most 0.018.
Values may be sent and summed in bfloat16 or wider, within the bound.
No kernel may reach another device: no remote copies, remote signals or barrier semaphores. Data moves between devices by JAX's collectives and lax.ppermute only.
A program may use at most 192 MiB of HBM per device.

```python
import math
import jax
import jax.numpy as jnp
from jax import lax

D = 1024
HEADS = 16
HEAD_DIM = 64
FF = 4096
ROW_LEN = 2048
QBLOCK = 512
TOKENS = 16384


pad_segment = 63


def draw_segments(key, part):
    row_total = TOKENS // ROW_LEN
    candidates = 40
    unit_len = ROW_LEN // 32

    def one_row(row_key, row_index):
        first_key, second_key = jax.random.split(row_key)
        exponents = jnp.minimum(jax.random.randint(first_key, (candidates,), 0, 6), jax.random.randint(second_key, (candidates,), 0, 6)).astype(jnp.int32)
        exponents = jnp.where(row_index == 0, jnp.full((candidates,), 5, jnp.int32), exponents)
        forced = jnp.concatenate([jnp.array([4, 3, 4], jnp.int32), exponents[3:]])
        exponents = jnp.where(row_index == row_total - 1, forced, exponents)
        lengths = unit_len * jnp.left_shift(jnp.ones_like(exponents), exponents)
        doc_ends = jnp.cumsum(lengths).astype(jnp.int32)
        position = jnp.arange(ROW_LEN, dtype=jnp.int32)
        document = jnp.sum((position[:, None] >= doc_ends[None, :]).astype(jnp.int32), axis=1)
        doc_end = jnp.take(doc_ends, document)
        return jnp.where(doc_end > ROW_LEN, pad_segment, document).astype(jnp.int32)
    row_keys = jax.random.split(key, row_total)
    packed = jax.vmap(one_row)(row_keys, jnp.arange(row_total, dtype=jnp.int32))
    return packed.reshape(TOKENS)


def levels(stream_key, shape, shards, low, top_value):
    gain = 1.0
    for axis_at, blocks in shards:
        steps = jax.random.uniform(jax.random.fold_in(jax.random.fold_in(stream_key, 6), axis_at), (blocks,), jnp.float32, low / len(shards), top_value / len(shards))
        gain = gain * jnp.repeat(jnp.exp(steps), shape[axis_at] // blocks).reshape((-1,) + (1,) * (len(shape) - 1 - axis_at))
    return gain


def bell_draw(stream_key, dims, width, bound, shards=(), held_as=jnp.bfloat16):
    result = width * jax.random.normal(stream_key, dims, jnp.float32)
    if shards:
        result = result * levels(stream_key, dims, shards, -0.22, 0.18)
    return jnp.clip(result, -bound, bound).astype(held_as)


def setup_inputs(seed: int = 0) -> dict:
    arg_keys = jax.random.split(jax.random.key(seed), 13)
    return {
        "hidden_in": bell_draw(arg_keys[0], (TOKENS, D), 1.0, 6.0, ((0, 32),)),
        "cotangent": bell_draw(arg_keys[1], (TOKENS, D), 1.0, 6.0, ((0, 32),)),
        "segments": draw_segments(jax.random.fold_in(arg_keys[12], 71), 0),
        "attn_weight": bell_draw(arg_keys[3], (4, D, HEADS * HEAD_DIM), D ** -0.5, 0.1875, ((1, 8), (2, 4)), jnp.float32),
        "mlp_weight": bell_draw(arg_keys[4], (3, D, FF), D ** -0.5, 0.1875, ((1, 8), (2, 4)), jnp.float32),
        "rates": jnp.clip(jax.random.uniform(arg_keys[5], (2, D), jnp.float32, 0.2, 0.6), 0.2, 0.6),
        "qk_scale": jnp.clip(0.9 + 0.6 * jax.random.uniform(arg_keys[6], (HEADS * HEAD_DIM,), jnp.float32) ** levels(arg_keys[6], (HEADS * HEAD_DIM,), ((0, 4),), -0.2, 0.2), 0.9, 1.5),
        "mlp_scales": jnp.clip(0.5 + 1.0 * jax.random.uniform(arg_keys[7], (2, FF), jnp.float32) ** levels(arg_keys[7], (2, FF), ((1, 4),), -0.2, 0.2), 0.5, 1.5),
        "attn_moment_one": bell_draw(arg_keys[8], (4, D, HEADS * HEAD_DIM), (7 * min(min(TOKENS // 64 + 16, TOKENS // 256 + 48), min(TOKENS // 1024 + 128, TOKENS // 4096 + 256)) // 40), 112.0, ((1, 8), (2, 4)), jnp.float32),
        "attn_moment_two": jnp.clip(jnp.exp(math.log(1638.0) - 2.307481 * jax.random.uniform(arg_keys[9], (4, D, HEADS * HEAD_DIM), jnp.float32) ** levels(arg_keys[9], (4, D, HEADS * HEAD_DIM), ((1, 8), (2, 4)), -0.2, 0.2)), 163.0, 1638.0),
        "mlp_moment_one": bell_draw(arg_keys[10], (3, D, FF), (3 * min(min(TOKENS // 64 + 16, TOKENS // 256 + 48), min(TOKENS // 1024 + 128, TOKENS // 4096 + 256)) // 40), 48.0, ((1, 8), (2, 4)), jnp.float32),
        "mlp_moment_two": jnp.clip(jnp.exp(math.log(256.0) - 2.3263016 * jax.random.uniform(arg_keys[11], (3, D, FF), jnp.float32) ** levels(arg_keys[11], (3, D, FF), ((1, 8), (2, 4)), -0.2, 0.2)), 25.0, 256.0),
    }


@jax.custom_vjp
def low(v):
    return lax.optimization_barrier(v.astype(jnp.bfloat16)).astype(jnp.float32)

@jax.custom_vjp
def low_back(v):
    return v

def low_keep(v):
    return (low(v), None)

def low_pass(kept, grad):
    return (grad,)

def back_keep(v):
    return (v, None)

def back_low(kept, grad):
    return (low(grad),)
low.defvjp(low_keep, low_pass)
low_back.defvjp(back_keep, back_low)
norm_eps = 1e-06
pad_segment = 63
masked_score = -1e+30
beta_one = 0.9
beta_two = 0.95
learning_rate = 0.01
adam_eps = 1e-08
bias_one = 1.0 - 0.9 ** 10
bias_two = 1.0 - 0.95 ** 10
highest = lax.Precision.HIGHEST

def rms_norm(vector):
    return vector * lax.rsqrt(lax.optimization_barrier(jnp.mean(vector * vector, axis=-1, keepdims=True)) + norm_eps)

def unit_norm(vector):
    return vector * lax.rsqrt(lax.optimization_barrier(jnp.sum(vector * vector, axis=-1, keepdims=True)) + norm_eps)

def sphere_mix(base, branch, rate):
    return rms_norm(base + rate * (rms_norm(branch) - base))

def gated_unit(up_part, gate_part, up_gain, gate_gain):
    scaled = gate_part * gate_gain
    return up_part * up_gain * (scaled * jax.nn.sigmoid(scaled))

def positions_of(segment_row):
    length = segment_row.shape[0]
    indices = jnp.arange(length, dtype=jnp.int32)
    changed = jnp.concatenate([jnp.ones((1,), dtype=jnp.bool_), segment_row[1:] != segment_row[:-1]])
    starts = lax.cummax(jnp.where(changed, indices, jnp.zeros_like(indices)), axis=0)
    return indices - starts

def rotary(vector, positions):
    half_dim = vector.shape[-1] // 2
    frequency = 10000.0 ** (-jnp.arange(half_dim, dtype=jnp.float32) / half_dim)
    angles = positions.astype(jnp.float32)[:, None] * frequency[None, :]
    cosine_table = jnp.cos(angles)[:, None, :]
    sine_table = jnp.sin(angles)[:, None, :]
    first_half = vector[..., :half_dim]
    second_half = vector[..., half_dim:]
    return jnp.concatenate([first_half * cosine_table - second_half * sine_table, second_half * cosine_table + first_half * sine_table], axis=-1)

def prepare_heads(raw, head_gains, positions):
    return unit_norm(rotary(raw, positions)) * head_gains

def attend_row(query_row, key_rows, value_rows, segment_row):
    length = segment_row.shape[0]
    block_count = length // QBLOCK
    scale_factor = math.sqrt(HEAD_DIM)
    key_index = jnp.arange(length, dtype=jnp.int32)

    def block_fn(block_index):
        offset = block_index * QBLOCK
        queries = lax.dynamic_slice_in_dim(query_row, offset, QBLOCK, 0)
        query_segments = lax.dynamic_slice_in_dim(segment_row, offset, QBLOCK, 0)
        query_index = offset + jnp.arange(QBLOCK, dtype=jnp.int32)
        scores = jnp.einsum('qhd,khd->hqk', queries, key_rows, precision=highest) * scale_factor
        scores = low_back(scores)
        allowed = (query_segments[:, None] == segment_row[None, :]) & (key_index[None, :] <= query_index[:, None])
        scores = jnp.where(allowed[None], scores, masked_score)
        row_peak = lax.optimization_barrier(jnp.max(scores, axis=-1, keepdims=True))
        weights = jnp.exp(scores - row_peak)
        attention_probs = weights / lax.optimization_barrier(jnp.sum(weights, axis=-1, keepdims=True))
        return jnp.einsum('hqk,khd->qhd', low(attention_probs), value_rows, precision=highest)
    outputs = lax.map(jax.checkpoint(block_fn), jnp.arange(block_count, dtype=jnp.int32))
    return outputs.reshape(length, -1)

def forward(tokens, attn_weight, mlp_weight, rates, qk_scale, mlp_scales, segments):
    token_total = tokens.shape[0]
    row_total = token_total // ROW_LEN
    attn_low = low(attn_weight)
    mlp_low = low(mlp_weight)
    inputs = low(tokens)
    head_gains = qk_scale.reshape(HEADS, HEAD_DIM)
    segment_rows = segments.reshape(row_total, ROW_LEN)

    def project(matrix):
        return jnp.dot(inputs, matrix, precision=highest)
    queries = low_back(project(attn_low[0]))
    key_part = low_back(project(attn_low[1]))
    values = low(low_back(project(attn_low[2])))

    def row_fn(row_items):
        query_row, key_row, value_row, segment_row = row_items
        positions = positions_of(segment_row)
        query_hat = low(prepare_heads(query_row.reshape(ROW_LEN, HEADS, HEAD_DIM), head_gains, positions))
        key_hat = low(prepare_heads(key_row.reshape(ROW_LEN, HEADS, HEAD_DIM), head_gains, positions))
        return attend_row(query_hat, key_hat, value_row.reshape(ROW_LEN, HEADS, HEAD_DIM), segment_row)
    attended = lax.map(row_fn, (queries.reshape(row_total, ROW_LEN, -1), key_part.reshape(row_total, ROW_LEN, -1), values.reshape(row_total, ROW_LEN, -1), segment_rows))
    attended = low(low_back(attended.reshape(token_total, -1)))
    branch = low_back(jnp.dot(attended, attn_low[3].T, precision=highest))
    middle = sphere_mix(tokens, branch, rates[0])
    middle_low = low(middle)
    up_part = low_back(jnp.dot(middle_low, mlp_low[0], precision=highest))
    gate_part = low_back(jnp.dot(middle_low, mlp_low[1], precision=highest))
    hidden_units = low(gated_unit(up_part, gate_part, mlp_scales[0], mlp_scales[1]))
    mlp_out = low_back(jnp.dot(hidden_units, mlp_low[2].T, precision=highest))
    return sphere_mix(middle, mlp_out, rates[1])

def adam_step(weight, gradient, moment_one, moment_two):
    moment_one_new = beta_one * moment_one + (1.0 - beta_one) * gradient
    moment_two_new = beta_two * moment_two + (1.0 - beta_two) * gradient * gradient
    moved = weight - learning_rate * (moment_one_new / bias_one) / (jnp.sqrt(moment_two_new / bias_two) + adam_eps)
    column_sq = lax.optimization_barrier(jnp.sum(moved * moved, axis=1, keepdims=True))
    return (moment_one_new, moment_two_new, moved * lax.rsqrt(column_sq + norm_eps))

def reference(hidden_in, cotangent, segments, attn_weight, mlp_weight, rates, qk_scale, mlp_scales, attn_moment_one, attn_moment_two, mlp_moment_one, mlp_moment_two):
    tokens = hidden_in.astype(jnp.float32)

    def loss_map(token_in, attn_in, mlp_in, rate_in, gain_in, scale_in):
        return forward(token_in, attn_in, mlp_in, rate_in, gain_in, scale_in, segments)
    output, pullback = jax.vjp(loss_map, tokens, attn_weight.astype(jnp.float32), mlp_weight.astype(jnp.float32), rates.astype(jnp.float32), qk_scale.astype(jnp.float32), mlp_scales.astype(jnp.float32))
    live_mask = (segments < pad_segment).astype(jnp.float32)
    gradients = pullback(cotangent.astype(jnp.float32) * live_mask[:, None])
    attn_one, attn_two, attn_new = adam_step(attn_weight, gradients[1], attn_moment_one, attn_moment_two)
    mlp_one, mlp_two, mlp_new = adam_step(mlp_weight, gradients[2], mlp_moment_one, mlp_moment_two)
    return (output.astype(jnp.bfloat16), gradients[0].astype(jnp.bfloat16), gradients[1], gradients[2], gradients[3], gradients[4], gradients[5], attn_one, attn_two, mlp_one, mlp_two, attn_new, mlp_new)
```

```python
import functools
import math

import jax
import jax.numpy as jnp
from jax import lax
from jax.experimental import pallas as pl
from jax.experimental.pallas import tpu as pltpu
from jax.sharding import PartitionSpec as P

HEAD_DIM = 64
LOG2E = 1.4426950408889634

norm_eps = 1e-06
pad_segment = 63
beta_one = 0.9
beta_two = 0.95
learning_rate = 0.01
adam_eps = 1e-08
bias_one = 1.0 - 0.9**10
bias_two = 1.0 - 0.95**10
scale_factor = math.sqrt(HEAD_DIM)
f32 = jnp.float32
bf16 = jnp.bfloat16


def rms_norm(vector):
    return vector * lax.rsqrt(jnp.mean(vector * vector, axis=-1, keepdims=True) + norm_eps)


def unit_norm(vector):
    return vector * lax.rsqrt(jnp.sum(vector * vector, axis=-1, keepdims=True) + norm_eps)


def sphere_mix(base, branch, rate):
    return rms_norm(base + rate * (rms_norm(branch) - base))


def starts_of(segment_row):
    indices = jnp.arange(segment_row.shape[0], dtype=jnp.int32)
    changed = jnp.concatenate(
        [jnp.ones((1,), dtype=jnp.bool_), segment_row[1:] != segment_row[:-1]]
    )
    return lax.cummax(jnp.where(changed, indices, jnp.zeros_like(indices)), axis=0)


def rotary(vector, positions):
    half_dim = vector.shape[-1] // 2
    frequency = 10000.0 ** (-jnp.arange(half_dim, dtype=jnp.float32) / half_dim)
    angles = positions.astype(jnp.float32)[:, None] * frequency[None, :]
    cosine_table = jnp.cos(angles)[:, None, :]
    sine_table = jnp.sin(angles)[:, None, :]
    first_half = vector[..., :half_dim]
    second_half = vector[..., half_dim:]
    return jnp.concatenate(
        [
            first_half * cosine_table - second_half * sine_table,
            second_half * cosine_table + first_half * sine_table,
        ],
        axis=-1,
    )


def adam_moved(weight, gradient, moment_one, moment_two):
    moment_one_new = beta_one * moment_one + (1.0 - beta_one) * gradient
    moment_two_new = beta_two * moment_two + (1.0 - beta_two) * gradient * gradient
    moved = weight - learning_rate * (moment_one_new / bias_one) / (
        jnp.sqrt(moment_two_new / bias_two) + adam_eps
    )
    return (moment_one_new, moment_two_new, moved)


def dot_nt(a, b):
    return lax.dot_general(a, b, (((1,), (1,)), ((), ())), preferred_element_type=f32)


def dot_nn(a, b):
    return lax.dot_general(a, b, (((1,), (0,)), ((), ())), preferred_element_type=f32)


def dot_tn(a, b):
    return lax.dot_general(a, b, (((0,), (0,)), ((), ())), preferred_element_type=f32)


def head_stack(x, heads):
    lane = lax.broadcasted_iota(jnp.int32, x.shape, 1) // HEAD_DIM
    zero = jnp.zeros_like(x)
    return jnp.concatenate([jnp.where(lane == h, x, zero) for h in range(heads)], axis=0)


def head_pick(stacked, heads, rows):
    width = stacked.shape[1]
    lane = lax.broadcasted_iota(jnp.int32, (rows, width), 1) // HEAD_DIM
    picked = jnp.zeros((rows, width), f32)
    for h in range(heads):
        picked = jnp.where(lane == h, stacked[h * rows : (h + 1) * rows], picked)
    return picked


def attend_kernel(heads, bq, bk, q_ref, k_ref, v_ref, start_ref, o_ref, of_ref, l_ref, acc, lsum):
    i = pl.program_id(0)
    qs = head_stack(q_ref[...], heads)
    acc[...] = jnp.zeros_like(acc)
    lsum[...] = jnp.zeros_like(lsum)
    start = jnp.concatenate([start_ref[...]] * heads, axis=0)

    def step(j, diagonal):
        offset = pl.multiple_of(j * bk, bk)
        keys = k_ref[pl.ds(offset, bk), :]
        values = v_ref[pl.ds(offset, bk), :]
        scores = dot_nt(qs, keys)
        key_index = offset + lax.broadcasted_iota(jnp.int32, scores.shape, 1)
        allowed = key_index >= start
        if diagonal:
            row = lax.rem(lax.broadcasted_iota(jnp.int32, scores.shape, 0), bq)
            allowed = allowed & (key_index <= i * bq + row)
        weights = jnp.where(allowed, jnp.exp2(scores * (scale_factor * LOG2E)), 0.0)
        total = weights[:, :128]
        for part in range(1, bk // 128):
            total = total + weights[:, part * 128 : (part + 1) * 128]
        lsum[...] += total
        acc[...] += dot_nn(weights.astype(bf16), values)

    def body(j, carry):
        step(j, False)
        return carry

    lax.fori_loop(0, i, body, 0)
    step(i, True)
    summed = jnp.sum(lsum[...], axis=1, keepdims=True)
    out = head_pick(acc[...] * (1.0 / summed), heads, bq)
    of_ref[...] = out
    o_ref[...] = out.astype(bf16)
    l_ref[...] = jnp.log2(summed).reshape(heads, bq)


def attend(q, k, v, start, block):
    length, width = q.shape
    heads = width // HEAD_DIM
    whole = pl.BlockSpec((length, width), lambda i: (0, 0))
    rows = pl.BlockSpec((block, width), lambda i: (i, 0))
    return pl.pallas_call(
        functools.partial(attend_kernel, heads, block, block),
        grid=(length // block,),
        in_specs=[rows, whole, whole, pl.BlockSpec((block, 1), lambda i: (i, 0))],
        out_specs=[rows, rows, pl.BlockSpec((heads, block), lambda i: (0, i))],
        out_shape=[
            jax.ShapeDtypeStruct((length, width), bf16),
            jax.ShapeDtypeStruct((length, width), f32),
            jax.ShapeDtypeStruct((heads, length), f32),
        ],
        scratch_shapes=[
            pltpu.VMEM((heads * block, width), f32),
            pltpu.VMEM((heads * block, 128), f32),
        ],
        cost_estimate=pl.CostEstimate(
            flops=20_000_000_000, bytes_accessed=8 * length * width, transcendentals=0
        ),
        name="attend",
    )(q, k, v, start)


def attend_back_kernel(
    heads, bq, bk, q_ref, do_ref, k_ref, v_ref, of_ref, l_ref, start_ref, dq_ref, dk_ref, dv_ref, acc
):
    i = pl.program_id(0)

    @pl.when(i == 0)
    def _():
        dk_ref[...] = jnp.zeros_like(dk_ref)
        dv_ref[...] = jnp.zeros_like(dv_ref)

    qs = head_stack(q_ref[...], heads)
    grads = do_ref[...]
    dos = head_stack(grads, heads)
    product = (grads.astype(f32) * of_ref[...]).T
    delta = jnp.concatenate(
        [
            jnp.sum(product[h * HEAD_DIM : (h + 1) * HEAD_DIM], axis=0, keepdims=True)
            for h in range(heads)
        ],
        axis=1,
    )
    log_sum = jnp.concatenate([l_ref[h : h + 1, :] for h in range(heads)], axis=1)
    start = jnp.concatenate([start_ref[...]] * heads, axis=1)
    acc[...] = jnp.zeros_like(acc)

    def step(j, diagonal):
        offset = pl.multiple_of(j * bk, bk)
        keys = k_ref[pl.ds(offset, bk), :]
        values = v_ref[pl.ds(offset, bk), :]
        scores = dot_nt(keys, qs)
        key_index = offset + lax.broadcasted_iota(jnp.int32, scores.shape, 0)
        allowed = key_index >= start
        if diagonal:
            column = lax.rem(lax.broadcasted_iota(jnp.int32, scores.shape, 1), bq)
            allowed = allowed & (key_index <= i * bq + column)
        probs = jnp.where(allowed, jnp.exp2(scores * (scale_factor * LOG2E) - log_sum), 0.0)
        prob_grad = dot_nt(values, dos)
        score_grad = (probs * (prob_grad - delta)).astype(bf16)
        dv_ref[pl.ds(offset, bk), :] += dot_nn(probs.astype(bf16), dos)
        dk_ref[pl.ds(offset, bk), :] += dot_nn(score_grad, qs)
        acc[...] += dot_tn(score_grad, keys)

    def body(j, carry):
        step(j, False)
        return carry

    lax.fori_loop(0, i, body, 0)
    step(i, True)
    dq_ref[...] = head_pick(acc[...], heads, bq)


def attend_back(q, k, v, grads, out, log_sum, start, block):
    length, width = q.shape
    heads = width // HEAD_DIM
    whole = pl.BlockSpec((length, width), lambda i: (0, 0))
    rows = pl.BlockSpec((block, width), lambda i: (i, 0))
    result = jax.ShapeDtypeStruct((length, width), f32)
    return pl.pallas_call(
        functools.partial(attend_back_kernel, heads, block, block),
        grid=(length // block,),
        in_specs=[
            rows,
            rows,
            whole,
            whole,
            rows,
            pl.BlockSpec((heads, block), lambda i: (0, i)),
            pl.BlockSpec((1, block), lambda i: (0, i)),
        ],
        out_specs=[rows, whole, whole],
        out_shape=[result, result, result],
        scratch_shapes=[pltpu.VMEM((heads * block, width), f32)],
        cost_estimate=pl.CostEstimate(
            flops=40_000_000_000, bytes_accessed=20 * length * width, transcendentals=0
        ),
        name="attend_back",
    )(q, grads, k, v, out, log_sum, start)


def feed_kernel(m_ref, w_ref, s_ref, up_ref, gate_ref, h_ref, out_ref):
    @pl.when(pl.program_id(0) == 0)
    def _():
        out_ref[...] = jnp.zeros_like(out_ref)

    tokens = m_ref[...]
    up = dot_nn(tokens, w_ref[0, 0])
    gate = dot_nn(tokens, w_ref[1, 0])
    up_ref[...] = up
    gate_ref[...] = gate
    scaled = gate * s_ref[1:2, :]
    hidden = (up * s_ref[0:1, :] * (scaled * jax.nn.sigmoid(scaled))).astype(bf16)
    h_ref[...] = hidden
    out_ref[...] += dot_nt(hidden, w_ref[2, 0])


def feed(middle, weights, scales, step):
    rows, model = middle.shape
    _, groups, _, local_width = weights.shape
    per = local_width // step
    total = groups * local_width
    columns = pl.BlockSpec((rows, step), lambda i: (0, i))
    return pl.pallas_call(
        feed_kernel,
        grid=(total // step,),
        in_specs=[
            pl.BlockSpec((rows, model), lambda i: (0, 0)),
            pl.BlockSpec((3, 1, model, step), lambda i: (0, i // per, 0, i % per)),
            pl.BlockSpec((2, step), lambda i: (0, i)),
        ],
        out_specs=[columns, columns, columns, pl.BlockSpec((rows, model), lambda i: (0, 0))],
        out_shape=[
            jax.ShapeDtypeStruct((rows, total), f32),
            jax.ShapeDtypeStruct((rows, total), f32),
            jax.ShapeDtypeStruct((rows, total), bf16),
            jax.ShapeDtypeStruct((rows, model), f32),
        ],
        cost_estimate=pl.CostEstimate(
            flops=6 * rows * model * total,
            bytes_accessed=6 * model * total + 10 * rows * total,
            transcendentals=0,
        ),
        name="feed",
    )(middle, weights, scales)


def feed_back_kernel(
    og_ref, mt_ref, w_ref, s_ref, up_ref, gate_ref, grad_ref, sg_ref, mg_ref
):
    @pl.when(pl.program_id(0) == 0)
    def _():
        mg_ref[...] = jnp.zeros_like(mg_ref)

    hidden_grad = dot_nn(og_ref[...], w_ref[2, 0])
    up = up_ref[...]
    gate = gate_ref[...]
    up_gain = s_ref[0:1, :]
    gate_gain = s_ref[1:2, :]
    scaled = gate * gate_gain
    sig = jax.nn.sigmoid(scaled)
    up_part = hidden_grad * (scaled * sig)
    gate_part = hidden_grad * (up * up_gain) * (sig * (1.0 + scaled * (1.0 - sig)))
    sg_ref[0:1, :] = jnp.sum(up_part * up, axis=0, keepdims=True)
    sg_ref[1:2, :] = jnp.sum(gate_part * gate, axis=0, keepdims=True)
    up_low = (up_part * up_gain).astype(bf16)
    gate_low = (gate_part * gate_gain).astype(bf16)
    tokens_t = mt_ref[...]
    grad_ref[0] = dot_nn(tokens_t, up_low).astype(bf16)
    grad_ref[1] = dot_nn(tokens_t, gate_low).astype(bf16)
    mg_ref[...] += dot_nt(up_low, w_ref[0, 0]) + dot_nt(gate_low, w_ref[1, 0])


def feed_back(out_grad, middle_t, weights, scales, up, gate, step):
    model, rows = middle_t.shape
    _, groups, _, local_width = weights.shape
    per = local_width // step
    total = groups * local_width
    columns = pl.BlockSpec((rows, step), lambda i: (0, i))
    return pl.pallas_call(
        feed_back_kernel,
        grid=(total // step,),
        in_specs=[
            pl.BlockSpec((rows, model), lambda i: (0, 0)),
            pl.BlockSpec((model, rows), lambda i: (0, 0)),
            pl.BlockSpec((3, 1, model, step), lambda i: (0, i // per, 0, i % per)),
            pl.BlockSpec((2, step), lambda i: (0, i)),
            columns,
            columns,
        ],
        out_specs=[
            pl.BlockSpec((2, model, step), lambda i: (0, 0, i)),
            pl.BlockSpec((2, step), lambda i: (0, i)),
            pl.BlockSpec((rows, model), lambda i: (0, 0)),
        ],
        out_shape=[
            jax.ShapeDtypeStruct((2, model, total), bf16),
            jax.ShapeDtypeStruct((2, total), f32),
            jax.ShapeDtypeStruct((rows, model), f32),
        ],
        cost_estimate=pl.CostEstimate(
            flops=10 * rows * model * total,
            bytes_accessed=10 * model * total + 8 * rows * total,
            transcendentals=0,
        ),
        name="feed_back",
    )(out_grad, middle_t, weights, scales, up, gate)


def shift(value, axis, distance, size):
    return lax.ppermute(value, axis, [(i, (i + distance) % size) for i in range(size)])


def butterfly(values, axis, size):
    step = 1
    while step < size:
        other = [lax.ppermute(v, axis, [(i, i ^ step) for i in range(size)]) for v in values]
        values = [v + o for v, o in zip(values, other)]
        step *= 2
    return values


def take_block(value, index, size, axis):
    return lax.dynamic_slice_in_dim(value, index * size, size, axis)


def put_block(whole, value, index, axis):
    return lax.dynamic_update_slice_in_dim(whole, value, index * value.shape[axis], axis)


def local(
    nd,
    nt,
    hidden_in,
    cotangent,
    segments,
    attn_weight,
    mlp_weight,
    rates,
    qk_scale,
    mlp_scales,
    attn_moment_one,
    attn_moment_two,
    mlp_moment_one,
    mlp_moment_two,
):
    rows, model = hidden_in.shape
    length = segments.shape[0]
    shard = attn_weight.shape[1]
    heads_width = attn_weight.shape[2]
    hidden_width = mlp_weight.shape[2]
    local_heads = heads_width // HEAD_DIM
    block = min(512, length)
    step = min(512, hidden_width)
    me = lax.axis_index("tensor")

    attn_low = attn_weight.astype(bf16)
    attn_shard = jnp.concatenate([attn_low[0], attn_low[1], attn_low[2], attn_low[3]], axis=1)
    attn_full = lax.all_gather(attn_shard, "dp", axis=0, tiled=True)
    mlp_low, attn_full = lax.optimization_barrier((mlp_weight.astype(bf16), attn_full))
    mlp_full = lax.all_gather(mlp_low, ("tensor", "dp"), axis=1, tiled=True)
    mlp_full = mlp_full.reshape(3, nt, model, hidden_width)
    qkv_matrix = attn_full[:, : 3 * heads_width]
    out_local = attn_full[:, 3 * heads_width :]

    hidden_row = jnp.zeros((length, model), bf16)
    hidden_row = put_block(hidden_row, hidden_in, me, 0)
    for d in range(1, nt):
        hidden_row = put_block(hidden_row, shift(hidden_in, "tensor", d, nt), (me - d) % nt, 0)
    scales_row = jnp.zeros((2, nt * hidden_width), f32)
    scales_row = put_block(scales_row, mlp_scales, me, 1)
    for d in range(1, nt):
        scales_row = put_block(scales_row, shift(mlp_scales, "tensor", d, nt), (me - d) % nt, 1)
    out_matrix = jnp.concatenate(
        [out_local] + [shift(out_local, "tensor", d, nt) for d in range(1, nt)], axis=1
    )

    projected = jnp.dot(hidden_row, qkv_matrix, preferred_element_type=f32)
    starts = starts_of(segments)
    positions = jnp.arange(length, dtype=jnp.int32) - starts

    def prepare_flat(raw, gain_flat):
        rotated = rotary(raw.reshape(length, local_heads, HEAD_DIM), positions)
        return (unit_norm(rotated) * gain_flat.reshape(local_heads, HEAD_DIM)).reshape(
            length, heads_width
        )

    query_raw = projected[:, :heads_width]
    key_raw = projected[:, heads_width : 2 * heads_width]
    query_hat = prepare_flat(query_raw, qk_scale).astype(bf16)
    key_hat = prepare_flat(key_raw, qk_scale).astype(bf16)
    value_hat = projected[:, 2 * heads_width :].astype(bf16)
    attended_row, attended_f32, log_sum = attend(
        query_hat, key_hat, value_hat, starts[:, None], block
    )
    attended = jnp.concatenate(
        [take_block(attended_row, me, rows, 0)]
        + [
            shift(take_block(attended_row, (me + d) % nt, rows, 0), "tensor", d, nt)
            for d in range(1, nt)
        ],
        axis=1,
    )
    branch = dot_nt(attended, out_matrix)
    tokens = hidden_in.astype(f32)
    middle = sphere_mix(tokens, branch, rates[0])
    middle_low = middle.astype(bf16)
    up, gate, hidden_units, mlp_out = feed(middle_low, mlp_full, scales_row, step)
    result = sphere_mix(middle, mlp_out, rates[1])
    row_segments = take_block(segments, me, rows, 0)
    upstream = cotangent.astype(f32) * (row_segments < pad_segment).astype(f32)[:, None]
    _, mlp_pull = jax.vjp(sphere_mix, middle, mlp_out, rates[1])
    middle_direct, mlp_out_grad, rate_mlp_grad = mlp_pull(upstream)
    mlp_out_low = mlp_out_grad.astype(bf16)
    down_grad = dot_tn(mlp_out_low, hidden_units).astype(bf16)
    down_part = lax.psum_scatter(down_grad, "dp", scatter_dimension=0, tiled=True)
    in_grad, scales_grad, middle_back = feed_back(
        mlp_out_low, middle_low.T, mlp_full, scales_row, up, gate, step
    )
    in_part = lax.psum_scatter(in_grad, "dp", scatter_dimension=1, tiled=True)
    _, attn_pull = jax.vjp(sphere_mix, tokens, branch, rates[0])
    token_direct, branch_grad, rate_attn_grad = attn_pull(middle_direct + middle_back)
    branch_low = branch_grad.astype(bf16)
    attended_grad = dot_nn(branch_low, out_matrix).astype(bf16)
    grad_row = jnp.zeros((length, heads_width), bf16)
    grad_row = put_block(grad_row, attended_grad[:, :heads_width], me, 0)
    for d in range(1, nt):
        piece = attended_grad[:, d * heads_width : (d + 1) * heads_width]
        grad_row = put_block(grad_row, shift(piece, "tensor", -d, nt), (me + d) % nt, 0)
    out_grad = dot_tn(branch_low, attended).astype(bf16)
    out_part = lax.psum_scatter(out_grad, "dp", scatter_dimension=0, tiled=True)

    query_hat_grad, key_hat_grad, value_grad = attend_back(
        query_hat, key_hat, value_hat, grad_row, attended_f32, log_sum, starts[None, :], block
    )
    _, query_pull = jax.vjp(prepare_flat, query_raw, qk_scale)
    query_raw_grad, gain_query = query_pull(query_hat_grad * scale_factor)
    _, key_pull = jax.vjp(prepare_flat, key_raw, qk_scale)
    key_raw_grad, gain_key = key_pull(key_hat_grad * scale_factor)
    qkv_grad = jnp.concatenate([query_raw_grad, key_raw_grad, value_grad], axis=1).astype(bf16)
    total = token_direct + dot_nt(take_block(qkv_grad, me, rows, 0), qkv_matrix)
    for d in range(1, nt):
        piece = dot_nt(take_block(qkv_grad, (me + d) % nt, rows, 0), qkv_matrix).astype(bf16)
        total = total + shift(piece, "tensor", d, nt).astype(f32)
    input_grad = total.astype(bf16)
    qkv_weight_grad = dot_tn(hidden_row, qkv_grad).astype(bf16)
    qkv_part = lax.psum_scatter(qkv_weight_grad, "dp", scatter_dimension=0, tiled=True)

    def own_sum(part, axis, width):
        total = take_block(part, me, width, axis).astype(f32)
        for d in range(1, nt):
            piece = take_block(part, (me + d) % nt, width, axis)
            total = total + shift(piece, "tensor", d, nt).astype(f32)
        return total

    out_own = out_part[:, :heads_width].astype(f32)
    for d in range(1, nt):
        piece = out_part[:, d * heads_width : (d + 1) * heads_width]
        out_own = out_own + shift(piece, "tensor", -d, nt).astype(f32)
    down_own = own_sum(down_part, 1, hidden_width)
    in_own = own_sum(in_part, 2, hidden_width)
    attn_weight_grad = jnp.stack(
        [
            qkv_part[:, :heads_width].astype(f32),
            qkv_part[:, heads_width : 2 * heads_width].astype(f32),
            qkv_part[:, 2 * heads_width :].astype(f32),
            out_own,
        ]
    )
    mlp_weight_grad = jnp.concatenate([in_own, down_own[None]], axis=0)

    rates_part = jnp.stack([rate_attn_grad, rate_mlp_grad])
    small = jnp.concatenate([rates_part, scales_grad.reshape(-1, model)], axis=0)
    (small,) = butterfly([small], "dp", nd)
    (small,) = butterfly([small], "tensor", nt)
    rates_grad = small[:2]
    mlp_scales_grad = small[2:].reshape(2, nt * hidden_width)

    attn_one, attn_two, attn_moved = adam_moved(
        attn_weight, attn_weight_grad, attn_moment_one, attn_moment_two
    )
    mlp_one, mlp_two, mlp_moved = adam_moved(
        mlp_weight, mlp_weight_grad, mlp_moment_one, mlp_moment_two
    )
    attn_square = jnp.sum(attn_moved * attn_moved, axis=1, keepdims=True)
    mlp_square = jnp.sum(mlp_moved * mlp_moved, axis=1, keepdims=True)
    gain = gain_query + gain_key
    (mlp_square,) = butterfly([mlp_square], "dp", nd)
    last = jnp.concatenate([attn_square.reshape(-1), gain])
    (last,) = butterfly([last], "dp", nd)
    attn_square = last[: 4 * heads_width].reshape(4, 1, heads_width)
    gain = last[4 * heads_width :]
    gain_row = put_block(jnp.zeros((nt * heads_width,), f32), gain, me, 0)
    for d in range(1, nt):
        gain_row = put_block(gain_row, shift(gain, "tensor", d, nt), (me - d) % nt, 0)
    attn_new = attn_moved * lax.rsqrt(attn_square + norm_eps)
    mlp_new = mlp_moved * lax.rsqrt(mlp_square + norm_eps)
    return (
        result.astype(bf16),
        input_grad,
        attn_weight_grad,
        mlp_weight_grad,
        rates_grad,
        gain_row,
        mlp_scales_grad,
        attn_one,
        attn_two,
        mlp_one,
        mlp_two,
        attn_new,
        mlp_new,
    )


def solution(mesh):
    weights = P(None, "dp", "tensor")
    tokens = P(("dp", "tensor"), None)
    return jax.shard_map(
        functools.partial(local, mesh.shape["dp"], mesh.shape["tensor"]),
        mesh=mesh,
        in_specs=(
            tokens,
            tokens,
            P("dp"),
            weights,
            weights,
            P(),
            P("tensor"),
            P(None, "tensor"),
            weights,
            weights,
            weights,
            weights,
        ),
        out_specs=(
            tokens,
            tokens,
            weights,
            weights,
            P(),
            P(),
            P(),
            weights,
            weights,
            weights,
            weights,
            weights,
            weights,
        ),
        check_vma=False,
    )
```

```python
import functools
import math

import jax
import jax.numpy as jnp
from jax import lax
from jax.experimental import pallas as pl
from jax.experimental.pallas import tpu as pltpu
from jax.sharding import PartitionSpec as P

HEAD_DIM = 64
LOG2E = 1.4426950408889634

norm_eps = 1e-06
pad_segment = 63
beta_one = 0.9
beta_two = 0.95
learning_rate = 0.01
adam_eps = 1e-08
bias_one = 1.0 - 0.9**10
bias_two = 1.0 - 0.95**10
scale_factor = math.sqrt(HEAD_DIM)
f32 = jnp.float32
bf16 = jnp.bfloat16


def starts_of(segment_row):
    indices = jnp.arange(segment_row.shape[0], dtype=jnp.int32)
    changed = jnp.concatenate(
        [jnp.ones((1,), dtype=jnp.bool_), segment_row[1:] != segment_row[:-1]]
    )
    return lax.cummax(jnp.where(changed, indices, jnp.zeros_like(indices)), axis=0)


def adam_moved(weight, gradient, moment_one, moment_two):
    moment_one_new = beta_one * moment_one + (1.0 - beta_one) * gradient
    moment_two_new = beta_two * moment_two + (1.0 - beta_two) * gradient * gradient
    moved = weight - learning_rate * (moment_one_new / bias_one) / (
        jnp.sqrt(moment_two_new / bias_two) + adam_eps
    )
    return (moment_one_new, moment_two_new, moved)


def dot_nt(a, b):
    return lax.dot_general(a, b, (((1,), (1,)), ((), ())), preferred_element_type=f32)


def dot_nn(a, b):
    return lax.dot_general(a, b, (((1,), (0,)), ((), ())), preferred_element_type=f32)


def dot_tn(a, b):
    return lax.dot_general(a, b, (((0,), (0,)), ((), ())), preferred_element_type=f32)


def head_stack(x, heads):
    lane = lax.broadcasted_iota(jnp.int32, x.shape, 1) // HEAD_DIM
    zero = jnp.zeros_like(x)
    return jnp.concatenate([jnp.where(lane == h, x, zero) for h in range(heads)], axis=0)


def head_pick(stacked, heads, rows):
    width = stacked.shape[1]
    lane = lax.broadcasted_iota(jnp.int32, (rows, width), 1) // HEAD_DIM
    picked = jnp.zeros((rows, width), f32)
    for h in range(heads):
        picked = jnp.where(lane == h, stacked[h * rows : (h + 1) * rows], picked)
    return picked


def attend_kernel(heads, bq, bk, q_ref, k_ref, v_ref, start_ref, o_ref, of_ref, l_ref, acc, lsum):
    i = pl.program_id(0)
    qs = head_stack(q_ref[...], heads)
    acc[...] = jnp.zeros_like(acc)
    lsum[...] = jnp.zeros_like(lsum)
    start = jnp.concatenate([start_ref[...]] * heads, axis=0)

    def step(j, diagonal):
        offset = pl.multiple_of(j * bk, bk)
        keys = k_ref[pl.ds(offset, bk), :]
        values = v_ref[pl.ds(offset, bk), :]
        scores = dot_nt(qs, keys)
        key_index = offset + lax.broadcasted_iota(jnp.int32, scores.shape, 1)
        allowed = key_index >= start
        if diagonal:
            row = lax.rem(lax.broadcasted_iota(jnp.int32, scores.shape, 0), bq)
            allowed = allowed & (key_index <= i * bq + row)
        weights = jnp.where(allowed, jnp.exp2(scores * (scale_factor * LOG2E)), 0.0)
        total = weights[:, :128]
        for part in range(1, bk // 128):
            total = total + weights[:, part * 128 : (part + 1) * 128]
        lsum[...] += total
        acc[...] += dot_nn(weights.astype(bf16), values)

    def body(j, carry):
        step(j, False)
        return carry

    lax.fori_loop(0, i, body, 0)
    step(i, True)
    summed = jnp.sum(lsum[...], axis=1, keepdims=True)
    out = head_pick(acc[...] * (1.0 / summed), heads, bq)
    of_ref[...] = out
    o_ref[...] = out.astype(bf16)
    l_ref[...] = jnp.log2(summed).reshape(heads, bq)


def attend(q, k, v, start, block):
    length, width = q.shape
    heads = width // HEAD_DIM
    whole = pl.BlockSpec((length, width), lambda i: (0, 0))
    rows = pl.BlockSpec((block, width), lambda i: (i, 0))
    return pl.pallas_call(
        functools.partial(attend_kernel, heads, block, block),
        grid=(length // block,),
        in_specs=[rows, whole, whole, pl.BlockSpec((block, 1), lambda i: (i, 0))],
        out_specs=[rows, rows, pl.BlockSpec((heads, block), lambda i: (0, i))],
        out_shape=[
            jax.ShapeDtypeStruct((length, width), bf16),
            jax.ShapeDtypeStruct((length, width), f32),
            jax.ShapeDtypeStruct((heads, length), f32),
        ],
        scratch_shapes=[
            pltpu.VMEM((heads * block, width), f32),
            pltpu.VMEM((heads * block, 128), f32),
        ],
        cost_estimate=pl.CostEstimate(
            flops=20_000_000_000, bytes_accessed=8 * length * width, transcendentals=0
        ),
        name="attend",
    )(q, k, v, start)


def attend_back_kernel(
    heads, bq, bk, q_ref, do_ref, k_ref, v_ref, of_ref, l_ref, start_ref, dq_ref, dk_ref, dv_ref, acc
):
    i = pl.program_id(0)

    @pl.when(i == 0)
    def _():
        dk_ref[...] = jnp.zeros_like(dk_ref)
        dv_ref[...] = jnp.zeros_like(dv_ref)

    qs = head_stack(q_ref[...], heads)
    grads = do_ref[...]
    dos = head_stack(grads, heads)
    product = (grads.astype(f32) * of_ref[...]).T
    delta = jnp.concatenate(
        [
            jnp.sum(product[h * HEAD_DIM : (h + 1) * HEAD_DIM], axis=0, keepdims=True)
            for h in range(heads)
        ],
        axis=1,
    )
    log_sum = jnp.concatenate([l_ref[h : h + 1, :] for h in range(heads)], axis=1)
    start = jnp.concatenate([start_ref[...]] * heads, axis=1)
    acc[...] = jnp.zeros_like(acc)

    def step(j, diagonal):
        offset = pl.multiple_of(j * bk, bk)
        keys = k_ref[pl.ds(offset, bk), :]
        values = v_ref[pl.ds(offset, bk), :]
        scores = dot_nt(keys, qs)
        key_index = offset + lax.broadcasted_iota(jnp.int32, scores.shape, 0)
        allowed = key_index >= start
        if diagonal:
            column = lax.rem(lax.broadcasted_iota(jnp.int32, scores.shape, 1), bq)
            allowed = allowed & (key_index <= i * bq + column)
        probs = jnp.where(allowed, jnp.exp2(scores * (scale_factor * LOG2E) - log_sum), 0.0)
        prob_grad = dot_nt(values, dos)
        score_grad = (probs * (prob_grad - delta)).astype(bf16)
        dv_ref[pl.ds(offset, bk), :] += dot_nn(probs.astype(bf16), dos)
        dk_ref[pl.ds(offset, bk), :] += dot_nn(score_grad, qs)
        acc[...] += dot_tn(score_grad, keys)

    def body(j, carry):
        step(j, False)
        return carry

    lax.fori_loop(0, i, body, 0)
    step(i, True)
    dq_ref[...] = head_pick(acc[...], heads, bq)


def attend_back(q, k, v, grads, out, log_sum, start, block):
    length, width = q.shape
    heads = width // HEAD_DIM
    whole = pl.BlockSpec((length, width), lambda i: (0, 0))
    rows = pl.BlockSpec((block, width), lambda i: (i, 0))
    result = jax.ShapeDtypeStruct((length, width), f32)
    return pl.pallas_call(
        functools.partial(attend_back_kernel, heads, block, block),
        grid=(length // block,),
        in_specs=[
            rows,
            rows,
            whole,
            whole,
            rows,
            pl.BlockSpec((heads, block), lambda i: (0, i)),
            pl.BlockSpec((1, block), lambda i: (0, i)),
        ],
        out_specs=[rows, whole, whole],
        out_shape=[result, result, result],
        scratch_shapes=[pltpu.VMEM((heads * block, width), f32)],
        cost_estimate=pl.CostEstimate(
            flops=40_000_000_000, bytes_accessed=20 * length * width, transcendentals=0
        ),
        name="attend_back",
    )(q, grads, k, v, out, log_sum, start)


def partner(x):
    width = x.shape[1]
    lane = lax.broadcasted_iota(jnp.int32, x.shape, 1)
    ahead = pltpu.roll(x, width - HEAD_DIM // 2, 1)
    behind = pltpu.roll(x, HEAD_DIM // 2, 1)
    return jnp.where(lax.rem(lane, HEAD_DIM) < HEAD_DIM // 2, ahead, behind)


def head_sums(x):
    width = x.shape[1]
    row = lax.broadcasted_iota(jnp.int32, (width, width), 0) // HEAD_DIM
    column = lax.broadcasted_iota(jnp.int32, (width, width), 1) // HEAD_DIM
    same = jnp.where(row == column, 1.0, 0.0).astype(f32)
    return lax.dot_general(
        x,
        same,
        (((1,), (0,)), ((), ())),
        precision=lax.Precision.HIGHEST,
        preferred_element_type=f32,
    )


def widen(table, width):
    return table if table.shape[1] == width else jnp.concatenate([table] * (width // 128), axis=1)


def project_kernel(index_ref, x_ref, wq_ref, wk_ref, wv_ref, cos_ref, sin_ref, gain_ref, *refs):
    q_ref, k_ref, v_ref, xq_ref, xk_ref = refs[-5:]
    x = x_ref[...]
    width = q_ref.shape[1]
    cosine = widen(cos_ref[...], width)
    sine = widen(sin_ref[...], width)
    gain = gain_ref[...]
    for w_ref, hat_ref, turned_ref in ((wq_ref, q_ref, xq_ref), (wk_ref, k_ref, xk_ref)):
        raw = dot_nn(x, w_ref[...])
        turned = raw * cosine + partner(raw) * sine
        turned_ref[...] = turned
        hat = turned * lax.rsqrt(head_sums(turned * turned) + norm_eps) * gain
        hat_ref[...] = hat.astype(bf16)
    v_ref[...] = dot_nn(x, wv_ref[...]).astype(bf16)


def project(index, x, weights, cosine, sine, gain, length, previous):
    rows, model = x.shape
    width = gain.shape[1]
    part = min(256, rows)
    per = rows // part

    def column(m):
        return pl.BlockSpec((model, width), lambda i, at: (0, m))

    table = pl.BlockSpec((part, 128), lambda i, at: (at[0] * per + i, 0))
    out = pl.BlockSpec((part, width), lambda i, at: (at[0] * per + i, 0))
    low = jax.ShapeDtypeStruct((length, width), bf16)
    wide = jax.ShapeDtypeStruct((length, width), f32)
    return pl.pallas_call(
        project_kernel,
        grid_spec=pltpu.PrefetchScalarGridSpec(
            num_scalar_prefetch=1,
            grid=(per,),
            in_specs=[
                pl.BlockSpec((part, model), lambda i, at: (i, 0)),
                column(0),
                column(1),
                column(2),
                table,
                table,
                pl.BlockSpec((1, width), lambda i, at: (0, 0)),
            ]
            + [pl.BlockSpec(memory_space=pl.ANY)] * len(previous),
            out_specs=[out] * 5,
        ),
        out_shape=[low, low, low, wide, wide],
        input_output_aliases={8 + i: i for i in range(len(previous))},
        cost_estimate=pl.CostEstimate(
            flops=6 * rows * model * width, bytes_accessed=8 * model * width, transcendentals=0
        ),
        name="project",
    )(index, x, weights, weights, weights, cosine, sine, gain, *previous)


def project_back_kernel(
    index_ref,
    dq_ref,
    dk_ref,
    dv_ref,
    xq_ref,
    xk_ref,
    wq_ref,
    wk_ref,
    wv_ref,
    cos_ref,
    sin_ref,
    gain_ref,
    grad_ref,
    piece_ref,
    gain_grad_ref,
):
    @pl.when(pl.program_id(0) == 0)
    def _():
        gain_grad_ref[...] = jnp.zeros_like(gain_grad_ref)

    width = dq_ref.shape[1]
    cosine = widen(cos_ref[...], width)
    sine = widen(sin_ref[...], width)
    gain = gain_ref[...]
    lows = []
    for d_ref, x_ref in ((dq_ref, xq_ref), (dk_ref, xk_ref)):
        turned = x_ref[...]
        inverse = lax.rsqrt(head_sums(turned * turned) + norm_eps)
        unit = turned * inverse
        hat_grad = d_ref[...] * scale_factor
        gain_grad_ref[...] += jnp.sum(hat_grad * unit, axis=0, keepdims=True)
        unit_grad = hat_grad * gain
        turned_grad = inverse * (unit_grad - unit * head_sums(unit * unit_grad))
        raw_grad = turned_grad * cosine - partner(turned_grad) * sine
        lows.append(raw_grad.astype(bf16))
    lows.append(dv_ref[...].astype(bf16))
    piece = jnp.zeros(piece_ref.shape, f32)
    for m, w_ref in enumerate((wq_ref, wk_ref, wv_ref)):
        grad_ref[:, m * width : (m + 1) * width] = lows[m]
        piece = piece + dot_nt(lows[m], w_ref[...])
    piece_ref[...] = piece.astype(bf16)


def project_back(index, grads, turned, weights, cosine, sine, gain, rows):
    length, width = grads[0].shape
    model = weights.shape[0]
    part = min(256, rows)
    per = rows // part
    blocks = length // part

    def column(m):
        return pl.BlockSpec((model, width), lambda i, at: (0, m))

    def turn(i, at):
        return (lax.rem(at[0] * per + i, blocks), 0)

    tall = pl.BlockSpec((part, width), turn)
    table = pl.BlockSpec((part, 128), turn)
    return pl.pallas_call(
        project_back_kernel,
        grid_spec=pltpu.PrefetchScalarGridSpec(
            num_scalar_prefetch=1,
            grid=(blocks,),
            in_specs=[tall] * 5
            + [column(0), column(1), column(2), table, table]
            + [pl.BlockSpec((1, width), lambda i, at: (0, 0))],
            out_specs=[
                pl.BlockSpec((part, 3 * width), lambda i, at: (i, 0)),
                pl.BlockSpec((part, model), lambda i, at: (i, 0)),
                pl.BlockSpec((1, width), lambda i, at: (0, 0)),
            ],
        ),
        out_shape=[
            jax.ShapeDtypeStruct((length, 3 * width), bf16),
            jax.ShapeDtypeStruct((length, model), bf16),
            jax.ShapeDtypeStruct((1, width), f32),
        ],
        cost_estimate=pl.CostEstimate(
            flops=8 * length * model * width,
            bytes_accessed=32 * length * width,
            transcendentals=0,
        ),
        name="project_back",
    )(index, *grads, *turned, weights, weights, weights, cosine, sine, gain)


def projection_grads_kernel(count, *refs):
    hidden, attended = refs[:count], refs[count : 2 * count]
    grad_ref, branch_ref, out_ref = refs[2 * count :]
    rows = branch_ref.shape[0]
    width = attended[0].shape[1]
    total = dot_tn(hidden[0][...], grad_ref[:rows, :])
    for d in range(1, count):
        total = total + dot_tn(hidden[d][...], grad_ref[d * rows : (d + 1) * rows, :])
    out_ref[:, : 3 * width] = total.astype(bf16)
    turned = branch_ref[...].T
    for d in range(count):
        out_ref[:, (3 + d) * width : (4 + d) * width] = dot_nn(turned, attended[d][...]).astype(
            bf16
        )


def projection_grads(hidden, attended, qkv_grad, branch_grad):
    count = len(hidden)
    rows, model = branch_grad.shape
    width = attended[0].shape[1]
    part = 256
    column = pl.BlockSpec((rows, part), lambda i: (0, i))

    def whole(x):
        return pl.BlockSpec(x.shape, lambda i: (0, 0))

    return pl.pallas_call(
        functools.partial(projection_grads_kernel, count),
        grid=(model // part,),
        in_specs=[column] * count + [whole(x) for x in attended] + [whole(qkv_grad), column],
        out_specs=pl.BlockSpec((part, (3 + count) * width), lambda i: (i, 0)),
        out_shape=jax.ShapeDtypeStruct((model, (3 + count) * width), bf16),
        cost_estimate=pl.CostEstimate(
            flops=8 * rows * count * model * width,
            bytes_accessed=4 * rows * count * model,
            transcendentals=0,
        ),
        name="projection_grads",
    )(*hidden, *attended, qkv_grad, branch_grad)


def rms_scale(x):
    return lax.rsqrt(jnp.mean(x * x, axis=-1, keepdims=True) + norm_eps)


def mix_kernel(count, *refs):
    pieces, weights = refs[:count], refs[count : 2 * count]
    hidden_ref, rates_ref, branch_ref, middle_ref, low_ref, turned_ref = refs[2 * count :]
    branch = dot_nt(pieces[0][...], weights[0][...])
    for d in range(1, count):
        branch = branch + dot_nt(pieces[d][...], weights[d][...])
    branch_ref[...] = branch
    hidden = hidden_ref[...].astype(f32)
    mixed = hidden + rates_ref[0:1, :] * (branch * rms_scale(branch) - hidden)
    middle = mixed * rms_scale(mixed)
    middle_ref[...] = middle
    low_ref[...] = middle.astype(bf16)
    turned_ref[...] = middle.T.astype(bf16)


def mix(pieces, weights, hidden, rates):
    count = len(pieces)
    rows, model = hidden.shape
    width = pieces[0].shape[1]
    part = min(128, rows)

    def column(d):
        return pl.BlockSpec((model, width), lambda i: (0, 3 + d))

    wide = pl.BlockSpec((part, model), lambda i: (i, 0))
    return pl.pallas_call(
        functools.partial(mix_kernel, count),
        grid=(rows // part,),
        in_specs=[pl.BlockSpec((part, width), lambda i: (i, 0))] * count
        + [column(d) for d in range(count)]
        + [wide, pl.BlockSpec((2, model), lambda i: (0, 0))],
        out_specs=[wide, wide, wide, pl.BlockSpec((model, part), lambda i: (0, i))],
        out_shape=[
            jax.ShapeDtypeStruct((rows, model), f32),
            jax.ShapeDtypeStruct((rows, model), f32),
            jax.ShapeDtypeStruct((rows, model), bf16),
            jax.ShapeDtypeStruct((model, rows), bf16),
        ],
        cost_estimate=pl.CostEstimate(
            flops=2 * rows * model * model, bytes_accessed=14 * rows * model, transcendentals=0
        ),
        name="mix",
    )(*pieces, *([weights] * count), hidden, rates)


def block_of(w_ref):
    value = w_ref[:, 0, 0]
    return value.reshape(value.shape[0] * value.shape[1], value.shape[2])


def feed_kernel(
    m_ref,
    wu_ref,
    wg_ref,
    wd_ref,
    s_ref,
    middle_ref,
    cot_ref,
    live_ref,
    rates_ref,
    up_ref,
    gate_ref,
    h_ref,
    result_ref,
    direct_ref,
    low_ref,
    turned_ref,
    rate_ref,
    acc,
):
    i = pl.program_id(0)
    tokens = m_ref[...]
    up = dot_nn(tokens, block_of(wu_ref))
    gate = dot_nn(tokens, block_of(wg_ref))
    up_ref[...] = up
    gate_ref[...] = gate
    scaled = gate * s_ref[1:2, :]
    hidden = (up * s_ref[0:1, :] * (scaled * jax.nn.sigmoid(scaled))).astype(bf16)
    h_ref[...] = hidden
    part_out = dot_nt(hidden, block_of(wd_ref))

    @pl.when(i == 0)
    def _():
        acc[...] = part_out

    @pl.when(i > 0)
    def _():
        acc[...] += part_out

    @pl.when(i == pl.num_programs(0) - 1)
    def _():
        rate_ref[...] = jnp.zeros_like(rate_ref)
        rate = rates_ref[1:2, :]
        part = 32

        def body(at, carry):
            rows = pl.ds(pl.multiple_of(at * part, part), part)
            out = acc[rows, :]
            middle = middle_ref[rows, :]
            out_scale = rms_scale(out)
            unit = out * out_scale
            mixed = middle + rate * (unit - middle)
            scale = rms_scale(mixed)
            final = mixed * scale
            result_ref[rows, :] = final.astype(bf16)
            grad = cot_ref[rows, :].astype(f32) * live_ref[rows, :]
            mixed_grad = scale * (grad - final * jnp.mean(final * grad, axis=-1, keepdims=True))
            direct_ref[rows, :] = mixed_grad * (1.0 - rate)
            rate_ref[...] += jnp.sum(mixed_grad * (unit - middle), axis=0, keepdims=True)
            unit_grad = mixed_grad * rate
            out_grad = out_scale * (
                unit_grad - unit * jnp.mean(unit * unit_grad, axis=-1, keepdims=True)
            )
            low_ref[rows, :] = out_grad.astype(bf16)
            return carry

        lax.fori_loop(0, acc.shape[0] // part, body, 0)
        for at in range(acc.shape[0] // 128):
            rows = slice(at * 128, (at + 1) * 128)
            turned_ref[:, rows] = low_ref[rows, :].T


def weight_specs(weights, step):
    nd, _, _, shard, local_width = weights.shape
    per = local_width // step

    def spec(m):
        return pl.BlockSpec((nd, 1, 1, shard, step), lambda i: (0, i // per, m, 0, i % per))

    return [spec(0), spec(1), spec(2)]


def feed(low, weights, scales, middle, cotangent, live, rates, step):
    rows, model = low.shape
    total = weights.shape[1] * weights.shape[4]
    columns = pl.BlockSpec((rows, step), lambda i: (0, i))
    whole = pl.BlockSpec((rows, model), lambda i: (0, 0))
    return pl.pallas_call(
        feed_kernel,
        grid=(total // step,),
        in_specs=[whole]
        + weight_specs(weights, step)
        + [
            pl.BlockSpec((2, step), lambda i: (0, i)),
            whole,
            whole,
            pl.BlockSpec((rows, 1), lambda i: (0, 0)),
            pl.BlockSpec((2, model), lambda i: (0, 0)),
        ],
        out_specs=[columns, columns, columns, whole, whole, whole]
        + [
            pl.BlockSpec((model, rows), lambda i: (0, 0)),
            pl.BlockSpec((1, model), lambda i: (0, 0)),
        ],
        out_shape=[
            jax.ShapeDtypeStruct((rows, total), f32),
            jax.ShapeDtypeStruct((rows, total), f32),
            jax.ShapeDtypeStruct((rows, total), bf16),
            jax.ShapeDtypeStruct((rows, model), bf16),
            jax.ShapeDtypeStruct((rows, model), f32),
            jax.ShapeDtypeStruct((rows, model), bf16),
            jax.ShapeDtypeStruct((model, rows), bf16),
            jax.ShapeDtypeStruct((1, model), f32),
        ],
        scratch_shapes=[pltpu.VMEM((rows, model), f32)],
        cost_estimate=pl.CostEstimate(
            flops=6 * rows * model * total,
            bytes_accessed=6 * model * total + 10 * rows * total,
            transcendentals=0,
        ),
        name="feed",
    )(low, weights, weights, weights, scales, middle, cotangent, live, rates)


def feed_back_kernel(
    og_ref,
    ogt_ref,
    mt_ref,
    wu_ref,
    wg_ref,
    wd_ref,
    s_ref,
    up_ref,
    gate_ref,
    h_ref,
    direct_ref,
    branch_ref,
    hidden_ref,
    rates_ref,
    grad_ref,
    sg_ref,
    token_ref,
    low_ref,
    rate_ref,
    acc,
):
    i = pl.program_id(0)
    grad_ref[2] = dot_nn(ogt_ref[...], h_ref[...]).astype(bf16)
    hidden_grad = dot_nn(og_ref[...], block_of(wd_ref))
    up = up_ref[...]
    gate = gate_ref[...]
    up_gain = s_ref[0:1, :]
    gate_gain = s_ref[1:2, :]
    scaled = gate * gate_gain
    sig = jax.nn.sigmoid(scaled)
    up_part = hidden_grad * (scaled * sig)
    gate_part = hidden_grad * (up * up_gain) * (sig * (1.0 + scaled * (1.0 - sig)))
    sg_ref[0:1, :] = jnp.sum(up_part * up, axis=0, keepdims=True)
    sg_ref[1:2, :] = jnp.sum(gate_part * gate, axis=0, keepdims=True)
    up_low = (up_part * up_gain).astype(bf16)
    gate_low = (gate_part * gate_gain).astype(bf16)
    tokens_t = mt_ref[...]
    grad_ref[0] = dot_nn(tokens_t, up_low).astype(bf16)
    grad_ref[1] = dot_nn(tokens_t, gate_low).astype(bf16)
    back = dot_nt(up_low, block_of(wu_ref)) + dot_nt(gate_low, block_of(wg_ref))

    @pl.when(i == 0)
    def _():
        acc[...] = direct_ref[...] + back

    @pl.when(i > 0)
    def _():
        acc[...] += back

    @pl.when(i == pl.num_programs(0) - 1)
    def _():
        rate_ref[...] = jnp.zeros_like(rate_ref)
        rate = rates_ref[0:1, :]
        part = 32

        def body(at, carry):
            rows = pl.ds(pl.multiple_of(at * part, part), part)
            grad = acc[rows, :]
            branch = branch_ref[rows, :]
            hidden = hidden_ref[rows, :].astype(f32)
            branch_scale = rms_scale(branch)
            unit = branch * branch_scale
            mixed = hidden + rate * (unit - hidden)
            scale = rms_scale(mixed)
            middle = mixed * scale
            mixed_grad = scale * (grad - middle * jnp.mean(middle * grad, axis=-1, keepdims=True))
            token_ref[rows, :] = mixed_grad * (1.0 - rate)
            rate_ref[...] += jnp.sum(mixed_grad * (unit - hidden), axis=0, keepdims=True)
            unit_grad = mixed_grad * rate
            branch_grad = branch_scale * (
                unit_grad - unit * jnp.mean(unit * unit_grad, axis=-1, keepdims=True)
            )
            low_ref[rows, :] = branch_grad.astype(bf16)
            return carry

        lax.fori_loop(0, acc.shape[0] // part, body, 0)


def feed_back(
    out_grad, out_grad_t, middle_t, weights, scales, up, gate, hidden_units, direct, branch, hidden, rates, step
):
    model, rows = middle_t.shape
    total = weights.shape[1] * weights.shape[4]
    columns = pl.BlockSpec((rows, step), lambda i: (0, i))
    whole = pl.BlockSpec((rows, model), lambda i: (0, 0))
    turned = pl.BlockSpec((model, rows), lambda i: (0, 0))
    return pl.pallas_call(
        feed_back_kernel,
        grid=(total // step,),
        in_specs=[whole, turned, turned]
        + weight_specs(weights, step)
        + [
            pl.BlockSpec((2, step), lambda i: (0, i)),
            columns,
            columns,
            columns,
            whole,
            whole,
            whole,
            pl.BlockSpec((2, model), lambda i: (0, 0)),
        ],
        out_specs=[
            pl.BlockSpec((3, model, step), lambda i: (0, 0, i)),
            pl.BlockSpec((2, step), lambda i: (0, i)),
            whole,
            whole,
            pl.BlockSpec((1, model), lambda i: (0, 0)),
        ],
        out_shape=[
            jax.ShapeDtypeStruct((3, model, total), bf16),
            jax.ShapeDtypeStruct((2, total), f32),
            jax.ShapeDtypeStruct((rows, model), f32),
            jax.ShapeDtypeStruct((rows, model), bf16),
            jax.ShapeDtypeStruct((1, model), f32),
        ],
        scratch_shapes=[pltpu.VMEM((rows, model), f32)],
        cost_estimate=pl.CostEstimate(
            flops=12 * rows * model * total,
            bytes_accessed=12 * model * total + 10 * rows * total,
            transcendentals=0,
        ),
        name="feed_back",
    )(
        out_grad,
        out_grad_t,
        middle_t,
        weights,
        weights,
        weights,
        scales,
        up,
        gate,
        hidden_units,
        direct,
        branch,
        hidden,
        rates,
    )


def shift(value, axis, distance, size):
    return lax.ppermute(value, axis, [(i, (i + distance) % size) for i in range(size)])


def butterfly(values, axis, size):
    step = 1
    while step < size:
        other = [lax.ppermute(v, axis, [(i, i ^ step) for i in range(size)]) for v in values]
        values = [v + o for v, o in zip(values, other)]
        step *= 2
    return values


def take_block(value, index, size, axis):
    return lax.dynamic_slice_in_dim(value, index * size, size, axis)


def put_block(whole, value, index, axis):
    return lax.dynamic_update_slice_in_dim(whole, value, index * value.shape[axis], axis)


def local(
    nd,
    nt,
    hidden_in,
    cotangent,
    segments,
    attn_weight,
    mlp_weight,
    rates,
    qk_scale,
    mlp_scales,
    attn_moment_one,
    attn_moment_two,
    mlp_moment_one,
    mlp_moment_two,
):
    rows, model = hidden_in.shape
    length = segments.shape[0]
    shard = attn_weight.shape[1]
    heads_width = attn_weight.shape[2]
    hidden_width = mlp_weight.shape[2]
    block = min(512, length)
    step = min(512, hidden_width)
    me = lax.axis_index("tensor")

    def gather(value):
        return [value] + [shift(value, "tensor", d, nt) for d in range(1, nt)]

    attn_low = attn_weight.astype(bf16)
    attn_shard = jnp.concatenate(
        [attn_low[0], attn_low[1], attn_low[2]] + gather(attn_low[3]), axis=1
    )
    attn_full = lax.all_gather(attn_shard, "dp", axis=0, tiled=True)
    mlp_low = mlp_weight.astype(bf16).reshape(3 * shard, hidden_width)
    mlp_parts = gather(mlp_low)
    scales_row = jnp.concatenate(gather(mlp_scales), axis=1)
    hidden_in, mlp_parts = lax.optimization_barrier((hidden_in, mlp_parts))
    mlp_full = lax.all_gather(jnp.concatenate(mlp_parts, axis=0), "dp", axis=0, tiled=True)
    mlp_full = mlp_full.reshape(nd, nt, 3, shard, hidden_width)

    starts = starts_of(segments)
    positions = (jnp.arange(length, dtype=jnp.int32) - starts).astype(f32)
    lane = jnp.arange(128, dtype=jnp.int32)
    half = HEAD_DIM // 2
    frequency = 10000.0 ** (-(lane % half).astype(f32) / half)
    sign = jnp.where(lane % HEAD_DIM < half, -1.0, 1.0)
    angles = positions[:, None] * frequency[None, :]
    cosine = jnp.cos(angles)
    sine = jnp.sin(angles) * sign[None, :]
    gain = qk_scale.reshape(1, heads_width)

    hidden_parts = gather(hidden_in)
    state = ()
    for d in range(nt):
        index = ((me + nt - d) % nt).reshape(1)
        state = project(index, hidden_parts[d], attn_full, cosine, sine, gain, length, state)
    query_hat, key_hat, value_hat, query_turned, key_turned = state
    attended_row, attended_f32, log_sum = attend(
        query_hat, key_hat, value_hat, starts[:, None], block
    )
    attended = [take_block(attended_row, me, rows, 0)] + [
        shift(take_block(attended_row, (me + d) % nt, rows, 0), "tensor", d, nt)
        for d in range(1, nt)
    ]
    branch, middle, middle_low, middle_t = mix(attended, attn_full, hidden_in, rates)
    row_segments = take_block(segments, me, rows, 0)
    live = (row_segments < pad_segment).astype(f32)[:, None]
    up, gate, hidden_units, result, middle_direct, mlp_out_low, mlp_out_t, rate_mlp_grad = feed(
        middle_low, mlp_full, scales_row, middle, cotangent, live, rates, step
    )
    mlp_grad, scales_grad, token_direct, branch_low, rate_attn_grad = feed_back(
        mlp_out_low,
        mlp_out_t,
        middle_t,
        mlp_full,
        scales_row,
        up,
        gate,
        hidden_units,
        middle_direct,
        branch,
        hidden_in,
        rates,
        step,
    )
    mlp_part = lax.psum_scatter(mlp_grad, "dp", scatter_dimension=1, tiled=True)

    def out_block(d):
        return attn_full[:, (3 + d) * heads_width : (4 + d) * heads_width]

    grad_row = jnp.zeros((length, heads_width), bf16)
    for d in list(range(1, nt)) + [0]:
        piece = dot_nn(branch_low, out_block(d)).astype(bf16)
        piece = shift(piece, "tensor", -d, nt) if d else piece
        grad_row = put_block(grad_row, piece, (me + d) % nt, 0)
    head_grads = attend_back(
        query_hat, key_hat, value_hat, grad_row, attended_f32, log_sum, starts[None, :], block
    )
    qkv_grad, pieces, gain_grad = project_back(
        me.reshape(1),
        head_grads,
        (query_turned, key_turned),
        attn_full,
        cosine,
        sine,
        gain,
        rows,
    )
    arrived = [
        shift(pieces[d * rows : (d + 1) * rows], "tensor", d, nt) for d in range(1, nt)
    ]
    total = token_direct + pieces[:rows].astype(f32)
    for piece in arrived:
        total = total + piece.astype(f32)
    input_grad = total.astype(bf16)
    hidden_turn = [hidden_parts[(nt - d) % nt] for d in range(nt)]
    attn_grad = projection_grads(hidden_turn, attended, qkv_grad, branch_low)
    attn_part = lax.psum_scatter(attn_grad, "dp", scatter_dimension=0, tiled=True)

    def own_sum(part, axis, width):
        total = lax.slice_in_dim(part, 0, width, axis=axis).astype(f32)
        for d in range(1, nt):
            piece = lax.slice_in_dim(part, d * width, (d + 1) * width, axis=axis)
            total = total + shift(piece, "tensor", -d, nt).astype(f32)
        return total

    mlp_part, arrived = lax.optimization_barrier((mlp_part, arrived))
    mlp_weight_grad = own_sum(mlp_part, 2, hidden_width)
    attn_part, mlp_weight_grad = lax.optimization_barrier((attn_part, mlp_weight_grad))
    out_own = own_sum(attn_part[:, 3 * heads_width :], 1, heads_width)
    attn_weight_grad = jnp.stack(
        [
            attn_part[:, :heads_width].astype(f32),
            attn_part[:, heads_width : 2 * heads_width].astype(f32),
            attn_part[:, 2 * heads_width : 3 * heads_width].astype(f32),
            out_own,
        ]
    )

    def spread(value):
        width = value.shape[1] // nt
        whole = jnp.zeros_like(value)
        for d in range(nt):
            piece = value[:, d * width : (d + 1) * width]
            whole = put_block(whole, piece, (me + nt - d) % nt, 1)
        return whole

    scales_grad = spread(scales_grad).reshape(-1, model)
    small = jnp.concatenate([rate_attn_grad, rate_mlp_grad, scales_grad], axis=0)
    (small,) = butterfly([small], "dp", nd)
    (small,) = butterfly([small], "tensor", nt)
    rates_grad = small[:2]
    mlp_scales_grad = small[2:].reshape(2, nt * hidden_width)

    attn_one, attn_two, attn_moved = adam_moved(
        attn_weight, attn_weight_grad, attn_moment_one, attn_moment_two
    )
    mlp_one, mlp_two, mlp_moved = adam_moved(
        mlp_weight, mlp_weight_grad, mlp_moment_one, mlp_moment_two
    )
    attn_square = jnp.sum(attn_moved * attn_moved, axis=1, keepdims=True)
    mlp_square = jnp.sum(mlp_moved * mlp_moved, axis=1, keepdims=True)
    (mlp_square,) = butterfly([mlp_square], "dp", nd)
    last = jnp.concatenate([attn_square.reshape(1, -1), gain_grad], axis=1)
    (last,) = butterfly([last], "dp", nd)
    attn_square = last[:, : 4 * heads_width].reshape(4, 1, heads_width)
    gain_row = spread(jnp.concatenate(gather(last[:, 4 * heads_width :]), axis=1)).reshape(-1)
    attn_new = attn_moved * lax.rsqrt(attn_square + norm_eps)
    mlp_new = mlp_moved * lax.rsqrt(mlp_square + norm_eps)
    return (
        result.astype(bf16),
        input_grad,
        attn_weight_grad,
        mlp_weight_grad,
        rates_grad,
        gain_row,
        mlp_scales_grad,
        attn_one,
        attn_two,
        mlp_one,
        mlp_two,
        attn_new,
        mlp_new,
    )


def solution(mesh):
    weights = P(None, "dp", "tensor")
    tokens = P(("dp", "tensor"), None)
    return jax.shard_map(
        functools.partial(local, mesh.shape["dp"], mesh.shape["tensor"]),
        mesh=mesh,
        in_specs=(
            tokens,
            tokens,
            P("dp"),
            weights,
            weights,
            P(),
            P("tensor"),
            P(None, "tensor"),
            weights,
            weights,
            weights,
            weights,
        ),
        out_specs=(
            tokens,
            tokens,
            weights,
            weights,
            P(),
            P(),
            P(),
            weights,
            weights,
            weights,
            weights,
            weights,
            weights,
        ),
        check_vma=False,
    )
```

```python
import functools
import math

import jax
import jax.numpy as jnp
from jax import lax
from jax.experimental import pallas as pl
from jax.experimental.pallas import tpu as pltpu
from jax.sharding import PartitionSpec as P

HEAD_DIM = 64
LOG2E = 1.4426950408889634

norm_eps = 1e-06
pad_segment = 63
beta_one = 0.9
beta_two = 0.95
learning_rate = 0.01
adam_eps = 1e-08
bias_one = 1.0 - 0.9**10
bias_two = 1.0 - 0.95**10
scale_factor = math.sqrt(HEAD_DIM)
f32 = jnp.float32
bf16 = jnp.bfloat16


def starts_of(segment_row):
    indices = jnp.arange(segment_row.shape[0], dtype=jnp.int32)
    changed = jnp.concatenate(
        [jnp.ones((1,), dtype=jnp.bool_), segment_row[1:] != segment_row[:-1]]
    )
    return lax.cummax(jnp.where(changed, indices, jnp.zeros_like(indices)), axis=0)


def adam_moved(weight, gradient, moment_one, moment_two):
    moment_one_new = beta_one * moment_one + (1.0 - beta_one) * gradient
    moment_two_new = beta_two * moment_two + (1.0 - beta_two) * gradient * gradient
    moved = weight - learning_rate * (moment_one_new / bias_one) / (
        jnp.sqrt(moment_two_new / bias_two) + adam_eps
    )
    return (moment_one_new, moment_two_new, moved)


def dot_nt(a, b):
    return lax.dot_general(a, b, (((1,), (1,)), ((), ())), preferred_element_type=f32)


def dot_nn(a, b):
    return lax.dot_general(a, b, (((1,), (0,)), ((), ())), preferred_element_type=f32)


def dot_tn(a, b):
    return lax.dot_general(a, b, (((0,), (0,)), ((), ())), preferred_element_type=f32)


def head_stack(x, heads):
    lane = lax.broadcasted_iota(jnp.int32, x.shape, 1) // HEAD_DIM
    zero = jnp.zeros_like(x)
    return jnp.concatenate([jnp.where(lane == h, x, zero) for h in range(heads)], axis=0)


def head_pick(stacked, heads, rows):
    width = stacked.shape[1]
    lane = lax.broadcasted_iota(jnp.int32, (rows, width), 1) // HEAD_DIM
    picked = jnp.zeros((rows, width), f32)
    for h in range(heads):
        picked = jnp.where(lane == h, stacked[h * rows : (h + 1) * rows], picked)
    return picked


def attend_kernel(heads, bq, bk, q_ref, k_ref, v_ref, start_ref, o_ref, of_ref, l_ref, acc, lsum):
    i = pl.program_id(0)
    qs = head_stack(q_ref[...], heads)
    acc[...] = jnp.zeros_like(acc)
    lsum[...] = jnp.zeros_like(lsum)
    start = jnp.concatenate([start_ref[...]] * heads, axis=0)

    def step(j, diagonal):
        offset = pl.multiple_of(j * bk, bk)
        keys = k_ref[pl.ds(offset, bk), :]
        values = v_ref[pl.ds(offset, bk), :]
        scores = dot_nt(qs, keys)
        key_index = offset + lax.broadcasted_iota(jnp.int32, scores.shape, 1)
        allowed = key_index >= start
        if diagonal:
            row = lax.rem(lax.broadcasted_iota(jnp.int32, scores.shape, 0), bq)
            allowed = allowed & (key_index <= i * bq + row)
        weights = jnp.where(allowed, jnp.exp2(scores * (scale_factor * LOG2E)), 0.0)
        total = weights[:, :128]
        for part in range(1, bk // 128):
            total = total + weights[:, part * 128 : (part + 1) * 128]
        lsum[...] += total
        acc[...] += dot_nn(weights.astype(bf16), values)

    def body(j, carry):
        step(j, False)
        return carry

    lax.fori_loop(0, i, body, 0)
    step(i, True)
    summed = jnp.sum(lsum[...], axis=1, keepdims=True)
    out = head_pick(acc[...] * (1.0 / summed), heads, bq)
    of_ref[...] = out
    o_ref[...] = out.astype(bf16)
    l_ref[...] = jnp.log2(summed).reshape(heads, bq)


def attend(q, k, v, start, block):
    length, width = q.shape
    heads = width // HEAD_DIM
    whole = pl.BlockSpec((length, width), lambda i: (0, 0))
    rows = pl.BlockSpec((block, width), lambda i: (i, 0))
    return pl.pallas_call(
        functools.partial(attend_kernel, heads, block, block),
        grid=(length // block,),
        in_specs=[rows, whole, whole, pl.BlockSpec((block, 1), lambda i: (i, 0))],
        out_specs=[rows, rows, pl.BlockSpec((heads, block), lambda i: (0, i))],
        out_shape=[
            jax.ShapeDtypeStruct((length, width), bf16),
            jax.ShapeDtypeStruct((length, width), f32),
            jax.ShapeDtypeStruct((heads, length), f32),
        ],
        scratch_shapes=[
            pltpu.VMEM((heads * block, width), f32),
            pltpu.VMEM((heads * block, 128), f32),
        ],
        cost_estimate=pl.CostEstimate(
            flops=20_000_000_000, bytes_accessed=8 * length * width, transcendentals=0
        ),
        name="attend",
    )(q, k, v, start)


def attend_back_kernel(
    heads, bq, bk, q_ref, do_ref, k_ref, v_ref, of_ref, l_ref, start_ref, dq_ref, dk_ref, dv_ref, acc
):
    i = pl.program_id(0)

    @pl.when(i == 0)
    def _():
        dk_ref[...] = jnp.zeros_like(dk_ref)
        dv_ref[...] = jnp.zeros_like(dv_ref)

    qs = head_stack(q_ref[...], heads)
    grads = do_ref[...]
    dos = head_stack(grads, heads)
    product = (grads.astype(f32) * of_ref[...]).T
    delta = jnp.concatenate(
        [
            jnp.sum(product[h * HEAD_DIM : (h + 1) * HEAD_DIM], axis=0, keepdims=True)
            for h in range(heads)
        ],
        axis=1,
    )
    log_sum = jnp.concatenate([l_ref[h : h + 1, :] for h in range(heads)], axis=1)
    start = jnp.concatenate([start_ref[...]] * heads, axis=1)
    acc[...] = jnp.zeros_like(acc)

    def step(j, diagonal):
        offset = pl.multiple_of(j * bk, bk)
        keys = k_ref[pl.ds(offset, bk), :]
        values = v_ref[pl.ds(offset, bk), :]
        scores = dot_nt(keys, qs)
        key_index = offset + lax.broadcasted_iota(jnp.int32, scores.shape, 0)
        allowed = key_index >= start
        if diagonal:
            column = lax.rem(lax.broadcasted_iota(jnp.int32, scores.shape, 1), bq)
            allowed = allowed & (key_index <= i * bq + column)
        probs = jnp.where(allowed, jnp.exp2(scores * (scale_factor * LOG2E) - log_sum), 0.0)
        prob_grad = dot_nt(values, dos)
        score_grad = (probs * (prob_grad - delta)).astype(bf16)
        dv_ref[pl.ds(offset, bk), :] += dot_nn(probs.astype(bf16), dos)
        dk_ref[pl.ds(offset, bk), :] += dot_nn(score_grad, qs)
        acc[...] += dot_tn(score_grad, keys)

    def body(j, carry):
        step(j, False)
        return carry

    lax.fori_loop(0, i, body, 0)
    step(i, True)
    dq_ref[...] = head_pick(acc[...], heads, bq)


def attend_back(q, k, v, grads, out, log_sum, start, block):
    length, width = q.shape
    heads = width // HEAD_DIM
    whole = pl.BlockSpec((length, width), lambda i: (0, 0))
    rows = pl.BlockSpec((block, width), lambda i: (i, 0))
    result = jax.ShapeDtypeStruct((length, width), f32)
    return pl.pallas_call(
        functools.partial(attend_back_kernel, heads, block, block),
        grid=(length // block,),
        in_specs=[
            rows,
            rows,
            whole,
            whole,
            rows,
            pl.BlockSpec((heads, block), lambda i: (0, i)),
            pl.BlockSpec((1, block), lambda i: (0, i)),
        ],
        out_specs=[rows, whole, whole],
        out_shape=[result, result, result],
        scratch_shapes=[pltpu.VMEM((heads * block, width), f32)],
        cost_estimate=pl.CostEstimate(
            flops=40_000_000_000, bytes_accessed=20 * length * width, transcendentals=0
        ),
        name="attend_back",
    )(q, grads, k, v, out, log_sum, start)


def partner(x):
    width = x.shape[1]
    lane = lax.broadcasted_iota(jnp.int32, x.shape, 1)
    ahead = pltpu.roll(x, width - HEAD_DIM // 2, 1)
    behind = pltpu.roll(x, HEAD_DIM // 2, 1)
    return jnp.where(lax.rem(lane, HEAD_DIM) < HEAD_DIM // 2, ahead, behind)


def head_sums(x):
    width = x.shape[1]
    row = lax.broadcasted_iota(jnp.int32, (width, width), 0) // HEAD_DIM
    column = lax.broadcasted_iota(jnp.int32, (width, width), 1) // HEAD_DIM
    same = jnp.where(row == column, 1.0, 0.0).astype(f32)
    return lax.dot_general(
        x,
        same,
        (((1,), (0,)), ((), ())),
        precision=lax.Precision.HIGHEST,
        preferred_element_type=f32,
    )


def widen(table, width):
    return table if table.shape[1] == width else jnp.concatenate([table] * (width // 128), axis=1)


def project_kernel(index_ref, x_ref, wq_ref, wk_ref, wv_ref, cos_ref, sin_ref, gain_ref, *refs):
    q_ref, k_ref, v_ref, xq_ref, xk_ref = refs[-5:]
    x = x_ref[...]
    width = q_ref.shape[1]
    cosine = widen(cos_ref[...], width)
    sine = widen(sin_ref[...], width)
    gain = gain_ref[...]
    for w_ref, hat_ref, turned_ref in ((wq_ref, q_ref, xq_ref), (wk_ref, k_ref, xk_ref)):
        raw = dot_nn(x, w_ref[...])
        turned = raw * cosine + partner(raw) * sine
        turned_ref[...] = turned
        hat = turned * lax.rsqrt(head_sums(turned * turned) + norm_eps) * gain
        hat_ref[...] = hat.astype(bf16)
    v_ref[...] = dot_nn(x, wv_ref[...]).astype(bf16)


def project(index, x, weights, cosine, sine, gain, length, previous):
    rows, model = x.shape
    width = gain.shape[1]
    part = min(256, rows)
    per = rows // part

    def column(m):
        return pl.BlockSpec((model, width), lambda i, at: (0, m))

    table = pl.BlockSpec((part, 128), lambda i, at: (at[0] * per + i, 0))
    out = pl.BlockSpec((part, width), lambda i, at: (at[0] * per + i, 0))
    low = jax.ShapeDtypeStruct((length, width), bf16)
    wide = jax.ShapeDtypeStruct((length, width), f32)
    return pl.pallas_call(
        project_kernel,
        grid_spec=pltpu.PrefetchScalarGridSpec(
            num_scalar_prefetch=1,
            grid=(per,),
            in_specs=[
                pl.BlockSpec((part, model), lambda i, at: (i, 0)),
                column(0),
                column(1),
                column(2),
                table,
                table,
                pl.BlockSpec((1, width), lambda i, at: (0, 0)),
            ]
            + [pl.BlockSpec(memory_space=pl.ANY)] * len(previous),
            out_specs=[out] * 5,
        ),
        out_shape=[low, low, low, wide, wide],
        input_output_aliases={8 + i: i for i in range(len(previous))},
        cost_estimate=pl.CostEstimate(
            flops=6 * rows * model * width, bytes_accessed=8 * model * width, transcendentals=0
        ),
        name="project",
    )(index, x, weights, weights, weights, cosine, sine, gain, *previous)


def project_back_kernel(
    index_ref,
    dq_ref,
    dk_ref,
    dv_ref,
    xq_ref,
    xk_ref,
    wq_ref,
    wk_ref,
    wv_ref,
    cos_ref,
    sin_ref,
    gain_ref,
    grad_ref,
    piece_ref,
    gain_grad_ref,
):
    @pl.when(pl.program_id(0) == 0)
    def _():
        gain_grad_ref[...] = jnp.zeros_like(gain_grad_ref)

    width = dq_ref.shape[1]
    cosine = widen(cos_ref[...], width)
    sine = widen(sin_ref[...], width)
    gain = gain_ref[...]
    lows = []
    for d_ref, x_ref in ((dq_ref, xq_ref), (dk_ref, xk_ref)):
        turned = x_ref[...]
        inverse = lax.rsqrt(head_sums(turned * turned) + norm_eps)
        unit = turned * inverse
        hat_grad = d_ref[...] * scale_factor
        gain_grad_ref[...] += jnp.sum(hat_grad * unit, axis=0, keepdims=True)
        unit_grad = hat_grad * gain
        turned_grad = inverse * (unit_grad - unit * head_sums(unit * unit_grad))
        raw_grad = turned_grad * cosine - partner(turned_grad) * sine
        lows.append(raw_grad.astype(bf16))
    lows.append(dv_ref[...].astype(bf16))
    piece = jnp.zeros(piece_ref.shape, f32)
    for m, w_ref in enumerate((wq_ref, wk_ref, wv_ref)):
        grad_ref[:, m * width : (m + 1) * width] = lows[m]
        piece = piece + dot_nt(lows[m], w_ref[...])
    piece_ref[...] = piece.astype(bf16)


def project_back(index, grads, turned, weights, cosine, sine, gain, rows):
    length, width = grads[0].shape
    model = weights.shape[0]
    part = min(256, rows)
    per = rows // part
    blocks = length // part

    def column(m):
        return pl.BlockSpec((model, width), lambda i, at: (0, m))

    def turn(i, at):
        return (lax.rem(at[0] * per + i, blocks), 0)

    tall = pl.BlockSpec((part, width), turn)
    table = pl.BlockSpec((part, 128), turn)
    return pl.pallas_call(
        project_back_kernel,
        grid_spec=pltpu.PrefetchScalarGridSpec(
            num_scalar_prefetch=1,
            grid=(blocks,),
            in_specs=[tall] * 5
            + [column(0), column(1), column(2), table, table]
            + [pl.BlockSpec((1, width), lambda i, at: (0, 0))],
            out_specs=[
                pl.BlockSpec((part, 3 * width), lambda i, at: (i, 0)),
                pl.BlockSpec((part, model), lambda i, at: (i, 0)),
                pl.BlockSpec((1, width), lambda i, at: (0, 0)),
            ],
        ),
        out_shape=[
            jax.ShapeDtypeStruct((length, 3 * width), bf16),
            jax.ShapeDtypeStruct((length, model), bf16),
            jax.ShapeDtypeStruct((1, width), f32),
        ],
        cost_estimate=pl.CostEstimate(
            flops=8 * length * model * width,
            bytes_accessed=32 * length * width,
            transcendentals=0,
        ),
        name="project_back",
    )(index, *grads, *turned, weights, weights, weights, cosine, sine, gain)


def projection_grads_kernel(count, *refs):
    hidden = refs[:count]
    grad_ref, out_ref = refs[count:]
    rows = hidden[0].shape[0]
    total = dot_tn(hidden[0][...], grad_ref[:rows, :])
    for d in range(1, count):
        total = total + dot_tn(hidden[d][...], grad_ref[d * rows : (d + 1) * rows, :])
    out_ref[...] = total.astype(bf16)


def projection_grads(hidden, qkv_grad):
    count = len(hidden)
    rows, model = hidden[0].shape
    width = qkv_grad.shape[1]
    part = 256
    column = pl.BlockSpec((rows, part), lambda i: (0, i))
    return pl.pallas_call(
        functools.partial(projection_grads_kernel, count),
        grid=(model // part,),
        in_specs=[column] * count + [pl.BlockSpec(qkv_grad.shape, lambda i: (0, 0))],
        out_specs=pl.BlockSpec((part, width), lambda i: (i, 0)),
        out_shape=jax.ShapeDtypeStruct((model, width), bf16),
        cost_estimate=pl.CostEstimate(
            flops=2 * rows * count * model * width,
            bytes_accessed=4 * rows * count * model,
            transcendentals=0,
        ),
        name="projection_grads",
    )(*hidden, qkv_grad)


def out_grads_kernel(count, *refs):
    attended = refs[:count]
    branch_ref, out_ref = refs[count:]
    width = attended[0].shape[1]
    turned = branch_ref[...].T
    for d in range(count):
        out_ref[:, d * width : (d + 1) * width] = dot_nn(turned, attended[d][...]).astype(bf16)


def out_grads(attended, branch_grad):
    count = len(attended)
    rows, model = branch_grad.shape
    width = attended[0].shape[1]
    part = 256
    return pl.pallas_call(
        functools.partial(out_grads_kernel, count),
        grid=(model // part,),
        in_specs=[pl.BlockSpec(x.shape, lambda i: (0, 0)) for x in attended]
        + [pl.BlockSpec((rows, part), lambda i: (0, i))],
        out_specs=pl.BlockSpec((part, count * width), lambda i: (i, 0)),
        out_shape=jax.ShapeDtypeStruct((model, count * width), bf16),
        cost_estimate=pl.CostEstimate(
            flops=2 * rows * count * model * width,
            bytes_accessed=4 * rows * count * model,
            transcendentals=0,
        ),
        name="out_grads",
    )(*attended, branch_grad)


def rms_scale(x):
    return lax.rsqrt(jnp.mean(x * x, axis=-1, keepdims=True) + norm_eps)


def mix_kernel(count, *refs):
    pieces, weights = refs[:count], refs[count : 2 * count]
    hidden_ref, rates_ref, branch_ref, middle_ref, low_ref, turned_ref = refs[2 * count :]
    branch = dot_nt(pieces[0][...], weights[0][...])
    for d in range(1, count):
        branch = branch + dot_nt(pieces[d][...], weights[d][...])
    branch_ref[...] = branch
    hidden = hidden_ref[...].astype(f32)
    mixed = hidden + rates_ref[0:1, :] * (branch * rms_scale(branch) - hidden)
    middle = mixed * rms_scale(mixed)
    middle_ref[...] = middle
    low_ref[...] = middle.astype(bf16)
    turned_ref[...] = middle.T.astype(bf16)


def mix(pieces, weights, hidden, rates):
    count = len(pieces)
    rows, model = hidden.shape
    width = pieces[0].shape[1]
    part = min(128, rows)

    def column(d):
        return pl.BlockSpec((model, width), lambda i: (0, 3 + d))

    wide = pl.BlockSpec((part, model), lambda i: (i, 0))
    return pl.pallas_call(
        functools.partial(mix_kernel, count),
        grid=(rows // part,),
        in_specs=[pl.BlockSpec((part, width), lambda i: (i, 0))] * count
        + [column(d) for d in range(count)]
        + [wide, pl.BlockSpec((2, model), lambda i: (0, 0))],
        out_specs=[wide, wide, wide, pl.BlockSpec((model, part), lambda i: (0, i))],
        out_shape=[
            jax.ShapeDtypeStruct((rows, model), f32),
            jax.ShapeDtypeStruct((rows, model), f32),
            jax.ShapeDtypeStruct((rows, model), bf16),
            jax.ShapeDtypeStruct((model, rows), bf16),
        ],
        cost_estimate=pl.CostEstimate(
            flops=2 * rows * model * model, bytes_accessed=14 * rows * model, transcendentals=0
        ),
        name="mix",
    )(*pieces, *([weights] * count), hidden, rates)


def block_of(w_ref):
    value = w_ref[:, 0, 0]
    return value.reshape(value.shape[0] * value.shape[1], value.shape[2])


def feed_kernel(
    m_ref,
    wu_ref,
    wg_ref,
    wd_ref,
    s_ref,
    middle_ref,
    cot_ref,
    live_ref,
    rates_ref,
    up_ref,
    gate_ref,
    h_ref,
    result_ref,
    direct_ref,
    low_ref,
    turned_ref,
    rate_ref,
    acc,
):
    i = pl.program_id(0)
    tokens = m_ref[...]
    up = dot_nn(tokens, block_of(wu_ref))
    gate = dot_nn(tokens, block_of(wg_ref))
    up_ref[...] = up
    gate_ref[...] = gate
    scaled = gate * s_ref[1:2, :]
    hidden = (up * s_ref[0:1, :] * (scaled * jax.nn.sigmoid(scaled))).astype(bf16)
    h_ref[...] = hidden
    part_out = dot_nt(hidden, block_of(wd_ref))

    @pl.when(i == 0)
    def _():
        acc[...] = part_out

    @pl.when(i > 0)
    def _():
        acc[...] += part_out

    @pl.when(i == pl.num_programs(0) - 1)
    def _():
        rate_ref[...] = jnp.zeros_like(rate_ref)
        rate = rates_ref[1:2, :]
        part = 32

        def body(at, carry):
            rows = pl.ds(pl.multiple_of(at * part, part), part)
            out = acc[rows, :]
            middle = middle_ref[rows, :]
            out_scale = rms_scale(out)
            unit = out * out_scale
            mixed = middle + rate * (unit - middle)
            scale = rms_scale(mixed)
            final = mixed * scale
            result_ref[rows, :] = final.astype(bf16)
            grad = cot_ref[rows, :].astype(f32) * live_ref[rows, :]
            mixed_grad = scale * (grad - final * jnp.mean(final * grad, axis=-1, keepdims=True))
            direct_ref[rows, :] = mixed_grad * (1.0 - rate)
            rate_ref[...] += jnp.sum(mixed_grad * (unit - middle), axis=0, keepdims=True)
            unit_grad = mixed_grad * rate
            out_grad = out_scale * (
                unit_grad - unit * jnp.mean(unit * unit_grad, axis=-1, keepdims=True)
            )
            low_ref[rows, :] = out_grad.astype(bf16)
            return carry

        lax.fori_loop(0, acc.shape[0] // part, body, 0)
        for at in range(acc.shape[0] // 128):
            rows = slice(at * 128, (at + 1) * 128)
            turned_ref[:, rows] = low_ref[rows, :].T


def weight_specs(weights, step, base=0):
    nd, _, _, shard, local_width = weights.shape
    per = local_width // step

    def spec(m):
        return pl.BlockSpec(
            (nd, 1, 1, shard, step), lambda i: (0, (i + base) // per, m, 0, (i + base) % per)
        )

    return [spec(0), spec(1), spec(2)]


def feed(low, weights, scales, middle, cotangent, live, rates, step):
    rows, model = low.shape
    total = weights.shape[1] * weights.shape[4]
    columns = pl.BlockSpec((rows, step), lambda i: (0, i))
    whole = pl.BlockSpec((rows, model), lambda i: (0, 0))
    return pl.pallas_call(
        feed_kernel,
        grid=(total // step,),
        in_specs=[whole]
        + weight_specs(weights, step)
        + [
            pl.BlockSpec((2, step), lambda i: (0, i)),
            whole,
            whole,
            pl.BlockSpec((rows, 1), lambda i: (0, 0)),
            pl.BlockSpec((2, model), lambda i: (0, 0)),
        ],
        out_specs=[columns, columns, columns, whole, whole, whole]
        + [
            pl.BlockSpec((model, rows), lambda i: (0, 0)),
            pl.BlockSpec((1, model), lambda i: (0, 0)),
        ],
        out_shape=[
            jax.ShapeDtypeStruct((rows, total), f32),
            jax.ShapeDtypeStruct((rows, total), f32),
            jax.ShapeDtypeStruct((rows, total), bf16),
            jax.ShapeDtypeStruct((rows, model), bf16),
            jax.ShapeDtypeStruct((rows, model), f32),
            jax.ShapeDtypeStruct((rows, model), bf16),
            jax.ShapeDtypeStruct((model, rows), bf16),
            jax.ShapeDtypeStruct((1, model), f32),
        ],
        scratch_shapes=[pltpu.VMEM((rows, model), f32)],
        cost_estimate=pl.CostEstimate(
            flops=6 * rows * model * total,
            bytes_accessed=6 * model * total + 10 * rows * total,
            transcendentals=0,
        ),
        name="feed",
    )(low, weights, weights, weights, scales, middle, cotangent, live, rates)


def feed_back_step(
    og_ref, ogt_ref, mt_ref, wu_ref, wg_ref, wd_ref, s_ref, up_ref, gate_ref, h_ref, start_ref, grad_ref, sg_ref, acc
):
    i = pl.program_id(0)
    grad_ref[2] = dot_nn(ogt_ref[...], h_ref[...]).astype(bf16)
    hidden_grad = dot_nn(og_ref[...], block_of(wd_ref))
    up = up_ref[...]
    gate = gate_ref[...]
    up_gain = s_ref[0:1, :]
    gate_gain = s_ref[1:2, :]
    scaled = gate * gate_gain
    sig = jax.nn.sigmoid(scaled)
    up_part = hidden_grad * (scaled * sig)
    gate_part = hidden_grad * (up * up_gain) * (sig * (1.0 + scaled * (1.0 - sig)))
    sg_ref[0:1, :] = jnp.sum(up_part * up, axis=0, keepdims=True)
    sg_ref[1:2, :] = jnp.sum(gate_part * gate, axis=0, keepdims=True)
    up_low = (up_part * up_gain).astype(bf16)
    gate_low = (gate_part * gate_gain).astype(bf16)
    tokens_t = mt_ref[...]
    grad_ref[0] = dot_nn(tokens_t, up_low).astype(bf16)
    grad_ref[1] = dot_nn(tokens_t, gate_low).astype(bf16)
    back = dot_nt(up_low, block_of(wu_ref)) + dot_nt(gate_low, block_of(wg_ref))

    @pl.when(i == 0)
    def _():
        acc[...] = start_ref[...] + back

    @pl.when(i > 0)
    def _():
        acc[...] += back


def feed_back_first_kernel(*refs):
    feed_back_step(*refs)


def feed_back_last_kernel(*refs):
    branch_ref, hidden_ref, rates_ref = refs[11:14]
    grad_ref, sg_ref, token_ref, low_ref, rate_ref, acc = refs[14:]
    feed_back_step(*refs[:11], grad_ref, sg_ref, acc)

    @pl.when(pl.program_id(0) == pl.num_programs(0) - 1)
    def _():
        rate_ref[...] = jnp.zeros_like(rate_ref)
        rate = rates_ref[0:1, :]
        part = 32

        def body(at, carry):
            rows = pl.ds(pl.multiple_of(at * part, part), part)
            grad = acc[rows, :]
            branch = branch_ref[rows, :]
            hidden = hidden_ref[rows, :].astype(f32)
            branch_scale = rms_scale(branch)
            unit = branch * branch_scale
            mixed = hidden + rate * (unit - hidden)
            scale = rms_scale(mixed)
            middle = mixed * scale
            mixed_grad = scale * (grad - middle * jnp.mean(middle * grad, axis=-1, keepdims=True))
            token_ref[rows, :] = mixed_grad * (1.0 - rate)
            rate_ref[...] += jnp.sum(mixed_grad * (unit - hidden), axis=0, keepdims=True)
            unit_grad = mixed_grad * rate
            branch_grad = branch_scale * (
                unit_grad - unit * jnp.mean(unit * unit_grad, axis=-1, keepdims=True)
            )
            low_ref[rows, :] = branch_grad.astype(bf16)
            return carry

        lax.fori_loop(0, acc.shape[0] // part, body, 0)


def feed_back(
    out_grad, out_grad_t, middle_t, weights, scales, up, gate, hidden_units, start, mixing, step, base, count
):
    model, rows = middle_t.shape
    width = count * step
    columns = pl.BlockSpec((rows, step), lambda i: (0, i + base))
    whole = pl.BlockSpec((rows, model), lambda i: (0, 0))
    turned = pl.BlockSpec((model, rows), lambda i: (0, 0))
    wide = jax.ShapeDtypeStruct((rows, model), f32)
    grads_specs = [
        pl.BlockSpec((3, model, step), lambda i: (0, 0, i)),
        pl.BlockSpec((2, step), lambda i: (0, i)),
    ]
    grads_shapes = [
        jax.ShapeDtypeStruct((3, model, width), bf16),
        jax.ShapeDtypeStruct((2, width), f32),
    ]
    last = bool(mixing)
    return pl.pallas_call(
        feed_back_last_kernel if last else feed_back_first_kernel,
        grid=(count,),
        in_specs=[whole, turned, turned]
        + weight_specs(weights, step, base)
        + [pl.BlockSpec((2, step), lambda i: (0, i + base)), columns, columns, columns, whole]
        + ([whole, whole, pl.BlockSpec((2, model), lambda i: (0, 0))] if last else []),
        out_specs=grads_specs
        + ([whole, whole, pl.BlockSpec((1, model), lambda i: (0, 0))] if last else [whole]),
        out_shape=grads_shapes
        + (
            [
                wide,
                jax.ShapeDtypeStruct((rows, model), bf16),
                jax.ShapeDtypeStruct((1, model), f32),
            ]
            if last
            else [wide]
        ),
        scratch_shapes=[pltpu.VMEM((rows, model), f32)] if last else [],
        cost_estimate=pl.CostEstimate(
            flops=12 * rows * model * width,
            bytes_accessed=12 * model * width + 10 * rows * width,
            transcendentals=0,
        ),
        name="feed_back_last" if last else "feed_back_first",
    )(
        out_grad,
        out_grad_t,
        middle_t,
        weights,
        weights,
        weights,
        scales,
        up,
        gate,
        hidden_units,
        start,
        *mixing,
    )


def shift(value, axis, distance, size):
    return lax.ppermute(value, axis, [(i, (i + distance) % size) for i in range(size)])


def carry_on(up, down, hop, axis, size):
    up = lax.ppermute(up, axis, [(i, i + 1) for i in range(hop - 1, size - 1)])
    down = lax.ppermute(down, axis, [(i, i - 1) for i in range(1, size - hop + 1)])
    return up, down


def line_sum(pieces, axis, size, second, other):
    up = down = None
    for hop in range(1, size):
        if hop == 2:
            up, down, second = lax.optimization_barrier((up, down, second))
        if hop == size - 1 and hop > 2:
            up, down, other = lax.optimization_barrier((up, down, other))
        ahead, behind = pieces[size - hop], pieces[hop]
        ahead = ahead if up is None else ahead + up
        behind = behind if down is None else behind + down
        up = lax.ppermute(ahead, axis, [(i, i + 1) for i in range(hop)])
        down = lax.ppermute(behind, axis, [(i, i - 1) for i in range(size - hop, size)])
    return up, down, second, other


def butterfly(values, axis, size):
    step = 1
    while step < size:
        other = [lax.ppermute(v, axis, [(i, i ^ step) for i in range(size)]) for v in values]
        values = [v + o for v, o in zip(values, other)]
        step *= 2
    return values


def take_block(value, index, size, axis):
    return lax.dynamic_slice_in_dim(value, index * size, size, axis)


def put_block(whole, value, index, axis):
    return lax.dynamic_update_slice_in_dim(whole, value, index * value.shape[axis], axis)


def local(
    nd,
    nt,
    hidden_in,
    cotangent,
    segments,
    attn_weight,
    mlp_weight,
    rates,
    qk_scale,
    mlp_scales,
    attn_moment_one,
    attn_moment_two,
    mlp_moment_one,
    mlp_moment_two,
):
    rows, model = hidden_in.shape
    length = segments.shape[0]
    shard = attn_weight.shape[1]
    heads_width = attn_weight.shape[2]
    hidden_width = mlp_weight.shape[2]
    block = min(512, length)
    step = min(512, hidden_width)
    me = lax.axis_index("tensor")

    def gather(value):
        return [value] + [shift(value, "tensor", d, nt) for d in range(1, nt)]

    def line(value):
        ups, downs = [value], [value]
        for hop in range(1, nt):
            up, down = carry_on(ups[-1], downs[-1], hop, "tensor", nt)
            ups.append(up)
            downs.append(down)
        return ups, downs

    def join(ups, downs, d):
        return ups[0] if d == 0 else jnp.where(me >= d, ups[d], downs[nt - d])

    attn_low = attn_weight.astype(bf16)
    attn_shard = jnp.concatenate(
        [attn_low[0], attn_low[1], attn_low[2]] + gather(attn_low[3]), axis=1
    )
    attn_full = lax.all_gather(attn_shard, "dp", axis=0, tiled=True)
    scales_row = jnp.concatenate(gather(mlp_scales), axis=1)
    ups, downs = line(mlp_weight.astype(bf16).reshape(3 * shard, hidden_width))
    before = max(1, nt - 2)
    hidden_in, ups[before], downs[before] = lax.optimization_barrier(
        (hidden_in, ups[before], downs[before])
    )
    mlp_full = lax.all_gather(
        jnp.concatenate([join(ups, downs, d) for d in range(nt)], axis=0), "dp", axis=0, tiled=True
    )
    mlp_full = mlp_full.reshape(nd, nt, 3, shard, hidden_width)

    starts = starts_of(segments)
    positions = (jnp.arange(length, dtype=jnp.int32) - starts).astype(f32)
    lane = jnp.arange(128, dtype=jnp.int32)
    half = HEAD_DIM // 2
    frequency = 10000.0 ** (-(lane % half).astype(f32) / half)
    sign = jnp.where(lane % HEAD_DIM < half, -1.0, 1.0)
    angles = positions[:, None] * frequency[None, :]
    cosine = jnp.cos(angles)
    sine = jnp.sin(angles) * sign[None, :]
    gain = qk_scale.reshape(1, heads_width)

    ups, downs = line(hidden_in)
    hidden_parts = [join(ups, downs, d) for d in range(nt)]
    state = ()
    for d in sorted(range(nt), key=lambda d: max(d, nt - d) if d else 0):
        index = ((me + nt - d) % nt).reshape(1)
        state = project(index, hidden_parts[d], attn_full, cosine, sine, gain, length, state)
    query_hat, key_hat, value_hat, query_turned, key_turned = state
    attended_row, attended_f32, log_sum = attend(
        query_hat, key_hat, value_hat, starts[:, None], block
    )
    attended = [take_block(attended_row, me, rows, 0)] + [
        shift(take_block(attended_row, (me + d) % nt, rows, 0), "tensor", d, nt)
        for d in range(1, nt)
    ]
    branch, middle, middle_low, middle_t = mix(attended, attn_full, hidden_in, rates)
    row_segments = take_block(segments, me, rows, 0)
    live = (row_segments < pad_segment).astype(f32)[:, None]
    up, gate, hidden_units, result, middle_direct, mlp_out_low, mlp_out_t, rate_mlp_grad = feed(
        middle_low, mlp_full, scales_row, middle, cotangent, live, rates, step
    )
    blocks = nt * hidden_width // step
    half = blocks // 2
    feed_args = (mlp_out_low, mlp_out_t, middle_t, mlp_full, scales_row, up, gate, hidden_units)
    far_grad, far_scales, partial = feed_back(
        *feed_args, middle_direct, (), step, half, blocks - half
    )
    far_part = lax.psum_scatter(far_grad, "dp", scatter_dimension=1, tiled=True)
    near_grad, near_scales, token_direct, branch_low, rate_attn_grad = feed_back(
        *feed_args, partial, (branch, hidden_in, rates), step, 0, half
    )
    near_part = lax.psum_scatter(near_grad, "dp", scatter_dimension=1, tiled=True)
    scales_grad = jnp.concatenate([near_scales, far_scales], axis=1)

    def out_block(d):
        return attn_full[:, (3 + d) * heads_width : (4 + d) * heads_width]

    grad_row = jnp.zeros((length, heads_width), bf16)
    for d in list(range(1, nt)) + [0]:
        piece = dot_nn(branch_low, out_block(d)).astype(bf16)
        piece = shift(piece, "tensor", -d, nt) if d else piece
        grad_row = put_block(grad_row, piece, (me + d) % nt, 0)
    out_grad = out_grads(attended, branch_low)
    small = jnp.concatenate([rate_attn_grad, rate_mlp_grad], axis=0)
    small, grad_row = lax.optimization_barrier((small, grad_row))
    head_grads = attend_back(
        query_hat, key_hat, value_hat, grad_row, attended_f32, log_sum, starts[None, :], block
    )
    head_grads, far_part, out_grad = lax.optimization_barrier((head_grads, far_part, out_grad))
    out_part = lax.psum_scatter(out_grad, "dp", scatter_dimension=0, tiled=True)
    qkv_grad, pieces, gain_grad = project_back(
        me.reshape(1),
        head_grads,
        (query_turned, key_turned),
        attn_full,
        cosine,
        sine,
        gain,
        rows,
    )
    pieces = [pieces[d * rows : (d + 1) * rows] for d in range(nt)]
    hidden_turn = [hidden_parts[(nt - d) % nt] for d in range(nt)]
    qkv_grad = projection_grads(hidden_turn, qkv_grad)
    total = token_direct + pieces[0].astype(f32)
    from_below, from_above, qkv_grad, near_part = line_sum(
        pieces, "tensor", nt, qkv_grad, near_part
    )
    qkv_part = lax.psum_scatter(qkv_grad, "dp", scatter_dimension=0, tiled=True)
    total = total + from_below.astype(f32) + from_above.astype(f32)
    input_grad = total.astype(bf16)

    def sent(part, axis, width, first):
        count = part.shape[axis] // width
        pieces = [lax.slice_in_dim(part, d * width, (d + 1) * width, axis=axis) for d in range(count)]
        return [
            (shift(piece, "tensor", -(d + first), nt) if d + first else piece).astype(f32)
            for d, piece in enumerate(pieces)
        ]

    out_own = sum(sent(out_part, 1, heads_width, 0))
    split = half * step // hidden_width
    mlp_weight_grad = sum(sent(near_part, 2, hidden_width, 0) + sent(far_part, 2, hidden_width, split))

    def spread(value):
        width = value.shape[1] // nt
        whole = jnp.zeros_like(value)
        for d in range(nt):
            piece = value[:, d * width : (d + 1) * width]
            whole = put_block(whole, piece, (me + nt - d) % nt, 1)
        return whole

    scales_grad = spread(scales_grad).reshape(-1, model)
    small = jnp.concatenate([small, scales_grad], axis=0)
    (small,) = butterfly([small], "dp", nd)
    (small,) = butterfly([small], "tensor", nt)
    rates_grad = small[:2]
    mlp_scales_grad = small[2:].reshape(2, nt * hidden_width)

    def adam(weight, gradient, one, two):
        one, two, moved = adam_moved(weight, gradient, one, two)
        return one, two, moved, jnp.sum(moved * moved, axis=1, keepdims=True)

    mlp_one, mlp_two, mlp_moved, mlp_square = adam(
        mlp_weight, mlp_weight_grad, mlp_moment_one, mlp_moment_two
    )
    out_one, out_two, out_moved, out_square = adam(
        attn_weight[3:], out_own[None], attn_moment_one[3:], attn_moment_two[3:]
    )
    early = jnp.concatenate(
        [mlp_square.reshape(1, -1), out_square.reshape(1, -1), gain_grad], axis=1
    )
    (early,) = butterfly([early], "dp", nd)
    qkv_part, early = lax.optimization_barrier((qkv_part, early))
    qkv_own = jnp.stack(
        [qkv_part[:, m * heads_width : (m + 1) * heads_width].astype(f32) for m in range(3)]
    )
    qkv_one, qkv_two, qkv_moved, qkv_square = adam(
        attn_weight[:3], qkv_own, attn_moment_one[:3], attn_moment_two[:3]
    )
    (qkv_square,) = butterfly([qkv_square], "dp", nd)
    mlp_square = early[:, : 3 * hidden_width].reshape(3, 1, hidden_width)
    out_square = early[:, 3 * hidden_width : 3 * hidden_width + heads_width].reshape(1, 1, heads_width)
    gain_row = spread(
        jnp.concatenate(gather(early[:, 3 * hidden_width + heads_width :]), axis=1)
    ).reshape(-1)
    attn_weight_grad = jnp.concatenate([qkv_own, out_own[None]], axis=0)
    attn_one = jnp.concatenate([qkv_one, out_one], axis=0)
    attn_two = jnp.concatenate([qkv_two, out_two], axis=0)
    attn_moved = jnp.concatenate([qkv_moved, out_moved], axis=0)
    attn_square = jnp.concatenate([qkv_square, out_square], axis=0)
    attn_new = attn_moved * lax.rsqrt(attn_square + norm_eps)
    mlp_new = mlp_moved * lax.rsqrt(mlp_square + norm_eps)
    return (
        result.astype(bf16),
        input_grad,
        attn_weight_grad,
        mlp_weight_grad,
        rates_grad,
        gain_row,
        mlp_scales_grad,
        attn_one,
        attn_two,
        mlp_one,
        mlp_two,
        attn_new,
        mlp_new,
    )


def solution(mesh):
    weights = P(None, "dp", "tensor")
    tokens = P(("dp", "tensor"), None)
    return jax.shard_map(
        functools.partial(local, mesh.shape["dp"], mesh.shape["tensor"]),
        mesh=mesh,
        in_specs=(
            tokens,
            tokens,
            P("dp"),
            weights,
            weights,
            P(),
            P("tensor"),
            P(None, "tensor"),
            weights,
            weights,
            weights,
            weights,
        ),
        out_specs=(
            tokens,
            tokens,
            weights,
            weights,
            P(),
            P(),
            P(),
            weights,
            weights,
            weights,
            weights,
            weights,
            weights,
        ),
        check_vma=False,
    )
```

```python
import functools
import math

import jax
import jax.numpy as jnp
from jax import lax
from jax.experimental import pallas as pl
from jax.experimental.pallas import tpu as pltpu
from jax.sharding import PartitionSpec as P

HEAD_DIM = 64
LOG2E = 1.4426950408889634

norm_eps = 1e-06
pad_segment = 63
beta_one = 0.9
beta_two = 0.95
learning_rate = 0.01
adam_eps = 1e-08
bias_one = 1.0 - 0.9**10
bias_two = 1.0 - 0.95**10
scale_factor = math.sqrt(HEAD_DIM)
f32 = jnp.float32
bf16 = jnp.bfloat16


def starts_of(segment_row):
    indices = jnp.arange(segment_row.shape[0], dtype=jnp.int32)
    changed = jnp.concatenate(
        [jnp.ones((1,), dtype=jnp.bool_), segment_row[1:] != segment_row[:-1]]
    )
    return lax.cummax(jnp.where(changed, indices, jnp.zeros_like(indices)), axis=0)


def adam_moved(weight, gradient, moment_one, moment_two):
    moment_one_new = beta_one * moment_one + (1.0 - beta_one) * gradient
    moment_two_new = beta_two * moment_two + (1.0 - beta_two) * gradient * gradient
    moved = weight - learning_rate * (moment_one_new / bias_one) / (
        jnp.sqrt(moment_two_new / bias_two) + adam_eps
    )
    return (moment_one_new, moment_two_new, moved)


def dot_nt(a, b):
    return lax.dot_general(a, b, (((1,), (1,)), ((), ())), preferred_element_type=f32)


def dot_nn(a, b):
    return lax.dot_general(a, b, (((1,), (0,)), ((), ())), preferred_element_type=f32)


def dot_tn(a, b):
    return lax.dot_general(a, b, (((0,), (0,)), ((), ())), preferred_element_type=f32)


def head_stack(x, heads):
    lane = lax.broadcasted_iota(jnp.int32, x.shape, 1) // HEAD_DIM
    zero = jnp.zeros_like(x)
    return jnp.concatenate([jnp.where(lane == h, x, zero) for h in range(heads)], axis=0)


def head_pick(stacked, heads, rows):
    width = stacked.shape[1]
    lane = lax.broadcasted_iota(jnp.int32, (rows, width), 1) // HEAD_DIM
    picked = jnp.zeros((rows, width), f32)
    for h in range(heads):
        picked = jnp.where(lane == h, stacked[h * rows : (h + 1) * rows], picked)
    return picked


def attend_kernel(heads, bq, bk, q_ref, k_ref, v_ref, start_ref, o_ref, of_ref, l_ref, acc, lsum):
    i = pl.program_id(0)
    qs = head_stack(q_ref[...], heads)
    acc[...] = jnp.zeros_like(acc)
    lsum[...] = jnp.zeros_like(lsum)
    start = jnp.concatenate([start_ref[...]] * heads, axis=0)

    def step(j, diagonal):
        offset = pl.multiple_of(j * bk, bk)
        keys = k_ref[pl.ds(offset, bk), :]
        values = v_ref[pl.ds(offset, bk), :]
        scores = dot_nt(qs, keys)
        key_index = offset + lax.broadcasted_iota(jnp.int32, scores.shape, 1)
        allowed = key_index >= start
        if diagonal:
            row = lax.rem(lax.broadcasted_iota(jnp.int32, scores.shape, 0), bq)
            allowed = allowed & (key_index <= i * bq + row)
        weights = jnp.where(allowed, jnp.exp2(scores * (scale_factor * LOG2E)), 0.0)
        total = weights[:, :128]
        for part in range(1, bk // 128):
            total = total + weights[:, part * 128 : (part + 1) * 128]
        lsum[...] += total
        acc[...] += dot_nn(weights.astype(bf16), values)

    def body(j, carry):
        step(j, False)
        return carry

    lax.fori_loop(0, i, body, 0)
    step(i, True)
    summed = jnp.sum(lsum[...], axis=1, keepdims=True)
    out = head_pick(acc[...] * (1.0 / summed), heads, bq)
    of_ref[...] = out
    o_ref[...] = out.astype(bf16)
    l_ref[...] = jnp.log2(summed).reshape(heads, bq)


def attend(q, k, v, start, block):
    length, width = q.shape
    heads = width // HEAD_DIM
    whole = pl.BlockSpec((length, width), lambda i: (0, 0))
    rows = pl.BlockSpec((block, width), lambda i: (i, 0))
    return pl.pallas_call(
        functools.partial(attend_kernel, heads, block, block),
        grid=(length // block,),
        in_specs=[rows, whole, whole, pl.BlockSpec((block, 1), lambda i: (i, 0))],
        out_specs=[rows, rows, pl.BlockSpec((heads, block), lambda i: (0, i))],
        out_shape=[
            jax.ShapeDtypeStruct((length, width), bf16),
            jax.ShapeDtypeStruct((length, width), f32),
            jax.ShapeDtypeStruct((heads, length), f32),
        ],
        scratch_shapes=[
            pltpu.VMEM((heads * block, width), f32),
            pltpu.VMEM((heads * block, 128), f32),
        ],
        cost_estimate=pl.CostEstimate(
            flops=20_000_000_000, bytes_accessed=8 * length * width, transcendentals=0
        ),
        name="attend",
    )(q, k, v, start)


def attend_back_kernel(
    heads, bq, bk, q_ref, do_ref, k_ref, v_ref, of_ref, l_ref, start_ref, dq_ref, dk_ref, dv_ref, acc
):
    i = pl.program_id(0)

    @pl.when(i == 0)
    def _():
        dk_ref[...] = jnp.zeros_like(dk_ref)
        dv_ref[...] = jnp.zeros_like(dv_ref)

    qs = head_stack(q_ref[...], heads)
    grads = do_ref[...]
    dos = head_stack(grads, heads)
    product = (grads.astype(f32) * of_ref[...]).T
    delta = jnp.concatenate(
        [
            jnp.sum(product[h * HEAD_DIM : (h + 1) * HEAD_DIM], axis=0, keepdims=True)
            for h in range(heads)
        ],
        axis=1,
    )
    log_sum = jnp.concatenate([l_ref[h : h + 1, :] for h in range(heads)], axis=1)
    start = jnp.concatenate([start_ref[...]] * heads, axis=1)
    acc[...] = jnp.zeros_like(acc)

    def step(j, diagonal):
        offset = pl.multiple_of(j * bk, bk)
        keys = k_ref[pl.ds(offset, bk), :]
        values = v_ref[pl.ds(offset, bk), :]
        scores = dot_nt(keys, qs)
        key_index = offset + lax.broadcasted_iota(jnp.int32, scores.shape, 0)
        allowed = key_index >= start
        if diagonal:
            column = lax.rem(lax.broadcasted_iota(jnp.int32, scores.shape, 1), bq)
            allowed = allowed & (key_index <= i * bq + column)
        probs = jnp.where(allowed, jnp.exp2(scores * (scale_factor * LOG2E) - log_sum), 0.0)
        prob_grad = dot_nt(values, dos)
        score_grad = (probs * (prob_grad - delta)).astype(bf16)
        dv_ref[pl.ds(offset, bk), :] += dot_nn(probs.astype(bf16), dos)
        dk_ref[pl.ds(offset, bk), :] += dot_nn(score_grad, qs)
        acc[...] += dot_tn(score_grad, keys)

    def body(j, carry):
        step(j, False)
        return carry

    lax.fori_loop(0, i, body, 0)
    step(i, True)
    dq_ref[...] = head_pick(acc[...], heads, bq)


def attend_back(q, k, v, grads, out, log_sum, start, block):
    length, width = q.shape
    heads = width // HEAD_DIM
    whole = pl.BlockSpec((length, width), lambda i: (0, 0))
    rows = pl.BlockSpec((block, width), lambda i: (i, 0))
    result = jax.ShapeDtypeStruct((length, width), f32)
    return pl.pallas_call(
        functools.partial(attend_back_kernel, heads, block, block),
        grid=(length // block,),
        in_specs=[
            rows,
            rows,
            whole,
            whole,
            rows,
            pl.BlockSpec((heads, block), lambda i: (0, i)),
            pl.BlockSpec((1, block), lambda i: (0, i)),
        ],
        out_specs=[rows, whole, whole],
        out_shape=[result, result, result],
        scratch_shapes=[pltpu.VMEM((heads * block, width), f32)],
        cost_estimate=pl.CostEstimate(
            flops=40_000_000_000, bytes_accessed=20 * length * width, transcendentals=0
        ),
        name="attend_back",
    )(q, grads, k, v, out, log_sum, start)


def partner(x):
    width = x.shape[1]
    lane = lax.broadcasted_iota(jnp.int32, x.shape, 1)
    ahead = pltpu.roll(x, width - HEAD_DIM // 2, 1)
    behind = pltpu.roll(x, HEAD_DIM // 2, 1)
    return jnp.where(lax.rem(lane, HEAD_DIM) < HEAD_DIM // 2, ahead, behind)


def head_sums(x):
    width = x.shape[1]
    row = lax.broadcasted_iota(jnp.int32, (width, width), 0) // HEAD_DIM
    column = lax.broadcasted_iota(jnp.int32, (width, width), 1) // HEAD_DIM
    same = jnp.where(row == column, 1.0, 0.0).astype(f32)
    return lax.dot_general(
        x,
        same,
        (((1,), (0,)), ((), ())),
        precision=lax.Precision.HIGHEST,
        preferred_element_type=f32,
    )


def widen(table, width):
    return table if table.shape[1] == width else jnp.concatenate([table] * (width // 128), axis=1)


def project_kernel(index_ref, x_ref, wq_ref, wk_ref, wv_ref, cos_ref, sin_ref, gain_ref, *refs):
    q_ref, k_ref, v_ref, xq_ref, xk_ref = refs[-5:]
    x = x_ref[...]
    width = q_ref.shape[1]
    cosine = widen(cos_ref[...], width)
    sine = widen(sin_ref[...], width)
    gain = gain_ref[...]
    for w_ref, hat_ref, turned_ref in ((wq_ref, q_ref, xq_ref), (wk_ref, k_ref, xk_ref)):
        raw = dot_nn(x, w_ref[...])
        turned = raw * cosine + partner(raw) * sine
        turned_ref[...] = turned
        hat = turned * lax.rsqrt(head_sums(turned * turned) + norm_eps) * gain
        hat_ref[...] = hat.astype(bf16)
    v_ref[...] = dot_nn(x, wv_ref[...]).astype(bf16)


def project(index, x, weights, cosine, sine, gain, length, previous):
    rows, model = x.shape
    width = gain.shape[1]
    part = min(256, rows)
    per = rows // part

    def column(m):
        return pl.BlockSpec((model, width), lambda i, at: (0, m))

    table = pl.BlockSpec((part, 128), lambda i, at: (at[0] * per + i, 0))
    out = pl.BlockSpec((part, width), lambda i, at: (at[0] * per + i, 0))
    low = jax.ShapeDtypeStruct((length, width), bf16)
    wide = jax.ShapeDtypeStruct((length, width), f32)
    return pl.pallas_call(
        project_kernel,
        grid_spec=pltpu.PrefetchScalarGridSpec(
            num_scalar_prefetch=1,
            grid=(per,),
            in_specs=[
                pl.BlockSpec((part, model), lambda i, at: (i, 0)),
                column(0),
                column(1),
                column(2),
                table,
                table,
                pl.BlockSpec((1, width), lambda i, at: (0, 0)),
            ]
            + [pl.BlockSpec(memory_space=pl.ANY)] * len(previous),
            out_specs=[out] * 5,
        ),
        out_shape=[low, low, low, wide, wide],
        input_output_aliases={8 + i: i for i in range(len(previous))},
        cost_estimate=pl.CostEstimate(
            flops=6 * rows * model * width, bytes_accessed=8 * model * width, transcendentals=0
        ),
        name="project",
    )(index, x, weights, weights, weights, cosine, sine, gain, *previous)


def project_back_kernel(
    index_ref,
    dq_ref,
    dk_ref,
    dv_ref,
    xq_ref,
    xk_ref,
    wq_ref,
    wk_ref,
    wv_ref,
    cos_ref,
    sin_ref,
    gain_ref,
    grad_ref,
    piece_ref,
    gain_grad_ref,
):
    @pl.when(pl.program_id(0) == 0)
    def _():
        gain_grad_ref[...] = jnp.zeros_like(gain_grad_ref)

    width = dq_ref.shape[1]
    cosine = widen(cos_ref[...], width)
    sine = widen(sin_ref[...], width)
    gain = gain_ref[...]
    lows = []
    for d_ref, x_ref in ((dq_ref, xq_ref), (dk_ref, xk_ref)):
        turned = x_ref[...]
        inverse = lax.rsqrt(head_sums(turned * turned) + norm_eps)
        unit = turned * inverse
        hat_grad = d_ref[...] * scale_factor
        gain_grad_ref[...] += jnp.sum(hat_grad * unit, axis=0, keepdims=True)
        unit_grad = hat_grad * gain
        turned_grad = inverse * (unit_grad - unit * head_sums(unit * unit_grad))
        raw_grad = turned_grad * cosine - partner(turned_grad) * sine
        lows.append(raw_grad.astype(bf16))
    lows.append(dv_ref[...].astype(bf16))
    piece = jnp.zeros(piece_ref.shape, f32)
    for m, w_ref in enumerate((wq_ref, wk_ref, wv_ref)):
        grad_ref[:, m * width : (m + 1) * width] = lows[m]
        piece = piece + dot_nt(lows[m], w_ref[...])
    piece_ref[...] = piece.astype(bf16)


def project_back(index, grads, turned, weights, cosine, sine, gain, rows):
    length, width = grads[0].shape
    model = weights.shape[0]
    part = min(256, rows)
    per = rows // part
    blocks = length // part

    def column(m):
        return pl.BlockSpec((model, width), lambda i, at: (0, m))

    def turn(i, at):
        return (lax.rem(at[0] * per + i, blocks), 0)

    tall = pl.BlockSpec((part, width), turn)
    table = pl.BlockSpec((part, 128), turn)
    return pl.pallas_call(
        project_back_kernel,
        grid_spec=pltpu.PrefetchScalarGridSpec(
            num_scalar_prefetch=1,
            grid=(blocks,),
            in_specs=[tall] * 5
            + [column(0), column(1), column(2), table, table]
            + [pl.BlockSpec((1, width), lambda i, at: (0, 0))],
            out_specs=[
                pl.BlockSpec((part, 3 * width), lambda i, at: (i, 0)),
                pl.BlockSpec((part, model), lambda i, at: (i, 0)),
                pl.BlockSpec((1, width), lambda i, at: (0, 0)),
            ],
        ),
        out_shape=[
            jax.ShapeDtypeStruct((length, 3 * width), bf16),
            jax.ShapeDtypeStruct((length, model), bf16),
            jax.ShapeDtypeStruct((1, width), f32),
        ],
        cost_estimate=pl.CostEstimate(
            flops=8 * length * model * width,
            bytes_accessed=32 * length * width,
            transcendentals=0,
        ),
        name="project_back",
    )(index, *grads, *turned, weights, weights, weights, cosine, sine, gain)


def projection_grads_kernel(count, *refs):
    hidden = refs[:count]
    grad_ref, out_ref = refs[count:]
    rows = hidden[0].shape[0]
    total = dot_tn(hidden[0][...], grad_ref[:rows, :])
    for d in range(1, count):
        total = total + dot_tn(hidden[d][...], grad_ref[d * rows : (d + 1) * rows, :])
    out_ref[...] = total.astype(bf16)


def projection_grads(hidden, qkv_grad):
    count = len(hidden)
    rows, model = hidden[0].shape
    width = qkv_grad.shape[1]
    part = 256
    column = pl.BlockSpec((rows, part), lambda i: (0, i))
    return pl.pallas_call(
        functools.partial(projection_grads_kernel, count),
        grid=(model // part,),
        in_specs=[column] * count + [pl.BlockSpec(qkv_grad.shape, lambda i: (0, 0))],
        out_specs=pl.BlockSpec((part, width), lambda i: (i, 0)),
        out_shape=jax.ShapeDtypeStruct((model, width), bf16),
        cost_estimate=pl.CostEstimate(
            flops=2 * rows * count * model * width,
            bytes_accessed=4 * rows * count * model,
            transcendentals=0,
        ),
        name="projection_grads",
    )(*hidden, qkv_grad)


def out_grads_kernel(count, *refs):
    attended = refs[:count]
    branch_ref, out_ref = refs[count:]
    width = attended[0].shape[1]
    turned = branch_ref[...].T
    for d in range(count):
        out_ref[:, d * width : (d + 1) * width] = dot_nn(turned, attended[d][...]).astype(bf16)


def out_grads(attended, branch_grad):
    count = len(attended)
    rows, model = branch_grad.shape
    width = attended[0].shape[1]
    part = 256
    return pl.pallas_call(
        functools.partial(out_grads_kernel, count),
        grid=(model // part,),
        in_specs=[pl.BlockSpec(x.shape, lambda i: (0, 0)) for x in attended]
        + [pl.BlockSpec((rows, part), lambda i: (0, i))],
        out_specs=pl.BlockSpec((part, count * width), lambda i: (i, 0)),
        out_shape=jax.ShapeDtypeStruct((model, count * width), bf16),
        cost_estimate=pl.CostEstimate(
            flops=2 * rows * count * model * width,
            bytes_accessed=4 * rows * count * model,
            transcendentals=0,
        ),
        name="out_grads",
    )(*attended, branch_grad)


def rms_scale(x):
    return lax.rsqrt(jnp.mean(x * x, axis=-1, keepdims=True) + norm_eps)


def mix_kernel(count, *refs):
    pieces, weights = refs[:count], refs[count : 2 * count]
    hidden_ref, rates_ref, branch_ref, middle_ref, low_ref, turned_ref = refs[2 * count :]
    branch = dot_nt(pieces[0][...], weights[0][...])
    for d in range(1, count):
        branch = branch + dot_nt(pieces[d][...], weights[d][...])
    branch_ref[...] = branch
    hidden = hidden_ref[...].astype(f32)
    mixed = hidden + rates_ref[0:1, :] * (branch * rms_scale(branch) - hidden)
    middle = mixed * rms_scale(mixed)
    middle_ref[...] = middle
    low_ref[...] = middle.astype(bf16)
    turned_ref[...] = middle.T.astype(bf16)


def mix(pieces, weights, hidden, rates):
    count = len(pieces)
    rows, model = hidden.shape
    width = pieces[0].shape[1]
    part = min(128, rows)

    def column(d):
        return pl.BlockSpec((model, width), lambda i: (0, d))

    wide = pl.BlockSpec((part, model), lambda i: (i, 0))
    return pl.pallas_call(
        functools.partial(mix_kernel, count),
        grid=(rows // part,),
        in_specs=[pl.BlockSpec((part, width), lambda i: (i, 0))] * count
        + [column(d) for d in range(count)]
        + [wide, pl.BlockSpec((2, model), lambda i: (0, 0))],
        out_specs=[wide, wide, wide, pl.BlockSpec((model, part), lambda i: (0, i))],
        out_shape=[
            jax.ShapeDtypeStruct((rows, model), f32),
            jax.ShapeDtypeStruct((rows, model), f32),
            jax.ShapeDtypeStruct((rows, model), bf16),
            jax.ShapeDtypeStruct((model, rows), bf16),
        ],
        cost_estimate=pl.CostEstimate(
            flops=2 * rows * model * model, bytes_accessed=14 * rows * model, transcendentals=0
        ),
        name="mix",
    )(*pieces, *([weights] * count), hidden, rates)


def block_of(w_ref):
    value = w_ref[:, 0, 0]
    return value.reshape(value.shape[0] * value.shape[1], value.shape[2])


def feed_kernel(
    m_ref,
    wu_ref,
    wg_ref,
    wd_ref,
    s_ref,
    middle_ref,
    cot_ref,
    live_ref,
    rates_ref,
    up_ref,
    gate_ref,
    h_ref,
    result_ref,
    direct_ref,
    low_ref,
    turned_ref,
    rate_ref,
    acc,
):
    i = pl.program_id(0)
    tokens = m_ref[...]
    up = dot_nn(tokens, block_of(wu_ref))
    gate = dot_nn(tokens, block_of(wg_ref))
    up_ref[...] = up
    gate_ref[...] = gate
    scaled = gate * s_ref[1:2, :]
    hidden = (up * s_ref[0:1, :] * (scaled * jax.nn.sigmoid(scaled))).astype(bf16)
    h_ref[...] = hidden
    part_out = dot_nt(hidden, block_of(wd_ref))

    @pl.when(i == 0)
    def _():
        acc[...] = part_out

    @pl.when(i > 0)
    def _():
        acc[...] += part_out

    @pl.when(i == pl.num_programs(0) - 1)
    def _():
        rate_ref[...] = jnp.zeros_like(rate_ref)
        rate = rates_ref[1:2, :]
        part = 32

        def body(at, carry):
            rows = pl.ds(pl.multiple_of(at * part, part), part)
            out = acc[rows, :]
            middle = middle_ref[rows, :]
            out_scale = rms_scale(out)
            unit = out * out_scale
            mixed = middle + rate * (unit - middle)
            scale = rms_scale(mixed)
            final = mixed * scale
            result_ref[rows, :] = final.astype(bf16)
            grad = cot_ref[rows, :].astype(f32) * live_ref[rows, :]
            mixed_grad = scale * (grad - final * jnp.mean(final * grad, axis=-1, keepdims=True))
            direct_ref[rows, :] = mixed_grad * (1.0 - rate)
            rate_ref[...] += jnp.sum(mixed_grad * (unit - middle), axis=0, keepdims=True)
            unit_grad = mixed_grad * rate
            out_grad = out_scale * (
                unit_grad - unit * jnp.mean(unit * unit_grad, axis=-1, keepdims=True)
            )
            low_ref[rows, :] = out_grad.astype(bf16)
            return carry

        lax.fori_loop(0, acc.shape[0] // part, body, 0)
        for at in range(acc.shape[0] // 128):
            rows = slice(at * 128, (at + 1) * 128)
            turned_ref[:, rows] = low_ref[rows, :].T


def weight_specs(weights, step, base=0):
    nd, _, _, shard, local_width = weights.shape
    per = local_width // step

    def spec(m):
        return pl.BlockSpec(
            (nd, 1, 1, shard, step), lambda i: (0, (i + base) // per, m, 0, (i + base) % per)
        )

    return [spec(0), spec(1), spec(2)]


def feed(low, weights, scales, middle, cotangent, live, rates, step):
    rows, model = low.shape
    total = weights.shape[1] * weights.shape[4]
    columns = pl.BlockSpec((rows, step), lambda i: (0, i))
    whole = pl.BlockSpec((rows, model), lambda i: (0, 0))
    return pl.pallas_call(
        feed_kernel,
        grid=(total // step,),
        in_specs=[whole]
        + weight_specs(weights, step)
        + [
            pl.BlockSpec((2, step), lambda i: (0, i)),
            whole,
            whole,
            pl.BlockSpec((rows, 1), lambda i: (0, 0)),
            pl.BlockSpec((2, model), lambda i: (0, 0)),
        ],
        out_specs=[columns, columns, columns, whole, whole, whole]
        + [
            pl.BlockSpec((model, rows), lambda i: (0, 0)),
            pl.BlockSpec((1, model), lambda i: (0, 0)),
        ],
        out_shape=[
            jax.ShapeDtypeStruct((rows, total), f32),
            jax.ShapeDtypeStruct((rows, total), f32),
            jax.ShapeDtypeStruct((rows, total), bf16),
            jax.ShapeDtypeStruct((rows, model), bf16),
            jax.ShapeDtypeStruct((rows, model), f32),
            jax.ShapeDtypeStruct((rows, model), bf16),
            jax.ShapeDtypeStruct((model, rows), bf16),
            jax.ShapeDtypeStruct((1, model), f32),
        ],
        scratch_shapes=[pltpu.VMEM((rows, model), f32)],
        cost_estimate=pl.CostEstimate(
            flops=6 * rows * model * total,
            bytes_accessed=6 * model * total + 10 * rows * total,
            transcendentals=0,
        ),
        name="feed",
    )(low, weights, weights, weights, scales, middle, cotangent, live, rates)


def feed_back_step(
    og_ref, ogt_ref, mt_ref, wu_ref, wg_ref, wd_ref, s_ref, up_ref, gate_ref, h_ref, start_ref, grad_ref, sg_ref, acc
):
    i = pl.program_id(0)
    grad_ref[2] = dot_nn(ogt_ref[...], h_ref[...]).astype(bf16)
    hidden_grad = dot_nn(og_ref[...], block_of(wd_ref))
    up = up_ref[...]
    gate = gate_ref[...]
    up_gain = s_ref[0:1, :]
    gate_gain = s_ref[1:2, :]
    scaled = gate * gate_gain
    sig = jax.nn.sigmoid(scaled)
    up_part = hidden_grad * (scaled * sig)
    gate_part = hidden_grad * (up * up_gain) * (sig * (1.0 + scaled * (1.0 - sig)))
    sg_ref[0:1, :] = jnp.sum(up_part * up, axis=0, keepdims=True)
    sg_ref[1:2, :] = jnp.sum(gate_part * gate, axis=0, keepdims=True)
    up_low = (up_part * up_gain).astype(bf16)
    gate_low = (gate_part * gate_gain).astype(bf16)
    tokens_t = mt_ref[...]
    grad_ref[0] = dot_nn(tokens_t, up_low).astype(bf16)
    grad_ref[1] = dot_nn(tokens_t, gate_low).astype(bf16)
    back = dot_nt(up_low, block_of(wu_ref)) + dot_nt(gate_low, block_of(wg_ref))

    @pl.when(i == 0)
    def _():
        acc[...] = start_ref[...] + back

    @pl.when(i > 0)
    def _():
        acc[...] += back


def feed_back_first_kernel(*refs):
    feed_back_step(*refs)


def feed_back_last_kernel(*refs):
    branch_ref, hidden_ref, rates_ref = refs[11:14]
    grad_ref, sg_ref, token_ref, low_ref, rate_ref, acc = refs[14:]
    feed_back_step(*refs[:11], grad_ref, sg_ref, acc)

    @pl.when(pl.program_id(0) == pl.num_programs(0) - 1)
    def _():
        rate_ref[...] = jnp.zeros_like(rate_ref)
        rate = rates_ref[0:1, :]
        part = 32

        def body(at, carry):
            rows = pl.ds(pl.multiple_of(at * part, part), part)
            grad = acc[rows, :]
            branch = branch_ref[rows, :]
            hidden = hidden_ref[rows, :].astype(f32)
            branch_scale = rms_scale(branch)
            unit = branch * branch_scale
            mixed = hidden + rate * (unit - hidden)
            scale = rms_scale(mixed)
            middle = mixed * scale
            mixed_grad = scale * (grad - middle * jnp.mean(middle * grad, axis=-1, keepdims=True))
            token_ref[rows, :] = mixed_grad * (1.0 - rate)
            rate_ref[...] += jnp.sum(mixed_grad * (unit - hidden), axis=0, keepdims=True)
            unit_grad = mixed_grad * rate
            branch_grad = branch_scale * (
                unit_grad - unit * jnp.mean(unit * unit_grad, axis=-1, keepdims=True)
            )
            low_ref[rows, :] = branch_grad.astype(bf16)
            return carry

        lax.fori_loop(0, acc.shape[0] // part, body, 0)


def feed_back(
    out_grad, out_grad_t, middle_t, weights, scales, up, gate, hidden_units, start, mixing, step, base, count
):
    model, rows = middle_t.shape
    width = count * step
    columns = pl.BlockSpec((rows, step), lambda i: (0, i + base))
    whole = pl.BlockSpec((rows, model), lambda i: (0, 0))
    turned = pl.BlockSpec((model, rows), lambda i: (0, 0))
    wide = jax.ShapeDtypeStruct((rows, model), f32)
    grads_specs = [
        pl.BlockSpec((3, model, step), lambda i: (0, 0, i)),
        pl.BlockSpec((2, step), lambda i: (0, i)),
    ]
    grads_shapes = [
        jax.ShapeDtypeStruct((3, model, width), bf16),
        jax.ShapeDtypeStruct((2, width), f32),
    ]
    last = bool(mixing)
    return pl.pallas_call(
        feed_back_last_kernel if last else feed_back_first_kernel,
        grid=(count,),
        in_specs=[whole, turned, turned]
        + weight_specs(weights, step, base)
        + [pl.BlockSpec((2, step), lambda i: (0, i + base)), columns, columns, columns, whole]
        + ([whole, whole, pl.BlockSpec((2, model), lambda i: (0, 0))] if last else []),
        out_specs=grads_specs
        + ([whole, whole, pl.BlockSpec((1, model), lambda i: (0, 0))] if last else [whole]),
        out_shape=grads_shapes
        + (
            [
                wide,
                jax.ShapeDtypeStruct((rows, model), bf16),
                jax.ShapeDtypeStruct((1, model), f32),
            ]
            if last
            else [wide]
        ),
        scratch_shapes=[pltpu.VMEM((rows, model), f32)] if last else [],
        cost_estimate=pl.CostEstimate(
            flops=12 * rows * model * width,
            bytes_accessed=12 * model * width + 10 * rows * width,
            transcendentals=0,
        ),
        name="feed_back_last" if last else "feed_back_first",
    )(
        out_grad,
        out_grad_t,
        middle_t,
        weights,
        weights,
        weights,
        scales,
        up,
        gate,
        hidden_units,
        start,
        *mixing,
    )


def shift(value, axis, distance, size):
    return lax.ppermute(value, axis, [(i, (i + distance) % size) for i in range(size)])


def carry_on(up, down, hop, axis, size):
    up = lax.ppermute(up, axis, [(i, i + 1) for i in range(hop - 1, size - 1)])
    down = lax.ppermute(down, axis, [(i, i - 1) for i in range(1, size - hop + 1)])
    return up, down


def line_sum(pieces, hop, up, down, axis, size):
    ahead, behind = pieces[size - hop], pieces[hop]
    ahead = ahead if up is None else ahead + up
    behind = behind if down is None else behind + down
    up = lax.ppermute(ahead, axis, [(i, i + 1) for i in range(hop)])
    down = lax.ppermute(behind, axis, [(i, i - 1) for i in range(size - hop, size)])
    return up, down


def halving(value, axis, size):
    rows, width = value.shape[0] // size, value.shape[1]
    index = lax.axis_index(axis)
    value = value.reshape(size, rows, width)
    step = 1
    while step < size:
        bit = (index // step) % 2
        pairs = value.reshape(-1, 2, rows, width)
        sent = lax.dynamic_index_in_dim(pairs, 1 - bit, 1, False)
        kept = lax.dynamic_index_in_dim(pairs, bit, 1, False)
        other = lax.ppermute(sent, axis, [(i, i ^ step) for i in range(size)])
        value = kept.astype(f32) + other.astype(f32)
        step *= 2
        value = value if step == size else value.astype(bf16)
    return value.reshape(rows, width).astype(f32)


def exchange_add(value, axis, size, step):
    return value + lax.ppermute(value, axis, [(i, i ^ step) for i in range(size)])


def doublings(size):
    return [1 << k for k in range(size.bit_length() - 1)]


def butterfly(value, axis, size):
    for step in doublings(size):
        value = exchange_add(value, axis, size, step)
    return value


def take_block(value, index, size, axis):
    return lax.dynamic_slice_in_dim(value, index * size, size, axis)


def put_block(whole, value, index, axis):
    return lax.dynamic_update_slice_in_dim(whole, value, index * value.shape[axis], axis)


def local(
    nd,
    nt,
    hidden_in,
    cotangent,
    segments,
    attn_weight,
    mlp_weight,
    rates,
    qk_scale,
    mlp_scales,
    attn_moment_one,
    attn_moment_two,
    mlp_moment_one,
    mlp_moment_two,
):
    rows, model = hidden_in.shape
    length = segments.shape[0]
    shard = attn_weight.shape[1]
    heads_width = attn_weight.shape[2]
    hidden_width = mlp_weight.shape[2]
    block = min(512, length)
    step = min(512, hidden_width)
    me = lax.axis_index("tensor")

    def gather(value):
        return [value] + [shift(value, "tensor", d, nt) for d in range(1, nt)]

    def line(value):
        ups, downs = [value], [value]
        for hop in range(1, nt):
            up, down = carry_on(ups[-1], downs[-1], hop, "tensor", nt)
            ups.append(up)
            downs.append(down)
        return ups, downs

    def join(ups, downs, d):
        return ups[0] if d == 0 else jnp.where(me >= d, ups[d], downs[nt - d])

    middle_hop = nt // 2
    order = [d for d in range(nt) if d != middle_hop] + [middle_hop]
    attn_low = attn_weight.astype(bf16)
    qkv_full = lax.all_gather(
        jnp.concatenate([attn_low[0], attn_low[1], attn_low[2]], axis=1), "dp", axis=0, tiled=True
    )
    ups, downs = line(mlp_weight.astype(bf16).reshape(3 * shard, hidden_width))
    out_full = lax.all_gather(
        jnp.concatenate(gather(attn_low[3]), axis=1), "dp", axis=0, tiled=True
    )
    before = max(1, nt - 2)
    hidden_in, ups[before], downs[before] = lax.optimization_barrier(
        (hidden_in, ups[before], downs[before])
    )
    mlp_full = lax.all_gather(
        jnp.concatenate([join(ups, downs, d) for d in order], axis=0), "dp", axis=0, tiled=True
    )
    mlp_full = mlp_full.reshape(nd, nt, 3, shard, hidden_width)
    scales_parts = gather(mlp_scales)
    scales_row = jnp.concatenate([scales_parts[d] for d in order], axis=1)

    starts = starts_of(segments)
    positions = (jnp.arange(length, dtype=jnp.int32) - starts).astype(f32)
    lane = jnp.arange(128, dtype=jnp.int32)
    half = HEAD_DIM // 2
    frequency = 10000.0 ** (-(lane % half).astype(f32) / half)
    sign = jnp.where(lane % HEAD_DIM < half, -1.0, 1.0)
    angles = positions[:, None] * frequency[None, :]
    cosine = jnp.cos(angles)
    sine = jnp.sin(angles) * sign[None, :]
    gain = qk_scale.reshape(1, heads_width)

    ups, downs, state = [hidden_in], [hidden_in], ()
    hidden_parts = [None] * nt

    def projected(hop, state):
        for d in range(nt):
            if (max(d, nt - d) if d else 0) == hop:
                hidden_parts[d] = join(ups, downs, d)
                index = ((me + nt - d) % nt).reshape(1)
                state = project(index, hidden_parts[d], qkv_full, cosine, sine, gain, length, state)
        return state

    for hop in range(1, nt):
        ups[-1], downs[-1], state = lax.optimization_barrier((ups[-1], downs[-1], state))
        up, down = carry_on(ups[-1], downs[-1], hop, "tensor", nt)
        ups.append(up)
        downs.append(down)
        state = projected(hop - 1, state)
    ups[-1], downs[-1], state = lax.optimization_barrier((ups[-1], downs[-1], state))
    state = projected(nt - 1, state)
    query_hat, key_hat, value_hat, query_turned, key_turned = state
    attended_row, attended_f32, log_sum = attend(
        query_hat, key_hat, value_hat, starts[:, None], block
    )
    attended = [take_block(attended_row, me, rows, 0)] + [
        shift(take_block(attended_row, (me + d) % nt, rows, 0), "tensor", d, nt)
        for d in range(1, nt)
    ]
    branch, middle, middle_low, middle_t = mix(attended, out_full, hidden_in, rates)
    row_segments = take_block(segments, me, rows, 0)
    live = (row_segments < pad_segment).astype(f32)[:, None]
    up, gate, hidden_units, result, middle_direct, mlp_out_low, mlp_out_t, rate_mlp_grad = feed(
        middle_low, mlp_full, scales_row, middle, cotangent, live, rates, step
    )
    def spread(value, places):
        width = value.shape[1] // nt
        whole = jnp.zeros_like(value)
        for p, d in enumerate(places):
            piece = value[:, p * width : (p + 1) * width]
            whole = put_block(whole, piece, (me + nt - d) % nt, 1)
        return whole

    per = hidden_width // step
    near = (nt - 1) * per
    feed_args = (mlp_out_low, mlp_out_t, middle_t, mlp_full, scales_row, up, gate, hidden_units)
    far_grad, far_scales, partial = feed_back(*feed_args, middle_direct, (), step, near, per)
    far_part = lax.psum_scatter(far_grad, "dp", scatter_dimension=1, tiled=True)
    near_grad, near_scales, token_direct, branch_low, rate_attn_grad = feed_back(
        *feed_args, partial, (branch, hidden_in, rates), step, 0, near
    )
    near_part = lax.psum_scatter(near_grad, "dp", scatter_dimension=1, tiled=True)

    grad_row = jnp.zeros((length, heads_width), bf16)
    for d in list(range(1, nt)) + [0]:
        piece = dot_nn(branch_low, out_full[:, d * heads_width : (d + 1) * heads_width])
        piece = piece.astype(bf16)
        piece = shift(piece, "tensor", -d, nt) if d else piece
        grad_row = put_block(grad_row, piece, (me + d) % nt, 0)
    out_grad = out_grads(attended, branch_low)

    scales_grad = spread(jnp.concatenate([near_scales, far_scales], axis=1), order)
    small = jnp.concatenate(
        [rate_attn_grad, rate_mlp_grad, scales_grad.reshape(-1, model)], axis=0
    )
    steps = [("tensor", nt, k) for k in doublings(nt)] + [("dp", nd, k) for k in doublings(nd)]

    def advance(small):
        return exchange_add(small, *steps.pop(0)) if steps else small

    far_part, grad_row, out_grad, small = lax.optimization_barrier(
        (far_part, grad_row, out_grad, small)
    )
    far_part = shift(far_part, "tensor", -middle_hop, nt)
    small = advance(small)
    head_grads = attend_back(
        query_hat, key_hat, value_hat, grad_row, attended_f32, log_sum, starts[None, :], block
    )
    head_grads, far_part, small = lax.optimization_barrier((head_grads, far_part, small))
    small = advance(small)
    out_sum = halving(out_grad, "dp", nd)
    qkv_grad, pieces, gain_grad = project_back(
        me.reshape(1),
        head_grads,
        (query_turned, key_turned),
        qkv_full,
        cosine,
        sine,
        gain,
        rows,
    )
    qkv_grad, pieces, small = lax.optimization_barrier((qkv_grad, pieces, small))
    pieces = [pieces[d * rows : (d + 1) * rows] for d in range(nt)]
    hidden_turn = [hidden_parts[(nt - d) % nt] for d in range(nt)]
    qkv_grad = projection_grads(hidden_turn, qkv_grad)
    gain_row = spread(jnp.concatenate(gather(gain_grad), axis=1), range(nt))

    def own_pieces(part, axis, width, places):
        pieces = [
            lax.slice_in_dim(part, p * width, (p + 1) * width, axis=axis)
            for p in range(len(places))
        ]
        return [shift(piece, "tensor", -d, nt) if d else piece for d, piece in zip(places, pieces)]

    ahead = behind = None
    for hop in range(1, nt):
        if hop == 2:
            small = advance(small)
            ahead, behind, qkv_grad, small = lax.optimization_barrier(
                (ahead, behind, qkv_grad, small)
            )
            small = advance(small)
            qkv_sum = halving(qkv_grad, "dp", nd)
            near_part, qkv_sum = lax.optimization_barrier((near_part, qkv_sum))
        if hop == max(2, nt - 1):
            ahead, behind, near_part, small = lax.optimization_barrier(
                (ahead, behind, near_part, small)
            )
        ahead, behind = line_sum(pieces, hop, ahead, behind, "tensor", nt)
    while steps:
        small = advance(small)
    total = token_direct + pieces[0].astype(f32)
    input_grad = (total + ahead.astype(f32) + behind.astype(f32)).astype(bf16)
    rates_grad = small[:2]
    mlp_scales_grad = small[2:].reshape(2, nt * hidden_width)

    out_own = sum(
        piece.astype(f32) for piece in own_pieces(out_sum.astype(bf16), 1, heads_width, range(nt))
    )
    attn_weight_grad = jnp.stack(
        [qkv_sum[:, m * heads_width : (m + 1) * heads_width] for m in range(3)] + [out_own]
    )
    attn_one, attn_two, attn_moved = adam_moved(
        attn_weight, attn_weight_grad, attn_moment_one, attn_moment_two
    )
    attn_square = jnp.sum(attn_moved * attn_moved, axis=1, keepdims=True)
    last = jnp.concatenate([attn_square.reshape(1, -1), gain_row], axis=1)
    last = butterfly(last, "dp", nd)
    attn_square = last[:, : 4 * heads_width].reshape(4, 1, heads_width)
    gain_row = last[:, 4 * heads_width :].reshape(-1)
    attn_new = attn_moved * lax.rsqrt(attn_square + norm_eps)

    mlp_pieces = own_pieces(near_part, 2, hidden_width, order[:-1]) + [far_part]
    mlp_weight_grad = sum(piece.astype(f32) for piece in mlp_pieces)
    mlp_one, mlp_two, mlp_moved = adam_moved(
        mlp_weight, mlp_weight_grad, mlp_moment_one, mlp_moment_two
    )
    mlp_square = jnp.sum(mlp_moved * mlp_moved, axis=1, keepdims=True)
    mlp_square = butterfly(mlp_square.reshape(1, -1), "dp", nd).reshape(mlp_square.shape)
    mlp_new = mlp_moved * lax.rsqrt(mlp_square + norm_eps)
    return (
        result.astype(bf16),
        input_grad,
        attn_weight_grad,
        mlp_weight_grad,
        rates_grad,
        gain_row,
        mlp_scales_grad,
        attn_one,
        attn_two,
        mlp_one,
        mlp_two,
        attn_new,
        mlp_new,
    )


def solution(mesh):
    weights = P(None, "dp", "tensor")
    tokens = P(("dp", "tensor"), None)
    return jax.shard_map(
        functools.partial(local, mesh.shape["dp"], mesh.shape["tensor"]),
        mesh=mesh,
        in_specs=(
            tokens,
            tokens,
            P("dp"),
            weights,
            weights,
            P(),
            P("tensor"),
            P(None, "tensor"),
            weights,
            weights,
            weights,
            weights,
        ),
        out_specs=(
            tokens,
            tokens,
            weights,
            weights,
            P(),
            P(),
            P(),
            weights,
            weights,
            weights,
            weights,
            weights,
            weights,
        ),
        check_vma=False,
    )
```

```python
import functools
import math

import jax
import jax.numpy as jnp
from jax import lax
from jax.experimental import pallas as pl
from jax.experimental.pallas import tpu as pltpu
from jax.sharding import PartitionSpec as P

HEAD_DIM = 64
LOG2E = 1.4426950408889634

norm_eps = 1e-06
pad_segment = 63
beta_one = 0.9
beta_two = 0.95
learning_rate = 0.01
adam_eps = 1e-08
bias_one = 1.0 - 0.9**10
bias_two = 1.0 - 0.95**10
scale_factor = math.sqrt(HEAD_DIM)
f32 = jnp.float32
bf16 = jnp.bfloat16


def starts_of(segment_row):
    indices = jnp.arange(segment_row.shape[0], dtype=jnp.int32)
    changed = jnp.concatenate(
        [jnp.ones((1,), dtype=jnp.bool_), segment_row[1:] != segment_row[:-1]]
    )
    return lax.cummax(jnp.where(changed, indices, jnp.zeros_like(indices)), axis=0)


def adam_moved(weight, gradient, moment_one, moment_two):
    moment_one_new = beta_one * moment_one + (1.0 - beta_one) * gradient
    moment_two_new = beta_two * moment_two + (1.0 - beta_two) * gradient * gradient
    moved = weight - learning_rate * (moment_one_new / bias_one) / (
        jnp.sqrt(moment_two_new / bias_two) + adam_eps
    )
    return (moment_one_new, moment_two_new, moved)


def dot_nt(a, b):
    return lax.dot_general(a, b, (((1,), (1,)), ((), ())), preferred_element_type=f32)


def dot_nn(a, b):
    return lax.dot_general(a, b, (((1,), (0,)), ((), ())), preferred_element_type=f32)


def dot_tn(a, b):
    return lax.dot_general(a, b, (((0,), (0,)), ((), ())), preferred_element_type=f32)


def head_stack(x, heads):
    lane = lax.broadcasted_iota(jnp.int32, x.shape, 1) // HEAD_DIM
    zero = jnp.zeros_like(x)
    return jnp.concatenate([jnp.where(lane == h, x, zero) for h in range(heads)], axis=0)


def head_pick(stacked, heads, rows):
    width = stacked.shape[1]
    lane = lax.broadcasted_iota(jnp.int32, (rows, width), 1) // HEAD_DIM
    picked = jnp.zeros((rows, width), f32)
    for h in range(heads):
        picked = jnp.where(lane == h, stacked[h * rows : (h + 1) * rows], picked)
    return picked


def attend_kernel(heads, bq, bk, q_ref, k_ref, v_ref, start_ref, o_ref, of_ref, l_ref, acc, lsum):
    i = pl.program_id(0)
    qs = head_stack(q_ref[...], heads)
    acc[...] = jnp.zeros_like(acc)
    lsum[...] = jnp.zeros_like(lsum)
    start = jnp.concatenate([start_ref[...]] * heads, axis=0)

    def step(j, diagonal):
        offset = pl.multiple_of(j * bk, bk)
        keys = k_ref[pl.ds(offset, bk), :]
        values = v_ref[pl.ds(offset, bk), :]
        scores = dot_nt(qs, keys)
        key_index = offset + lax.broadcasted_iota(jnp.int32, scores.shape, 1)
        allowed = key_index >= start
        if diagonal:
            row = lax.rem(lax.broadcasted_iota(jnp.int32, scores.shape, 0), bq)
            allowed = allowed & (key_index <= i * bq + row)
        weights = jnp.where(allowed, jnp.exp2(scores * (scale_factor * LOG2E)), 0.0)
        total = weights[:, :128]
        for part in range(1, bk // 128):
            total = total + weights[:, part * 128 : (part + 1) * 128]
        lsum[...] += total
        acc[...] += dot_nn(weights.astype(bf16), values)

    def body(j, carry):
        step(j, False)
        return carry

    lax.fori_loop(0, i, body, 0)
    step(i, True)
    summed = jnp.sum(lsum[...], axis=1, keepdims=True)
    out = head_pick(acc[...] * (1.0 / summed), heads, bq)
    of_ref[...] = out
    o_ref[...] = out.astype(bf16)
    l_ref[...] = jnp.log2(summed).reshape(heads, bq)


def attend(q, k, v, start, block):
    length, width = q.shape
    heads = width // HEAD_DIM
    whole = pl.BlockSpec((length, width), lambda i: (0, 0))
    rows = pl.BlockSpec((block, width), lambda i: (i, 0))
    return pl.pallas_call(
        functools.partial(attend_kernel, heads, block, block),
        grid=(length // block,),
        in_specs=[rows, whole, whole, pl.BlockSpec((block, 1), lambda i: (i, 0))],
        out_specs=[rows, rows, pl.BlockSpec((heads, block), lambda i: (0, i))],
        out_shape=[
            jax.ShapeDtypeStruct((length, width), bf16),
            jax.ShapeDtypeStruct((length, width), f32),
            jax.ShapeDtypeStruct((heads, length), f32),
        ],
        scratch_shapes=[
            pltpu.VMEM((heads * block, width), f32),
            pltpu.VMEM((heads * block, 128), f32),
        ],
        cost_estimate=pl.CostEstimate(
            flops=20_000_000_000, bytes_accessed=8 * length * width, transcendentals=0
        ),
        name="attend",
    )(q, k, v, start)


def attend_back_kernel(
    heads, bq, bk, q_ref, do_ref, k_ref, v_ref, of_ref, l_ref, start_ref, dq_ref, dk_ref, dv_ref, acc
):
    i = pl.program_id(0)

    @pl.when(i == 0)
    def _():
        dk_ref[...] = jnp.zeros_like(dk_ref)
        dv_ref[...] = jnp.zeros_like(dv_ref)

    qs = head_stack(q_ref[...], heads)
    grads = do_ref[...]
    dos = head_stack(grads, heads)
    product = (grads.astype(f32) * of_ref[...]).T
    delta = jnp.concatenate(
        [
            jnp.sum(product[h * HEAD_DIM : (h + 1) * HEAD_DIM], axis=0, keepdims=True)
            for h in range(heads)
        ],
        axis=1,
    )
    log_sum = jnp.concatenate([l_ref[h : h + 1, :] for h in range(heads)], axis=1)
    start = jnp.concatenate([start_ref[...]] * heads, axis=1)
    acc[...] = jnp.zeros_like(acc)

    def step(j, diagonal):
        offset = pl.multiple_of(j * bk, bk)
        keys = k_ref[pl.ds(offset, bk), :]
        values = v_ref[pl.ds(offset, bk), :]
        scores = dot_nt(keys, qs)
        key_index = offset + lax.broadcasted_iota(jnp.int32, scores.shape, 0)
        allowed = key_index >= start
        if diagonal:
            column = lax.rem(lax.broadcasted_iota(jnp.int32, scores.shape, 1), bq)
            allowed = allowed & (key_index <= i * bq + column)
        probs = jnp.where(allowed, jnp.exp2(scores * (scale_factor * LOG2E) - log_sum), 0.0)
        prob_grad = dot_nt(values, dos)
        score_grad = (probs * (prob_grad - delta)).astype(bf16)
        dv_ref[pl.ds(offset, bk), :] += dot_nn(probs.astype(bf16), dos)
        dk_ref[pl.ds(offset, bk), :] += dot_nn(score_grad, qs)
        acc[...] += dot_tn(score_grad, keys)

    def body(j, carry):
        step(j, False)
        return carry

    lax.fori_loop(0, i, body, 0)
    step(i, True)
    dq_ref[...] = head_pick(acc[...], heads, bq)


def attend_back(q, k, v, grads, out, log_sum, start, block):
    length, width = q.shape
    heads = width // HEAD_DIM
    whole = pl.BlockSpec((length, width), lambda i: (0, 0))
    rows = pl.BlockSpec((block, width), lambda i: (i, 0))
    result = jax.ShapeDtypeStruct((length, width), f32)
    return pl.pallas_call(
        functools.partial(attend_back_kernel, heads, block, block),
        grid=(length // block,),
        in_specs=[
            rows,
            rows,
            whole,
            whole,
            rows,
            pl.BlockSpec((heads, block), lambda i: (0, i)),
            pl.BlockSpec((1, block), lambda i: (0, i)),
        ],
        out_specs=[rows, whole, whole],
        out_shape=[result, result, result],
        scratch_shapes=[pltpu.VMEM((heads * block, width), f32)],
        cost_estimate=pl.CostEstimate(
            flops=40_000_000_000, bytes_accessed=20 * length * width, transcendentals=0
        ),
        name="attend_back",
    )(q, grads, k, v, out, log_sum, start)


def partner(x):
    width = x.shape[1]
    lane = lax.broadcasted_iota(jnp.int32, x.shape, 1)
    ahead = pltpu.roll(x, width - HEAD_DIM // 2, 1)
    behind = pltpu.roll(x, HEAD_DIM // 2, 1)
    return jnp.where(lax.rem(lane, HEAD_DIM) < HEAD_DIM // 2, ahead, behind)


def head_sums(x):
    width = x.shape[1]
    row = lax.broadcasted_iota(jnp.int32, (width, width), 0) // HEAD_DIM
    column = lax.broadcasted_iota(jnp.int32, (width, width), 1) // HEAD_DIM
    same = jnp.where(row == column, 1.0, 0.0).astype(f32)
    return lax.dot_general(
        x,
        same,
        (((1,), (0,)), ((), ())),
        precision=lax.Precision.HIGHEST,
        preferred_element_type=f32,
    )


def widen(table, width):
    return table if table.shape[1] == width else jnp.concatenate([table] * (width // 128), axis=1)


def added(refs):
    total = refs[0][...]
    for ref in refs[1:]:
        total = total + ref[...]
    return total


def project_kernel(count, index_ref, *refs):
    wq_ref, wk_ref, wv_ref, cos_ref, sin_ref, gain_ref = refs[count : count + 6]
    q_ref, k_ref, v_ref, xq_ref, xk_ref = refs[-5:]
    x = added(refs[:count])
    width = q_ref.shape[1]
    cosine = widen(cos_ref[...], width)
    sine = widen(sin_ref[...], width)
    gain = gain_ref[...]
    for w_ref, hat_ref, turned_ref in ((wq_ref, q_ref, xq_ref), (wk_ref, k_ref, xk_ref)):
        raw = dot_nn(x, w_ref[...])
        turned = raw * cosine + partner(raw) * sine
        turned_ref[...] = turned
        hat = turned * lax.rsqrt(head_sums(turned * turned) + norm_eps) * gain
        hat_ref[...] = hat.astype(bf16)
    v_ref[...] = dot_nn(x, wv_ref[...]).astype(bf16)


def project(index, parts, weights, cosine, sine, gain, length, previous):
    rows, model = parts[0].shape
    count = len(parts)
    width = gain.shape[1]
    part = min(256, rows)
    per = rows // part

    def column(m):
        return pl.BlockSpec((model, width), lambda i, at: (0, m))

    table = pl.BlockSpec((part, 128), lambda i, at: (at[0] * per + i, 0))
    out = pl.BlockSpec((part, width), lambda i, at: (at[0] * per + i, 0))
    low = jax.ShapeDtypeStruct((length, width), bf16)
    wide = jax.ShapeDtypeStruct((length, width), f32)
    return pl.pallas_call(
        functools.partial(project_kernel, count),
        grid_spec=pltpu.PrefetchScalarGridSpec(
            num_scalar_prefetch=1,
            grid=(per,),
            in_specs=[pl.BlockSpec((part, model), lambda i, at: (i, 0))] * count
            + [
                column(0),
                column(1),
                column(2),
                table,
                table,
                pl.BlockSpec((1, width), lambda i, at: (0, 0)),
            ]
            + [pl.BlockSpec(memory_space=pl.ANY)] * len(previous),
            out_specs=[out] * 5,
        ),
        out_shape=[low, low, low, wide, wide],
        input_output_aliases={7 + count + i: i for i in range(len(previous))},
        cost_estimate=pl.CostEstimate(
            flops=6 * rows * model * width, bytes_accessed=8 * model * width, transcendentals=0
        ),
        name="project",
    )(index, *parts, weights, weights, weights, cosine, sine, gain, *previous)


def project_back_kernel(
    index_ref,
    dq_ref,
    dk_ref,
    dv_ref,
    xq_ref,
    xk_ref,
    wq_ref,
    wk_ref,
    wv_ref,
    cos_ref,
    sin_ref,
    gain_ref,
    grad_ref,
    gain_grad_ref,
    *piece_refs,
):
    @pl.when(pl.program_id(0) == 0)
    def _():
        gain_grad_ref[...] = jnp.zeros_like(gain_grad_ref)

    width = dq_ref.shape[1]
    cosine = widen(cos_ref[...], width)
    sine = widen(sin_ref[...], width)
    gain = gain_ref[...]
    lows = []
    for d_ref, x_ref in ((dq_ref, xq_ref), (dk_ref, xk_ref)):
        turned = x_ref[...]
        inverse = lax.rsqrt(head_sums(turned * turned) + norm_eps)
        unit = turned * inverse
        hat_grad = d_ref[...] * scale_factor
        gain_grad_ref[...] += jnp.sum(hat_grad * unit, axis=0, keepdims=True)
        unit_grad = hat_grad * gain
        turned_grad = inverse * (unit_grad - unit * head_sums(unit * unit_grad))
        raw_grad = turned_grad * cosine - partner(turned_grad) * sine
        lows.append(raw_grad.astype(bf16))
    lows.append(dv_ref[...].astype(bf16))
    piece = jnp.zeros(piece_refs[0].shape, f32)
    for m, w_ref in enumerate((wq_ref, wk_ref, wv_ref)):
        grad_ref[:, m * width : (m + 1) * width] = lows[m]
        piece = piece + dot_nt(lows[m], w_ref[...])
    low = piece.astype(bf16)
    block = pl.program_id(0) // (pl.num_programs(0) // len(piece_refs))
    for d, piece_ref in enumerate(piece_refs):

        @pl.when(block == d)
        def _(piece_ref=piece_ref):
            piece_ref[...] = low


def project_back(index, grads, turned, weights, cosine, sine, gain, rows):
    length, width = grads[0].shape
    model = weights.shape[0]
    part = min(256, rows)
    per = rows // part
    blocks = length // part

    def column(m):
        return pl.BlockSpec((model, width), lambda i, at: (0, m))

    def turn(i, at):
        return (lax.rem(at[0] * per + i, blocks), 0)

    def piece_block(d):
        return pl.BlockSpec((part, model), lambda i, at: (jnp.clip(i - d * per, 0, per - 1), 0))

    tall = pl.BlockSpec((part, width), turn)
    table = pl.BlockSpec((part, 128), turn)
    return pl.pallas_call(
        project_back_kernel,
        grid_spec=pltpu.PrefetchScalarGridSpec(
            num_scalar_prefetch=1,
            grid=(blocks,),
            in_specs=[tall] * 5
            + [column(0), column(1), column(2), table, table]
            + [pl.BlockSpec((1, width), lambda i, at: (0, 0))],
            out_specs=[
                pl.BlockSpec((part, 3 * width), lambda i, at: (i, 0)),
                pl.BlockSpec((1, width), lambda i, at: (0, 0)),
            ]
            + [piece_block(d) for d in range(length // rows)],
        ),
        out_shape=[
            jax.ShapeDtypeStruct((length, 3 * width), bf16),
            jax.ShapeDtypeStruct((1, width), f32),
        ]
        + [jax.ShapeDtypeStruct((rows, model), bf16)] * (length // rows),
        cost_estimate=pl.CostEstimate(
            flops=8 * length * model * width,
            bytes_accessed=32 * length * width,
            transcendentals=0,
        ),
        name="project_back",
    )(index, *grads, *turned, weights, weights, weights, cosine, sine, gain)


def projection_grads_kernel(counts, *refs):
    grad_ref, out_ref = refs[-2:]
    total = None
    for d, count in enumerate(counts):
        hidden = added(refs[:count])
        refs = refs[count:]
        rows = hidden.shape[0]
        part = dot_tn(hidden, grad_ref[d * rows : (d + 1) * rows, :])
        total = part if total is None else total + part
    out_ref[...] = total.astype(bf16)


def projection_grads(hidden, qkv_grad):
    rows, model = hidden[0][0].shape
    length, width = qkv_grad.shape
    counts = tuple(len(parts) for parts in hidden)
    part = 256
    return pl.pallas_call(
        functools.partial(projection_grads_kernel, counts),
        grid=(model // part,),
        in_specs=[pl.BlockSpec((rows, part), lambda i: (0, i))] * sum(counts)
        + [pl.BlockSpec(qkv_grad.shape, lambda i: (0, 0))],
        out_specs=pl.BlockSpec((part, width), lambda i: (i, 0)),
        out_shape=jax.ShapeDtypeStruct((model, width), bf16),
        cost_estimate=pl.CostEstimate(
            flops=2 * length * model * width,
            bytes_accessed=8 * length * model,
            transcendentals=0,
        ),
        name="projection_grads",
    )(*[x for parts in hidden for x in parts], qkv_grad)


def out_grads_kernel(count, *refs):
    attended = refs[:count]
    branch_ref, out_ref = refs[count:]
    width = attended[0].shape[1]
    turned = branch_ref[...].T
    for d in range(count):
        out_ref[:, d * width : (d + 1) * width] = dot_nn(turned, attended[d][...]).astype(bf16)


def out_grads(attended, branch_grad):
    count = len(attended)
    rows, model = branch_grad.shape
    width = attended[0].shape[1]
    part = 256
    return pl.pallas_call(
        functools.partial(out_grads_kernel, count),
        grid=(model // part,),
        in_specs=[pl.BlockSpec(x.shape, lambda i: (0, 0)) for x in attended]
        + [pl.BlockSpec((rows, part), lambda i: (0, i))],
        out_specs=pl.BlockSpec((part, count * width), lambda i: (i, 0)),
        out_shape=jax.ShapeDtypeStruct((model, count * width), bf16),
        cost_estimate=pl.CostEstimate(
            flops=2 * rows * count * model * width,
            bytes_accessed=4 * rows * count * model,
            transcendentals=0,
        ),
        name="out_grads",
    )(*attended, branch_grad)


def rms_scale(x):
    return lax.rsqrt(jnp.mean(x * x, axis=-1, keepdims=True) + norm_eps)


def mix_kernel(count, *refs):
    pieces, weights = refs[:count], refs[count : 2 * count]
    hidden_ref, rates_ref, branch_ref, middle_ref, low_ref, turned_ref = refs[2 * count :]
    branch = dot_nt(pieces[0][...], weights[0][...])
    for d in range(1, count):
        branch = branch + dot_nt(pieces[d][...], weights[d][...])
    branch_ref[...] = branch
    hidden = hidden_ref[...].astype(f32)
    mixed = hidden + rates_ref[0:1, :] * (branch * rms_scale(branch) - hidden)
    middle = mixed * rms_scale(mixed)
    middle_ref[...] = middle
    low_ref[...] = middle.astype(bf16)
    turned_ref[...] = middle.T.astype(bf16)


def mix(pieces, weights, hidden, rates):
    count = len(pieces)
    rows, model = hidden.shape
    width = pieces[0].shape[1]
    part = min(128, rows)

    def column(d):
        return pl.BlockSpec((model, width), lambda i: (0, d))

    wide = pl.BlockSpec((part, model), lambda i: (i, 0))
    return pl.pallas_call(
        functools.partial(mix_kernel, count),
        grid=(rows // part,),
        in_specs=[pl.BlockSpec((part, width), lambda i: (i, 0))] * count
        + [column(d) for d in range(count)]
        + [wide, pl.BlockSpec((2, model), lambda i: (0, 0))],
        out_specs=[wide, wide, wide, pl.BlockSpec((model, part), lambda i: (0, i))],
        out_shape=[
            jax.ShapeDtypeStruct((rows, model), f32),
            jax.ShapeDtypeStruct((rows, model), f32),
            jax.ShapeDtypeStruct((rows, model), bf16),
            jax.ShapeDtypeStruct((model, rows), bf16),
        ],
        cost_estimate=pl.CostEstimate(
            flops=2 * rows * model * model, bytes_accessed=14 * rows * model, transcendentals=0
        ),
        name="mix",
    )(*pieces, *([weights] * count), hidden, rates)


def block_of(w_ref):
    value = w_ref[:, 0, 0]
    return value.reshape(value.shape[0] * value.shape[1], value.shape[2])


def feed_kernel(
    m_ref,
    wu_ref,
    wg_ref,
    wd_ref,
    s_ref,
    middle_ref,
    cot_ref,
    live_ref,
    rates_ref,
    up_ref,
    gate_ref,
    h_ref,
    result_ref,
    direct_ref,
    low_ref,
    turned_ref,
    rate_ref,
    acc,
):
    i = pl.program_id(0)
    tokens = m_ref[...]
    up = dot_nn(tokens, block_of(wu_ref))
    gate = dot_nn(tokens, block_of(wg_ref))
    up_ref[...] = up
    gate_ref[...] = gate
    scaled = gate * s_ref[1:2, :]
    hidden = (up * s_ref[0:1, :] * (scaled * jax.nn.sigmoid(scaled))).astype(bf16)
    h_ref[...] = hidden
    part_out = dot_nt(hidden, block_of(wd_ref))

    @pl.when(i == 0)
    def _():
        acc[...] = part_out

    @pl.when(i > 0)
    def _():
        acc[...] += part_out

    @pl.when(i == pl.num_programs(0) - 1)
    def _():
        rate_ref[...] = jnp.zeros_like(rate_ref)
        rate = rates_ref[1:2, :]
        part = 32

        def body(at, carry):
            rows = pl.ds(pl.multiple_of(at * part, part), part)
            out = acc[rows, :]
            middle = middle_ref[rows, :]
            out_scale = rms_scale(out)
            unit = out * out_scale
            mixed = middle + rate * (unit - middle)
            scale = rms_scale(mixed)
            final = mixed * scale
            result_ref[rows, :] = final.astype(bf16)
            grad = cot_ref[rows, :].astype(f32) * live_ref[rows, :]
            mixed_grad = scale * (grad - final * jnp.mean(final * grad, axis=-1, keepdims=True))
            direct_ref[rows, :] = mixed_grad * (1.0 - rate)
            rate_ref[...] += jnp.sum(mixed_grad * (unit - middle), axis=0, keepdims=True)
            unit_grad = mixed_grad * rate
            out_grad = out_scale * (
                unit_grad - unit * jnp.mean(unit * unit_grad, axis=-1, keepdims=True)
            )
            low_ref[rows, :] = out_grad.astype(bf16)
            return carry

        lax.fori_loop(0, acc.shape[0] // part, body, 0)
        for at in range(acc.shape[0] // 128):
            rows = slice(at * 128, (at + 1) * 128)
            turned_ref[:, rows] = low_ref[rows, :].T


def weight_specs(weights, step, base=0):
    nd, _, _, shard, local_width = weights.shape
    per = local_width // step

    def spec(m):
        return pl.BlockSpec(
            (nd, 1, 1, shard, step), lambda i: (0, (i + base) // per, m, 0, (i + base) % per)
        )

    return [spec(0), spec(1), spec(2)]


def feed(low, weights, scales, middle, cotangent, live, rates, step):
    rows, model = low.shape
    total = weights.shape[1] * weights.shape[4]
    columns = pl.BlockSpec((rows, step), lambda i: (0, i))
    whole = pl.BlockSpec((rows, model), lambda i: (0, 0))
    return pl.pallas_call(
        feed_kernel,
        grid=(total // step,),
        in_specs=[whole]
        + weight_specs(weights, step)
        + [
            pl.BlockSpec((2, step), lambda i: (0, i)),
            whole,
            whole,
            pl.BlockSpec((rows, 1), lambda i: (0, 0)),
            pl.BlockSpec((2, model), lambda i: (0, 0)),
        ],
        out_specs=[columns, columns, columns, whole, whole, whole]
        + [
            pl.BlockSpec((model, rows), lambda i: (0, 0)),
            pl.BlockSpec((1, model), lambda i: (0, 0)),
        ],
        out_shape=[
            jax.ShapeDtypeStruct((rows, total), f32),
            jax.ShapeDtypeStruct((rows, total), f32),
            jax.ShapeDtypeStruct((rows, total), bf16),
            jax.ShapeDtypeStruct((rows, model), bf16),
            jax.ShapeDtypeStruct((rows, model), f32),
            jax.ShapeDtypeStruct((rows, model), bf16),
            jax.ShapeDtypeStruct((model, rows), bf16),
            jax.ShapeDtypeStruct((1, model), f32),
        ],
        scratch_shapes=[pltpu.VMEM((rows, model), f32)],
        cost_estimate=pl.CostEstimate(
            flops=6 * rows * model * total,
            bytes_accessed=6 * model * total + 10 * rows * total,
            transcendentals=0,
        ),
        name="feed",
    )(low, weights, weights, weights, scales, middle, cotangent, live, rates)


def feed_back_step(
    og_ref, ogt_ref, mt_ref, wu_ref, wg_ref, wd_ref, s_ref, up_ref, gate_ref, h_ref, start_ref, grad_ref, sg_ref, acc
):
    i = pl.program_id(0)
    grad_ref[2] = dot_nn(ogt_ref[...], h_ref[...]).astype(bf16)
    hidden_grad = dot_nn(og_ref[...], block_of(wd_ref))
    up = up_ref[...]
    gate = gate_ref[...]
    up_gain = s_ref[0:1, :]
    gate_gain = s_ref[1:2, :]
    scaled = gate * gate_gain
    sig = jax.nn.sigmoid(scaled)
    up_part = hidden_grad * (scaled * sig)
    gate_part = hidden_grad * (up * up_gain) * (sig * (1.0 + scaled * (1.0 - sig)))
    sg_ref[0:1, :] = jnp.sum(up_part * up, axis=0, keepdims=True)
    sg_ref[1:2, :] = jnp.sum(gate_part * gate, axis=0, keepdims=True)
    up_low = (up_part * up_gain).astype(bf16)
    gate_low = (gate_part * gate_gain).astype(bf16)
    tokens_t = mt_ref[...]
    grad_ref[0] = dot_nn(tokens_t, up_low).astype(bf16)
    grad_ref[1] = dot_nn(tokens_t, gate_low).astype(bf16)
    back = dot_nt(up_low, block_of(wu_ref)) + dot_nt(gate_low, block_of(wg_ref))

    @pl.when(i == 0)
    def _():
        acc[...] = start_ref[...] + back

    @pl.when(i > 0)
    def _():
        acc[...] += back


def feed_back_first_kernel(*refs):
    feed_back_step(*refs)


def feed_back_last_kernel(*refs):
    branch_ref, hidden_ref, rates_ref = refs[11:14]
    grad_ref, sg_ref, token_ref, low_ref, rate_ref, acc = refs[14:]
    feed_back_step(*refs[:11], grad_ref, sg_ref, acc)

    @pl.when(pl.program_id(0) == pl.num_programs(0) - 1)
    def _():
        rate_ref[...] = jnp.zeros_like(rate_ref)
        rate = rates_ref[0:1, :]
        part = 32

        def body(at, carry):
            rows = pl.ds(pl.multiple_of(at * part, part), part)
            grad = acc[rows, :]
            branch = branch_ref[rows, :]
            hidden = hidden_ref[rows, :].astype(f32)
            branch_scale = rms_scale(branch)
            unit = branch * branch_scale
            mixed = hidden + rate * (unit - hidden)
            scale = rms_scale(mixed)
            middle = mixed * scale
            mixed_grad = scale * (grad - middle * jnp.mean(middle * grad, axis=-1, keepdims=True))
            token_ref[rows, :] = mixed_grad * (1.0 - rate)
            rate_ref[...] += jnp.sum(mixed_grad * (unit - hidden), axis=0, keepdims=True)
            unit_grad = mixed_grad * rate
            branch_grad = branch_scale * (
                unit_grad - unit * jnp.mean(unit * unit_grad, axis=-1, keepdims=True)
            )
            low_ref[rows, :] = branch_grad.astype(bf16)
            return carry

        lax.fori_loop(0, acc.shape[0] // part, body, 0)


def feed_back(
    out_grad, out_grad_t, middle_t, weights, scales, up, gate, hidden_units, start, mixing, step, base, count
):
    model, rows = middle_t.shape
    width = count * step
    columns = pl.BlockSpec((rows, step), lambda i: (0, i + base))
    whole = pl.BlockSpec((rows, model), lambda i: (0, 0))
    turned = pl.BlockSpec((model, rows), lambda i: (0, 0))
    wide = jax.ShapeDtypeStruct((rows, model), f32)
    grads_specs = [
        pl.BlockSpec((3, model, step), lambda i: (0, 0, i)),
        pl.BlockSpec((2, step), lambda i: (0, i)),
    ]
    grads_shapes = [
        jax.ShapeDtypeStruct((3, model, width), bf16),
        jax.ShapeDtypeStruct((2, width), f32),
    ]
    last = bool(mixing)
    return pl.pallas_call(
        feed_back_last_kernel if last else feed_back_first_kernel,
        grid=(count,),
        in_specs=[whole, turned, turned]
        + weight_specs(weights, step, base)
        + [pl.BlockSpec((2, step), lambda i: (0, i + base)), columns, columns, columns, whole]
        + ([whole, whole, pl.BlockSpec((2, model), lambda i: (0, 0))] if last else []),
        out_specs=grads_specs
        + ([whole, whole, pl.BlockSpec((1, model), lambda i: (0, 0))] if last else [whole]),
        out_shape=grads_shapes
        + (
            [
                wide,
                jax.ShapeDtypeStruct((rows, model), bf16),
                jax.ShapeDtypeStruct((1, model), f32),
            ]
            if last
            else [wide]
        ),
        scratch_shapes=[pltpu.VMEM((rows, model), f32)] if last else [],
        cost_estimate=pl.CostEstimate(
            flops=12 * rows * model * width,
            bytes_accessed=12 * model * width + 10 * rows * width,
            transcendentals=0,
        ),
        name="feed_back_last" if last else "feed_back_first",
    )(
        out_grad,
        out_grad_t,
        middle_t,
        weights,
        weights,
        weights,
        scales,
        up,
        gate,
        hidden_units,
        start,
        *mixing,
    )


def shift(value, axis, distance, size):
    return lax.ppermute(value, axis, [(i, (i + distance) % size) for i in range(size)])


def carry_on(up, down, hop, axis, size):
    up = lax.ppermute(up, axis, [(i, i + 1) for i in range(hop - 1, size - 1)])
    down = lax.ppermute(down, axis, [(i, i - 1) for i in range(1, size - hop + 1)])
    return up, down


def line_sum(pieces, hop, up, down, axis, size):
    ahead, behind = pieces[size - hop], pieces[hop]
    ahead = ahead if up is None else ahead + up
    behind = behind if down is None else behind + down
    up = lax.ppermute(ahead, axis, [(i, i + 1) for i in range(hop)])
    down = lax.ppermute(behind, axis, [(i, i - 1) for i in range(size - hop, size)])
    return up, down


def halving(value, axis, size, step):
    count, rows, width = value.shape
    bit = (lax.axis_index(axis) // step) % 2
    pairs = value.reshape(count // 2, 2, rows, width)
    sent = lax.dynamic_index_in_dim(pairs, 1 - bit, 1, False)
    kept = lax.dynamic_index_in_dim(pairs, bit, 1, False)
    other = lax.ppermute(sent, axis, [(i, i ^ step) for i in range(size)])
    value = kept.astype(f32) + other.astype(f32)
    return value[0] if 2 * step == size else value.astype(bf16)


def exchange_add(value, axis, size, step):
    return value + lax.ppermute(value, axis, [(i, i ^ step) for i in range(size)])


def doublings(size):
    return [1 << k for k in range(size.bit_length() - 1)]


def butterfly(value, axis, size):
    for step in doublings(size):
        value = exchange_add(value, axis, size, step)
    return value


def take_block(value, index, size, axis):
    return lax.dynamic_slice_in_dim(value, index * size, size, axis)


def put_block(whole, value, index, axis):
    return lax.dynamic_update_slice_in_dim(whole, value, index * value.shape[axis], axis)


def local(
    nd,
    nt,
    hidden_in,
    cotangent,
    segments,
    attn_weight,
    mlp_weight,
    rates,
    qk_scale,
    mlp_scales,
    attn_moment_one,
    attn_moment_two,
    mlp_moment_one,
    mlp_moment_two,
):
    rows, model = hidden_in.shape
    length = segments.shape[0]
    shard = attn_weight.shape[1]
    heads_width = attn_weight.shape[2]
    hidden_width = mlp_weight.shape[2]
    block = min(512, length)
    step = min(512, hidden_width)
    me = lax.axis_index("tensor")

    def gather(value):
        return [value] + [shift(value, "tensor", d, nt) for d in range(1, nt)]

    def both(ups, downs, d):
        return (ups[0],) if d == 0 else (ups[d], downs[nt - d])

    middle_hop = nt // 2
    order = [d for d in range(nt) if d != middle_hop] + [middle_hop]
    attn_low = attn_weight.astype(bf16)
    qkv_full = lax.all_gather(
        jnp.concatenate([attn_low[0], attn_low[1], attn_low[2]], axis=1), "dp", axis=0, tiled=True
    )
    mlp_low = mlp_weight.astype(bf16).reshape(3 * shard, hidden_width)
    out_low = attn_low[3]
    ups, downs = [mlp_low], [mlp_low]
    for hop in range(1, nt):
        if hop == 2:
            ups[1], downs[1], out_low = lax.optimization_barrier((ups[1], downs[1], out_low))
        if hop == nt - 1:
            ups[-1], downs[-1], hidden_in = lax.optimization_barrier((ups[-1], downs[-1], hidden_in))
        up, down = carry_on(ups[-1], downs[-1], hop, "tensor", nt)
        ups.append(up)
        downs.append(down)
    out_full = lax.all_gather(jnp.concatenate(gather(out_low), axis=1), "dp", axis=0, tiled=True)
    mlp_full = lax.all_gather(
        jnp.concatenate([sum(both(ups, downs, d)) for d in order], axis=0), "dp", axis=0, tiled=True
    )
    mlp_full = mlp_full.reshape(nd, nt, 3, shard, hidden_width)
    scales_parts = gather(mlp_scales)
    scales_row = jnp.concatenate([scales_parts[d] for d in order], axis=1)

    starts = starts_of(segments)
    positions = (jnp.arange(length, dtype=jnp.int32) - starts).astype(f32)
    lane = jnp.arange(128, dtype=jnp.int32)
    half = HEAD_DIM // 2
    frequency = 10000.0 ** (-(lane % half).astype(f32) / half)
    sign = jnp.where(lane % HEAD_DIM < half, -1.0, 1.0)
    angles = positions[:, None] * frequency[None, :]
    cosine = jnp.cos(angles)
    sine = jnp.sin(angles) * sign[None, :]
    gain = qk_scale.reshape(1, heads_width)

    ups, downs, state = [hidden_in], [hidden_in], ()
    hidden_parts = [None] * nt

    def projected(hop, state):
        for d in range(nt):
            if (max(d, nt - d) if d else 0) == hop:
                hidden_parts[d] = both(ups, downs, d)
                index = ((me + nt - d) % nt).reshape(1)
                state = project(index, hidden_parts[d], qkv_full, cosine, sine, gain, length, state)
        return state

    for hop in range(1, nt):
        ups[-1], downs[-1], state = lax.optimization_barrier((ups[-1], downs[-1], state))
        up, down = carry_on(ups[-1], downs[-1], hop, "tensor", nt)
        ups.append(up)
        downs.append(down)
        state = projected(hop - 1, state)
    ups[-1], downs[-1], state = lax.optimization_barrier((ups[-1], downs[-1], state))
    state = projected(nt - 1, state)
    query_hat, key_hat, value_hat, query_turned, key_turned = state
    attended_row, attended_f32, log_sum = attend(
        query_hat, key_hat, value_hat, starts[:, None], block
    )
    attended = [take_block(attended_row, me, rows, 0)] + [
        shift(take_block(attended_row, (me + d) % nt, rows, 0), "tensor", d, nt)
        for d in range(1, nt)
    ]
    branch, middle, middle_low, middle_t = mix(attended, out_full, hidden_in, rates)
    row_segments = take_block(segments, me, rows, 0)
    live = (row_segments < pad_segment).astype(f32)[:, None]
    up, gate, hidden_units, result, middle_direct, mlp_out_low, mlp_out_t, rate_mlp_grad = feed(
        middle_low, mlp_full, scales_row, middle, cotangent, live, rates, step
    )
    def spread(value, places):
        width = value.shape[1] // nt
        whole = jnp.zeros_like(value)
        for p, d in enumerate(places):
            piece = value[:, p * width : (p + 1) * width]
            whole = put_block(whole, piece, (me + nt - d) % nt, 1)
        return whole

    per = hidden_width // step
    near = (nt - 1) * per
    feed_args = (mlp_out_low, mlp_out_t, middle_t, mlp_full, scales_row, up, gate, hidden_units)
    far_grad, far_scales, partial = feed_back(*feed_args, middle_direct, (), step, near, per)
    far_part = lax.psum_scatter(far_grad, "dp", scatter_dimension=1, tiled=True)
    near_grad, near_scales, token_direct, branch_low, rate_attn_grad = feed_back(
        *feed_args, partial, (branch, hidden_in, rates), step, 0, near
    )
    near_part = lax.psum_scatter(near_grad, "dp", scatter_dimension=1, tiled=True)

    grad_row = jnp.zeros((length, heads_width), bf16)
    for d in list(range(1, nt)) + [0]:
        piece = dot_nn(branch_low, out_full[:, d * heads_width : (d + 1) * heads_width])
        piece = piece.astype(bf16)
        piece = shift(piece, "tensor", -d, nt) if d else piece
        grad_row = put_block(grad_row, piece, (me + d) % nt, 0)
    out_grad = out_grads(attended, branch_low)

    scales_grad = spread(jnp.concatenate([near_scales, far_scales], axis=1), order)
    small = jnp.concatenate(
        [rate_attn_grad, rate_mlp_grad, scales_grad.reshape(-1, model)], axis=0
    )
    steps = [("tensor", nt, k) for k in doublings(nt)] + [("dp", nd, k) for k in doublings(nd)]

    def advance(small):
        return exchange_add(small, *steps.pop(0)) if steps else small

    far_part, grad_row, out_grad, small = lax.optimization_barrier(
        (far_part, grad_row, out_grad, small)
    )
    small = advance(small)
    halvings = doublings(nd)
    out_sum = halving(out_grad.reshape(nd, shard, -1), "dp", nd, halvings[0])
    head_grads = attend_back(
        query_hat, key_hat, value_hat, grad_row, attended_f32, log_sum, starts[None, :], block
    )
    head_grads, far_part, small, out_sum = lax.optimization_barrier(
        (head_grads, far_part, small, out_sum)
    )
    far_part = shift(far_part, "tensor", -middle_hop, nt)
    small = advance(small)
    out_sum = halving(out_sum, "dp", nd, halvings[1])
    qkv_grad, gain_grad, *pieces = project_back(
        me.reshape(1),
        head_grads,
        (query_turned, key_turned),
        qkv_full,
        cosine,
        sine,
        gain,
        rows,
    )
    qkv_grad, pieces, small, out_sum, far_part = lax.optimization_barrier(
        (qkv_grad, pieces, small, out_sum, far_part)
    )
    for k in halvings[2:]:
        out_sum = halving(out_sum, "dp", nd, k)
    hidden_turn = [hidden_parts[(nt - d) % nt] for d in range(nt)]
    qkv_sum = projection_grads(hidden_turn, qkv_grad)
    qkv_sum = qkv_sum.reshape(nd, shard, -1)

    def own_pieces(part, axis, width, places):
        pieces = [
            lax.slice_in_dim(part, p * width, (p + 1) * width, axis=axis)
            for p in range(len(places))
        ]
        return [shift(piece, "tensor", -d, nt) if d else piece for d, piece in zip(places, pieces)]

    ahead = behind = None
    for hop in range(1, nt):
        if hop == 2:
            ahead, behind, qkv_sum, out_sum = lax.optimization_barrier(
                (ahead, behind, qkv_sum, out_sum)
            )
            out_pieces = own_pieces(out_sum.astype(bf16), 1, heads_width, range(nt))
            gain_parts = gather(gain_grad)
        if hop == max(2, nt - 1):
            ahead, behind, near_part, qkv_sum, out_pieces, gain_parts, small = (
                lax.optimization_barrier(
                    (ahead, behind, near_part, qkv_sum, out_pieces, gain_parts, small)
                )
            )
            near_pieces = own_pieces(near_part, 2, hidden_width, order[:-1])
            for k in halvings[:2]:
                qkv_sum = halving(qkv_sum, "dp", nd, k)
            ahead, behind, qkv_sum = lax.optimization_barrier((ahead, behind, qkv_sum))
        ahead, behind = line_sum(pieces, hop, ahead, behind, "tensor", nt)
    for k in halvings[2:]:
        qkv_sum = halving(qkv_sum, "dp", nd, k)
    near_pieces, qkv_sum = lax.optimization_barrier((near_pieces, qkv_sum))
    gain_row = spread(jnp.concatenate(gain_parts, axis=1), range(nt))
    while steps:
        small = advance(small)
    total = token_direct + pieces[0].astype(f32)
    input_grad = (total + ahead.astype(f32) + behind.astype(f32)).astype(bf16)
    rates_grad = small[:2]
    mlp_scales_grad = small[2:].reshape(2, nt * hidden_width)

    out_own = sum(piece.astype(f32) for piece in out_pieces)
    attn_weight_grad = jnp.stack(
        [qkv_sum[:, m * heads_width : (m + 1) * heads_width] for m in range(3)] + [out_own]
    )
    attn_one, attn_two, attn_moved = adam_moved(
        attn_weight, attn_weight_grad, attn_moment_one, attn_moment_two
    )
    attn_square = jnp.sum(attn_moved * attn_moved, axis=1, keepdims=True)
    last = jnp.concatenate([attn_square.reshape(1, -1), gain_row], axis=1)
    last = butterfly(last, "dp", nd)
    attn_square = last[:, : 4 * heads_width].reshape(4, 1, heads_width)
    gain_row = last[:, 4 * heads_width :].reshape(-1)
    attn_new = attn_moved * lax.rsqrt(attn_square + norm_eps)

    mlp_weight_grad = sum(piece.astype(f32) for piece in near_pieces + [far_part])
    mlp_one, mlp_two, mlp_moved = adam_moved(
        mlp_weight, mlp_weight_grad, mlp_moment_one, mlp_moment_two
    )
    mlp_square = jnp.sum(mlp_moved * mlp_moved, axis=1, keepdims=True)
    mlp_square = butterfly(mlp_square.reshape(1, -1), "dp", nd).reshape(mlp_square.shape)
    mlp_new = mlp_moved * lax.rsqrt(mlp_square + norm_eps)
    return (
        result.astype(bf16),
        input_grad,
        attn_weight_grad,
        mlp_weight_grad,
        rates_grad,
        gain_row,
        mlp_scales_grad,
        attn_one,
        attn_two,
        mlp_one,
        mlp_two,
        attn_new,
        mlp_new,
    )


def solution(mesh):
    weights = P(None, "dp", "tensor")
    tokens = P(("dp", "tensor"), None)
    return jax.shard_map(
        functools.partial(local, mesh.shape["dp"], mesh.shape["tensor"]),
        mesh=mesh,
        in_specs=(
            tokens,
            tokens,
            P("dp"),
            weights,
            weights,
            P(),
            P("tensor"),
            P(None, "tensor"),
            weights,
            weights,
            weights,
            weights,
        ),
        out_specs=(
            tokens,
            tokens,
            weights,
            weights,
            P(),
            P(),
            P(),
            weights,
            weights,
            weights,
            weights,
            weights,
            weights,
        ),
        check_vma=False,
    )
```

```python
import functools
import math

import jax
import jax.numpy as jnp
from jax import lax
from jax.experimental import pallas as pl
from jax.experimental.pallas import tpu as pltpu
from jax.sharding import PartitionSpec as P

HEAD_DIM = 64
LOG2E = 1.4426950408889634

norm_eps = 1e-06
pad_segment = 63
beta_one = 0.9
beta_two = 0.95
learning_rate = 0.01
adam_eps = 1e-08
bias_one = 1.0 - 0.9**10
bias_two = 1.0 - 0.95**10
scale_factor = math.sqrt(HEAD_DIM)
f32 = jnp.float32
bf16 = jnp.bfloat16


def starts_of(segment_row):
    indices = jnp.arange(segment_row.shape[0], dtype=jnp.int32)
    changed = jnp.concatenate(
        [jnp.ones((1,), dtype=jnp.bool_), segment_row[1:] != segment_row[:-1]]
    )
    return lax.cummax(jnp.where(changed, indices, jnp.zeros_like(indices)), axis=0)


def adam_moved(weight, gradient, moment_one, moment_two):
    moment_one_new = beta_one * moment_one + (1.0 - beta_one) * gradient
    moment_two_new = beta_two * moment_two + (1.0 - beta_two) * gradient * gradient
    moved = weight - learning_rate * (moment_one_new / bias_one) / (
        jnp.sqrt(moment_two_new / bias_two) + adam_eps
    )
    return (moment_one_new, moment_two_new, moved)


def dot_nt(a, b):
    return lax.dot_general(a, b, (((1,), (1,)), ((), ())), preferred_element_type=f32)


def dot_nn(a, b):
    return lax.dot_general(a, b, (((1,), (0,)), ((), ())), preferred_element_type=f32)


def dot_tn(a, b):
    return lax.dot_general(a, b, (((0,), (0,)), ((), ())), preferred_element_type=f32)


def head_stack(x, heads):
    lane = lax.broadcasted_iota(jnp.int32, x.shape, 1) // HEAD_DIM
    zero = jnp.zeros_like(x)
    return jnp.concatenate([jnp.where(lane == h, x, zero) for h in range(heads)], axis=0)


def head_pick(stacked, heads, rows):
    width = stacked.shape[1]
    lane = lax.broadcasted_iota(jnp.int32, (rows, width), 1) // HEAD_DIM
    picked = jnp.zeros((rows, width), f32)
    for h in range(heads):
        picked = jnp.where(lane == h, stacked[h * rows : (h + 1) * rows], picked)
    return picked


def attend_kernel(heads, bq, bk, q_ref, k_ref, v_ref, start_ref, o_ref, of_ref, l_ref, acc, lsum):
    i = pl.program_id(0)
    qs = head_stack(q_ref[...], heads)
    acc[...] = jnp.zeros_like(acc)
    lsum[...] = jnp.zeros_like(lsum)
    start = jnp.concatenate([start_ref[...]] * heads, axis=0)

    def step(j, diagonal):
        offset = pl.multiple_of(j * bk, bk)
        keys = k_ref[pl.ds(offset, bk), :]
        values = v_ref[pl.ds(offset, bk), :]
        scores = dot_nt(qs, keys)
        key_index = offset + lax.broadcasted_iota(jnp.int32, scores.shape, 1)
        allowed = key_index >= start
        if diagonal:
            row = lax.rem(lax.broadcasted_iota(jnp.int32, scores.shape, 0), bq)
            allowed = allowed & (key_index <= i * bq + row)
        weights = jnp.where(allowed, jnp.exp2(scores * (scale_factor * LOG2E)), 0.0)
        total = weights[:, :128]
        for part in range(1, bk // 128):
            total = total + weights[:, part * 128 : (part + 1) * 128]
        lsum[...] += total
        acc[...] += dot_nn(weights.astype(bf16), values)

    def body(j, carry):
        step(j, False)
        return carry

    lax.fori_loop(0, i, body, 0)
    step(i, True)
    summed = jnp.sum(lsum[...], axis=1, keepdims=True)
    out = head_pick(acc[...] * (1.0 / summed), heads, bq)
    of_ref[...] = out
    o_ref[...] = out.astype(bf16)
    l_ref[...] = jnp.log2(summed).reshape(heads, bq)


def attend(q, k, v, start, block):
    length, width = q.shape
    heads = width // HEAD_DIM
    whole = pl.BlockSpec((length, width), lambda i: (0, 0))
    rows = pl.BlockSpec((block, width), lambda i: (i, 0))
    return pl.pallas_call(
        functools.partial(attend_kernel, heads, block, block),
        grid=(length // block,),
        in_specs=[rows, whole, whole, pl.BlockSpec((block, 1), lambda i: (i, 0))],
        out_specs=[rows, rows, pl.BlockSpec((heads, block), lambda i: (0, i))],
        out_shape=[
            jax.ShapeDtypeStruct((length, width), bf16),
            jax.ShapeDtypeStruct((length, width), f32),
            jax.ShapeDtypeStruct((heads, length), f32),
        ],
        scratch_shapes=[
            pltpu.VMEM((heads * block, width), f32),
            pltpu.VMEM((heads * block, 128), f32),
        ],
        cost_estimate=pl.CostEstimate(
            flops=20_000_000_000, bytes_accessed=8 * length * width, transcendentals=0
        ),
        name="attend",
    )(q, k, v, start)


def attend_back_kernel(
    first, heads, bq, bk, q_ref, do_ref, k_ref, v_ref, of_ref, l_ref, start_ref, dq_ref, dk_ref, dv_ref, acc
):
    i = pl.program_id(0)

    @pl.when(i == 0)
    def _():
        dk_ref[...] = jnp.zeros_like(dk_ref)
        dv_ref[...] = jnp.zeros_like(dv_ref)

    qs = head_stack(q_ref[...], heads)
    grads = do_ref[...]
    dos = head_stack(grads, heads)
    product = (grads.astype(f32) * of_ref[...]).T
    delta = jnp.concatenate(
        [
            jnp.sum(product[h * HEAD_DIM : (h + 1) * HEAD_DIM], axis=0, keepdims=True)
            for h in range(heads)
        ],
        axis=1,
    )
    log_sum = jnp.concatenate([l_ref[first + h : first + h + 1, :] for h in range(heads)], axis=1)
    start = jnp.concatenate([start_ref[...]] * heads, axis=1)
    acc[...] = jnp.zeros_like(acc)

    def step(j, diagonal):
        offset = pl.multiple_of(j * bk, bk)
        keys = k_ref[pl.ds(offset, bk), :]
        values = v_ref[pl.ds(offset, bk), :]
        scores = dot_nt(keys, qs)
        key_index = offset + lax.broadcasted_iota(jnp.int32, scores.shape, 0)
        allowed = key_index >= start
        if diagonal:
            column = lax.rem(lax.broadcasted_iota(jnp.int32, scores.shape, 1), bq)
            allowed = allowed & (key_index <= i * bq + column)
        probs = jnp.where(allowed, jnp.exp2(scores * (scale_factor * LOG2E) - log_sum), 0.0)
        prob_grad = dot_nt(values, dos)
        score_grad = (probs * (prob_grad - delta)).astype(bf16)
        dv_ref[pl.ds(offset, bk), :] += dot_nn(probs.astype(bf16), dos)
        dk_ref[pl.ds(offset, bk), :] += dot_nn(score_grad, qs)
        acc[...] += dot_tn(score_grad, keys)

    def body(j, carry):
        step(j, False)
        return carry

    lax.fori_loop(0, i, body, 0)
    step(i, True)
    dq_ref[...] = head_pick(acc[...], heads, bq)


def attend_back(q, k, v, grads, out, log_sum, start, block, group, width):
    length = q.shape[0]
    heads = width // HEAD_DIM
    taken = pl.BlockSpec((length, width), lambda i: (0, group))
    taken_rows = pl.BlockSpec((block, width), lambda i: (i, group))
    whole = pl.BlockSpec((length, width), lambda i: (0, 0))
    rows = pl.BlockSpec((block, width), lambda i: (i, 0))
    result = jax.ShapeDtypeStruct((length, width), f32)
    return pl.pallas_call(
        functools.partial(attend_back_kernel, group * heads, heads, block, block),
        grid=(length // block,),
        in_specs=[
            taken_rows,
            taken_rows,
            taken,
            taken,
            taken_rows,
            pl.BlockSpec((log_sum.shape[0], block), lambda i: (0, i)),
            pl.BlockSpec((1, block), lambda i: (0, i)),
        ],
        out_specs=[rows, whole, whole],
        out_shape=[result, result, result],
        scratch_shapes=[pltpu.VMEM((heads * block, width), f32)],
        cost_estimate=pl.CostEstimate(
            flops=40_000_000_000, bytes_accessed=20 * length * width, transcendentals=0
        ),
        name="attend_back",
    )(q, grads, k, v, out, log_sum, start)


def partner(x):
    width = x.shape[1]
    lane = lax.broadcasted_iota(jnp.int32, x.shape, 1)
    ahead = pltpu.roll(x, width - HEAD_DIM // 2, 1)
    behind = pltpu.roll(x, HEAD_DIM // 2, 1)
    return jnp.where(lax.rem(lane, HEAD_DIM) < HEAD_DIM // 2, ahead, behind)


def head_sums(x):
    width = x.shape[1]
    row = lax.broadcasted_iota(jnp.int32, (width, width), 0) // HEAD_DIM
    column = lax.broadcasted_iota(jnp.int32, (width, width), 1) // HEAD_DIM
    same = jnp.where(row == column, 1.0, 0.0).astype(f32)
    return lax.dot_general(
        x,
        same,
        (((1,), (0,)), ((), ())),
        precision=lax.Precision.HIGHEST,
        preferred_element_type=f32,
    )


def widen(table, width):
    return table if table.shape[1] == width else jnp.concatenate([table] * (width // 128), axis=1)


def added(refs):
    total = refs[0][...]
    for ref in refs[1:]:
        total = total + ref[...]
    return total


def project_kernel(count, index_ref, *refs):
    wq_ref, wk_ref, wv_ref, cos_ref, sin_ref, gain_ref = refs[count : count + 6]
    q_ref, k_ref, v_ref, xq_ref, xk_ref = refs[-5:]
    x = added(refs[:count])
    width = q_ref.shape[1]
    cosine = widen(cos_ref[...], width)
    sine = widen(sin_ref[...], width)
    gain = gain_ref[...]
    for w_ref, hat_ref, turned_ref in ((wq_ref, q_ref, xq_ref), (wk_ref, k_ref, xk_ref)):
        raw = dot_nn(x, w_ref[...])
        turned = raw * cosine + partner(raw) * sine
        turned_ref[...] = turned
        hat = turned * lax.rsqrt(head_sums(turned * turned) + norm_eps) * gain
        hat_ref[...] = hat.astype(bf16)
    v_ref[...] = dot_nn(x, wv_ref[...]).astype(bf16)


def project(index, parts, weights, cosine, sine, gain, length, previous):
    rows, model = parts[0].shape
    count = len(parts)
    width = gain.shape[1]
    part = min(256, rows)
    per = rows // part

    def column(m):
        return pl.BlockSpec((model, width), lambda i, at: (0, m))

    table = pl.BlockSpec((part, 128), lambda i, at: (at[0] * per + i, 0))
    out = pl.BlockSpec((part, width), lambda i, at: (at[0] * per + i, 0))
    low = jax.ShapeDtypeStruct((length, width), bf16)
    wide = jax.ShapeDtypeStruct((length, width), f32)
    return pl.pallas_call(
        functools.partial(project_kernel, count),
        grid_spec=pltpu.PrefetchScalarGridSpec(
            num_scalar_prefetch=1,
            grid=(per,),
            in_specs=[pl.BlockSpec((part, model), lambda i, at: (i, 0))] * count
            + [
                column(0),
                column(1),
                column(2),
                table,
                table,
                pl.BlockSpec((1, width), lambda i, at: (0, 0)),
            ]
            + [pl.BlockSpec(memory_space=pl.ANY)] * len(previous),
            out_specs=[out] * 5,
        ),
        out_shape=[low, low, low, wide, wide],
        input_output_aliases={7 + count + i: i for i in range(len(previous))},
        cost_estimate=pl.CostEstimate(
            flops=6 * rows * model * width, bytes_accessed=8 * model * width, transcendentals=0
        ),
        name="project",
    )(index, *parts, weights, weights, weights, cosine, sine, gain, *previous)


def project_back_kernel(groups, index_ref, *refs):
    dq_refs, dk_refs, dv_refs = (refs[m * groups : (m + 1) * groups] for m in range(3))
    (
        xq_ref,
        xk_ref,
        wq_ref,
        wk_ref,
        wv_ref,
        cos_ref,
        sin_ref,
        gain_ref,
        grad_ref,
        gain_grad_ref,
        *piece_refs,
    ) = refs[3 * groups :]

    @pl.when(pl.program_id(0) == 0)
    def _():
        gain_grad_ref[...] = jnp.zeros_like(gain_grad_ref)

    def joined(refs):
        return jnp.concatenate([ref[...] for ref in refs], axis=1) if groups > 1 else refs[0][...]

    width = xq_ref.shape[1]
    cosine = widen(cos_ref[...], width)
    sine = widen(sin_ref[...], width)
    gain = gain_ref[...]
    lows = []
    for d_refs, x_ref in ((dq_refs, xq_ref), (dk_refs, xk_ref)):
        turned = x_ref[...]
        inverse = lax.rsqrt(head_sums(turned * turned) + norm_eps)
        unit = turned * inverse
        hat_grad = joined(d_refs) * scale_factor
        gain_grad_ref[...] += jnp.sum(hat_grad * unit, axis=0, keepdims=True)
        unit_grad = hat_grad * gain
        turned_grad = inverse * (unit_grad - unit * head_sums(unit * unit_grad))
        raw_grad = turned_grad * cosine - partner(turned_grad) * sine
        lows.append(raw_grad.astype(bf16))
    lows.append(joined(dv_refs).astype(bf16))
    piece = jnp.zeros(piece_refs[0].shape, f32)
    for m, w_ref in enumerate((wq_ref, wk_ref, wv_ref)):
        grad_ref[:, m * width : (m + 1) * width] = lows[m]
        piece = piece + dot_nt(lows[m], w_ref[...])
    low = piece.astype(bf16)
    block = pl.program_id(0) // (pl.num_programs(0) // len(piece_refs))
    for d, piece_ref in enumerate(piece_refs):

        @pl.when(block == d)
        def _(piece_ref=piece_ref):
            piece_ref[...] = low


def project_back(index, grads, turned, weights, cosine, sine, gain, rows):
    length, width = turned[0].shape
    groups = len(grads)
    model = weights.shape[0]
    part = min(256, rows)
    per = rows // part
    blocks = length // part

    def column(m):
        return pl.BlockSpec((model, width), lambda i, at: (0, m))

    def turn(i, at):
        return (lax.rem(at[0] * per + i, blocks), 0)

    def piece_block(d):
        return pl.BlockSpec((part, model), lambda i, at: (jnp.clip(i - d * per, 0, per - 1), 0))

    tall = pl.BlockSpec((part, width), turn)
    table = pl.BlockSpec((part, 128), turn)
    return pl.pallas_call(
        functools.partial(project_back_kernel, groups),
        grid_spec=pltpu.PrefetchScalarGridSpec(
            num_scalar_prefetch=1,
            grid=(blocks,),
            in_specs=[pl.BlockSpec((part, width // groups), turn)] * (3 * groups)
            + [tall] * 2
            + [column(0), column(1), column(2), table, table]
            + [pl.BlockSpec((1, width), lambda i, at: (0, 0))],
            out_specs=[
                pl.BlockSpec((part, 3 * width), lambda i, at: (i, 0)),
                pl.BlockSpec((1, width), lambda i, at: (0, 0)),
            ]
            + [piece_block(d) for d in range(length // rows)],
        ),
        out_shape=[
            jax.ShapeDtypeStruct((length, 3 * width), bf16),
            jax.ShapeDtypeStruct((1, width), f32),
        ]
        + [jax.ShapeDtypeStruct((rows, model), bf16)] * (length // rows),
        cost_estimate=pl.CostEstimate(
            flops=length * width, bytes_accessed=length * width, transcendentals=0
        ),
        name="project_back",
    )(index, *[g[m] for m in range(3) for g in grads], *turned, weights, weights, weights, cosine, sine, gain)


def projection_grads_kernel(counts, *refs):
    grad_ref, out_ref = refs[-2:]
    total = None
    for d, count in enumerate(counts):
        hidden = added(refs[:count])
        refs = refs[count:]
        rows = hidden.shape[0]
        part = dot_tn(hidden, grad_ref[d * rows : (d + 1) * rows, :])
        total = part if total is None else total + part
    out_ref[...] = total.astype(bf16)


def projection_grads(hidden, qkv_grad):
    rows, model = hidden[0][0].shape
    length, width = qkv_grad.shape
    counts = tuple(len(parts) for parts in hidden)
    part = 256
    return pl.pallas_call(
        functools.partial(projection_grads_kernel, counts),
        grid=(model // part,),
        in_specs=[pl.BlockSpec((rows, part), lambda i: (0, i))] * sum(counts)
        + [pl.BlockSpec(qkv_grad.shape, lambda i: (0, 0))],
        out_specs=pl.BlockSpec((part, width), lambda i: (i, 0)),
        out_shape=jax.ShapeDtypeStruct((model, width), bf16),
        cost_estimate=pl.CostEstimate(
            flops=2 * length * model * width,
            bytes_accessed=8 * length * model,
            transcendentals=0,
        ),
        name="projection_grads",
    )(*[x for parts in hidden for x in parts], qkv_grad)


def out_grads_kernel(count, *refs):
    attended = refs[:count]
    branch_ref, out_ref = refs[count:]
    width = attended[0].shape[1]
    turned = branch_ref[...].T
    for d in range(count):
        out_ref[:, d * width : (d + 1) * width] = dot_nn(turned, attended[d][...]).astype(bf16)


def out_grads(attended, branch_grad):
    count = len(attended)
    rows, model = branch_grad.shape
    width = attended[0].shape[1]
    part = 256
    return pl.pallas_call(
        functools.partial(out_grads_kernel, count),
        grid=(model // part,),
        in_specs=[pl.BlockSpec(x.shape, lambda i: (0, 0)) for x in attended]
        + [pl.BlockSpec((rows, part), lambda i: (0, i))],
        out_specs=pl.BlockSpec((part, count * width), lambda i: (i, 0)),
        out_shape=jax.ShapeDtypeStruct((model, count * width), bf16),
        cost_estimate=pl.CostEstimate(
            flops=2 * rows * count * model * width,
            bytes_accessed=4 * rows * count * model,
            transcendentals=0,
        ),
        name="out_grads",
    )(*attended, branch_grad)


def rms_scale(x):
    return lax.rsqrt(jnp.mean(x * x, axis=-1, keepdims=True) + norm_eps)


def mix_kernel(count, *refs):
    pieces, weights = refs[:count], refs[count : 2 * count]
    hidden_ref, rates_ref, branch_ref, middle_ref, low_ref, turned_ref = refs[2 * count :]
    branch = dot_nt(pieces[0][...], weights[0][...])
    for d in range(1, count):
        branch = branch + dot_nt(pieces[d][...], weights[d][...])
    branch_ref[...] = branch
    hidden = hidden_ref[...].astype(f32)
    mixed = hidden + rates_ref[0:1, :] * (branch * rms_scale(branch) - hidden)
    middle = mixed * rms_scale(mixed)
    middle_ref[...] = middle
    low_ref[...] = middle.astype(bf16)
    turned_ref[...] = middle.T.astype(bf16)


def mix(pieces, weights, hidden, rates):
    count = len(pieces)
    rows, model = hidden.shape
    width = pieces[0].shape[1]
    part = min(128, rows)

    def column(d):
        return pl.BlockSpec((model, width), lambda i: (0, d))

    wide = pl.BlockSpec((part, model), lambda i: (i, 0))
    return pl.pallas_call(
        functools.partial(mix_kernel, count),
        grid=(rows // part,),
        in_specs=[pl.BlockSpec((part, width), lambda i: (i, 0))] * count
        + [column(d) for d in range(count)]
        + [wide, pl.BlockSpec((2, model), lambda i: (0, 0))],
        out_specs=[wide, wide, wide, pl.BlockSpec((model, part), lambda i: (0, i))],
        out_shape=[
            jax.ShapeDtypeStruct((rows, model), f32),
            jax.ShapeDtypeStruct((rows, model), f32),
            jax.ShapeDtypeStruct((rows, model), bf16),
            jax.ShapeDtypeStruct((model, rows), bf16),
        ],
        cost_estimate=pl.CostEstimate(
            flops=2 * rows * model * model, bytes_accessed=14 * rows * model, transcendentals=0
        ),
        name="mix",
    )(*pieces, *([weights] * count), hidden, rates)


def block_of(w_ref):
    value = w_ref[:, 0, 0]
    return value.reshape(value.shape[0] * value.shape[1], value.shape[2])


def feed_kernel(
    m_ref,
    wu_ref,
    wg_ref,
    wd_ref,
    s_ref,
    middle_ref,
    cot_ref,
    live_ref,
    rates_ref,
    up_ref,
    gate_ref,
    h_ref,
    result_ref,
    direct_ref,
    low_ref,
    turned_ref,
    rate_ref,
    acc,
):
    i = pl.program_id(0)
    tokens = m_ref[...]
    up = dot_nn(tokens, block_of(wu_ref))
    gate = dot_nn(tokens, block_of(wg_ref))
    up_ref[...] = up
    gate_ref[...] = gate
    scaled = gate * s_ref[1:2, :]
    hidden = (up * s_ref[0:1, :] * (scaled * jax.nn.sigmoid(scaled))).astype(bf16)
    h_ref[...] = hidden
    part_out = dot_nt(hidden, block_of(wd_ref))

    @pl.when(i == 0)
    def _():
        acc[...] = part_out

    @pl.when(i > 0)
    def _():
        acc[...] += part_out

    @pl.when(i == pl.num_programs(0) - 1)
    def _():
        rate_ref[...] = jnp.zeros_like(rate_ref)
        rate = rates_ref[1:2, :]
        part = 32

        def body(at, carry):
            rows = pl.ds(pl.multiple_of(at * part, part), part)
            out = acc[rows, :]
            middle = middle_ref[rows, :]
            out_scale = rms_scale(out)
            unit = out * out_scale
            mixed = middle + rate * (unit - middle)
            scale = rms_scale(mixed)
            final = mixed * scale
            result_ref[rows, :] = final.astype(bf16)
            grad = cot_ref[rows, :].astype(f32) * live_ref[rows, :]
            mixed_grad = scale * (grad - final * jnp.mean(final * grad, axis=-1, keepdims=True))
            direct_ref[rows, :] = mixed_grad * (1.0 - rate)
            rate_ref[...] += jnp.sum(mixed_grad * (unit - middle), axis=0, keepdims=True)
            unit_grad = mixed_grad * rate
            out_grad = out_scale * (
                unit_grad - unit * jnp.mean(unit * unit_grad, axis=-1, keepdims=True)
            )
            low_ref[rows, :] = out_grad.astype(bf16)
            return carry

        lax.fori_loop(0, acc.shape[0] // part, body, 0)
        for at in range(acc.shape[0] // 128):
            rows = slice(at * 128, (at + 1) * 128)
            turned_ref[:, rows] = low_ref[rows, :].T


def weight_specs(weights, step, base=0):
    nd, _, _, shard, local_width = weights.shape
    per = local_width // step

    def spec(m):
        return pl.BlockSpec(
            (nd, 1, 1, shard, step), lambda i: (0, (i + base) // per, m, 0, (i + base) % per)
        )

    return [spec(0), spec(1), spec(2)]


def feed(low, weights, scales, middle, cotangent, live, rates, step):
    rows, model = low.shape
    total = weights.shape[1] * weights.shape[4]
    columns = pl.BlockSpec((rows, step), lambda i: (0, i))
    whole = pl.BlockSpec((rows, model), lambda i: (0, 0))
    return pl.pallas_call(
        feed_kernel,
        grid=(total // step,),
        in_specs=[whole]
        + weight_specs(weights, step)
        + [
            pl.BlockSpec((2, step), lambda i: (0, i)),
            whole,
            whole,
            pl.BlockSpec((rows, 1), lambda i: (0, 0)),
            pl.BlockSpec((2, model), lambda i: (0, 0)),
        ],
        out_specs=[columns, columns, columns, whole, whole, whole]
        + [
            pl.BlockSpec((model, rows), lambda i: (0, 0)),
            pl.BlockSpec((1, model), lambda i: (0, 0)),
        ],
        out_shape=[
            jax.ShapeDtypeStruct((rows, total), f32),
            jax.ShapeDtypeStruct((rows, total), f32),
            jax.ShapeDtypeStruct((rows, total), bf16),
            jax.ShapeDtypeStruct((rows, model), bf16),
            jax.ShapeDtypeStruct((rows, model), f32),
            jax.ShapeDtypeStruct((rows, model), bf16),
            jax.ShapeDtypeStruct((model, rows), bf16),
            jax.ShapeDtypeStruct((1, model), f32),
        ],
        scratch_shapes=[pltpu.VMEM((rows, model), f32)],
        cost_estimate=pl.CostEstimate(
            flops=6 * rows * model * total,
            bytes_accessed=6 * model * total + 10 * rows * total,
            transcendentals=0,
        ),
        name="feed",
    )(low, weights, weights, weights, scales, middle, cotangent, live, rates)


def feed_back_step(
    og_ref, ogt_ref, mt_ref, wu_ref, wg_ref, wd_ref, s_ref, up_ref, gate_ref, h_ref, start_ref, grad_ref, sg_ref, acc
):
    i = pl.program_id(0)
    grad_ref[2] = dot_nn(ogt_ref[...], h_ref[...]).astype(bf16)
    hidden_grad = dot_nn(og_ref[...], block_of(wd_ref))
    up = up_ref[...]
    gate = gate_ref[...]
    up_gain = s_ref[0:1, :]
    gate_gain = s_ref[1:2, :]
    scaled = gate * gate_gain
    sig = jax.nn.sigmoid(scaled)
    up_part = hidden_grad * (scaled * sig)
    gate_part = hidden_grad * (up * up_gain) * (sig * (1.0 + scaled * (1.0 - sig)))
    sg_ref[0:1, :] = jnp.sum(up_part * up, axis=0, keepdims=True)
    sg_ref[1:2, :] = jnp.sum(gate_part * gate, axis=0, keepdims=True)
    up_low = (up_part * up_gain).astype(bf16)
    gate_low = (gate_part * gate_gain).astype(bf16)
    tokens_t = mt_ref[...]
    grad_ref[0] = dot_nn(tokens_t, up_low).astype(bf16)
    grad_ref[1] = dot_nn(tokens_t, gate_low).astype(bf16)
    back = dot_nt(up_low, block_of(wu_ref)) + dot_nt(gate_low, block_of(wg_ref))

    @pl.when(i == 0)
    def _():
        acc[...] = start_ref[...] + back

    @pl.when(i > 0)
    def _():
        acc[...] += back


def feed_back_first_kernel(*refs):
    feed_back_step(*refs)


def feed_back_last_kernel(*refs):
    branch_ref, hidden_ref, rates_ref = refs[11:14]
    grad_ref, sg_ref, token_ref, low_ref, rate_ref, acc = refs[14:]
    feed_back_step(*refs[:11], grad_ref, sg_ref, acc)

    @pl.when(pl.program_id(0) == pl.num_programs(0) - 1)
    def _():
        rate_ref[...] = jnp.zeros_like(rate_ref)
        rate = rates_ref[0:1, :]
        part = 32

        def body(at, carry):
            rows = pl.ds(pl.multiple_of(at * part, part), part)
            grad = acc[rows, :]
            branch = branch_ref[rows, :]
            hidden = hidden_ref[rows, :].astype(f32)
            branch_scale = rms_scale(branch)
            unit = branch * branch_scale
            mixed = hidden + rate * (unit - hidden)
            scale = rms_scale(mixed)
            middle = mixed * scale
            mixed_grad = scale * (grad - middle * jnp.mean(middle * grad, axis=-1, keepdims=True))
            token_ref[rows, :] = mixed_grad * (1.0 - rate)
            rate_ref[...] += jnp.sum(mixed_grad * (unit - hidden), axis=0, keepdims=True)
            unit_grad = mixed_grad * rate
            branch_grad = branch_scale * (
                unit_grad - unit * jnp.mean(unit * unit_grad, axis=-1, keepdims=True)
            )
            low_ref[rows, :] = branch_grad.astype(bf16)
            return carry

        lax.fori_loop(0, acc.shape[0] // part, body, 0)


def feed_back(
    out_grad, out_grad_t, middle_t, weights, scales, up, gate, hidden_units, start, mixing, step, base, count
):
    model, rows = middle_t.shape
    width = count * step
    columns = pl.BlockSpec((rows, step), lambda i: (0, i + base))
    whole = pl.BlockSpec((rows, model), lambda i: (0, 0))
    turned = pl.BlockSpec((model, rows), lambda i: (0, 0))
    wide = jax.ShapeDtypeStruct((rows, model), f32)
    grads_specs = [
        pl.BlockSpec((3, model, step), lambda i: (0, 0, i)),
        pl.BlockSpec((2, step), lambda i: (0, i)),
    ]
    grads_shapes = [
        jax.ShapeDtypeStruct((3, model, width), bf16),
        jax.ShapeDtypeStruct((2, width), f32),
    ]
    last = bool(mixing)
    return pl.pallas_call(
        feed_back_last_kernel if last else feed_back_first_kernel,
        grid=(count,),
        in_specs=[whole, turned, turned]
        + weight_specs(weights, step, base)
        + [pl.BlockSpec((2, step), lambda i: (0, i + base)), columns, columns, columns, whole]
        + ([whole, whole, pl.BlockSpec((2, model), lambda i: (0, 0))] if last else []),
        out_specs=grads_specs
        + ([whole, whole, pl.BlockSpec((1, model), lambda i: (0, 0))] if last else [whole]),
        out_shape=grads_shapes
        + (
            [
                wide,
                jax.ShapeDtypeStruct((rows, model), bf16),
                jax.ShapeDtypeStruct((1, model), f32),
            ]
            if last
            else [wide]
        ),
        scratch_shapes=[pltpu.VMEM((rows, model), f32)] if last else [],
        cost_estimate=pl.CostEstimate(
            flops=12 * rows * model * width,
            bytes_accessed=12 * model * width + 10 * rows * width,
            transcendentals=0,
        ),
        name="feed_back_last" if last else "feed_back_first",
    )(
        out_grad,
        out_grad_t,
        middle_t,
        weights,
        weights,
        weights,
        scales,
        up,
        gate,
        hidden_units,
        start,
        *mixing,
    )


def shift(value, axis, distance, size):
    return lax.ppermute(value, axis, [(i, (i + distance) % size) for i in range(size)])


def carry_on(up, down, hop, axis, size):
    up = lax.ppermute(up, axis, [(i, i + 1) for i in range(hop - 1, size - 1)])
    down = lax.ppermute(down, axis, [(i, i - 1) for i in range(1, size - hop + 1)])
    return up, down


def line_sum(pieces, hop, up, down, axis, size):
    ahead, behind = pieces[size - hop], pieces[hop]
    ahead = ahead if up is None else ahead + up
    behind = behind if down is None else behind + down
    up = lax.ppermute(ahead, axis, [(i, i + 1) for i in range(hop)])
    down = lax.ppermute(behind, axis, [(i, i - 1) for i in range(size - hop, size)])
    return up, down


def halving(value, axis, size, step):
    lead, (count, rows, width) = value.shape[:-3], value.shape[-3:]
    bit = (lax.axis_index(axis) // step) % 2
    pairs = value.reshape(lead + (count // 2, 2, rows, width))
    sent = lax.dynamic_index_in_dim(pairs, 1 - bit, len(lead) + 1, False)
    kept = lax.dynamic_index_in_dim(pairs, bit, len(lead) + 1, False)
    other = lax.ppermute(sent, axis, [(i, i ^ step) for i in range(size)])
    value = kept.astype(f32) + other.astype(f32)
    return value.reshape(lead + (rows, width)) if 2 * step == size else value.astype(bf16)


def exchange_add(value, axis, size, step):
    return value + lax.ppermute(value, axis, [(i, i ^ step) for i in range(size)])


def doublings(size):
    return [1 << k for k in range(size.bit_length() - 1)]


def butterfly(value, axis, size):
    for step in doublings(size):
        value = exchange_add(value, axis, size, step)
    return value


def take_block(value, index, size, axis):
    return lax.dynamic_slice_in_dim(value, index * size, size, axis)


def put_block(whole, value, index, axis):
    return lax.dynamic_update_slice_in_dim(whole, value, index * value.shape[axis], axis)


def local(
    nd,
    nt,
    hidden_in,
    cotangent,
    segments,
    attn_weight,
    mlp_weight,
    rates,
    qk_scale,
    mlp_scales,
    attn_moment_one,
    attn_moment_two,
    mlp_moment_one,
    mlp_moment_two,
):
    rows, model = hidden_in.shape
    length = segments.shape[0]
    shard = attn_weight.shape[1]
    heads_width = attn_weight.shape[2]
    hidden_width = mlp_weight.shape[2]
    block = min(512, length)
    step = min(512, hidden_width)
    me = lax.axis_index("tensor")

    def gather(value):
        return [value] + [shift(value, "tensor", d, nt) for d in range(1, nt)]

    def both(ups, downs, d):
        return (ups[0],) if d == 0 else (ups[d], downs[nt - d])

    middle_hop = nt // 2
    order = [d for d in range(nt) if d != middle_hop] + [middle_hop]
    attn_low = attn_weight.astype(bf16)
    qkv_full = lax.all_gather(
        jnp.concatenate([attn_low[0], attn_low[1], attn_low[2]], axis=1), "dp", axis=0, tiled=True
    )
    mlp_low = mlp_weight.astype(bf16).reshape(3 * shard, hidden_width)
    out_low = attn_low[3]
    ups, downs = [mlp_low], [mlp_low]
    for hop in range(1, nt):
        if hop == 2:
            ups[1], downs[1], out_low = lax.optimization_barrier((ups[1], downs[1], out_low))
        if hop == nt - 1:
            ups[-1], downs[-1], hidden_in = lax.optimization_barrier((ups[-1], downs[-1], hidden_in))
        up, down = carry_on(ups[-1], downs[-1], hop, "tensor", nt)
        ups.append(up)
        downs.append(down)
    out_full = lax.all_gather(jnp.concatenate(gather(out_low), axis=1), "dp", axis=0, tiled=True)
    mlp_full = lax.all_gather(
        jnp.concatenate([sum(both(ups, downs, d)) for d in order], axis=0), "dp", axis=0, tiled=True
    )
    mlp_full = mlp_full.reshape(nd, nt, 3, shard, hidden_width)
    scales_parts = gather(mlp_scales)
    scales_row = jnp.concatenate([scales_parts[d] for d in order], axis=1)

    starts = starts_of(segments)
    positions = (jnp.arange(length, dtype=jnp.int32) - starts).astype(f32)
    lane = jnp.arange(128, dtype=jnp.int32)
    half = HEAD_DIM // 2
    frequency = 10000.0 ** (-(lane % half).astype(f32) / half)
    sign = jnp.where(lane % HEAD_DIM < half, -1.0, 1.0)
    angles = positions[:, None] * frequency[None, :]
    cosine = jnp.cos(angles)
    sine = jnp.sin(angles) * sign[None, :]
    gain = qk_scale.reshape(1, heads_width)

    ups, downs, state = [hidden_in], [hidden_in], ()
    hidden_parts = [None] * nt

    def projected(hop, state):
        for d in range(nt):
            if (max(d, nt - d) if d else 0) == hop:
                hidden_parts[d] = both(ups, downs, d)
                index = ((me + nt - d) % nt).reshape(1)
                state = project(index, hidden_parts[d], qkv_full, cosine, sine, gain, length, state)
        return state

    for hop in range(1, nt):
        ups[-1], downs[-1], state = lax.optimization_barrier((ups[-1], downs[-1], state))
        up, down = carry_on(ups[-1], downs[-1], hop, "tensor", nt)
        ups.append(up)
        downs.append(down)
        state = projected(hop - 1, state)
    ups[-1], downs[-1], state = lax.optimization_barrier((ups[-1], downs[-1], state))
    state = projected(nt - 1, state)
    query_hat, key_hat, value_hat, query_turned, key_turned = state
    attended_row, attended_f32, log_sum = attend(
        query_hat, key_hat, value_hat, starts[:, None], block
    )
    attended = [take_block(attended_row, me, rows, 0)] + [
        shift(take_block(attended_row, (me + d) % nt, rows, 0), "tensor", d, nt)
        for d in range(1, nt)
    ]
    branch, middle, middle_low, middle_t = mix(attended, out_full, hidden_in, rates)
    row_segments = take_block(segments, me, rows, 0)
    live = (row_segments < pad_segment).astype(f32)[:, None]
    up, gate, hidden_units, result, middle_direct, mlp_out_low, mlp_out_t, rate_mlp_grad = feed(
        middle_low, mlp_full, scales_row, middle, cotangent, live, rates, step
    )
    def spread(value, places):
        width = value.shape[1] // nt
        whole = jnp.zeros_like(value)
        for p, d in enumerate(places):
            piece = value[:, p * width : (p + 1) * width]
            whole = put_block(whole, piece, (me + nt - d) % nt, 1)
        return whole

    per = hidden_width // step
    near = (nt - 1) * per
    feed_args = (mlp_out_low, mlp_out_t, middle_t, mlp_full, scales_row, up, gate, hidden_units)
    far_grad, far_scales, partial = feed_back(*feed_args, middle_direct, (), step, near, per)
    halvings = doublings(nd)
    far_part = lax.psum_scatter(far_grad, "dp", scatter_dimension=1, tiled=True)
    near_grad, near_scales, token_direct, branch_low, rate_attn_grad = feed_back(
        *feed_args, partial, (branch, hidden_in, rates), step, 0, near
    )
    near_part = lax.psum_scatter(near_grad, "dp", scatter_dimension=1, tiled=True)

    grad_row = jnp.zeros((length, heads_width), bf16)
    for d in list(range(1, nt)) + [0]:
        piece = dot_nn(branch_low, out_full[:, d * heads_width : (d + 1) * heads_width])
        piece = piece.astype(bf16)
        piece = shift(piece, "tensor", -d, nt) if d else piece
        grad_row = put_block(grad_row, piece, (me + d) % nt, 0)
    out_grad = out_grads(attended, branch_low)

    scales_grad = spread(jnp.concatenate([near_scales, far_scales], axis=1), order)
    small = jnp.concatenate(
        [rate_attn_grad, rate_mlp_grad, scales_grad.reshape(-1, model)], axis=0
    )
    steps = [("tensor", nt, k) for k in doublings(nt)] + [("dp", nd, k) for k in doublings(nd)]

    def advance(small):
        return exchange_add(small, *steps.pop(0)) if steps else small

    far_part, grad_row, out_grad, small = lax.optimization_barrier(
        (far_part, grad_row, out_grad, small)
    )
    small = advance(small)
    out_sum = halving(out_grad.reshape(nd, shard, -1), "dp", nd, halvings[0])
    head_group = max(128, heads_width // 2)
    head_grads = []
    for group in range(heads_width // head_group):
        if group == 1:
            head_grads, grad_row, far_part, small, out_sum = lax.optimization_barrier(
                (head_grads, grad_row, far_part, small, out_sum)
            )
            small = advance(small)
            out_sum = halving(out_sum, "dp", nd, halvings[1])
        head_grads.append(
            attend_back(
                query_hat,
                key_hat,
                value_hat,
                grad_row,
                attended_f32,
                log_sum,
                starts[None, :],
                block,
                group,
                head_group,
            )
        )
    far_first = shift(far_part[:2], "tensor", -middle_hop, nt)
    far_last = far_part[2:]
    head_grads, small, out_sum, far_first, far_last = lax.optimization_barrier(
        (head_grads, small, out_sum, far_first, far_last)
    )
    far_last = shift(far_last, "tensor", -middle_hop, nt)
    small = advance(small)
    for k in halvings[1 if len(head_grads) == 1 else 2 :]:
        out_sum = halving(out_sum, "dp", nd, k)
    qkv_grad, gain_grad, *pieces = project_back(
        me.reshape(1),
        head_grads,
        (query_turned, key_turned),
        qkv_full,
        cosine,
        sine,
        gain,
        rows,
    )
    qkv_grad, pieces, small, out_sum, far_last = lax.optimization_barrier(
        (qkv_grad, pieces, small, out_sum, far_last)
    )
    far_part = jnp.concatenate([far_first, far_last], axis=0)
    small = advance(small)
    hidden_turn = [hidden_parts[(nt - d) % nt] for d in range(nt)]
    qkv_sum = projection_grads(hidden_turn, qkv_grad)
    qkv_sum = qkv_sum.reshape(nd, shard, -1)

    def own_pieces(part, axis, width, places):
        pieces = [
            lax.slice_in_dim(part, p * width, (p + 1) * width, axis=axis)
            for p in range(len(places))
        ]
        return [shift(piece, "tensor", -d, nt) if d else piece for d, piece in zip(places, pieces)]

    ahead = behind = None
    for hop in range(1, nt):
        if hop == 2:
            ahead, behind, qkv_sum = lax.optimization_barrier((ahead, behind, qkv_sum))
            out_pieces = own_pieces(out_sum.astype(bf16), 1, heads_width, range(nt))
            gain_parts = gather(gain_grad)
        if hop == max(2, nt - 1):
            ahead, behind, near_part, qkv_sum, out_pieces, gain_parts, small = (
                lax.optimization_barrier(
                    (ahead, behind, near_part, qkv_sum, out_pieces, gain_parts, small)
                )
            )
            near_pieces = own_pieces(near_part, 2, hidden_width, order[:-1])
        ahead, behind = line_sum(pieces, hop, ahead, behind, "tensor", nt)
        if hop == 2:
            qkv_sum = halving(qkv_sum, "dp", nd, halvings[0])
    for k in halvings[1:]:
        qkv_sum = halving(qkv_sum, "dp", nd, k)
    gain_row = spread(jnp.concatenate(gain_parts, axis=1), range(nt))
    while steps:
        small = advance(small)
    rates_grad = small[:2]
    mlp_scales_grad = small[2:].reshape(2, nt * hidden_width)

    out_own = sum(piece.astype(f32) for piece in out_pieces)
    attn_weight_grad = jnp.stack(
        [qkv_sum[:, m * heads_width : (m + 1) * heads_width] for m in range(3)] + [out_own]
    )
    attn_one, attn_two, attn_moved = adam_moved(
        attn_weight, attn_weight_grad, attn_moment_one, attn_moment_two
    )
    attn_square = jnp.sum(attn_moved * attn_moved, axis=1, keepdims=True)
    last = jnp.concatenate([attn_square.reshape(1, -1), gain_row], axis=1)
    last = butterfly(last, "dp", nd)
    near_pieces, last = lax.optimization_barrier((near_pieces, last))
    attn_square = last[:, : 4 * heads_width].reshape(4, 1, heads_width)
    gain_row = last[:, 4 * heads_width :].reshape(-1)
    attn_new = attn_moved * lax.rsqrt(attn_square + norm_eps)

    mlp_weight_grad = sum(piece.astype(f32) for piece in near_pieces + [far_part])
    mlp_one, mlp_two, mlp_moved = adam_moved(
        mlp_weight, mlp_weight_grad, mlp_moment_one, mlp_moment_two
    )
    mlp_square = jnp.sum(mlp_moved * mlp_moved, axis=1, keepdims=True)
    mlp_square = butterfly(mlp_square.reshape(1, -1), "dp", nd).reshape(mlp_square.shape)
    mlp_square, ahead, behind = lax.optimization_barrier((mlp_square, ahead, behind))
    total = token_direct + pieces[0].astype(f32)
    input_grad = (total + ahead.astype(f32) + behind.astype(f32)).astype(bf16)
    mlp_new = mlp_moved * lax.rsqrt(mlp_square + norm_eps)
    return (
        result.astype(bf16),
        input_grad,
        attn_weight_grad,
        mlp_weight_grad,
        rates_grad,
        gain_row,
        mlp_scales_grad,
        attn_one,
        attn_two,
        mlp_one,
        mlp_two,
        attn_new,
        mlp_new,
    )


def solution(mesh):
    weights = P(None, "dp", "tensor")
    tokens = P(("dp", "tensor"), None)
    return jax.shard_map(
        functools.partial(local, mesh.shape["dp"], mesh.shape["tensor"]),
        mesh=mesh,
        in_specs=(
            tokens,
            tokens,
            P("dp"),
            weights,
            weights,
            P(),
            P("tensor"),
            P(None, "tensor"),
            weights,
            weights,
            weights,
            weights,
        ),
        out_specs=(
            tokens,
            tokens,
            weights,
            weights,
            P(),
            P(),
            P(),
            weights,
            weights,
            weights,
            weights,
            weights,
            weights,
        ),
        check_vma=False,
    )
```

```python
import functools
import math

import jax
import jax.numpy as jnp
from jax import lax
from jax.experimental import pallas as pl
from jax.experimental.pallas import tpu as pltpu
from jax.sharding import PartitionSpec as P

HEAD_DIM = 64
LOG2E = 1.4426950408889634

norm_eps = 1e-06
pad_segment = 63
beta_one = 0.9
beta_two = 0.95
learning_rate = 0.01
adam_eps = 1e-08
bias_one = 1.0 - 0.9**10
bias_two = 1.0 - 0.95**10
scale_factor = math.sqrt(HEAD_DIM)
f32 = jnp.float32
bf16 = jnp.bfloat16


def starts_of(segment_row):
    indices = jnp.arange(segment_row.shape[0], dtype=jnp.int32)
    changed = jnp.concatenate(
        [jnp.ones((1,), dtype=jnp.bool_), segment_row[1:] != segment_row[:-1]]
    )
    return lax.cummax(jnp.where(changed, indices, jnp.zeros_like(indices)), axis=0)


def adam_moved(weight, gradient, moment_one, moment_two):
    moment_one_new = beta_one * moment_one + (1.0 - beta_one) * gradient
    moment_two_new = beta_two * moment_two + (1.0 - beta_two) * gradient * gradient
    moved = weight - learning_rate * (moment_one_new / bias_one) / (
        jnp.sqrt(moment_two_new / bias_two) + adam_eps
    )
    return (moment_one_new, moment_two_new, moved)


def dot_nt(a, b):
    return lax.dot_general(a, b, (((1,), (1,)), ((), ())), preferred_element_type=f32)


def dot_nn(a, b):
    return lax.dot_general(a, b, (((1,), (0,)), ((), ())), preferred_element_type=f32)


def dot_tn(a, b):
    return lax.dot_general(a, b, (((0,), (0,)), ((), ())), preferred_element_type=f32)


def head_stack(x, heads):
    lane = lax.broadcasted_iota(jnp.int32, x.shape, 1) // HEAD_DIM
    zero = jnp.zeros_like(x)
    return jnp.concatenate([jnp.where(lane == h, x, zero) for h in range(heads)], axis=0)


def head_pick(stacked, heads, rows):
    width = stacked.shape[1]
    lane = lax.broadcasted_iota(jnp.int32, (rows, width), 1) // HEAD_DIM
    picked = jnp.zeros((rows, width), f32)
    for h in range(heads):
        picked = jnp.where(lane == h, stacked[h * rows : (h + 1) * rows], picked)
    return picked


def attend_kernel(heads, bq, bk, q_ref, k_ref, v_ref, start_ref, o_ref, of_ref, l_ref, acc, lsum):
    i = pl.program_id(0)
    qs = head_stack(q_ref[...], heads)
    acc[...] = jnp.zeros_like(acc)
    lsum[...] = jnp.zeros_like(lsum)
    start = jnp.concatenate([start_ref[...]] * heads, axis=0)

    def step(j, diagonal):
        offset = pl.multiple_of(j * bk, bk)
        keys = k_ref[pl.ds(offset, bk), :]
        values = v_ref[pl.ds(offset, bk), :]
        scores = dot_nt(qs, keys)
        key_index = offset + lax.broadcasted_iota(jnp.int32, scores.shape, 1)
        allowed = key_index >= start
        if diagonal:
            row = lax.rem(lax.broadcasted_iota(jnp.int32, scores.shape, 0), bq)
            allowed = allowed & (key_index <= i * bq + row)
        weights = jnp.where(allowed, jnp.exp2(scores * (scale_factor * LOG2E)), 0.0)
        total = weights[:, :128]
        for part in range(1, bk // 128):
            total = total + weights[:, part * 128 : (part + 1) * 128]
        lsum[...] += total
        acc[...] += dot_nn(weights.astype(bf16), values)

    def body(j, carry):
        step(j, False)
        return carry

    lax.fori_loop(0, i, body, 0)
    step(i, True)
    summed = jnp.sum(lsum[...], axis=1, keepdims=True)
    out = head_pick(acc[...] * (1.0 / summed), heads, bq)
    of_ref[...] = out
    o_ref[...] = out.astype(bf16)
    l_ref[...] = jnp.log2(summed).reshape(heads, bq)


def attend(q, k, v, start, block):
    length, width = q.shape
    heads = width // HEAD_DIM
    whole = pl.BlockSpec((length, width), lambda i: (0, 0))
    rows = pl.BlockSpec((block, width), lambda i: (i, 0))
    return pl.pallas_call(
        functools.partial(attend_kernel, heads, block, block),
        grid=(length // block,),
        in_specs=[rows, whole, whole, pl.BlockSpec((block, 1), lambda i: (i, 0))],
        out_specs=[rows, rows, pl.BlockSpec((heads, block), lambda i: (0, i))],
        out_shape=[
            jax.ShapeDtypeStruct((length, width), bf16),
            jax.ShapeDtypeStruct((length, width), f32),
            jax.ShapeDtypeStruct((heads, length), f32),
        ],
        scratch_shapes=[
            pltpu.VMEM((heads * block, width), f32),
            pltpu.VMEM((heads * block, 128), f32),
        ],
        cost_estimate=pl.CostEstimate(
            flops=20_000_000_000, bytes_accessed=8 * length * width, transcendentals=0
        ),
        name="attend",
    )(q, k, v, start)


def attend_back_kernel(
    first, heads, bq, bk, q_ref, do_ref, k_ref, v_ref, of_ref, l_ref, start_ref, dq_ref, dk_ref, dv_ref, acc
):
    i = pl.program_id(0)

    @pl.when(i == 0)
    def _():
        dk_ref[...] = jnp.zeros_like(dk_ref)
        dv_ref[...] = jnp.zeros_like(dv_ref)

    qs = head_stack(q_ref[...], heads)
    grads = do_ref[...]
    dos = head_stack(grads, heads)
    product = (grads.astype(f32) * of_ref[...]).T
    delta = jnp.concatenate(
        [
            jnp.sum(product[h * HEAD_DIM : (h + 1) * HEAD_DIM], axis=0, keepdims=True)
            for h in range(heads)
        ],
        axis=1,
    )
    log_sum = jnp.concatenate([l_ref[first + h : first + h + 1, :] for h in range(heads)], axis=1)
    start = jnp.concatenate([start_ref[...]] * heads, axis=1)
    acc[...] = jnp.zeros_like(acc)

    def step(j, diagonal):
        offset = pl.multiple_of(j * bk, bk)
        keys = k_ref[pl.ds(offset, bk), :]
        values = v_ref[pl.ds(offset, bk), :]
        scores = dot_nt(keys, qs)
        key_index = offset + lax.broadcasted_iota(jnp.int32, scores.shape, 0)
        allowed = key_index >= start
        if diagonal:
            column = lax.rem(lax.broadcasted_iota(jnp.int32, scores.shape, 1), bq)
            allowed = allowed & (key_index <= i * bq + column)
        probs = jnp.where(allowed, jnp.exp2(scores * (scale_factor * LOG2E) - log_sum), 0.0)
        prob_grad = dot_nt(values, dos)
        score_grad = (probs * (prob_grad - delta)).astype(bf16)
        dv_ref[pl.ds(offset, bk), :] += dot_nn(probs.astype(bf16), dos)
        dk_ref[pl.ds(offset, bk), :] += dot_nn(score_grad, qs)
        acc[...] += dot_tn(score_grad, keys)

    def body(j, carry):
        step(j, False)
        return carry

    lax.fori_loop(0, i, body, 0)
    step(i, True)
    dq_ref[...] = head_pick(acc[...], heads, bq)


def attend_back(q, k, v, grads, out, log_sum, start, block, group, width):
    length = q.shape[0]
    heads = width // HEAD_DIM
    taken = pl.BlockSpec((length, width), lambda i: (0, group))
    taken_rows = pl.BlockSpec((block, width), lambda i: (i, group))
    whole = pl.BlockSpec((length, width), lambda i: (0, 0))
    rows = pl.BlockSpec((block, width), lambda i: (i, 0))
    result = jax.ShapeDtypeStruct((length, width), f32)
    return pl.pallas_call(
        functools.partial(attend_back_kernel, group * heads, heads, block, block),
        grid=(length // block,),
        in_specs=[
            taken_rows,
            taken_rows,
            taken,
            taken,
            taken_rows,
            pl.BlockSpec((log_sum.shape[0], block), lambda i: (0, i)),
            pl.BlockSpec((1, block), lambda i: (0, i)),
        ],
        out_specs=[rows, whole, whole],
        out_shape=[result, result, result],
        scratch_shapes=[pltpu.VMEM((heads * block, width), f32)],
        cost_estimate=pl.CostEstimate(
            flops=40_000_000_000, bytes_accessed=20 * length * width, transcendentals=0
        ),
        name="attend_back",
    )(q, grads, k, v, out, log_sum, start)


def partner(x):
    width = x.shape[1]
    lane = lax.broadcasted_iota(jnp.int32, x.shape, 1)
    ahead = pltpu.roll(x, width - HEAD_DIM // 2, 1)
    behind = pltpu.roll(x, HEAD_DIM // 2, 1)
    return jnp.where(lax.rem(lane, HEAD_DIM) < HEAD_DIM // 2, ahead, behind)


def head_sums(x):
    width = x.shape[1]
    row = lax.broadcasted_iota(jnp.int32, (width, width), 0) // HEAD_DIM
    column = lax.broadcasted_iota(jnp.int32, (width, width), 1) // HEAD_DIM
    same = jnp.where(row == column, 1.0, 0.0).astype(bf16)
    high = x.astype(bf16)
    low = (x - high.astype(f32)).astype(bf16)
    return dot_nn(high, same) + dot_nn(low, same)


def widen(table, width):
    return table if table.shape[1] == width else jnp.concatenate([table] * (width // 128), axis=1)


def added(refs):
    total = refs[0][...]
    for ref in refs[1:]:
        total = total + ref[...]
    return total


def project_kernel(count, index_ref, *refs):
    wq_ref, wk_ref, wv_ref, cos_ref, sin_ref, gain_ref = refs[count : count + 6]
    q_ref, k_ref, v_ref, xq_ref, xk_ref = refs[-5:]
    x = added(refs[:count])
    width = q_ref.shape[1]
    cosine = widen(cos_ref[...], width)
    sine = widen(sin_ref[...], width)
    gain = gain_ref[...]
    for w_ref, hat_ref, turned_ref in ((wq_ref, q_ref, xq_ref), (wk_ref, k_ref, xk_ref)):
        raw = dot_nn(x, w_ref[...])
        turned = raw * cosine + partner(raw) * sine
        turned_ref[...] = turned
        hat = turned * lax.rsqrt(head_sums(turned * turned) + norm_eps) * gain
        hat_ref[...] = hat.astype(bf16)
    v_ref[...] = dot_nn(x, wv_ref[...]).astype(bf16)


def project(index, parts, weights, cosine, sine, gain, length, previous):
    rows, model = parts[0].shape
    count = len(parts)
    width = gain.shape[1]
    part = min(256, rows)
    per = rows // part

    def column(m):
        return pl.BlockSpec((model, width), lambda i, at: (0, m))

    table = pl.BlockSpec((part, 128), lambda i, at: (at[0] * per + i, 0))
    out = pl.BlockSpec((part, width), lambda i, at: (at[0] * per + i, 0))
    low = jax.ShapeDtypeStruct((length, width), bf16)
    wide = jax.ShapeDtypeStruct((length, width), f32)
    return pl.pallas_call(
        functools.partial(project_kernel, count),
        grid_spec=pltpu.PrefetchScalarGridSpec(
            num_scalar_prefetch=1,
            grid=(per,),
            in_specs=[pl.BlockSpec((part, model), lambda i, at: (i, 0))] * count
            + [
                column(0),
                column(1),
                column(2),
                table,
                table,
                pl.BlockSpec((1, width), lambda i, at: (0, 0)),
            ]
            + [pl.BlockSpec(memory_space=pl.ANY)] * len(previous),
            out_specs=[out] * 5,
        ),
        out_shape=[low, low, low, wide, wide],
        input_output_aliases={7 + count + i: i for i in range(len(previous))},
        cost_estimate=pl.CostEstimate(
            flops=6 * rows * model * width, bytes_accessed=8 * model * width, transcendentals=0
        ),
        name="project",
    )(index, *parts, weights, weights, weights, cosine, sine, gain, *previous)


def project_back_kernel(groups, index_ref, *refs):
    dq_refs, dk_refs, dv_refs = (refs[m * groups : (m + 1) * groups] for m in range(3))
    (
        xq_ref,
        xk_ref,
        wq_ref,
        wk_ref,
        wv_ref,
        cos_ref,
        sin_ref,
        gain_ref,
        grad_ref,
        gain_grad_ref,
        *piece_refs,
    ) = refs[3 * groups :]

    @pl.when(pl.program_id(0) == 0)
    def _():
        gain_grad_ref[...] = jnp.zeros_like(gain_grad_ref)

    def joined(refs):
        return jnp.concatenate([ref[...] for ref in refs], axis=1) if groups > 1 else refs[0][...]

    width = xq_ref.shape[1]
    cosine = widen(cos_ref[...], width)
    sine = widen(sin_ref[...], width)
    gain = gain_ref[...]
    lows = []
    for d_refs, x_ref in ((dq_refs, xq_ref), (dk_refs, xk_ref)):
        turned = x_ref[...]
        inverse = lax.rsqrt(head_sums(turned * turned) + norm_eps)
        unit = turned * inverse
        hat_grad = joined(d_refs) * scale_factor
        gain_grad_ref[...] += jnp.sum(hat_grad * unit, axis=0, keepdims=True)
        unit_grad = hat_grad * gain
        turned_grad = inverse * (unit_grad - unit * head_sums(unit * unit_grad))
        raw_grad = turned_grad * cosine - partner(turned_grad) * sine
        lows.append(raw_grad.astype(bf16))
    lows.append(joined(dv_refs).astype(bf16))
    piece = jnp.zeros(piece_refs[0].shape, f32)
    for m, w_ref in enumerate((wq_ref, wk_ref, wv_ref)):
        grad_ref[:, m * width : (m + 1) * width] = lows[m]
        piece = piece + dot_nt(lows[m], w_ref[...])
    low = piece.astype(bf16)
    block = pl.program_id(0) // (pl.num_programs(0) // len(piece_refs))
    for d, piece_ref in enumerate(piece_refs):

        @pl.when(block == d)
        def _(piece_ref=piece_ref):
            piece_ref[...] = low


def project_back(index, grads, turned, weights, cosine, sine, gain, rows):
    length, width = turned[0].shape
    groups = len(grads)
    model = weights.shape[0]
    part = min(256, rows)
    per = rows // part
    blocks = length // part

    def column(m):
        return pl.BlockSpec((model, width), lambda i, at: (0, m))

    def turn(i, at):
        return (lax.rem(at[0] * per + i, blocks), 0)

    def piece_block(d):
        return pl.BlockSpec((part, model), lambda i, at: (jnp.clip(i - d * per, 0, per - 1), 0))

    tall = pl.BlockSpec((part, width), turn)
    table = pl.BlockSpec((part, 128), turn)
    return pl.pallas_call(
        functools.partial(project_back_kernel, groups),
        grid_spec=pltpu.PrefetchScalarGridSpec(
            num_scalar_prefetch=1,
            grid=(blocks,),
            in_specs=[pl.BlockSpec((part, width // groups), turn)] * (3 * groups)
            + [tall] * 2
            + [column(0), column(1), column(2), table, table]
            + [pl.BlockSpec((1, width), lambda i, at: (0, 0))],
            out_specs=[
                pl.BlockSpec((part, 3 * width), lambda i, at: (i, 0)),
                pl.BlockSpec((1, width), lambda i, at: (0, 0)),
            ]
            + [piece_block(d) for d in range(length // rows)],
        ),
        out_shape=[
            jax.ShapeDtypeStruct((length, 3 * width), bf16),
            jax.ShapeDtypeStruct((1, width), f32),
        ]
        + [jax.ShapeDtypeStruct((rows, model), bf16)] * (length // rows),
        cost_estimate=pl.CostEstimate(
            flops=length * width, bytes_accessed=length * width, transcendentals=0
        ),
        name="project_back",
    )(index, *[g[m] for m in range(3) for g in grads], *turned, weights, weights, weights, cosine, sine, gain)


def projection_grads_kernel(counts, *refs):
    grad_ref, out_ref = refs[-2:]
    total = None
    for d, count in enumerate(counts):
        hidden = added(refs[:count])
        refs = refs[count:]
        rows = hidden.shape[0]
        part = dot_tn(hidden, grad_ref[d * rows : (d + 1) * rows, :])
        total = part if total is None else total + part
    out_ref[...] = total.astype(bf16)


def projection_grads(hidden, qkv_grad):
    rows, model = hidden[0][0].shape
    length, width = qkv_grad.shape
    counts = tuple(len(parts) for parts in hidden)
    part = 256
    return pl.pallas_call(
        functools.partial(projection_grads_kernel, counts),
        grid=(model // part,),
        in_specs=[pl.BlockSpec((rows, part), lambda i: (0, i))] * sum(counts)
        + [pl.BlockSpec(qkv_grad.shape, lambda i: (0, 0))],
        out_specs=pl.BlockSpec((part, width), lambda i: (i, 0)),
        out_shape=jax.ShapeDtypeStruct((model, width), bf16),
        cost_estimate=pl.CostEstimate(
            flops=2 * length * model * width,
            bytes_accessed=8 * length * model,
            transcendentals=0,
        ),
        name="projection_grads",
    )(*[x for parts in hidden for x in parts], qkv_grad)


def out_grads_kernel(count, *refs):
    attended = refs[:count]
    branch_ref, out_ref = refs[count:]
    width = attended[0].shape[1]
    turned = branch_ref[...].T
    for d in range(count):
        out_ref[:, d * width : (d + 1) * width] = dot_nn(turned, attended[d][...]).astype(bf16)


def out_grads(attended, branch_grad):
    count = len(attended)
    rows, model = branch_grad.shape
    width = attended[0].shape[1]
    part = 256
    return pl.pallas_call(
        functools.partial(out_grads_kernel, count),
        grid=(model // part,),
        in_specs=[pl.BlockSpec(x.shape, lambda i: (0, 0)) for x in attended]
        + [pl.BlockSpec((rows, part), lambda i: (0, i))],
        out_specs=pl.BlockSpec((part, count * width), lambda i: (i, 0)),
        out_shape=jax.ShapeDtypeStruct((model, count * width), bf16),
        cost_estimate=pl.CostEstimate(
            flops=2 * rows * count * model * width,
            bytes_accessed=4 * rows * count * model,
            transcendentals=0,
        ),
        name="out_grads",
    )(*attended, branch_grad)


def rms_scale(x):
    return lax.rsqrt(jnp.mean(x * x, axis=-1, keepdims=True) + norm_eps)


def mix_kernel(count, *refs):
    pieces, weights = refs[:count], refs[count : 2 * count]
    hidden_ref, rates_ref, branch_ref, middle_ref, low_ref, turned_ref, out_ref = refs[2 * count :]
    branch = dot_nt(pieces[0][...], block_of(weights[0]))
    for d in range(1, count):
        branch = branch + dot_nt(pieces[d][...], block_of(weights[d]))

    @pl.when(pl.program_id(0) == 0)
    def _():
        width = pieces[0].shape[1]
        for d in range(count):
            out_ref[:, d * width : (d + 1) * width] = block_of(weights[d])

    branch_ref[...] = branch
    hidden = hidden_ref[...].astype(f32)
    mixed = hidden + rates_ref[0:1, :] * (branch * rms_scale(branch) - hidden)
    middle = mixed * rms_scale(mixed)
    middle_ref[...] = middle
    low_ref[...] = middle.astype(bf16)
    turned_ref[...] = middle.T.astype(bf16)


def mix(pieces, weights, hidden, rates):
    count = len(pieces)
    rows, model = hidden.shape
    width = pieces[0].shape[1]
    part = min(128, rows)

    nd, blocks, shard, local_width = weights.shape
    per = local_width // width
    first = blocks - count // per

    def column(d):
        return pl.BlockSpec((nd, 1, shard, width), lambda i: (0, first + d // per, 0, d % per))

    wide = pl.BlockSpec((part, model), lambda i: (i, 0))
    return pl.pallas_call(
        functools.partial(mix_kernel, count),
        grid=(rows // part,),
        in_specs=[pl.BlockSpec((part, width), lambda i: (i, 0))] * count
        + [column(d) for d in range(count)]
        + [wide, pl.BlockSpec((2, model), lambda i: (0, 0))],
        out_specs=[wide, wide, wide, pl.BlockSpec((model, part), lambda i: (0, i))]
        + [pl.BlockSpec((model, count * width), lambda i: (0, 0))],
        out_shape=[
            jax.ShapeDtypeStruct((rows, model), f32),
            jax.ShapeDtypeStruct((rows, model), f32),
            jax.ShapeDtypeStruct((rows, model), bf16),
            jax.ShapeDtypeStruct((model, rows), bf16),
            jax.ShapeDtypeStruct((model, count * width), bf16),
        ],
        cost_estimate=pl.CostEstimate(
            flops=2 * rows * model * model, bytes_accessed=14 * rows * model, transcendentals=0
        ),
        name="mix",
    )(*pieces, *([weights] * count), hidden, rates)


def block_of(w_ref):
    value = w_ref[:, 0]
    return value.reshape(value.shape[0] * value.shape[1], value.shape[2])


def feed_kernel(
    m_ref,
    wu_ref,
    wg_ref,
    wd_ref,
    s_ref,
    middle_ref,
    cot_ref,
    live_ref,
    rates_ref,
    up_ref,
    gate_ref,
    h_ref,
    result_ref,
    direct_ref,
    low_ref,
    turned_ref,
    rate_ref,
    acc,
):
    i = pl.program_id(0)
    tokens = m_ref[...]
    up = dot_nn(tokens, block_of(wu_ref))
    gate = dot_nn(tokens, block_of(wg_ref))
    up_ref[...] = up
    gate_ref[...] = gate
    scaled = gate * s_ref[1:2, :]
    hidden = (up * s_ref[0:1, :] * (scaled * jax.nn.sigmoid(scaled))).astype(bf16)
    h_ref[...] = hidden
    part_out = dot_nt(hidden, block_of(wd_ref))

    @pl.when(i == 0)
    def _():
        acc[...] = part_out

    @pl.when(i > 0)
    def _():
        acc[...] += part_out

    @pl.when(i == pl.num_programs(0) - 1)
    def _():
        rate_ref[...] = jnp.zeros_like(rate_ref)
        rate = rates_ref[1:2, :]
        part = min(64, acc.shape[0])

        def body(at, carry):
            rows = pl.ds(pl.multiple_of(at * part, part), part)
            out = acc[rows, :]
            middle = middle_ref[rows, :]
            out_scale = rms_scale(out)
            unit = out * out_scale
            mixed = middle + rate * (unit - middle)
            scale = rms_scale(mixed)
            final = mixed * scale
            result_ref[rows, :] = final.astype(bf16)
            grad = cot_ref[rows, :].astype(f32) * live_ref[rows, :]
            mixed_grad = scale * (grad - final * jnp.mean(final * grad, axis=-1, keepdims=True))
            direct_ref[rows, :] = mixed_grad * (1.0 - rate)
            rate_ref[...] += jnp.sum(mixed_grad * (unit - middle), axis=0, keepdims=True)
            unit_grad = mixed_grad * rate
            out_grad = out_scale * (
                unit_grad - unit * jnp.mean(unit * unit_grad, axis=-1, keepdims=True)
            )
            low_ref[rows, :] = out_grad.astype(bf16)
            return carry

        lax.fori_loop(0, acc.shape[0] // part, body, 0)
        for at in range(acc.shape[0] // 128):
            rows = slice(at * 128, (at + 1) * 128)
            turned_ref[:, rows] = low_ref[rows, :].T


def weight_specs(weights, step, base=0):
    nd, _, shard, local_width = weights.shape
    per = local_width // step

    def spec(m):
        return pl.BlockSpec(
            (nd, 1, shard, step), lambda i: (0, 3 * ((i + base) // per) + m, 0, (i + base) % per)
        )

    return [spec(0), spec(1), spec(2)]


def feed(low, weights, scales, middle, cotangent, live, rates, step):
    rows, model = low.shape
    total = scales.shape[1]
    columns = pl.BlockSpec((rows, step), lambda i: (0, i))
    whole = pl.BlockSpec((rows, model), lambda i: (0, 0))
    return pl.pallas_call(
        feed_kernel,
        grid=(total // step,),
        in_specs=[whole]
        + weight_specs(weights, step)
        + [
            pl.BlockSpec((2, step), lambda i: (0, i)),
            whole,
            whole,
            pl.BlockSpec((rows, 1), lambda i: (0, 0)),
            pl.BlockSpec((2, model), lambda i: (0, 0)),
        ],
        out_specs=[columns, columns, columns, whole, whole, whole]
        + [
            pl.BlockSpec((model, rows), lambda i: (0, 0)),
            pl.BlockSpec((1, model), lambda i: (0, 0)),
        ],
        out_shape=[
            jax.ShapeDtypeStruct((rows, total), f32),
            jax.ShapeDtypeStruct((rows, total), f32),
            jax.ShapeDtypeStruct((rows, total), bf16),
            jax.ShapeDtypeStruct((rows, model), bf16),
            jax.ShapeDtypeStruct((rows, model), f32),
            jax.ShapeDtypeStruct((rows, model), bf16),
            jax.ShapeDtypeStruct((model, rows), bf16),
            jax.ShapeDtypeStruct((1, model), f32),
        ],
        scratch_shapes=[pltpu.VMEM((rows, model), f32)],
        cost_estimate=pl.CostEstimate(
            flops=6 * rows * model * total,
            bytes_accessed=6 * model * total + 10 * rows * total,
            transcendentals=0,
        ),
        name="feed",
    )(low, weights, weights, weights, scales, middle, cotangent, live, rates)


def feed_back_step(
    og_ref, ogt_ref, mt_ref, wu_ref, wg_ref, wd_ref, s_ref, up_ref, gate_ref, h_ref, start_ref, grad_ref, sg_ref, acc
):
    i = pl.program_id(0)
    grad_ref[2] = dot_nn(ogt_ref[...], h_ref[...]).astype(bf16)
    hidden_grad = dot_nn(og_ref[...], block_of(wd_ref))
    up = up_ref[...]
    gate = gate_ref[...]
    up_gain = s_ref[0:1, :]
    gate_gain = s_ref[1:2, :]
    scaled = gate * gate_gain
    sig = jax.nn.sigmoid(scaled)
    up_part = hidden_grad * (scaled * sig)
    gate_part = hidden_grad * (up * up_gain) * (sig * (1.0 + scaled * (1.0 - sig)))
    sg_ref[0:1, :] = jnp.sum(up_part * up, axis=0, keepdims=True)
    sg_ref[1:2, :] = jnp.sum(gate_part * gate, axis=0, keepdims=True)
    up_low = (up_part * up_gain).astype(bf16)
    gate_low = (gate_part * gate_gain).astype(bf16)
    tokens_t = mt_ref[...]
    grad_ref[0] = dot_nn(tokens_t, up_low).astype(bf16)
    grad_ref[1] = dot_nn(tokens_t, gate_low).astype(bf16)
    back = dot_nt(up_low, block_of(wu_ref)) + dot_nt(gate_low, block_of(wg_ref))

    @pl.when(i == 0)
    def _():
        acc[...] = start_ref[...] + back

    @pl.when(i > 0)
    def _():
        acc[...] += back


def feed_back_first_kernel(*refs):
    feed_back_step(*refs)


def feed_back_last_kernel(*refs):
    branch_ref, hidden_ref, rates_ref = refs[11:14]
    grad_ref, sg_ref, token_ref, low_ref, rate_ref, acc = refs[14:]
    feed_back_step(*refs[:11], grad_ref, sg_ref, acc)

    @pl.when(pl.program_id(0) == pl.num_programs(0) - 1)
    def _():
        rate_ref[...] = jnp.zeros_like(rate_ref)
        rate = rates_ref[0:1, :]
        part = min(64, acc.shape[0])

        def body(at, carry):
            rows = pl.ds(pl.multiple_of(at * part, part), part)
            grad = acc[rows, :]
            branch = branch_ref[rows, :]
            hidden = hidden_ref[rows, :].astype(f32)
            branch_scale = rms_scale(branch)
            unit = branch * branch_scale
            mixed = hidden + rate * (unit - hidden)
            scale = rms_scale(mixed)
            middle = mixed * scale
            mixed_grad = scale * (grad - middle * jnp.mean(middle * grad, axis=-1, keepdims=True))
            token_ref[rows, :] = mixed_grad * (1.0 - rate)
            rate_ref[...] += jnp.sum(mixed_grad * (unit - hidden), axis=0, keepdims=True)
            unit_grad = mixed_grad * rate
            branch_grad = branch_scale * (
                unit_grad - unit * jnp.mean(unit * unit_grad, axis=-1, keepdims=True)
            )
            low_ref[rows, :] = branch_grad.astype(bf16)
            return carry

        lax.fori_loop(0, acc.shape[0] // part, body, 0)


def feed_back(
    out_grad, out_grad_t, middle_t, weights, scales, up, gate, hidden_units, start, mixing, step, base, count
):
    model, rows = middle_t.shape
    width = count * step
    columns = pl.BlockSpec((rows, step), lambda i: (0, i + base))
    whole = pl.BlockSpec((rows, model), lambda i: (0, 0))
    turned = pl.BlockSpec((model, rows), lambda i: (0, 0))
    wide = jax.ShapeDtypeStruct((rows, model), f32)
    grads_specs = [
        pl.BlockSpec((3, model, step), lambda i: (0, 0, i)),
        pl.BlockSpec((2, step), lambda i: (0, i)),
    ]
    grads_shapes = [
        jax.ShapeDtypeStruct((3, model, width), bf16),
        jax.ShapeDtypeStruct((2, width), f32),
    ]
    last = bool(mixing)
    return pl.pallas_call(
        feed_back_last_kernel if last else feed_back_first_kernel,
        grid=(count,),
        in_specs=[whole, turned, turned]
        + weight_specs(weights, step, base)
        + [pl.BlockSpec((2, step), lambda i: (0, i + base)), columns, columns, columns, whole]
        + ([whole, whole, pl.BlockSpec((2, model), lambda i: (0, 0))] if last else []),
        out_specs=grads_specs
        + ([whole, whole, pl.BlockSpec((1, model), lambda i: (0, 0))] if last else [whole]),
        out_shape=grads_shapes
        + (
            [
                wide,
                jax.ShapeDtypeStruct((rows, model), bf16),
                jax.ShapeDtypeStruct((1, model), f32),
            ]
            if last
            else [wide]
        ),
        scratch_shapes=[pltpu.VMEM((rows, model), f32)] if last else [],
        cost_estimate=pl.CostEstimate(
            flops=12 * rows * model * width,
            bytes_accessed=12 * model * width + 10 * rows * width,
            transcendentals=0,
        ),
        name="feed_back_last" if last else "feed_back_first",
    )(
        out_grad,
        out_grad_t,
        middle_t,
        weights,
        weights,
        weights,
        scales,
        up,
        gate,
        hidden_units,
        start,
        *mixing,
    )


def shift(value, axis, distance, size):
    return lax.ppermute(value, axis, [(i, (i + distance) % size) for i in range(size)])


def carry_on(up, down, hop, axis, size):
    up = lax.ppermute(up, axis, [(i, i + 1) for i in range(hop - 1, size - 1)])
    down = lax.ppermute(down, axis, [(i, i - 1) for i in range(1, size - hop + 1)])
    return up, down


def line_sum(pieces, hop, up, down, axis, size):
    ahead, behind = pieces[size - hop], pieces[hop]
    ahead = ahead if up is None else ahead + up
    behind = behind if down is None else behind + down
    up = lax.ppermute(ahead, axis, [(i, i + 1) for i in range(hop)])
    down = lax.ppermute(behind, axis, [(i, i - 1) for i in range(size - hop, size)])
    return up, down


def halving(value, axis, size, step):
    lead, (count, rows, width) = value.shape[:-3], value.shape[-3:]
    bit = (lax.axis_index(axis) // step) % 2
    pairs = value.reshape(lead + (count // 2, 2, rows, width))
    sent = lax.dynamic_index_in_dim(pairs, 1 - bit, len(lead) + 1, False)
    kept = lax.dynamic_index_in_dim(pairs, bit, len(lead) + 1, False)
    other = lax.ppermute(sent, axis, [(i, i ^ step) for i in range(size)])
    value = kept.astype(f32) + other.astype(f32)
    return value.reshape(lead + (rows, width)) if 2 * step == size else value.astype(bf16)


def exchange_add(value, axis, size, step):
    return value + lax.ppermute(value, axis, [(i, i ^ step) for i in range(size)])


def doublings(size):
    return [1 << k for k in range(size.bit_length() - 1)]


def butterfly(value, axis, size):
    for step in doublings(size):
        value = exchange_add(value, axis, size, step)
    return value


def take_block(value, index, size, axis):
    return lax.dynamic_slice_in_dim(value, index * size, size, axis)


def put_block(whole, value, index, axis):
    return lax.dynamic_update_slice_in_dim(whole, value, index * value.shape[axis], axis)


def local(
    nd,
    nt,
    hidden_in,
    cotangent,
    segments,
    attn_weight,
    mlp_weight,
    rates,
    qk_scale,
    mlp_scales,
    attn_moment_one,
    attn_moment_two,
    mlp_moment_one,
    mlp_moment_two,
):
    rows, model = hidden_in.shape
    length = segments.shape[0]
    shard = attn_weight.shape[1]
    heads_width = attn_weight.shape[2]
    hidden_width = mlp_weight.shape[2]
    block = min(512, length)
    step = min(512, hidden_width)
    me = lax.axis_index("tensor")

    def gather(value):
        return [value] + [shift(value, "tensor", d, nt) for d in range(1, nt)]

    def both(ups, downs, d):
        return (ups[0],) if d == 0 else (ups[d], downs[nt - d])

    middle_hop = nt // 2
    order = [d for d in range(nt) if d != middle_hop] + [middle_hop]
    attn_low = attn_weight.astype(bf16)
    qkv_full = lax.all_gather(
        jnp.concatenate([attn_low[0], attn_low[1], attn_low[2]], axis=1), "dp", axis=0, tiled=True
    )
    low_block = jnp.concatenate(
        [
            mlp_weight.astype(bf16).reshape(3 * shard, hidden_width),
            attn_low[3].reshape(-1, hidden_width),
        ],
        axis=0,
    )
    ups, downs = [low_block], [low_block]
    for hop in range(1, nt):
        if hop == nt - 1:
            ups[-1], downs[-1], hidden_in = lax.optimization_barrier((ups[-1], downs[-1], hidden_in))
        up, down = carry_on(ups[-1], downs[-1], hop, "tensor", nt)
        ups.append(up)
        downs.append(down)
    low_blocks = [sum(both(ups, downs, d)) for d in range(nt)]
    out_low = jnp.concatenate(
        [low[3 * shard :].reshape(shard, heads_width) for low in low_blocks], axis=1
    )
    mlp_full = lax.all_gather(
        jnp.concatenate(
            [low_blocks[d][: 3 * shard] for d in order]
            + [
                out_low[:, at : at + hidden_width]
                for at in range(0, nt * heads_width, hidden_width)
            ],
            axis=0,
        ),
        "dp",
        axis=0,
        tiled=True,
    )
    mlp_full = mlp_full.reshape(nd, -1, shard, hidden_width)
    scales_parts = gather(mlp_scales)
    scales_row = jnp.concatenate([scales_parts[d] for d in order], axis=1)

    starts = starts_of(segments)
    positions = (jnp.arange(length, dtype=jnp.int32) - starts).astype(f32)
    lane = jnp.arange(128, dtype=jnp.int32)
    half = HEAD_DIM // 2
    frequency = 10000.0 ** (-(lane % half).astype(f32) / half)
    sign = jnp.where(lane % HEAD_DIM < half, -1.0, 1.0)
    angles = positions[:, None] * frequency[None, :]
    cosine = jnp.cos(angles)
    sine = jnp.sin(angles) * sign[None, :]
    gain = qk_scale.reshape(1, heads_width)

    ups, downs, state = [hidden_in], [hidden_in], ()
    hidden_parts = [None] * nt

    def projected(hop, state):
        for d in range(nt):
            if (max(d, nt - d) if d else 0) == hop:
                hidden_parts[d] = both(ups, downs, d)
                index = ((me + nt - d) % nt).reshape(1)
                state = project(index, hidden_parts[d], qkv_full, cosine, sine, gain, length, state)
        return state

    for hop in range(1, nt):
        ups[-1], downs[-1], state = lax.optimization_barrier((ups[-1], downs[-1], state))
        up, down = carry_on(ups[-1], downs[-1], hop, "tensor", nt)
        ups.append(up)
        downs.append(down)
        state = projected(hop - 1, state)
    ups[-1], downs[-1], state = lax.optimization_barrier((ups[-1], downs[-1], state))
    state = projected(nt - 1, state)
    query_hat, key_hat, value_hat, query_turned, key_turned = state
    attended_row, attended_f32, log_sum = attend(
        query_hat, key_hat, value_hat, starts[:, None], block
    )
    attended = [take_block(attended_row, me, rows, 0)] + [
        shift(take_block(attended_row, (me + d) % nt, rows, 0), "tensor", d, nt)
        for d in range(1, nt)
    ]
    branch, middle, middle_low, middle_t, out_full = mix(attended, mlp_full, hidden_in, rates)
    row_segments = take_block(segments, me, rows, 0)
    live = (row_segments < pad_segment).astype(f32)[:, None]
    up, gate, hidden_units, result, middle_direct, mlp_out_low, mlp_out_t, rate_mlp_grad = feed(
        middle_low, mlp_full, scales_row, middle, cotangent, live, rates, step
    )
    def spread(value, places):
        width = value.shape[1] // nt
        whole = jnp.zeros_like(value)
        for p, d in enumerate(places):
            piece = value[:, p * width : (p + 1) * width]
            whole = put_block(whole, piece, (me + nt - d) % nt, 1)
        return whole

    per = hidden_width // step
    near = (nt - 1) * per
    feed_args = (mlp_out_low, mlp_out_t, middle_t, mlp_full, scales_row, up, gate, hidden_units)
    far_grad, far_scales, partial = feed_back(*feed_args, middle_direct, (), step, near, per)
    halvings = doublings(nd)
    far_part = lax.psum_scatter(far_grad, "dp", scatter_dimension=1, tiled=True)
    near_grad, near_scales, token_direct, branch_low, rate_attn_grad = feed_back(
        *feed_args, partial, (branch, hidden_in, rates), step, 0, near
    )
    near_part = lax.psum_scatter(near_grad, "dp", scatter_dimension=1, tiled=True)

    grad_row = jnp.zeros((length, heads_width), bf16)
    for d in list(range(1, nt)) + [0]:
        piece = dot_nn(branch_low, out_full[:, d * heads_width : (d + 1) * heads_width])
        piece = piece.astype(bf16)
        piece = shift(piece, "tensor", -d, nt) if d else piece
        grad_row = put_block(grad_row, piece, (me + d) % nt, 0)
    out_grad = out_grads(attended, branch_low)

    scales_grad = spread(jnp.concatenate([near_scales, far_scales], axis=1), order)
    small = jnp.concatenate(
        [rate_attn_grad, rate_mlp_grad, scales_grad.reshape(-1, model)], axis=0
    )
    steps = [("tensor", nt, k) for k in doublings(nt)] + [("dp", nd, k) for k in doublings(nd)]

    def advance(small):
        return exchange_add(small, *steps.pop(0)) if steps else small

    far_part, grad_row, out_grad, small = lax.optimization_barrier(
        (far_part, grad_row, out_grad, small)
    )
    small = advance(small)
    out_sum = halving(out_grad.reshape(nd, shard, -1), "dp", nd, halvings[0])
    head_group = max(128, heads_width // 2)
    head_grads = []
    for group in range(heads_width // head_group):
        if group == 1:
            head_grads, grad_row, far_part, small, out_sum = lax.optimization_barrier(
                (head_grads, grad_row, far_part, small, out_sum)
            )
            small = advance(small)
            out_sum = halving(out_sum, "dp", nd, halvings[1])
        head_grads.append(
            attend_back(
                query_hat,
                key_hat,
                value_hat,
                grad_row,
                attended_f32,
                log_sum,
                starts[None, :],
                block,
                group,
                head_group,
            )
        )
    far_first = shift(far_part[:2], "tensor", -middle_hop, nt)
    far_last = far_part[2:]
    head_grads, small, out_sum, far_first, far_last = lax.optimization_barrier(
        (head_grads, small, out_sum, far_first, far_last)
    )
    far_last = shift(far_last, "tensor", -middle_hop, nt)
    small = advance(small)
    for k in halvings[1 if len(head_grads) == 1 else 2 :]:
        out_sum = halving(out_sum, "dp", nd, k)
    qkv_grad, gain_grad, *pieces = project_back(
        me.reshape(1),
        head_grads,
        (query_turned, key_turned),
        qkv_full,
        cosine,
        sine,
        gain,
        rows,
    )
    qkv_grad, pieces, small, out_sum, far_last = lax.optimization_barrier(
        (qkv_grad, pieces, small, out_sum, far_last)
    )
    far_part = jnp.concatenate([far_first, far_last], axis=0)
    hidden_turn = [hidden_parts[(nt - d) % nt] for d in range(nt)]
    qkv_sum = projection_grads(hidden_turn, qkv_grad)
    qkv_sum = qkv_sum.reshape(nd, shard, -1)

    def blocks_of(part, axis, width):
        return [
            lax.slice_in_dim(part, at, at + width, axis=axis)
            for at in range(0, part.shape[axis], width)
        ]

    def to_owners(pieces, places):
        return [shift(piece, "tensor", -d, nt) if d else piece for d, piece in zip(places, pieces)]

    out_sum, gain_grad, qkv_sum = lax.optimization_barrier((out_sum, gain_grad, qkv_sum))
    out_pieces = to_owners(blocks_of(out_sum.astype(bf16), 1, heads_width), range(nt))
    gain_parts = gather(gain_grad)
    ahead = behind = None
    for hop in range(1, nt):
        if hop == 2:
            ahead, behind, qkv_sum, out_pieces, gain_parts = lax.optimization_barrier(
                (ahead, behind, qkv_sum, out_pieces, gain_parts)
            )
        if hop == max(2, nt - 1):
            ahead, behind, near_part, qkv_sum = lax.optimization_barrier(
                (ahead, behind, near_part, qkv_sum)
            )
            near_pieces = blocks_of(near_part, 2, hidden_width)
            near_pieces, qkv_sum, small = lax.optimization_barrier((near_pieces, qkv_sum, small))
            near_pieces = to_owners(near_pieces, order[:-1])
        ahead, behind = line_sum(pieces, hop, ahead, behind, "tensor", nt)
        if hop == 2:
            for k in halvings[:2]:
                qkv_sum = halving(qkv_sum, "dp", nd, k)
    for k in halvings[2:]:
        qkv_sum = halving(qkv_sum, "dp", nd, k)
    gain_row = spread(jnp.concatenate(gain_parts, axis=1), range(nt))
    while steps:
        small = advance(small)
    out_own = sum(piece.astype(f32) for piece in out_pieces)
    attn_weight_grad = jnp.stack(
        [qkv_sum[:, m * heads_width : (m + 1) * heads_width] for m in range(3)] + [out_own]
    )
    attn_one, attn_two, attn_moved = adam_moved(
        attn_weight, attn_weight_grad, attn_moment_one, attn_moment_two
    )
    attn_square = jnp.sum(attn_moved * attn_moved, axis=1, keepdims=True)
    last = jnp.concatenate([attn_square.reshape(1, -1), gain_row], axis=1)
    last = butterfly(last, "dp", nd)
    near_pieces, last, small = lax.optimization_barrier((near_pieces, last, small))
    rates_grad = small[:2]
    mlp_scales_grad = small[2:].reshape(2, nt * hidden_width)

    attn_square = last[:, : 4 * heads_width].reshape(4, 1, heads_width)
    gain_row = last[:, 4 * heads_width :].reshape(-1)
    attn_new = attn_moved * lax.rsqrt(attn_square + norm_eps)

    mlp_weight_grad = sum(piece.astype(f32) for piece in near_pieces + [far_part])
    mlp_one, mlp_two, mlp_moved = adam_moved(
        mlp_weight, mlp_weight_grad, mlp_moment_one, mlp_moment_two
    )
    mlp_square = jnp.sum(mlp_moved * mlp_moved, axis=1, keepdims=True)
    mlp_square = butterfly(mlp_square.reshape(1, -1), "dp", nd).reshape(mlp_square.shape)
    mlp_square, ahead, behind = lax.optimization_barrier((mlp_square, ahead, behind))
    total = token_direct + pieces[0].astype(f32)
    input_grad = (total + ahead.astype(f32) + behind.astype(f32)).astype(bf16)
    mlp_new = mlp_moved * lax.rsqrt(mlp_square + norm_eps)
    return (
        result.astype(bf16),
        input_grad,
        attn_weight_grad,
        mlp_weight_grad,
        rates_grad,
        gain_row,
        mlp_scales_grad,
        attn_one,
        attn_two,
        mlp_one,
        mlp_two,
        attn_new,
        mlp_new,
    )


def solution(mesh):
    weights = P(None, "dp", "tensor")
    tokens = P(("dp", "tensor"), None)
    return jax.shard_map(
        functools.partial(local, mesh.shape["dp"], mesh.shape["tensor"]),
        mesh=mesh,
        in_specs=(
            tokens,
            tokens,
            P("dp"),
            weights,
            weights,
            P(),
            P("tensor"),
            P(None, "tensor"),
            weights,
            weights,
            weights,
            weights,
        ),
        out_specs=(
            tokens,
            tokens,
            weights,
            weights,
            P(),
            P(),
            P(),
            weights,
            weights,
            weights,
            weights,
            weights,
            weights,
        ),
        check_vma=False,
    )
```

```python
import functools
import math

import jax
import jax.numpy as jnp
from jax import lax
from jax.experimental import pallas as pl
from jax.experimental.pallas import tpu as pltpu
from jax.sharding import PartitionSpec as P

HEAD_DIM = 64
LOG2E = 1.4426950408889634

norm_eps = 1e-06
pad_segment = 63
beta_one = 0.9
beta_two = 0.95
learning_rate = 0.01
adam_eps = 1e-08
bias_one = 1.0 - 0.9**10
bias_two = 1.0 - 0.95**10
scale_factor = math.sqrt(HEAD_DIM)
f32 = jnp.float32
bf16 = jnp.bfloat16


def starts_of(segment_row):
    indices = jnp.arange(segment_row.shape[0], dtype=jnp.int32)
    changed = jnp.concatenate(
        [jnp.ones((1,), dtype=jnp.bool_), segment_row[1:] != segment_row[:-1]]
    )
    return lax.cummax(jnp.where(changed, indices, jnp.zeros_like(indices)), axis=0)


def adam_moved(weight, gradient, moment_one, moment_two):
    moment_one_new = beta_one * moment_one + (1.0 - beta_one) * gradient
    moment_two_new = beta_two * moment_two + (1.0 - beta_two) * gradient * gradient
    moved = weight - learning_rate * (moment_one_new / bias_one) / (
        jnp.sqrt(moment_two_new / bias_two) + adam_eps
    )
    return (moment_one_new, moment_two_new, moved)


def dot_nt(a, b):
    return lax.dot_general(a, b, (((1,), (1,)), ((), ())), preferred_element_type=f32)


def dot_nn(a, b):
    return lax.dot_general(a, b, (((1,), (0,)), ((), ())), preferred_element_type=f32)


def dot_tn(a, b):
    return lax.dot_general(a, b, (((0,), (0,)), ((), ())), preferred_element_type=f32)


def head_stack(x, heads):
    lane = lax.broadcasted_iota(jnp.int32, x.shape, 1) // HEAD_DIM
    zero = jnp.zeros_like(x)
    return jnp.concatenate([jnp.where(lane == h, x, zero) for h in range(heads)], axis=0)


def head_pick(stacked, heads, rows):
    width = stacked.shape[1]
    lane = lax.broadcasted_iota(jnp.int32, (rows, width), 1) // HEAD_DIM
    picked = jnp.zeros((rows, width), f32)
    for h in range(heads):
        picked = jnp.where(lane == h, stacked[h * rows : (h + 1) * rows], picked)
    return picked


def attend_kernel(heads, bq, bk, bounds_ref, q_ref, k_ref, v_ref, start_ref, o_ref, of_ref, l_ref, acc, lsum):
    i = pl.program_id(0)
    qs = head_stack(q_ref[...], heads)
    acc[...] = jnp.zeros_like(acc)
    lsum[...] = jnp.zeros_like(lsum)
    start = jnp.concatenate([start_ref[...]] * heads, axis=0)

    def step(j, masked, diagonal):
        offset = pl.multiple_of(j * bk, bk)
        keys = k_ref[pl.ds(offset, bk), :]
        values = v_ref[pl.ds(offset, bk), :]
        scores = dot_nt(qs, keys)
        weights = jnp.exp2(scores * (scale_factor * LOG2E))
        if masked:
            key_index = offset + lax.broadcasted_iota(jnp.int32, scores.shape, 1)
            allowed = key_index >= start
            if diagonal:
                row = lax.rem(lax.broadcasted_iota(jnp.int32, scores.shape, 0), bq)
                allowed = allowed & (key_index <= i * bq + row)
            weights = jnp.where(allowed, weights, 0.0)
        total = weights[:, :128]
        for part in range(1, bk // 128):
            total = total + weights[:, part * 128 : (part + 1) * 128]
        lsum[...] += total
        acc[...] += dot_nn(weights.astype(bf16), values)

    def body(masked, j, carry):
        step(j, masked, False)
        return carry

    inside = bounds_ref[1, i]
    lax.fori_loop(bounds_ref[0, i], inside, functools.partial(body, True), 0)
    lax.fori_loop(inside, i, functools.partial(body, False), 0)
    step(i, True, True)
    summed = jnp.sum(lsum[...], axis=1, keepdims=True)
    out = head_pick(acc[...] * (1.0 / summed), heads, bq)
    of_ref[...] = out
    o_ref[...] = out.astype(bf16)
    l_ref[...] = jnp.log2(summed).reshape(heads, bq)


def key_bounds(starts, block):
    blocks = jnp.arange(starts.shape[0] // block, dtype=jnp.int32)
    first = starts[::block] // block
    inside = (starts[block - 1 :: block] + (block - 1)) // block
    return jnp.stack([first, jnp.clip(inside, first, blocks)])


def attend(bounds, q, k, v, start, block):
    length, width = q.shape
    heads = width // HEAD_DIM
    whole = pl.BlockSpec((length, width), lambda i: (0, 0))
    rows = pl.BlockSpec((block, width), lambda i: (i, 0))
    return pl.pallas_call(
        functools.partial(attend_kernel, heads, block, block),
        grid=(length // block,),
        in_specs=[pl.BlockSpec(memory_space=pltpu.SMEM), rows, whole, whole]
        + [pl.BlockSpec((block, 1), lambda i: (i, 0))],
        out_specs=[rows, rows, pl.BlockSpec((heads, block), lambda i: (0, i))],
        out_shape=[
            jax.ShapeDtypeStruct((length, width), bf16),
            jax.ShapeDtypeStruct((length, width), f32),
            jax.ShapeDtypeStruct((heads, length), f32),
        ],
        scratch_shapes=[
            pltpu.VMEM((heads * block, width), f32),
            pltpu.VMEM((heads * block, 128), f32),
        ],
        cost_estimate=pl.CostEstimate(
            flops=20_000_000_000, bytes_accessed=8 * length * width, transcendentals=0
        ),
        name="attend",
    )(bounds, q, k, v, start)


def attend_back_kernel(
    first, heads, bq, bk, bounds_ref, q_ref, do_ref, k_ref, v_ref, of_ref, l_ref, start_ref, dq_ref, dk_ref, dv_ref, acc
):
    i = pl.program_id(0)

    @pl.when(i == 0)
    def _():
        dk_ref[...] = jnp.zeros_like(dk_ref)
        dv_ref[...] = jnp.zeros_like(dv_ref)

    qs = head_stack(q_ref[...], heads)
    grads = do_ref[...]
    dos = head_stack(grads, heads)
    product = (grads.astype(f32) * of_ref[...]).T
    delta = jnp.concatenate(
        [
            jnp.sum(product[h * HEAD_DIM : (h + 1) * HEAD_DIM], axis=0, keepdims=True)
            for h in range(heads)
        ],
        axis=1,
    )
    log_sum = jnp.concatenate([l_ref[first + h : first + h + 1, :] for h in range(heads)], axis=1)
    start = jnp.concatenate([start_ref[...]] * heads, axis=1)
    acc[...] = jnp.zeros_like(acc)

    def step(j, masked, diagonal):
        offset = pl.multiple_of(j * bk, bk)
        keys = k_ref[pl.ds(offset, bk), :]
        values = v_ref[pl.ds(offset, bk), :]
        scores = dot_nt(keys, qs)
        probs = jnp.exp2(scores * (scale_factor * LOG2E) - log_sum)
        if masked:
            key_index = offset + lax.broadcasted_iota(jnp.int32, scores.shape, 0)
            allowed = key_index >= start
            if diagonal:
                column = lax.rem(lax.broadcasted_iota(jnp.int32, scores.shape, 1), bq)
                allowed = allowed & (key_index <= i * bq + column)
            probs = jnp.where(allowed, probs, 0.0)
        prob_grad = dot_nt(values, dos)
        score_grad = (probs * (prob_grad - delta)).astype(bf16)
        dv_ref[pl.ds(offset, bk), :] += dot_nn(probs.astype(bf16), dos)
        dk_ref[pl.ds(offset, bk), :] += dot_nn(score_grad, qs)
        acc[...] += dot_tn(score_grad, keys)

    def body(masked, j, carry):
        step(j, masked, False)
        return carry

    inside = bounds_ref[1, i]
    lax.fori_loop(bounds_ref[0, i], inside, functools.partial(body, True), 0)
    lax.fori_loop(inside, i, functools.partial(body, False), 0)
    step(i, True, True)
    dq_ref[...] = head_pick(acc[...], heads, bq)


def attend_back(bounds, q, k, v, grads, out, log_sum, start, block, group, width):
    length = q.shape[0]
    heads = width // HEAD_DIM
    taken = pl.BlockSpec((length, width), lambda i: (0, group))
    taken_rows = pl.BlockSpec((block, width), lambda i: (i, group))
    whole = pl.BlockSpec((length, width), lambda i: (0, 0))
    rows = pl.BlockSpec((block, width), lambda i: (i, 0))
    result = jax.ShapeDtypeStruct((length, width), f32)
    return pl.pallas_call(
        functools.partial(attend_back_kernel, group * heads, heads, block, block),
        grid=(length // block,),
        in_specs=[
            pl.BlockSpec(memory_space=pltpu.SMEM),
            taken_rows,
            taken_rows,
            taken,
            taken,
            taken_rows,
            pl.BlockSpec((log_sum.shape[0], block), lambda i: (0, i)),
            pl.BlockSpec((1, block), lambda i: (0, i)),
        ],
        out_specs=[rows, whole, whole],
        out_shape=[result, result, result],
        scratch_shapes=[pltpu.VMEM((heads * block, width), f32)],
        cost_estimate=pl.CostEstimate(
            flops=40_000_000_000, bytes_accessed=20 * length * width, transcendentals=0
        ),
        name="attend_back",
    )(bounds, q, grads, k, v, out, log_sum, start)


def partner(x):
    width = x.shape[1]
    lane = lax.broadcasted_iota(jnp.int32, x.shape, 1)
    ahead = pltpu.roll(x, width - HEAD_DIM // 2, 1)
    behind = pltpu.roll(x, HEAD_DIM // 2, 1)
    return jnp.where(lax.rem(lane, HEAD_DIM) < HEAD_DIM // 2, ahead, behind)


def head_sums(x):
    width = x.shape[1]
    row = lax.broadcasted_iota(jnp.int32, (width, width), 0) // HEAD_DIM
    column = lax.broadcasted_iota(jnp.int32, (width, width), 1) // HEAD_DIM
    same = jnp.where(row == column, 1.0, 0.0).astype(bf16)
    high = x.astype(bf16)
    low = (x - high.astype(f32)).astype(bf16)
    return dot_nn(high, same) + dot_nn(low, same)


def widen(table, width):
    return table if table.shape[1] == width else jnp.concatenate([table] * (width // 128), axis=1)


def added(refs):
    total = refs[0][...]
    for ref in refs[1:]:
        total = total + ref[...]
    return total


def project_kernel(count, index_ref, *refs):
    wq_ref, wk_ref, wv_ref, cos_ref, sin_ref, gain_ref = refs[count : count + 6]
    q_ref, k_ref, v_ref, xq_ref, xk_ref = refs[-5:]
    x = added(refs[:count])
    width = q_ref.shape[1]
    cosine = widen(cos_ref[...], width)
    sine = widen(sin_ref[...], width)
    gain = gain_ref[...]
    for w_ref, hat_ref, turned_ref in ((wq_ref, q_ref, xq_ref), (wk_ref, k_ref, xk_ref)):
        raw = dot_nn(x, w_ref[...])
        turned = raw * cosine + partner(raw) * sine
        turned_ref[...] = turned
        hat = turned * lax.rsqrt(head_sums(turned * turned) + norm_eps) * gain
        hat_ref[...] = hat.astype(bf16)
    v_ref[...] = dot_nn(x, wv_ref[...]).astype(bf16)


def project(index, parts, weights, cosine, sine, gain, length, previous):
    rows, model = parts[0].shape
    count = len(parts)
    width = gain.shape[1]
    part = min(256, rows)
    per = rows // part

    def column(m):
        return pl.BlockSpec((model, width), lambda i, at: (0, m))

    table = pl.BlockSpec((part, 128), lambda i, at: (at[0] * per + i, 0))
    out = pl.BlockSpec((part, width), lambda i, at: (at[0] * per + i, 0))
    low = jax.ShapeDtypeStruct((length, width), bf16)
    wide = jax.ShapeDtypeStruct((length, width), f32)
    return pl.pallas_call(
        functools.partial(project_kernel, count),
        grid_spec=pltpu.PrefetchScalarGridSpec(
            num_scalar_prefetch=1,
            grid=(per,),
            in_specs=[pl.BlockSpec((part, model), lambda i, at: (i, 0))] * count
            + [
                column(0),
                column(1),
                column(2),
                table,
                table,
                pl.BlockSpec((1, width), lambda i, at: (0, 0)),
            ]
            + [pl.BlockSpec(memory_space=pl.ANY)] * len(previous),
            out_specs=[out] * 5,
        ),
        out_shape=[low, low, low, wide, wide],
        input_output_aliases={7 + count + i: i for i in range(len(previous))},
        cost_estimate=pl.CostEstimate(
            flops=6 * rows * model * width, bytes_accessed=8 * model * width, transcendentals=0
        ),
        name="project",
    )(index, *parts, weights, weights, weights, cosine, sine, gain, *previous)


def project_back_kernel(groups, index_ref, *refs):
    dq_refs, dk_refs, dv_refs = (refs[m * groups : (m + 1) * groups] for m in range(3))
    (
        xq_ref,
        xk_ref,
        wq_ref,
        wk_ref,
        wv_ref,
        cos_ref,
        sin_ref,
        gain_ref,
        grad_ref,
        gain_grad_ref,
        *piece_refs,
    ) = refs[3 * groups :]

    @pl.when(pl.program_id(0) == 0)
    def _():
        gain_grad_ref[...] = jnp.zeros_like(gain_grad_ref)

    def joined(refs):
        return jnp.concatenate([ref[...] for ref in refs], axis=1) if groups > 1 else refs[0][...]

    width = xq_ref.shape[1]
    cosine = widen(cos_ref[...], width)
    sine = widen(sin_ref[...], width)
    gain = gain_ref[...]
    lows = []
    for d_refs, x_ref in ((dq_refs, xq_ref), (dk_refs, xk_ref)):
        turned = x_ref[...]
        inverse = lax.rsqrt(head_sums(turned * turned) + norm_eps)
        unit = turned * inverse
        hat_grad = joined(d_refs) * scale_factor
        gain_grad_ref[...] += jnp.sum(hat_grad * unit, axis=0, keepdims=True)
        unit_grad = hat_grad * gain
        turned_grad = inverse * (unit_grad - unit * head_sums(unit * unit_grad))
        raw_grad = turned_grad * cosine - partner(turned_grad) * sine
        lows.append(raw_grad.astype(bf16))
    lows.append(joined(dv_refs).astype(bf16))
    piece = jnp.zeros(piece_refs[0].shape, f32)
    for m, w_ref in enumerate((wq_ref, wk_ref, wv_ref)):
        grad_ref[:, m * width : (m + 1) * width] = lows[m]
        piece = piece + dot_nt(lows[m], w_ref[...])
    low = piece.astype(bf16)
    block = pl.program_id(0) // (pl.num_programs(0) // len(piece_refs))
    for d, piece_ref in enumerate(piece_refs):

        @pl.when(block == d)
        def _(piece_ref=piece_ref):
            piece_ref[...] = low


def project_back(index, grads, turned, weights, cosine, sine, gain, rows):
    length, width = turned[0].shape
    groups = len(grads)
    model = weights.shape[0]
    part = min(256, rows)
    per = rows // part
    blocks = length // part

    def column(m):
        return pl.BlockSpec((model, width), lambda i, at: (0, m))

    def turn(i, at):
        return (lax.rem(at[0] * per + i, blocks), 0)

    def piece_block(d):
        return pl.BlockSpec((part, model), lambda i, at: (jnp.clip(i - d * per, 0, per - 1), 0))

    tall = pl.BlockSpec((part, width), turn)
    table = pl.BlockSpec((part, 128), turn)
    return pl.pallas_call(
        functools.partial(project_back_kernel, groups),
        grid_spec=pltpu.PrefetchScalarGridSpec(
            num_scalar_prefetch=1,
            grid=(blocks,),
            in_specs=[pl.BlockSpec((part, width // groups), turn)] * (3 * groups)
            + [tall] * 2
            + [column(0), column(1), column(2), table, table]
            + [pl.BlockSpec((1, width), lambda i, at: (0, 0))],
            out_specs=[
                pl.BlockSpec((part, 3 * width), lambda i, at: (i, 0)),
                pl.BlockSpec((1, width), lambda i, at: (0, 0)),
            ]
            + [piece_block(d) for d in range(length // rows)],
        ),
        out_shape=[
            jax.ShapeDtypeStruct((length, 3 * width), bf16),
            jax.ShapeDtypeStruct((1, width), f32),
        ]
        + [jax.ShapeDtypeStruct((rows, model), bf16)] * (length // rows),
        cost_estimate=pl.CostEstimate(
            flops=length * width, bytes_accessed=length * width, transcendentals=0
        ),
        name="project_back",
    )(index, *[g[m] for m in range(3) for g in grads], *turned, weights, weights, weights, cosine, sine, gain)


def projection_grads_kernel(counts, *refs):
    grad_ref, out_ref = refs[-2:]
    total = None
    for d, count in enumerate(counts):
        hidden = added(refs[:count])
        refs = refs[count:]
        rows = hidden.shape[0]
        part = dot_tn(hidden, grad_ref[d * rows : (d + 1) * rows, :])
        total = part if total is None else total + part
    out_ref[...] = total.astype(bf16)


def projection_grads(hidden, qkv_grad):
    rows, model = hidden[0][0].shape
    length, width = qkv_grad.shape
    counts = tuple(len(parts) for parts in hidden)
    part = 256
    return pl.pallas_call(
        functools.partial(projection_grads_kernel, counts),
        grid=(model // part,),
        in_specs=[pl.BlockSpec((rows, part), lambda i: (0, i))] * sum(counts)
        + [pl.BlockSpec(qkv_grad.shape, lambda i: (0, 0))],
        out_specs=pl.BlockSpec((part, width), lambda i: (i, 0)),
        out_shape=jax.ShapeDtypeStruct((model, width), bf16),
        cost_estimate=pl.CostEstimate(
            flops=2 * length * model * width,
            bytes_accessed=8 * length * model,
            transcendentals=0,
        ),
        name="projection_grads",
    )(*[x for parts in hidden for x in parts], qkv_grad)


def out_grads_kernel(count, *refs):
    attended = refs[:count]
    branch_ref, out_ref = refs[count:]
    width = attended[0].shape[1]
    turned = branch_ref[...].T
    for d in range(count):
        out_ref[:, d * width : (d + 1) * width] = dot_nn(turned, attended[d][...]).astype(bf16)


def out_grads(attended, branch_grad):
    count = len(attended)
    rows, model = branch_grad.shape
    width = attended[0].shape[1]
    part = 256
    return pl.pallas_call(
        functools.partial(out_grads_kernel, count),
        grid=(model // part,),
        in_specs=[pl.BlockSpec(x.shape, lambda i: (0, 0)) for x in attended]
        + [pl.BlockSpec((rows, part), lambda i: (0, i))],
        out_specs=pl.BlockSpec((part, count * width), lambda i: (i, 0)),
        out_shape=jax.ShapeDtypeStruct((model, count * width), bf16),
        cost_estimate=pl.CostEstimate(
            flops=2 * rows * count * model * width,
            bytes_accessed=4 * rows * count * model,
            transcendentals=0,
        ),
        name="out_grads",
    )(*attended, branch_grad)


def rms_scale(x):
    return lax.rsqrt(jnp.mean(x * x, axis=-1, keepdims=True) + norm_eps)


def mix_kernel(count, *refs):
    pieces, weights = refs[:count], refs[count : 2 * count]
    hidden_ref, rates_ref, branch_ref, middle_ref, low_ref, turned_ref, out_ref = refs[2 * count :]
    branch = dot_nt(pieces[0][...], block_of(weights[0]))
    for d in range(1, count):
        branch = branch + dot_nt(pieces[d][...], block_of(weights[d]))

    @pl.when(pl.program_id(0) == 0)
    def _():
        width = pieces[0].shape[1]
        for d in range(count):
            out_ref[:, d * width : (d + 1) * width] = block_of(weights[d])

    branch_ref[...] = branch
    hidden = hidden_ref[...].astype(f32)
    mixed = hidden + rates_ref[0:1, :] * (branch * rms_scale(branch) - hidden)
    middle = mixed * rms_scale(mixed)
    middle_ref[...] = middle
    low_ref[...] = middle.astype(bf16)
    turned_ref[...] = middle.T.astype(bf16)


def mix(pieces, weights, hidden, rates):
    count = len(pieces)
    rows, model = hidden.shape
    width = pieces[0].shape[1]
    part = min(128, rows)

    nd, blocks, shard, local_width = weights.shape
    per = local_width // width
    first = blocks - count // per

    def column(d):
        return pl.BlockSpec((nd, 1, shard, width), lambda i: (0, first + d // per, 0, d % per))

    wide = pl.BlockSpec((part, model), lambda i: (i, 0))
    return pl.pallas_call(
        functools.partial(mix_kernel, count),
        grid=(rows // part,),
        in_specs=[pl.BlockSpec((part, width), lambda i: (i, 0))] * count
        + [column(d) for d in range(count)]
        + [wide, pl.BlockSpec((2, model), lambda i: (0, 0))],
        out_specs=[wide, wide, wide, pl.BlockSpec((model, part), lambda i: (0, i))]
        + [pl.BlockSpec((model, count * width), lambda i: (0, 0))],
        out_shape=[
            jax.ShapeDtypeStruct((rows, model), f32),
            jax.ShapeDtypeStruct((rows, model), f32),
            jax.ShapeDtypeStruct((rows, model), bf16),
            jax.ShapeDtypeStruct((model, rows), bf16),
            jax.ShapeDtypeStruct((model, count * width), bf16),
        ],
        cost_estimate=pl.CostEstimate(
            flops=2 * rows * model * model, bytes_accessed=14 * rows * model, transcendentals=0
        ),
        name="mix",
    )(*pieces, *([weights] * count), hidden, rates)


def block_of(w_ref):
    value = w_ref[:, 0]
    return value.reshape(value.shape[0] * value.shape[1], value.shape[2])


def feed_kernel(
    m_ref,
    wu_ref,
    wg_ref,
    wd_ref,
    s_ref,
    middle_ref,
    cot_ref,
    live_ref,
    rates_ref,
    up_ref,
    gate_ref,
    h_ref,
    result_ref,
    direct_ref,
    low_ref,
    turned_ref,
    rate_ref,
    acc,
):
    i = pl.program_id(0)
    tokens = m_ref[...]
    up = dot_nn(tokens, block_of(wu_ref))
    gate = dot_nn(tokens, block_of(wg_ref))
    up_ref[...] = up
    gate_ref[...] = gate
    scaled = gate * s_ref[1:2, :]
    hidden = (up * s_ref[0:1, :] * (scaled * jax.nn.sigmoid(scaled))).astype(bf16)
    h_ref[...] = hidden
    part_out = dot_nt(hidden, block_of(wd_ref))

    @pl.when(i == 0)
    def _():
        acc[...] = part_out

    @pl.when(i > 0)
    def _():
        acc[...] += part_out

    @pl.when(i == pl.num_programs(0) - 1)
    def _():
        rate_ref[...] = jnp.zeros_like(rate_ref)
        rate = rates_ref[1:2, :]
        part = min(128, acc.shape[0])

        def body(at, carry):
            rows = pl.ds(pl.multiple_of(at * part, part), part)
            out = acc[rows, :]
            middle = middle_ref[rows, :]
            out_scale = rms_scale(out)
            unit = out * out_scale
            mixed = middle + rate * (unit - middle)
            scale = rms_scale(mixed)
            final = mixed * scale
            result_ref[rows, :] = final.astype(bf16)
            grad = cot_ref[rows, :].astype(f32) * live_ref[rows, :]
            mixed_grad = scale * (grad - final * jnp.mean(final * grad, axis=-1, keepdims=True))
            direct_ref[rows, :] = mixed_grad * (1.0 - rate)
            rate_ref[...] += jnp.sum(mixed_grad * (unit - middle), axis=0, keepdims=True)
            unit_grad = mixed_grad * rate
            out_grad = out_scale * (
                unit_grad - unit * jnp.mean(unit * unit_grad, axis=-1, keepdims=True)
            )
            low_ref[rows, :] = out_grad.astype(bf16)
            return carry

        lax.fori_loop(0, acc.shape[0] // part, body, 0)
        for at in range(acc.shape[0] // 128):
            rows = slice(at * 128, (at + 1) * 128)
            turned_ref[:, rows] = low_ref[rows, :].T


def weight_specs(weights, step, base=0):
    nd, _, shard, local_width = weights.shape
    per = local_width // step

    def spec(m):
        return pl.BlockSpec(
            (nd, 1, shard, step), lambda i: (0, 3 * ((i + base) // per) + m, 0, (i + base) % per)
        )

    return [spec(0), spec(1), spec(2)]


def feed(low, weights, scales, middle, cotangent, live, rates, step):
    rows, model = low.shape
    total = scales.shape[1]
    columns = pl.BlockSpec((rows, step), lambda i: (0, i))
    whole = pl.BlockSpec((rows, model), lambda i: (0, 0))
    return pl.pallas_call(
        feed_kernel,
        grid=(total // step,),
        in_specs=[whole]
        + weight_specs(weights, step)
        + [
            pl.BlockSpec((2, step), lambda i: (0, i)),
            whole,
            whole,
            pl.BlockSpec((rows, 1), lambda i: (0, 0)),
            pl.BlockSpec((2, model), lambda i: (0, 0)),
        ],
        out_specs=[columns, columns, columns, whole, whole, whole]
        + [
            pl.BlockSpec((model, rows), lambda i: (0, 0)),
            pl.BlockSpec((1, model), lambda i: (0, 0)),
        ],
        out_shape=[
            jax.ShapeDtypeStruct((rows, total), f32),
            jax.ShapeDtypeStruct((rows, total), f32),
            jax.ShapeDtypeStruct((rows, total), bf16),
            jax.ShapeDtypeStruct((rows, model), bf16),
            jax.ShapeDtypeStruct((rows, model), f32),
            jax.ShapeDtypeStruct((rows, model), bf16),
            jax.ShapeDtypeStruct((model, rows), bf16),
            jax.ShapeDtypeStruct((1, model), f32),
        ],
        scratch_shapes=[pltpu.VMEM((rows, model), f32)],
        cost_estimate=pl.CostEstimate(
            flops=6 * rows * model * total,
            bytes_accessed=6 * model * total + 10 * rows * total,
            transcendentals=0,
        ),
        name="feed",
    )(low, weights, weights, weights, scales, middle, cotangent, live, rates)


def feed_back_step(
    og_ref, ogt_ref, mt_ref, wu_ref, wg_ref, wd_ref, s_ref, up_ref, gate_ref, h_ref, start_ref, grad_ref, sg_ref, acc
):
    i = pl.program_id(0)
    grad_ref[2] = dot_nn(ogt_ref[...], h_ref[...]).astype(bf16)
    hidden_grad = dot_nn(og_ref[...], block_of(wd_ref))
    up = up_ref[...]
    gate = gate_ref[...]
    up_gain = s_ref[0:1, :]
    gate_gain = s_ref[1:2, :]
    scaled = gate * gate_gain
    sig = jax.nn.sigmoid(scaled)
    up_part = hidden_grad * (scaled * sig)
    gate_part = hidden_grad * (up * up_gain) * (sig * (1.0 + scaled * (1.0 - sig)))
    sg_ref[0:1, :] = jnp.sum(up_part * up, axis=0, keepdims=True)
    sg_ref[1:2, :] = jnp.sum(gate_part * gate, axis=0, keepdims=True)
    up_low = (up_part * up_gain).astype(bf16)
    gate_low = (gate_part * gate_gain).astype(bf16)
    tokens_t = mt_ref[...]
    grad_ref[0] = dot_nn(tokens_t, up_low).astype(bf16)
    grad_ref[1] = dot_nn(tokens_t, gate_low).astype(bf16)
    back = dot_nt(up_low, block_of(wu_ref)) + dot_nt(gate_low, block_of(wg_ref))

    @pl.when(i == 0)
    def _():
        acc[...] = start_ref[...] + back

    @pl.when(i > 0)
    def _():
        acc[...] += back


def feed_back_first_kernel(*refs):
    feed_back_step(*refs)


def feed_back_last_kernel(*refs):
    branch_ref, hidden_ref, rates_ref = refs[11:14]
    grad_ref, sg_ref, token_ref, low_ref, rate_ref, acc = refs[14:]
    feed_back_step(*refs[:11], grad_ref, sg_ref, acc)

    @pl.when(pl.program_id(0) == pl.num_programs(0) - 1)
    def _():
        rate_ref[...] = jnp.zeros_like(rate_ref)
        rate = rates_ref[0:1, :]
        part = min(128, acc.shape[0])

        def body(at, carry):
            rows = pl.ds(pl.multiple_of(at * part, part), part)
            grad = acc[rows, :]
            branch = branch_ref[rows, :]
            hidden = hidden_ref[rows, :].astype(f32)
            branch_scale = rms_scale(branch)
            unit = branch * branch_scale
            mixed = hidden + rate * (unit - hidden)
            scale = rms_scale(mixed)
            middle = mixed * scale
            mixed_grad = scale * (grad - middle * jnp.mean(middle * grad, axis=-1, keepdims=True))
            token_ref[rows, :] = mixed_grad * (1.0 - rate)
            rate_ref[...] += jnp.sum(mixed_grad * (unit - hidden), axis=0, keepdims=True)
            unit_grad = mixed_grad * rate
            branch_grad = branch_scale * (
                unit_grad - unit * jnp.mean(unit * unit_grad, axis=-1, keepdims=True)
            )
            low_ref[rows, :] = branch_grad.astype(bf16)
            return carry

        lax.fori_loop(0, acc.shape[0] // part, body, 0)


def feed_back(
    out_grad, out_grad_t, middle_t, weights, scales, up, gate, hidden_units, start, mixing, step, base, count
):
    model, rows = middle_t.shape
    width = count * step
    columns = pl.BlockSpec((rows, step), lambda i: (0, i + base))
    whole = pl.BlockSpec((rows, model), lambda i: (0, 0))
    turned = pl.BlockSpec((model, rows), lambda i: (0, 0))
    wide = jax.ShapeDtypeStruct((rows, model), f32)
    grads_specs = [
        pl.BlockSpec((3, model, step), lambda i: (0, 0, i)),
        pl.BlockSpec((2, step), lambda i: (0, i)),
    ]
    grads_shapes = [
        jax.ShapeDtypeStruct((3, model, width), bf16),
        jax.ShapeDtypeStruct((2, width), f32),
    ]
    last = bool(mixing)
    return pl.pallas_call(
        feed_back_last_kernel if last else feed_back_first_kernel,
        grid=(count,),
        in_specs=[whole, turned, turned]
        + weight_specs(weights, step, base)
        + [pl.BlockSpec((2, step), lambda i: (0, i + base)), columns, columns, columns, whole]
        + ([whole, whole, pl.BlockSpec((2, model), lambda i: (0, 0))] if last else []),
        out_specs=grads_specs
        + ([whole, whole, pl.BlockSpec((1, model), lambda i: (0, 0))] if last else [whole]),
        out_shape=grads_shapes
        + (
            [
                wide,
                jax.ShapeDtypeStruct((rows, model), bf16),
                jax.ShapeDtypeStruct((1, model), f32),
            ]
            if last
            else [wide]
        ),
        scratch_shapes=[pltpu.VMEM((rows, model), f32)] if last else [],
        cost_estimate=pl.CostEstimate(
            flops=12 * rows * model * width,
            bytes_accessed=12 * model * width + 10 * rows * width,
            transcendentals=0,
        ),
        name="feed_back_last" if last else "feed_back_first",
    )(
        out_grad,
        out_grad_t,
        middle_t,
        weights,
        weights,
        weights,
        scales,
        up,
        gate,
        hidden_units,
        start,
        *mixing,
    )


def shift(value, axis, distance, size):
    return lax.ppermute(value, axis, [(i, (i + distance) % size) for i in range(size)])


def carry_on(up, down, hop, axis, size):
    up = lax.ppermute(up, axis, [(i, i + 1) for i in range(hop - 1, size - 1)])
    down = lax.ppermute(down, axis, [(i, i - 1) for i in range(1, size - hop + 1)])
    return up, down


def line_sum(pieces, hop, up, down, axis, size):
    ahead, behind = pieces[size - hop], pieces[hop]
    ahead = ahead if up is None else ahead + up
    behind = behind if down is None else behind + down
    up = lax.ppermute(ahead, axis, [(i, i + 1) for i in range(hop)])
    down = lax.ppermute(behind, axis, [(i, i - 1) for i in range(size - hop, size)])
    return up, down


def halving(value, axis, size, step):
    lead, (count, rows, width) = value.shape[:-3], value.shape[-3:]
    bit = (lax.axis_index(axis) // step) % 2
    pairs = value.reshape(lead + (count // 2, 2, rows, width))
    sent = lax.dynamic_index_in_dim(pairs, 1 - bit, len(lead) + 1, False)
    kept = lax.dynamic_index_in_dim(pairs, bit, len(lead) + 1, False)
    other = lax.ppermute(sent, axis, [(i, i ^ step) for i in range(size)])
    value = kept.astype(f32) + other.astype(f32)
    return value.reshape(lead + (rows, width)) if 2 * step == size else value.astype(bf16)


def exchange_add(value, axis, size, step):
    return value + lax.ppermute(value, axis, [(i, i ^ step) for i in range(size)])


def doublings(size):
    return [1 << k for k in range(size.bit_length() - 1)]


def butterfly(value, axis, size):
    for step in doublings(size):
        value = exchange_add(value, axis, size, step)
    return value


def take_block(value, index, size, axis):
    return lax.dynamic_slice_in_dim(value, index * size, size, axis)


def put_block(whole, value, index, axis):
    return lax.dynamic_update_slice_in_dim(whole, value, index * value.shape[axis], axis)


def local(
    nd,
    nt,
    hidden_in,
    cotangent,
    segments,
    attn_weight,
    mlp_weight,
    rates,
    qk_scale,
    mlp_scales,
    attn_moment_one,
    attn_moment_two,
    mlp_moment_one,
    mlp_moment_two,
):
    rows, model = hidden_in.shape
    length = segments.shape[0]
    shard = attn_weight.shape[1]
    heads_width = attn_weight.shape[2]
    hidden_width = mlp_weight.shape[2]
    block = min(512, length)
    step = min(512, hidden_width)
    me = lax.axis_index("tensor")

    def gather(value):
        return [value] + [shift(value, "tensor", d, nt) for d in range(1, nt)]

    def both(ups, downs, d):
        return (ups[0],) if d == 0 else (ups[d], downs[nt - d])

    middle_hop = nt // 2
    order = [d for d in range(nt) if d != middle_hop] + [middle_hop]
    attn_low = attn_weight.astype(bf16)
    qkv_full = lax.all_gather(
        jnp.concatenate([attn_low[0], attn_low[1], attn_low[2]], axis=1), "dp", axis=0, tiled=True
    )
    low_block = jnp.concatenate(
        [
            mlp_weight.astype(bf16).reshape(3 * shard, hidden_width),
            attn_low[3].reshape(-1, hidden_width),
        ],
        axis=0,
    )
    ups, downs = [low_block], [low_block]
    for hop in range(1, nt):
        if hop == nt - 1:
            ups[-1], downs[-1], hidden_in = lax.optimization_barrier((ups[-1], downs[-1], hidden_in))
        up, down = carry_on(ups[-1], downs[-1], hop, "tensor", nt)
        ups.append(up)
        downs.append(down)
    low_blocks = [sum(both(ups, downs, d)) for d in range(nt)]
    out_low = jnp.concatenate(
        [low[3 * shard :].reshape(shard, heads_width) for low in low_blocks], axis=1
    )
    mlp_full = lax.all_gather(
        jnp.concatenate(
            [low_blocks[d][: 3 * shard] for d in order]
            + [
                out_low[:, at : at + hidden_width]
                for at in range(0, nt * heads_width, hidden_width)
            ],
            axis=0,
        ),
        "dp",
        axis=0,
        tiled=True,
    )
    mlp_full = mlp_full.reshape(nd, -1, shard, hidden_width)
    scales_parts = gather(mlp_scales)
    scales_row = jnp.concatenate([scales_parts[d] for d in order], axis=1)

    starts = starts_of(segments)
    positions = (jnp.arange(length, dtype=jnp.int32) - starts).astype(f32)
    lane = jnp.arange(128, dtype=jnp.int32)
    half = HEAD_DIM // 2
    frequency = 10000.0 ** (-(lane % half).astype(f32) / half)
    sign = jnp.where(lane % HEAD_DIM < half, -1.0, 1.0)
    angles = positions[:, None] * frequency[None, :]
    cosine = jnp.cos(angles)
    sine = jnp.sin(angles) * sign[None, :]
    gain = qk_scale.reshape(1, heads_width)

    ups, downs, state = [hidden_in], [hidden_in], ()
    hidden_parts = [None] * nt

    def projected(hop, state):
        for d in range(nt):
            if (max(d, nt - d) if d else 0) == hop:
                hidden_parts[d] = both(ups, downs, d)
                index = ((me + nt - d) % nt).reshape(1)
                state = project(index, hidden_parts[d], qkv_full, cosine, sine, gain, length, state)
        return state

    for hop in range(1, nt):
        ups[-1], downs[-1], state = lax.optimization_barrier((ups[-1], downs[-1], state))
        up, down = carry_on(ups[-1], downs[-1], hop, "tensor", nt)
        ups.append(up)
        downs.append(down)
        state = projected(hop - 1, state)
    ups[-1], downs[-1], state = lax.optimization_barrier((ups[-1], downs[-1], state))
    state = projected(nt - 1, state)
    query_hat, key_hat, value_hat, query_turned, key_turned = state
    bounds = key_bounds(starts, block)
    attended_row, attended_f32, log_sum = attend(
        bounds, query_hat, key_hat, value_hat, starts[:, None], block
    )
    attended = [take_block(attended_row, me, rows, 0)] + [
        shift(take_block(attended_row, (me + d) % nt, rows, 0), "tensor", d, nt)
        for d in range(1, nt)
    ]
    branch, middle, middle_low, middle_t, out_full = mix(attended, mlp_full, hidden_in, rates)
    row_segments = take_block(segments, me, rows, 0)
    live = (row_segments < pad_segment).astype(f32)[:, None]
    up, gate, hidden_units, result, middle_direct, mlp_out_low, mlp_out_t, rate_mlp_grad = feed(
        middle_low, mlp_full, scales_row, middle, cotangent, live, rates, step
    )
    def spread(value, places):
        width = value.shape[1] // nt
        whole = jnp.zeros_like(value)
        for p, d in enumerate(places):
            piece = value[:, p * width : (p + 1) * width]
            whole = put_block(whole, piece, (me + nt - d) % nt, 1)
        return whole

    def blocks_of(part, axis, width):
        return [
            lax.slice_in_dim(part, at, at + width, axis=axis)
            for at in range(0, part.shape[axis], width)
        ]

    def to_owners(pieces, places):
        return [shift(piece, "tensor", -d, nt) if d else piece for d, piece in zip(places, pieces)]

    per = hidden_width // step
    near = (nt - 1) * per
    feed_args = (mlp_out_low, mlp_out_t, middle_t, mlp_full, scales_row, up, gate, hidden_units)
    far_grad, far_scales, partial = feed_back(*feed_args, middle_direct, (), step, near, per)
    halvings = doublings(nd)
    far_part = lax.psum_scatter(far_grad, "dp", scatter_dimension=1, tiled=True)
    near_grad, near_scales, token_direct, branch_low, rate_attn_grad = feed_back(
        *feed_args, partial, (branch, hidden_in, rates), step, 0, near
    )
    near_part = lax.psum_scatter(near_grad, "dp", scatter_dimension=1, tiled=True)

    grad_pieces = []
    for d in list(range(1, nt)) + [0]:
        piece = dot_nn(branch_low, out_full[:, d * heads_width : (d + 1) * heads_width])
        piece = piece.astype(bf16)
        grad_pieces.append((d, shift(piece, "tensor", -d, nt) if d else piece))
    grad_row = jnp.zeros((length, heads_width), bf16)
    for d, piece in grad_pieces[-1:] + grad_pieces[:-1]:
        grad_row = put_block(grad_row, piece, (me + d) % nt, 0)
    out_sum = out_grads(attended, branch_low).reshape(nd, shard, -1)
    out_sum = halving(out_sum, "dp", nd, halvings[0])

    scales_grad = spread(jnp.concatenate([near_scales, far_scales], axis=1), order)
    small = jnp.concatenate(
        [rate_attn_grad, rate_mlp_grad, scales_grad.reshape(-1, model)], axis=0
    )
    steps = [("tensor", nt, k) for k in doublings(nt)] + [("dp", nd, k) for k in doublings(nd)]

    def advance(small):
        return exchange_add(small, *steps.pop(0)) if steps else small

    far_part, grad_row, out_sum, small = lax.optimization_barrier(
        (far_part, grad_row, out_sum, small)
    )
    small = advance(small)
    out_sum = halving(out_sum, "dp", nd, halvings[1])
    head_group = max(128, heads_width // 2)
    head_grads = []
    for group in range(heads_width // head_group):
        if group == 1:
            head_grads, grad_row, far_part, small, out_sum = lax.optimization_barrier(
                (head_grads, grad_row, far_part, small, out_sum)
            )
            small = advance(small)
            out_sum = halving(out_sum, "dp", nd, halvings[2])
        head_grads.append(
            attend_back(
                bounds,
                query_hat,
                key_hat,
                value_hat,
                grad_row,
                attended_f32,
                log_sum,
                starts[None, :],
                block,
                group,
                head_group,
            )
        )
    far_first = shift(far_part[:2], "tensor", -middle_hop, nt)
    far_last = far_part[2:]
    head_grads, small, out_sum, far_first, far_last = lax.optimization_barrier(
        (head_grads, small, out_sum, far_first, far_last)
    )
    far_last = shift(far_last, "tensor", -middle_hop, nt)
    small = advance(small)
    for k in halvings[2 if len(head_grads) == 1 else 3 :]:
        out_sum = halving(out_sum, "dp", nd, k)
    out_pieces = to_owners(blocks_of(out_sum.astype(bf16), 1, heads_width), range(nt))
    qkv_grad, gain_grad, *pieces = project_back(
        me.reshape(1),
        head_grads,
        (query_turned, key_turned),
        qkv_full,
        cosine,
        sine,
        gain,
        rows,
    )
    qkv_grad, pieces, small, out_pieces, far_last = lax.optimization_barrier(
        (qkv_grad, pieces, small, out_pieces, far_last)
    )
    far_part = jnp.concatenate([far_first, far_last], axis=0)
    hidden_turn = [hidden_parts[(nt - d) % nt] for d in range(nt)]
    qkv_sum = projection_grads(hidden_turn, qkv_grad)
    qkv_sum = qkv_sum.reshape(nd, shard, -1)

    ahead = behind = None
    for hop in range(1, nt):
        if hop == 2:
            ahead, behind, qkv_sum, gain_grad = lax.optimization_barrier(
                (ahead, behind, qkv_sum, gain_grad)
            )
            gain_parts = gather(gain_grad)
        if hop == max(2, nt - 1):
            ahead, behind, near_part, qkv_sum, gain_parts = lax.optimization_barrier(
                (ahead, behind, near_part, qkv_sum, gain_parts)
            )
            near_pieces = blocks_of(near_part, 2, hidden_width)
            near_pieces, qkv_sum, small = lax.optimization_barrier((near_pieces, qkv_sum, small))
            near_pieces = to_owners(near_pieces, order[:-1])
        ahead, behind = line_sum(pieces, hop, ahead, behind, "tensor", nt)
        if hop == 2:
            for k in halvings[:2]:
                qkv_sum = halving(qkv_sum, "dp", nd, k)
    for k in halvings[2:]:
        qkv_sum = halving(qkv_sum, "dp", nd, k)
    gain_row = spread(jnp.concatenate(gain_parts, axis=1), range(nt))
    while steps:
        small = advance(small)
    out_own = sum(piece.astype(f32) for piece in out_pieces)
    attn_weight_grad = jnp.stack(
        [qkv_sum[:, m * heads_width : (m + 1) * heads_width] for m in range(3)] + [out_own]
    )
    attn_one, attn_two, attn_moved = adam_moved(
        attn_weight, attn_weight_grad, attn_moment_one, attn_moment_two
    )
    attn_square = jnp.sum(attn_moved * attn_moved, axis=1, keepdims=True)
    last = jnp.concatenate([attn_square.reshape(1, -1), gain_row], axis=1)
    last = butterfly(last, "dp", nd)
    near_pieces, last, small = lax.optimization_barrier((near_pieces, last, small))
    rates_grad = small[:2]
    mlp_scales_grad = small[2:].reshape(2, nt * hidden_width)

    attn_square = last[:, : 4 * heads_width].reshape(4, 1, heads_width)
    gain_row = last[:, 4 * heads_width :].reshape(-1)
    attn_new = attn_moved * lax.rsqrt(attn_square + norm_eps)

    mlp_weight_grad = sum(piece.astype(f32) for piece in near_pieces + [far_part])
    mlp_one, mlp_two, mlp_moved = adam_moved(
        mlp_weight, mlp_weight_grad, mlp_moment_one, mlp_moment_two
    )
    mlp_square = jnp.sum(mlp_moved * mlp_moved, axis=1, keepdims=True)
    mlp_square = butterfly(mlp_square.reshape(1, -1), "dp", nd).reshape(mlp_square.shape)
    mlp_square, ahead, behind = lax.optimization_barrier((mlp_square, ahead, behind))
    total = token_direct + pieces[0].astype(f32)
    input_grad = (total + ahead.astype(f32) + behind.astype(f32)).astype(bf16)
    mlp_new = mlp_moved * lax.rsqrt(mlp_square + norm_eps)
    return (
        result.astype(bf16),
        input_grad,
        attn_weight_grad,
        mlp_weight_grad,
        rates_grad,
        gain_row,
        mlp_scales_grad,
        attn_one,
        attn_two,
        mlp_one,
        mlp_two,
        attn_new,
        mlp_new,
    )


def solution(mesh):
    weights = P(None, "dp", "tensor")
    tokens = P(("dp", "tensor"), None)
    return jax.shard_map(
        functools.partial(local, mesh.shape["dp"], mesh.shape["tensor"]),
        mesh=mesh,
        in_specs=(
            tokens,
            tokens,
            P("dp"),
            weights,
            weights,
            P(),
            P("tensor"),
            P(None, "tensor"),
            weights,
            weights,
            weights,
            weights,
        ),
        out_specs=(
            tokens,
            tokens,
            weights,
            weights,
            P(),
            P(),
            P(),
            weights,
            weights,
            weights,
            weights,
            weights,
            weights,
        ),
        check_vma=False,
    )
```

```python
import functools
import math

import jax
import jax.numpy as jnp
from jax import lax
from jax.experimental import pallas as pl
from jax.experimental.pallas import tpu as pltpu
from jax.sharding import PartitionSpec as P

HEAD_DIM = 64
LOG2E = 1.4426950408889634

norm_eps = 1e-06
pad_segment = 63
beta_one = 0.9
beta_two = 0.95
learning_rate = 0.01
adam_eps = 1e-08
bias_one = 1.0 - 0.9**10
bias_two = 1.0 - 0.95**10
scale_factor = math.sqrt(HEAD_DIM)
f32 = jnp.float32
bf16 = jnp.bfloat16


def starts_of(segment_row):
    indices = jnp.arange(segment_row.shape[0], dtype=jnp.int32)
    changed = jnp.concatenate(
        [jnp.ones((1,), dtype=jnp.bool_), segment_row[1:] != segment_row[:-1]]
    )
    return lax.cummax(jnp.where(changed, indices, jnp.zeros_like(indices)), axis=0)


def adam_moved(weight, gradient, moment_one, moment_two):
    moment_one_new = beta_one * moment_one + (1.0 - beta_one) * gradient
    moment_two_new = beta_two * moment_two + (1.0 - beta_two) * gradient * gradient
    moved = weight - learning_rate * (moment_one_new / bias_one) / (
        jnp.sqrt(moment_two_new / bias_two) + adam_eps
    )
    return (moment_one_new, moment_two_new, moved)


def dot_nt(a, b):
    return lax.dot_general(a, b, (((1,), (1,)), ((), ())), preferred_element_type=f32)


def dot_nn(a, b):
    return lax.dot_general(a, b, (((1,), (0,)), ((), ())), preferred_element_type=f32)


def dot_tn(a, b):
    return lax.dot_general(a, b, (((0,), (0,)), ((), ())), preferred_element_type=f32)


def head_stack(x, heads):
    lane = lax.broadcasted_iota(jnp.int32, x.shape, 1) // HEAD_DIM
    zero = jnp.zeros_like(x)
    return jnp.concatenate([jnp.where(lane == h, x, zero) for h in range(heads)], axis=0)


def head_pick(stacked, heads, rows):
    width = stacked.shape[1]
    lane = lax.broadcasted_iota(jnp.int32, (rows, width), 1) // HEAD_DIM
    picked = jnp.zeros((rows, width), f32)
    for h in range(heads):
        picked = jnp.where(lane == h, stacked[h * rows : (h + 1) * rows], picked)
    return picked


def attend_kernel(heads, bq, bk, bounds_ref, q_ref, k_ref, v_ref, start_ref, o_ref, of_ref, l_ref, acc, lsum):
    i = pl.program_id(0)
    qs = head_stack(q_ref[...], heads)
    acc[...] = jnp.zeros_like(acc)
    lsum[...] = jnp.zeros_like(lsum)
    start = jnp.concatenate([start_ref[...]] * heads, axis=0)

    def step(j, masked, diagonal):
        offset = pl.multiple_of(j * bk, bk)
        keys = k_ref[pl.ds(offset, bk), :]
        values = v_ref[pl.ds(offset, bk), :]
        scores = dot_nt(qs, keys)
        weights = jnp.exp2(scores * (scale_factor * LOG2E))
        if masked:
            key_index = offset + lax.broadcasted_iota(jnp.int32, scores.shape, 1)
            allowed = key_index >= start
            if diagonal:
                row = lax.rem(lax.broadcasted_iota(jnp.int32, scores.shape, 0), bq)
                allowed = allowed & (key_index <= i * bq + row)
            weights = jnp.where(allowed, weights, 0.0)
        total = weights[:, :128]
        for part in range(1, bk // 128):
            total = total + weights[:, part * 128 : (part + 1) * 128]
        lsum[...] += total
        acc[...] += dot_nn(weights.astype(bf16), values)

    def body(masked, j, carry):
        step(j, masked, False)
        return carry

    inside = bounds_ref[1, i]
    lax.fori_loop(bounds_ref[0, i], inside, functools.partial(body, True), 0)
    lax.fori_loop(inside, i, functools.partial(body, False), 0)
    step(i, True, True)
    summed = jnp.sum(lsum[...], axis=1, keepdims=True)
    out = head_pick(acc[...] * (1.0 / summed), heads, bq)
    of_ref[...] = out
    o_ref[...] = out.astype(bf16)
    l_ref[...] = jnp.log2(summed).reshape(heads, bq)


def key_bounds(starts, block):
    blocks = jnp.arange(starts.shape[0] // block, dtype=jnp.int32)
    first = starts[::block] // block
    inside = (starts[block - 1 :: block] + (block - 1)) // block
    return jnp.stack([first, jnp.clip(inside, first, blocks)])


def attend(bounds, q, k, v, start, block):
    length, width = q.shape
    heads = width // HEAD_DIM
    whole = pl.BlockSpec((length, width), lambda i: (0, 0))
    rows = pl.BlockSpec((block, width), lambda i: (i, 0))
    return pl.pallas_call(
        functools.partial(attend_kernel, heads, block, block),
        grid=(length // block,),
        in_specs=[pl.BlockSpec(memory_space=pltpu.SMEM), rows, whole, whole]
        + [pl.BlockSpec((block, 1), lambda i: (i, 0))],
        out_specs=[rows, rows, pl.BlockSpec((heads, block), lambda i: (0, i))],
        out_shape=[
            jax.ShapeDtypeStruct((length, width), bf16),
            jax.ShapeDtypeStruct((length, width), f32),
            jax.ShapeDtypeStruct((heads, length), f32),
        ],
        scratch_shapes=[
            pltpu.VMEM((heads * block, width), f32),
            pltpu.VMEM((heads * block, 128), f32),
        ],
        cost_estimate=pl.CostEstimate(
            flops=20_000_000_000, bytes_accessed=8 * length * width, transcendentals=0
        ),
        name="attend",
    )(bounds, q, k, v, start)


def attend_back_kernel(
    first, heads, bq, bk, bounds_ref, q_ref, do_ref, k_ref, v_ref, of_ref, l_ref, start_ref, dq_ref, dk_ref, dv_ref, acc
):
    i = pl.program_id(0)

    @pl.when(i == 0)
    def _():
        dk_ref[...] = jnp.zeros_like(dk_ref)
        dv_ref[...] = jnp.zeros_like(dv_ref)

    qs = head_stack(q_ref[...], heads)
    grads = do_ref[...]
    dos = head_stack(grads, heads)
    product = (grads.astype(f32) * of_ref[...]).T
    delta = jnp.concatenate(
        [
            jnp.sum(product[h * HEAD_DIM : (h + 1) * HEAD_DIM], axis=0, keepdims=True)
            for h in range(heads)
        ],
        axis=1,
    )
    log_sum = jnp.concatenate([l_ref[first + h : first + h + 1, :] for h in range(heads)], axis=1)
    start = jnp.concatenate([start_ref[...]] * heads, axis=1)
    acc[...] = jnp.zeros_like(acc)

    def step(j, masked, diagonal):
        offset = pl.multiple_of(j * bk, bk)
        keys = k_ref[pl.ds(offset, bk), :]
        values = v_ref[pl.ds(offset, bk), :]
        scores = dot_nt(keys, qs)
        probs = jnp.exp2(scores * (scale_factor * LOG2E) - log_sum)
        if masked:
            key_index = offset + lax.broadcasted_iota(jnp.int32, scores.shape, 0)
            allowed = key_index >= start
            if diagonal:
                column = lax.rem(lax.broadcasted_iota(jnp.int32, scores.shape, 1), bq)
                allowed = allowed & (key_index <= i * bq + column)
            probs = jnp.where(allowed, probs, 0.0)
        prob_grad = dot_nt(values, dos)
        score_grad = (probs * (prob_grad - delta)).astype(bf16)
        dv_ref[pl.ds(offset, bk), :] += dot_nn(probs.astype(bf16), dos)
        dk_ref[pl.ds(offset, bk), :] += dot_nn(score_grad, qs)
        acc[...] += dot_tn(score_grad, keys)

    def body(masked, j, carry):
        step(j, masked, False)
        return carry

    inside = bounds_ref[1, i]
    lax.fori_loop(bounds_ref[0, i], inside, functools.partial(body, True), 0)
    lax.fori_loop(inside, i, functools.partial(body, False), 0)
    step(i, True, True)
    dq_ref[...] = head_pick(acc[...], heads, bq)


def attend_back(bounds, q, k, v, grads, out, log_sum, start, block, group, width):
    length = q.shape[0]
    heads = width // HEAD_DIM
    taken = pl.BlockSpec((length, width), lambda i: (0, group))
    taken_rows = pl.BlockSpec((block, width), lambda i: (i, group))
    whole = pl.BlockSpec((length, width), lambda i: (0, 0))
    rows = pl.BlockSpec((block, width), lambda i: (i, 0))
    result = jax.ShapeDtypeStruct((length, width), f32)
    return pl.pallas_call(
        functools.partial(attend_back_kernel, group * heads, heads, block, block),
        grid=(length // block,),
        in_specs=[
            pl.BlockSpec(memory_space=pltpu.SMEM),
            taken_rows,
            taken_rows,
            taken,
            taken,
            taken_rows,
            pl.BlockSpec((log_sum.shape[0], block), lambda i: (0, i)),
            pl.BlockSpec((1, block), lambda i: (0, i)),
        ],
        out_specs=[rows, whole, whole],
        out_shape=[result, result, result],
        scratch_shapes=[pltpu.VMEM((heads * block, width), f32)],
        cost_estimate=pl.CostEstimate(
            flops=40_000_000_000, bytes_accessed=20 * length * width, transcendentals=0
        ),
        name="attend_back",
    )(bounds, q, grads, k, v, out, log_sum, start)


def partner(x):
    width = x.shape[1]
    lane = lax.broadcasted_iota(jnp.int32, x.shape, 1)
    ahead = pltpu.roll(x, width - HEAD_DIM // 2, 1)
    behind = pltpu.roll(x, HEAD_DIM // 2, 1)
    return jnp.where(lax.rem(lane, HEAD_DIM) < HEAD_DIM // 2, ahead, behind)


def head_sums(x):
    width = x.shape[1]
    row = lax.broadcasted_iota(jnp.int32, (width, width), 0) // HEAD_DIM
    column = lax.broadcasted_iota(jnp.int32, (width, width), 1) // HEAD_DIM
    same = jnp.where(row == column, 1.0, 0.0).astype(bf16)
    high = x.astype(bf16)
    low = (x - high.astype(f32)).astype(bf16)
    return dot_nn(high, same) + dot_nn(low, same)


def widen(table, width):
    return table if table.shape[1] == width else jnp.concatenate([table] * (width // 128), axis=1)


def added(refs):
    total = refs[0][...]
    for ref in refs[1:]:
        total = total + ref[...]
    return total


def project_kernel(count, index_ref, *refs):
    wq_ref, wk_ref, wv_ref, cos_ref, sin_ref, gain_ref = refs[count : count + 6]
    q_ref, k_ref, v_ref, xq_ref, xk_ref = refs[-5:]
    x = added(refs[:count])
    width = q_ref.shape[1]
    cosine = widen(cos_ref[...], width)
    sine = widen(sin_ref[...], width)
    gain = gain_ref[...]
    for w_ref, hat_ref, turned_ref in ((wq_ref, q_ref, xq_ref), (wk_ref, k_ref, xk_ref)):
        raw = dot_nn(x, w_ref[...])
        turned = raw * cosine + partner(raw) * sine
        turned_ref[...] = turned
        hat = turned * lax.rsqrt(head_sums(turned * turned) + norm_eps) * gain
        hat_ref[...] = hat.astype(bf16)
    v_ref[...] = dot_nn(x, wv_ref[...]).astype(bf16)


def project(index, parts, weights, cosine, sine, gain, length, previous):
    rows, model = parts[0].shape
    count = len(parts)
    width = gain.shape[1]
    part = min(256, rows)
    per = rows // part

    def column(m):
        return pl.BlockSpec((model, width), lambda i, at: (0, m))

    table = pl.BlockSpec((part, 128), lambda i, at: (at[0] * per + i, 0))
    out = pl.BlockSpec((part, width), lambda i, at: (at[0] * per + i, 0))
    low = jax.ShapeDtypeStruct((length, width), bf16)
    wide = jax.ShapeDtypeStruct((length, width), f32)
    return pl.pallas_call(
        functools.partial(project_kernel, count),
        grid_spec=pltpu.PrefetchScalarGridSpec(
            num_scalar_prefetch=1,
            grid=(per,),
            in_specs=[pl.BlockSpec((part, model), lambda i, at: (i, 0))] * count
            + [
                column(0),
                column(1),
                column(2),
                table,
                table,
                pl.BlockSpec((1, width), lambda i, at: (0, 0)),
            ]
            + [pl.BlockSpec(memory_space=pl.ANY)] * len(previous),
            out_specs=[out] * 5,
        ),
        out_shape=[low, low, low, wide, wide],
        input_output_aliases={7 + count + i: i for i in range(len(previous))},
        cost_estimate=pl.CostEstimate(
            flops=6 * rows * model * width, bytes_accessed=8 * model * width, transcendentals=0
        ),
        name="project",
    )(index, *parts, weights, weights, weights, cosine, sine, gain, *previous)


def project_back_kernel(groups, index_ref, *refs):
    dq_refs, dk_refs, dv_refs = (refs[m * groups : (m + 1) * groups] for m in range(3))
    (
        xq_ref,
        xk_ref,
        wq_ref,
        wk_ref,
        wv_ref,
        cos_ref,
        sin_ref,
        gain_ref,
        grad_ref,
        gain_grad_ref,
        *piece_refs,
    ) = refs[3 * groups :]

    @pl.when(pl.program_id(0) == 0)
    def _():
        gain_grad_ref[...] = jnp.zeros_like(gain_grad_ref)

    def joined(refs):
        return jnp.concatenate([ref[...] for ref in refs], axis=1) if groups > 1 else refs[0][...]

    width = xq_ref.shape[1]
    cosine = widen(cos_ref[...], width)
    sine = widen(sin_ref[...], width)
    gain = gain_ref[...]
    lows = []
    for d_refs, x_ref in ((dq_refs, xq_ref), (dk_refs, xk_ref)):
        turned = x_ref[...]
        inverse = lax.rsqrt(head_sums(turned * turned) + norm_eps)
        unit = turned * inverse
        hat_grad = joined(d_refs) * scale_factor
        gain_grad_ref[...] += jnp.sum(hat_grad * unit, axis=0, keepdims=True)
        unit_grad = hat_grad * gain
        turned_grad = inverse * (unit_grad - unit * head_sums(unit * unit_grad))
        raw_grad = turned_grad * cosine - partner(turned_grad) * sine
        lows.append(raw_grad.astype(bf16))
    lows.append(joined(dv_refs).astype(bf16))
    piece = jnp.zeros(piece_refs[0].shape, f32)
    for m, w_ref in enumerate((wq_ref, wk_ref, wv_ref)):
        grad_ref[:, m * width : (m + 1) * width] = lows[m]
        piece = piece + dot_nt(lows[m], w_ref[...])
    low = piece.astype(bf16)
    block = pl.program_id(0) // (pl.num_programs(0) // len(piece_refs))
    for d, piece_ref in enumerate(piece_refs):

        @pl.when(block == d)
        def _(piece_ref=piece_ref):
            piece_ref[...] = low


def project_back(index, grads, turned, weights, cosine, sine, gain, rows):
    width = turned[0].shape[1]
    count = index.shape[0]
    groups = len(grads)
    model = weights.shape[0]
    part = min(256, rows)
    per = rows // part

    def column(m):
        return pl.BlockSpec((model, width), lambda i, at: (0, m))

    def turn(i, at):
        return (at[i // per] * per + i % per, 0)

    def piece_block(d):
        return pl.BlockSpec((part, model), lambda i, at: (jnp.clip(i - d * per, 0, per - 1), 0))

    tall = pl.BlockSpec((part, width), turn)
    table = pl.BlockSpec((part, 128), turn)
    return pl.pallas_call(
        functools.partial(project_back_kernel, groups),
        grid_spec=pltpu.PrefetchScalarGridSpec(
            num_scalar_prefetch=1,
            grid=(count * per,),
            in_specs=[pl.BlockSpec((part, width // groups), turn)] * (3 * groups)
            + [tall] * 2
            + [column(0), column(1), column(2), table, table]
            + [pl.BlockSpec((1, width), lambda i, at: (0, 0))],
            out_specs=[
                pl.BlockSpec((part, 3 * width), lambda i, at: (i, 0)),
                pl.BlockSpec((1, width), lambda i, at: (0, 0)),
            ]
            + [piece_block(d) for d in range(count)],
        ),
        out_shape=[
            jax.ShapeDtypeStruct((count * rows, 3 * width), bf16),
            jax.ShapeDtypeStruct((1, width), f32),
        ]
        + [jax.ShapeDtypeStruct((rows, model), bf16)] * count,
        cost_estimate=pl.CostEstimate(
            flops=rows * width, bytes_accessed=rows * width, transcendentals=0
        ),
        name="project_back",
    )(index, *[g[m] for m in range(3) for g in grads], *turned, weights, weights, weights, cosine, sine, gain)


def projection_grads_kernel(counts, *refs):
    calls = sum(1 for _ in counts)
    grads, out_ref = refs[-calls - 1 : -1], refs[-1]
    total = None
    for call, grad_ref in zip(counts, grads):
        for d, count in enumerate(call):
            hidden = added(refs[:count])
            refs = refs[count:]
            rows = hidden.shape[0]
            part = dot_tn(hidden, grad_ref[d * rows : (d + 1) * rows, :])
            total = part if total is None else total + part
    out_ref[...] = total.astype(bf16)


def projection_grads(hidden, grads):
    rows, model = hidden[0][0][0].shape
    width = grads[0].shape[1]
    length = sum(g.shape[0] for g in grads)
    counts = tuple(tuple(len(parts) for parts in call) for call in hidden)
    part = 256
    return pl.pallas_call(
        functools.partial(projection_grads_kernel, counts),
        grid=(model // part,),
        in_specs=[pl.BlockSpec((rows, part), lambda i: (0, i))] * sum(sum(c) for c in counts)
        + [pl.BlockSpec(g.shape, lambda i: (0, 0)) for g in grads],
        out_specs=pl.BlockSpec((part, width), lambda i: (i, 0)),
        out_shape=jax.ShapeDtypeStruct((model, width), bf16),
        cost_estimate=pl.CostEstimate(
            flops=2 * length * model * width,
            bytes_accessed=8 * length * model,
            transcendentals=0,
        ),
        name="projection_grads",
    )(*[x for call in hidden for parts in call for x in parts], *grads)


def out_grads_kernel(count, *refs):
    attended = refs[:count]
    branch_ref, out_ref = refs[count:]
    width = attended[0].shape[1]
    turned = branch_ref[...].T
    for d in range(count):
        out_ref[:, d * width : (d + 1) * width] = dot_nn(turned, attended[d][...]).astype(bf16)


def out_grads(attended, branch_grad):
    count = len(attended)
    rows, model = branch_grad.shape
    width = attended[0].shape[1]
    part = 256
    return pl.pallas_call(
        functools.partial(out_grads_kernel, count),
        grid=(model // part,),
        in_specs=[pl.BlockSpec(x.shape, lambda i: (0, 0)) for x in attended]
        + [pl.BlockSpec((rows, part), lambda i: (0, i))],
        out_specs=pl.BlockSpec((part, count * width), lambda i: (i, 0)),
        out_shape=jax.ShapeDtypeStruct((model, count * width), bf16),
        cost_estimate=pl.CostEstimate(
            flops=2 * rows * count * model * width,
            bytes_accessed=4 * rows * count * model,
            transcendentals=0,
        ),
        name="out_grads",
    )(*attended, branch_grad)


def rms_scale(x):
    return lax.rsqrt(jnp.mean(x * x, axis=-1, keepdims=True) + norm_eps)


def mix_kernel(count, *refs):
    pieces, weights = refs[:count], refs[count : 2 * count]
    hidden_ref, rates_ref, branch_ref, middle_ref, low_ref, turned_ref, out_ref = refs[2 * count :]
    branch = dot_nt(pieces[0][...], block_of(weights[0]))
    for d in range(1, count):
        branch = branch + dot_nt(pieces[d][...], block_of(weights[d]))

    @pl.when(pl.program_id(0) == 0)
    def _():
        width = pieces[0].shape[1]
        for d in range(count):
            out_ref[:, d * width : (d + 1) * width] = block_of(weights[d])

    branch_ref[...] = branch
    hidden = hidden_ref[...].astype(f32)
    mixed = hidden + rates_ref[0:1, :] * (branch * rms_scale(branch) - hidden)
    middle = mixed * rms_scale(mixed)
    middle_ref[...] = middle
    low_ref[...] = middle.astype(bf16)
    turned_ref[...] = middle.T.astype(bf16)


def mix(pieces, weights, hidden, rates):
    count = len(pieces)
    rows, model = hidden.shape
    width = pieces[0].shape[1]
    part = min(128, rows)

    nd, blocks, shard, local_width = weights.shape
    per = local_width // width
    first = blocks - count // per

    def column(d):
        return pl.BlockSpec((nd, 1, shard, width), lambda i: (0, first + d // per, 0, d % per))

    wide = pl.BlockSpec((part, model), lambda i: (i, 0))
    return pl.pallas_call(
        functools.partial(mix_kernel, count),
        grid=(rows // part,),
        in_specs=[pl.BlockSpec((part, width), lambda i: (i, 0))] * count
        + [column(d) for d in range(count)]
        + [wide, pl.BlockSpec((2, model), lambda i: (0, 0))],
        out_specs=[wide, wide, wide, pl.BlockSpec((model, part), lambda i: (0, i))]
        + [pl.BlockSpec((model, count * width), lambda i: (0, 0))],
        out_shape=[
            jax.ShapeDtypeStruct((rows, model), f32),
            jax.ShapeDtypeStruct((rows, model), f32),
            jax.ShapeDtypeStruct((rows, model), bf16),
            jax.ShapeDtypeStruct((model, rows), bf16),
            jax.ShapeDtypeStruct((model, count * width), bf16),
        ],
        cost_estimate=pl.CostEstimate(
            flops=2 * rows * model * model, bytes_accessed=14 * rows * model, transcendentals=0
        ),
        name="mix",
    )(*pieces, *([weights] * count), hidden, rates)


def block_of(w_ref):
    value = w_ref[:, 0]
    return value.reshape(value.shape[0] * value.shape[1], value.shape[2])


def feed_kernel(
    m_ref,
    wu_ref,
    wg_ref,
    wd_ref,
    s_ref,
    middle_ref,
    cot_ref,
    live_ref,
    rates_ref,
    up_ref,
    gate_ref,
    h_ref,
    result_ref,
    direct_ref,
    low_ref,
    turned_ref,
    rate_ref,
    acc,
):
    i = pl.program_id(0)
    tokens = m_ref[...]
    up = dot_nn(tokens, block_of(wu_ref))
    gate = dot_nn(tokens, block_of(wg_ref))
    up_ref[...] = up
    gate_ref[...] = gate
    scaled = gate * s_ref[1:2, :]
    hidden = (up * s_ref[0:1, :] * (scaled * jax.nn.sigmoid(scaled))).astype(bf16)
    h_ref[...] = hidden
    part_out = dot_nt(hidden, block_of(wd_ref))

    @pl.when(i == 0)
    def _():
        acc[...] = part_out

    @pl.when(i > 0)
    def _():
        acc[...] += part_out

    @pl.when(i == pl.num_programs(0) - 1)
    def _():
        rate_ref[...] = jnp.zeros_like(rate_ref)
        rate = rates_ref[1:2, :]
        part = min(128, acc.shape[0])

        def body(at, carry):
            rows = pl.ds(pl.multiple_of(at * part, part), part)
            out = acc[rows, :]
            middle = middle_ref[rows, :]
            out_scale = rms_scale(out)
            unit = out * out_scale
            mixed = middle + rate * (unit - middle)
            scale = rms_scale(mixed)
            final = mixed * scale
            result_ref[rows, :] = final.astype(bf16)
            grad = cot_ref[rows, :].astype(f32) * live_ref[rows, :]
            mixed_grad = scale * (grad - final * jnp.mean(final * grad, axis=-1, keepdims=True))
            direct_ref[rows, :] = mixed_grad * (1.0 - rate)
            rate_ref[...] += jnp.sum(mixed_grad * (unit - middle), axis=0, keepdims=True)
            unit_grad = mixed_grad * rate
            out_grad = out_scale * (
                unit_grad - unit * jnp.mean(unit * unit_grad, axis=-1, keepdims=True)
            )
            low_ref[rows, :] = out_grad.astype(bf16)
            return carry

        lax.fori_loop(0, acc.shape[0] // part, body, 0)
        for at in range(acc.shape[0] // 128):
            rows = slice(at * 128, (at + 1) * 128)
            turned_ref[:, rows] = low_ref[rows, :].T


def weight_specs(weights, step, total, base=0):
    nd, _, shard, local_width = weights.shape
    per = local_width // step

    def spec(m):
        def place(i):
            p = (i + base) // per
            return (0, 2 * p + m if m < 2 else 2 * (total // local_width) + p, 0, (i + base) % per)

        return pl.BlockSpec((nd, 1, shard, step), place)

    return [spec(0), spec(1), spec(2)]


def feed(low, weights, scales, middle, cotangent, live, rates, step):
    rows, model = low.shape
    total = scales.shape[1]
    columns = pl.BlockSpec((rows, step), lambda i: (0, i))
    whole = pl.BlockSpec((rows, model), lambda i: (0, 0))
    return pl.pallas_call(
        feed_kernel,
        grid=(total // step,),
        in_specs=[whole]
        + weight_specs(weights, step, total)
        + [
            pl.BlockSpec((2, step), lambda i: (0, i)),
            whole,
            whole,
            pl.BlockSpec((rows, 1), lambda i: (0, 0)),
            pl.BlockSpec((2, model), lambda i: (0, 0)),
        ],
        out_specs=[columns, columns, columns, whole, whole, whole]
        + [
            pl.BlockSpec((model, rows), lambda i: (0, 0)),
            pl.BlockSpec((1, model), lambda i: (0, 0)),
        ],
        out_shape=[
            jax.ShapeDtypeStruct((rows, total), f32),
            jax.ShapeDtypeStruct((rows, total), f32),
            jax.ShapeDtypeStruct((rows, total), bf16),
            jax.ShapeDtypeStruct((rows, model), bf16),
            jax.ShapeDtypeStruct((rows, model), f32),
            jax.ShapeDtypeStruct((rows, model), bf16),
            jax.ShapeDtypeStruct((model, rows), bf16),
            jax.ShapeDtypeStruct((1, model), f32),
        ],
        scratch_shapes=[pltpu.VMEM((rows, model), f32)],
        cost_estimate=pl.CostEstimate(
            flops=6 * rows * model * total,
            bytes_accessed=6 * model * total + 10 * rows * total,
            transcendentals=0,
        ),
        name="feed",
    )(low, weights, weights, weights, scales, middle, cotangent, live, rates)


def feed_back_step(
    og_ref, ogt_ref, mt_ref, wu_ref, wg_ref, wd_ref, s_ref, up_ref, gate_ref, h_ref, start_ref, grad_ref, sg_ref, acc
):
    i = pl.program_id(0)
    grad_ref[2] = dot_nn(ogt_ref[...], h_ref[...]).astype(bf16)
    hidden_grad = dot_nn(og_ref[...], block_of(wd_ref))
    up = up_ref[...]
    gate = gate_ref[...]
    up_gain = s_ref[0:1, :]
    gate_gain = s_ref[1:2, :]
    scaled = gate * gate_gain
    sig = jax.nn.sigmoid(scaled)
    up_part = hidden_grad * (scaled * sig)
    gate_part = hidden_grad * (up * up_gain) * (sig * (1.0 + scaled * (1.0 - sig)))
    sg_ref[0:1, :] = jnp.sum(up_part * up, axis=0, keepdims=True)
    sg_ref[1:2, :] = jnp.sum(gate_part * gate, axis=0, keepdims=True)
    up_low = (up_part * up_gain).astype(bf16)
    gate_low = (gate_part * gate_gain).astype(bf16)
    tokens_t = mt_ref[...]
    grad_ref[0] = dot_nn(tokens_t, up_low).astype(bf16)
    grad_ref[1] = dot_nn(tokens_t, gate_low).astype(bf16)
    back = dot_nt(up_low, block_of(wu_ref)) + dot_nt(gate_low, block_of(wg_ref))

    @pl.when(i == 0)
    def _():
        acc[...] = start_ref[...] + back

    @pl.when(i > 0)
    def _():
        acc[...] += back


def feed_back_first_kernel(*refs):
    feed_back_step(*refs)


def feed_back_last_kernel(*refs):
    branch_ref, hidden_ref, rates_ref = refs[11:14]
    grad_ref, sg_ref, token_ref, low_ref, rate_ref, acc = refs[14:]
    feed_back_step(*refs[:11], grad_ref, sg_ref, acc)

    @pl.when(pl.program_id(0) == pl.num_programs(0) - 1)
    def _():
        rate_ref[...] = jnp.zeros_like(rate_ref)
        rate = rates_ref[0:1, :]
        part = min(128, acc.shape[0])

        def body(at, carry):
            rows = pl.ds(pl.multiple_of(at * part, part), part)
            grad = acc[rows, :]
            branch = branch_ref[rows, :]
            hidden = hidden_ref[rows, :].astype(f32)
            branch_scale = rms_scale(branch)
            unit = branch * branch_scale
            mixed = hidden + rate * (unit - hidden)
            scale = rms_scale(mixed)
            middle = mixed * scale
            mixed_grad = scale * (grad - middle * jnp.mean(middle * grad, axis=-1, keepdims=True))
            token_ref[rows, :] = mixed_grad * (1.0 - rate)
            rate_ref[...] += jnp.sum(mixed_grad * (unit - hidden), axis=0, keepdims=True)
            unit_grad = mixed_grad * rate
            branch_grad = branch_scale * (
                unit_grad - unit * jnp.mean(unit * unit_grad, axis=-1, keepdims=True)
            )
            low_ref[rows, :] = branch_grad.astype(bf16)
            return carry

        lax.fori_loop(0, acc.shape[0] // part, body, 0)


def feed_back(
    out_grad, out_grad_t, middle_t, weights, scales, up, gate, hidden_units, start, mixing, step, base, count
):
    model, rows = middle_t.shape
    width = count * step
    columns = pl.BlockSpec((rows, step), lambda i: (0, i + base))
    whole = pl.BlockSpec((rows, model), lambda i: (0, 0))
    turned = pl.BlockSpec((model, rows), lambda i: (0, 0))
    wide = jax.ShapeDtypeStruct((rows, model), f32)
    grads_specs = [
        pl.BlockSpec((3, model, step), lambda i: (0, 0, i)),
        pl.BlockSpec((2, step), lambda i: (0, i)),
    ]
    grads_shapes = [
        jax.ShapeDtypeStruct((3, model, width), bf16),
        jax.ShapeDtypeStruct((2, width), f32),
    ]
    last = bool(mixing)
    return pl.pallas_call(
        feed_back_last_kernel if last else feed_back_first_kernel,
        grid=(count,),
        in_specs=[whole, turned, turned]
        + weight_specs(weights, step, scales.shape[1], base)
        + [pl.BlockSpec((2, step), lambda i: (0, i + base)), columns, columns, columns, whole]
        + ([whole, whole, pl.BlockSpec((2, model), lambda i: (0, 0))] if last else []),
        out_specs=grads_specs
        + ([whole, whole, pl.BlockSpec((1, model), lambda i: (0, 0))] if last else [whole]),
        out_shape=grads_shapes
        + (
            [
                wide,
                jax.ShapeDtypeStruct((rows, model), bf16),
                jax.ShapeDtypeStruct((1, model), f32),
            ]
            if last
            else [wide]
        ),
        scratch_shapes=[pltpu.VMEM((rows, model), f32)] if last else [],
        cost_estimate=pl.CostEstimate(
            flops=12 * rows * model * width,
            bytes_accessed=12 * model * width + 10 * rows * width,
            transcendentals=0,
        ),
        name="feed_back_last" if last else "feed_back_first",
    )(
        out_grad,
        out_grad_t,
        middle_t,
        weights,
        weights,
        weights,
        scales,
        up,
        gate,
        hidden_units,
        start,
        *mixing,
    )


def shift(value, axis, distance, size):
    return lax.ppermute(value, axis, [(i, (i + distance) % size) for i in range(size)])


def carry_on(up, down, hop, axis, size):
    up = lax.ppermute(up, axis, [(i, i + 1) for i in range(hop - 1, size - 1)])
    down = lax.ppermute(down, axis, [(i, i - 1) for i in range(1, size - hop + 1)])
    return up, down


def line_sum(pieces, hop, up, down, axis, size):
    ahead, behind = pieces[size - hop], pieces[hop]
    ahead = ahead if up is None else ahead + up
    behind = behind if down is None else behind + down
    up = lax.ppermute(ahead, axis, [(i, i + 1) for i in range(hop)])
    down = lax.ppermute(behind, axis, [(i, i - 1) for i in range(size - hop, size)])
    return up, down


def halving(value, axis, size, step):
    lead, (count, rows, width) = value.shape[:-3], value.shape[-3:]
    bit = (lax.axis_index(axis) // step) % 2
    pairs = value.reshape(lead + (count // 2, 2, rows, width))
    sent = lax.dynamic_index_in_dim(pairs, 1 - bit, len(lead) + 1, False)
    kept = lax.dynamic_index_in_dim(pairs, bit, len(lead) + 1, False)
    other = lax.ppermute(sent, axis, [(i, i ^ step) for i in range(size)])
    value = kept.astype(f32) + other.astype(f32)
    return value.reshape(lead + (rows, width)) if 2 * step == size else value.astype(bf16)


def exchange_add(value, axis, size, step):
    return value + lax.ppermute(value, axis, [(i, i ^ step) for i in range(size)])


def doublings(size):
    return [1 << k for k in range(size.bit_length() - 1)]


def butterfly(value, axis, size):
    for step in doublings(size):
        value = exchange_add(value, axis, size, step)
    return value


def take_block(value, index, size, axis):
    return lax.dynamic_slice_in_dim(value, index * size, size, axis)


def put_block(whole, value, index, axis):
    return lax.dynamic_update_slice_in_dim(whole, value, index * value.shape[axis], axis)


def local(
    nd,
    nt,
    hidden_in,
    cotangent,
    segments,
    attn_weight,
    mlp_weight,
    rates,
    qk_scale,
    mlp_scales,
    attn_moment_one,
    attn_moment_two,
    mlp_moment_one,
    mlp_moment_two,
):
    rows, model = hidden_in.shape
    length = segments.shape[0]
    shard = attn_weight.shape[1]
    heads_width = attn_weight.shape[2]
    hidden_width = mlp_weight.shape[2]
    block = min(512, length)
    step = min(512, hidden_width)
    me = lax.axis_index("tensor")

    def gather(value):
        return [value] + [shift(value, "tensor", d, nt) for d in range(1, nt)]

    def both(ups, downs, d):
        return (ups[0],) if d == 0 else (ups[d], downs[nt - d])

    middle_hop = nt // 2
    order = [d for d in range(nt) if d != middle_hop] + [middle_hop]
    attn_low = attn_weight.astype(bf16)
    qkv_full = lax.all_gather(
        jnp.concatenate([attn_low[0], attn_low[1], attn_low[2]], axis=1), "dp", axis=0, tiled=True
    )
    mlp_low = mlp_weight.astype(bf16)
    chunks = [
        mlp_low[:2].reshape(2 * shard, hidden_width),
        jnp.concatenate([mlp_low[2], attn_low[3].reshape(-1, hidden_width)], axis=0),
    ]
    lines = [([chunk], [chunk]) for chunk in chunks]
    for hop in range(1, nt):
        for c, (ups, downs) in enumerate(lines):
            if hop == nt - 1 and c == 1:
                ups[-1], downs[-1], hidden_in = lax.optimization_barrier(
                    (ups[-1], downs[-1], hidden_in)
                )
            up, down = carry_on(ups[-1], downs[-1], hop, "tensor", nt)
            ups.append(up)
            downs.append(down)
    wide_blocks, low_blocks = [
        [sum(both(ups, downs, d)) for d in range(nt)] for ups, downs in lines
    ]
    out_low = jnp.concatenate(
        [low[shard:].reshape(shard, heads_width) for low in low_blocks], axis=1
    )
    mlp_full = lax.all_gather(
        jnp.concatenate(
            [wide_blocks[d] for d in order]
            + [low_blocks[d][:shard] for d in order]
            + [
                out_low[:, at : at + hidden_width]
                for at in range(0, nt * heads_width, hidden_width)
            ],
            axis=0,
        ),
        "dp",
        axis=0,
        tiled=True,
    )
    mlp_full = mlp_full.reshape(nd, -1, shard, hidden_width)
    scales_parts = gather(mlp_scales)
    scales_row = jnp.concatenate([scales_parts[d] for d in order], axis=1)

    starts = starts_of(segments)
    positions = (jnp.arange(length, dtype=jnp.int32) - starts).astype(f32)
    lane = jnp.arange(128, dtype=jnp.int32)
    half = HEAD_DIM // 2
    frequency = 10000.0 ** (-(lane % half).astype(f32) / half)
    sign = jnp.where(lane % HEAD_DIM < half, -1.0, 1.0)
    angles = positions[:, None] * frequency[None, :]
    cosine = jnp.cos(angles)
    sine = jnp.sin(angles) * sign[None, :]
    gain = qk_scale.reshape(1, heads_width)

    ups, downs, state = [hidden_in], [hidden_in], ()
    hidden_parts = [None] * nt

    def projected(hop, state):
        for d in range(nt):
            if (max(d, nt - d) if d else 0) == hop:
                hidden_parts[d] = both(ups, downs, d)
                index = ((me + nt - d) % nt).reshape(1)
                state = project(index, hidden_parts[d], qkv_full, cosine, sine, gain, length, state)
        return state

    for hop in range(1, nt):
        ups[-1], downs[-1], state = lax.optimization_barrier((ups[-1], downs[-1], state))
        up, down = carry_on(ups[-1], downs[-1], hop, "tensor", nt)
        ups.append(up)
        downs.append(down)
        state = projected(hop - 1, state)
    ups[-1], downs[-1], state = lax.optimization_barrier((ups[-1], downs[-1], state))
    state = projected(nt - 1, state)
    query_hat, key_hat, value_hat, query_turned, key_turned = state
    bounds = key_bounds(starts, block)
    attended_row, attended_f32, log_sum = attend(
        bounds, query_hat, key_hat, value_hat, starts[:, None], block
    )
    attended = [take_block(attended_row, me, rows, 0)] + [
        shift(take_block(attended_row, (me + d) % nt, rows, 0), "tensor", d, nt)
        for d in range(1, nt)
    ]
    branch, middle, middle_low, middle_t, out_full = mix(attended, mlp_full, hidden_in, rates)
    row_segments = take_block(segments, me, rows, 0)
    live = (row_segments < pad_segment).astype(f32)[:, None]
    up, gate, hidden_units, result, middle_direct, mlp_out_low, mlp_out_t, rate_mlp_grad = feed(
        middle_low, mlp_full, scales_row, middle, cotangent, live, rates, step
    )
    def spread(value, places):
        width = value.shape[1] // nt
        whole = jnp.zeros_like(value)
        for p, d in enumerate(places):
            piece = value[:, p * width : (p + 1) * width]
            whole = put_block(whole, piece, (me + nt - d) % nt, 1)
        return whole

    def blocks_of(part, axis, width):
        return [
            lax.slice_in_dim(part, at, at + width, axis=axis)
            for at in range(0, part.shape[axis], width)
        ]

    def to_owners(pieces, places):
        return [shift(piece, "tensor", -d, nt) if d else piece for d, piece in zip(places, pieces)]

    per = hidden_width // step
    near = (nt - 1) * per
    feed_args = (mlp_out_low, mlp_out_t, middle_t, mlp_full, scales_row, up, gate, hidden_units)
    far_grad, far_scales, partial = feed_back(*feed_args, middle_direct, (), step, near, per)
    halvings = doublings(nd)
    far_part = lax.psum_scatter(far_grad, "dp", scatter_dimension=1, tiled=True)
    near_grad, near_scales, token_direct, branch_low, rate_attn_grad = feed_back(
        *feed_args, partial, (branch, hidden_in, rates), step, 0, near
    )
    near_part = lax.psum_scatter(near_grad, "dp", scatter_dimension=1, tiled=True)

    grad_pieces = []
    for d in list(range(1, nt)) + [0]:
        piece = dot_nn(branch_low, out_full[:, d * heads_width : (d + 1) * heads_width])
        piece = piece.astype(bf16)
        grad_pieces.append((d, shift(piece, "tensor", -d, nt) if d else piece))
    grad_row = jnp.zeros((length, heads_width), bf16)
    for d, piece in grad_pieces[-1:] + grad_pieces[:-1]:
        grad_row = put_block(grad_row, piece, (me + d) % nt, 0)
    out_sum = out_grads(attended, branch_low).reshape(nd, shard, -1)
    out_sum = halving(out_sum, "dp", nd, halvings[0])

    scales_grad = spread(jnp.concatenate([near_scales, far_scales], axis=1), order)
    small = jnp.concatenate(
        [rate_attn_grad, rate_mlp_grad, scales_grad.reshape(-1, model)], axis=0
    )
    steps = [("tensor", nt, k) for k in doublings(nt)] + [("dp", nd, k) for k in doublings(nd)]

    def advance(small):
        return exchange_add(small, *steps.pop(0)) if steps else small

    far_part, grad_row, out_sum, small = lax.optimization_barrier(
        (far_part, grad_row, out_sum, small)
    )
    small = advance(small)
    out_sum = halving(out_sum, "dp", nd, halvings[1])
    head_group = max(128, heads_width // 2)
    head_grads = []
    for group in range(heads_width // head_group):
        if group == 1:
            head_grads, grad_row, far_part, small, out_sum = lax.optimization_barrier(
                (head_grads, grad_row, far_part, small, out_sum)
            )
            small = advance(small)
            out_sum = halving(out_sum, "dp", nd, halvings[2])
        head_grads.append(
            attend_back(
                bounds,
                query_hat,
                key_hat,
                value_hat,
                grad_row,
                attended_f32,
                log_sum,
                starts[None, :],
                block,
                group,
                head_group,
            )
        )
    far_first = shift(far_part[:2], "tensor", -middle_hop, nt)
    far_last = far_part[2:]
    head_grads, small, out_sum, far_first, far_last = lax.optimization_barrier(
        (head_grads, small, out_sum, far_first, far_last)
    )
    far_last = shift(far_last, "tensor", -middle_hop, nt)
    small = advance(small)
    for k in halvings[2 if len(head_grads) == 1 else 3 :]:
        out_sum = halving(out_sum, "dp", nd, k)
    out_pieces = to_owners(blocks_of(out_sum.astype(bf16), 1, heads_width), range(nt))
    places = [[nt - 1, 1], [d for d in range(nt) if d not in (nt - 1, 1)]]
    pieces, qkv_grads, gain_grads = [None] * nt, [], []

    def back(call):
        grad, gain_grad, *results = project_back(
            jnp.stack([(me + d) % nt for d in call]),
            head_grads,
            (query_turned, key_turned),
            qkv_full,
            cosine,
            sine,
            gain,
            rows,
        )
        qkv_grads.append(grad)
        gain_grads.append(gain_grad)
        for d, piece in zip(call, results):
            pieces[d] = piece

    back(places[0])
    pieces[1], pieces[nt - 1], small, out_pieces, far_last, head_grads = lax.optimization_barrier(
        (pieces[1], pieces[nt - 1], small, out_pieces, far_last, head_grads)
    )
    far_part = jnp.concatenate([far_first, far_last], axis=0)
    ahead, behind = line_sum(pieces, 1, None, None, "tensor", nt)
    back(places[1])
    gain_grad = sum(gain_grads)
    hidden_turn = [[hidden_parts[(nt - d) % nt] for d in call] for call in places]
    qkv_sum = projection_grads(hidden_turn, qkv_grads).reshape(nd, shard, -1)
    for hop in range(2, nt):
        if hop == 2:
            ahead, behind, qkv_sum, gain_grad = lax.optimization_barrier(
                (ahead, behind, qkv_sum, gain_grad)
            )
            gain_parts = gather(gain_grad)
        if hop == max(2, nt - 1):
            ahead, behind, near_part, qkv_sum, gain_parts = lax.optimization_barrier(
                (ahead, behind, near_part, qkv_sum, gain_parts)
            )
            near_pieces = blocks_of(near_part, 2, hidden_width)
            near_pieces, qkv_sum, small = lax.optimization_barrier((near_pieces, qkv_sum, small))
            near_pieces = to_owners(near_pieces, order[:-1])
        ahead, behind = line_sum(pieces, hop, ahead, behind, "tensor", nt)
        if hop == 2:
            for k in halvings[:2]:
                qkv_sum = halving(qkv_sum, "dp", nd, k)
    for k in halvings[2:]:
        qkv_sum = halving(qkv_sum, "dp", nd, k)
    gain_row = spread(jnp.concatenate(gain_parts, axis=1), range(nt))
    while steps:
        small = advance(small)
    out_own = sum(piece.astype(f32) for piece in out_pieces)
    attn_weight_grad = jnp.stack(
        [qkv_sum[:, m * heads_width : (m + 1) * heads_width] for m in range(3)] + [out_own]
    )
    attn_one, attn_two, attn_moved = adam_moved(
        attn_weight, attn_weight_grad, attn_moment_one, attn_moment_two
    )
    attn_square = jnp.sum(attn_moved * attn_moved, axis=1, keepdims=True)
    last = jnp.concatenate([attn_square.reshape(1, -1), gain_row], axis=1)
    last = butterfly(last, "dp", nd)
    near_pieces, last, small = lax.optimization_barrier((near_pieces, last, small))
    rates_grad = small[:2]
    mlp_scales_grad = small[2:].reshape(2, nt * hidden_width)

    attn_square = last[:, : 4 * heads_width].reshape(4, 1, heads_width)
    gain_row = last[:, 4 * heads_width :].reshape(-1)
    attn_new = attn_moved * lax.rsqrt(attn_square + norm_eps)

    mlp_weight_grad = sum(piece.astype(f32) for piece in near_pieces + [far_part])
    mlp_one, mlp_two, mlp_moved = adam_moved(
        mlp_weight, mlp_weight_grad, mlp_moment_one, mlp_moment_two
    )
    mlp_square = jnp.sum(mlp_moved * mlp_moved, axis=1, keepdims=True)
    mlp_square = butterfly(mlp_square.reshape(1, -1), "dp", nd).reshape(mlp_square.shape)
    mlp_square, ahead, behind = lax.optimization_barrier((mlp_square, ahead, behind))
    total = token_direct + pieces[0].astype(f32)
    input_grad = (total + ahead.astype(f32) + behind.astype(f32)).astype(bf16)
    mlp_new = mlp_moved * lax.rsqrt(mlp_square + norm_eps)
    return (
        result.astype(bf16),
        input_grad,
        attn_weight_grad,
        mlp_weight_grad,
        rates_grad,
        gain_row,
        mlp_scales_grad,
        attn_one,
        attn_two,
        mlp_one,
        mlp_two,
        attn_new,
        mlp_new,
    )


def solution(mesh):
    weights = P(None, "dp", "tensor")
    tokens = P(("dp", "tensor"), None)
    return jax.shard_map(
        functools.partial(local, mesh.shape["dp"], mesh.shape["tensor"]),
        mesh=mesh,
        in_specs=(
            tokens,
            tokens,
            P("dp"),
            weights,
            weights,
            P(),
            P("tensor"),
            P(None, "tensor"),
            weights,
            weights,
            weights,
            weights,
        ),
        out_specs=(
            tokens,
            tokens,
            weights,
            weights,
            P(),
            P(),
            P(),
            weights,
            weights,
            weights,
            weights,
            weights,
            weights,
        ),
        check_vma=False,
    )
```

```python
import functools
import math

import jax
import jax.numpy as jnp
from jax import lax
from jax.experimental import pallas as pl
from jax.experimental.pallas import tpu as pltpu
from jax.sharding import PartitionSpec as P

HEAD_DIM = 64
LOG2E = 1.4426950408889634

norm_eps = 1e-06
pad_segment = 63
beta_one = 0.9
beta_two = 0.95
learning_rate = 0.01
adam_eps = 1e-08
bias_one = 1.0 - 0.9**10
bias_two = 1.0 - 0.95**10
scale_factor = math.sqrt(HEAD_DIM)
f32 = jnp.float32
bf16 = jnp.bfloat16


def starts_of(segment_row):
    indices = jnp.arange(segment_row.shape[0], dtype=jnp.int32)
    changed = jnp.concatenate(
        [jnp.ones((1,), dtype=jnp.bool_), segment_row[1:] != segment_row[:-1]]
    )
    return lax.cummax(jnp.where(changed, indices, jnp.zeros_like(indices)), axis=0)


def adam_moved(weight, gradient, moment_one, moment_two):
    moment_one_new = beta_one * moment_one + (1.0 - beta_one) * gradient
    moment_two_new = beta_two * moment_two + (1.0 - beta_two) * gradient * gradient
    moved = weight - learning_rate * (moment_one_new / bias_one) / (
        jnp.sqrt(moment_two_new / bias_two) + adam_eps
    )
    return (moment_one_new, moment_two_new, moved)


def dot_nt(a, b):
    return lax.dot_general(a, b, (((1,), (1,)), ((), ())), preferred_element_type=f32)


def dot_nn(a, b):
    return lax.dot_general(a, b, (((1,), (0,)), ((), ())), preferred_element_type=f32)


def dot_tn(a, b):
    return lax.dot_general(a, b, (((0,), (0,)), ((), ())), preferred_element_type=f32)


def head_stack(x, heads):
    lane = lax.broadcasted_iota(jnp.int32, x.shape, 1) // HEAD_DIM
    zero = jnp.zeros_like(x)
    return jnp.concatenate([jnp.where(lane == h, x, zero) for h in range(heads)], axis=0)


def head_pick(stacked, heads, rows):
    width = stacked.shape[1]
    lane = lax.broadcasted_iota(jnp.int32, (rows, width), 1) // HEAD_DIM
    picked = jnp.zeros((rows, width), f32)
    for h in range(heads):
        picked = jnp.where(lane == h, stacked[h * rows : (h + 1) * rows], picked)
    return picked


def attend_kernel(heads, bq, bk, bounds_ref, q_ref, k_ref, v_ref, start_ref, o_ref, of_ref, l_ref, acc, lsum):
    i = pl.program_id(0)
    qs = head_stack(q_ref[...], heads)
    acc[...] = jnp.zeros_like(acc)
    lsum[...] = jnp.zeros_like(lsum)
    start = jnp.concatenate([start_ref[...]] * heads, axis=0)

    def step(j, masked, diagonal):
        offset = pl.multiple_of(j * bk, bk)
        keys = k_ref[pl.ds(offset, bk), :]
        values = v_ref[pl.ds(offset, bk), :]
        scores = dot_nt(qs, keys)
        weights = jnp.exp2(scores * (scale_factor * LOG2E))
        if masked:
            key_index = offset + lax.broadcasted_iota(jnp.int32, scores.shape, 1)
            allowed = key_index >= start
            if diagonal:
                row = lax.rem(lax.broadcasted_iota(jnp.int32, scores.shape, 0), bq)
                allowed = allowed & (key_index <= i * bq + row)
            weights = jnp.where(allowed, weights, 0.0)
        total = weights[:, :128]
        for part in range(1, bk // 128):
            total = total + weights[:, part * 128 : (part + 1) * 128]
        lsum[...] += total
        acc[...] += dot_nn(weights.astype(bf16), values)

    def body(masked, j, carry):
        step(j, masked, False)
        return carry

    inside = bounds_ref[1, i]
    lax.fori_loop(bounds_ref[0, i], inside, functools.partial(body, True), 0)
    lax.fori_loop(inside, i, functools.partial(body, False), 0)
    step(i, True, True)
    summed = jnp.sum(lsum[...], axis=1, keepdims=True)
    out = head_pick(acc[...] * (1.0 / summed), heads, bq)
    of_ref[...] = out
    o_ref[...] = out.astype(bf16)
    l_ref[...] = jnp.log2(summed).reshape(heads, bq)


def key_bounds(starts, block):
    blocks = jnp.arange(starts.shape[0] // block, dtype=jnp.int32)
    first = starts[::block] // block
    inside = (starts[block - 1 :: block] + (block - 1)) // block
    return jnp.stack([first, jnp.clip(inside, first, blocks)])


def attend(bounds, q, k, v, start, block):
    length, width = q.shape
    heads = width // HEAD_DIM
    whole = pl.BlockSpec((length, width), lambda i: (0, 0))
    rows = pl.BlockSpec((block, width), lambda i: (i, 0))
    return pl.pallas_call(
        functools.partial(attend_kernel, heads, block, block),
        grid=(length // block,),
        in_specs=[pl.BlockSpec(memory_space=pltpu.SMEM), rows, whole, whole]
        + [pl.BlockSpec((block, 1), lambda i: (i, 0))],
        out_specs=[rows, rows, pl.BlockSpec((heads, block), lambda i: (0, i))],
        out_shape=[
            jax.ShapeDtypeStruct((length, width), bf16),
            jax.ShapeDtypeStruct((length, width), f32),
            jax.ShapeDtypeStruct((heads, length), f32),
        ],
        scratch_shapes=[
            pltpu.VMEM((heads * block, width), f32),
            pltpu.VMEM((heads * block, 128), f32),
        ],
        cost_estimate=pl.CostEstimate(
            flops=20_000_000_000, bytes_accessed=8 * length * width, transcendentals=0
        ),
        name="attend",
    )(bounds, q, k, v, start)


def attend_back_kernel(
    first, heads, bq, bk, bounds_ref, q_ref, do_ref, k_ref, v_ref, of_ref, l_ref, start_ref, dq_ref, dk_ref, dv_ref, acc
):
    i = pl.program_id(0)

    @pl.when(i == 0)
    def _():
        dk_ref[...] = jnp.zeros_like(dk_ref)
        dv_ref[...] = jnp.zeros_like(dv_ref)

    qs = head_stack(q_ref[...], heads)
    grads = do_ref[...]
    dos = head_stack(grads, heads)
    product = (grads.astype(f32) * of_ref[...]).T
    delta = jnp.concatenate(
        [
            jnp.sum(product[h * HEAD_DIM : (h + 1) * HEAD_DIM], axis=0, keepdims=True)
            for h in range(heads)
        ],
        axis=1,
    )
    log_sum = jnp.concatenate([l_ref[first + h : first + h + 1, :] for h in range(heads)], axis=1)
    start = jnp.concatenate([start_ref[...]] * heads, axis=1)
    acc[...] = jnp.zeros_like(acc)

    def step(j, masked, diagonal):
        offset = pl.multiple_of(j * bk, bk)
        keys = k_ref[pl.ds(offset, bk), :]
        values = v_ref[pl.ds(offset, bk), :]
        scores = dot_nt(keys, qs)
        probs = jnp.exp2(scores * (scale_factor * LOG2E) - log_sum)
        if masked:
            key_index = offset + lax.broadcasted_iota(jnp.int32, scores.shape, 0)
            allowed = key_index >= start
            if diagonal:
                column = lax.rem(lax.broadcasted_iota(jnp.int32, scores.shape, 1), bq)
                allowed = allowed & (key_index <= i * bq + column)
            probs = jnp.where(allowed, probs, 0.0)
        prob_grad = dot_nt(values, dos)
        score_grad = (probs * (prob_grad - delta)).astype(bf16)
        dv_ref[pl.ds(offset, bk), :] += dot_nn(probs.astype(bf16), dos)
        dk_ref[pl.ds(offset, bk), :] += dot_nn(score_grad, qs)
        acc[...] += dot_tn(score_grad, keys)

    def body(masked, j, carry):
        step(j, masked, False)
        return carry

    inside = bounds_ref[1, i]
    lax.fori_loop(bounds_ref[0, i], inside, functools.partial(body, True), 0)
    lax.fori_loop(inside, i, functools.partial(body, False), 0)
    step(i, True, True)
    dq_ref[...] = head_pick(acc[...], heads, bq)


def attend_back(bounds, q, k, v, grads, out, log_sum, start, block, group, width):
    length = q.shape[0]
    heads = width // HEAD_DIM
    taken = pl.BlockSpec((length, width), lambda i: (0, group))
    taken_rows = pl.BlockSpec((block, width), lambda i: (i, group))
    whole = pl.BlockSpec((length, width), lambda i: (0, 0))
    rows = pl.BlockSpec((block, width), lambda i: (i, 0))
    result = jax.ShapeDtypeStruct((length, width), f32)
    return pl.pallas_call(
        functools.partial(attend_back_kernel, group * heads, heads, block, block),
        grid=(length // block,),
        in_specs=[
            pl.BlockSpec(memory_space=pltpu.SMEM),
            taken_rows,
            taken_rows,
            taken,
            taken,
            taken_rows,
            pl.BlockSpec((log_sum.shape[0], block), lambda i: (0, i)),
            pl.BlockSpec((1, block), lambda i: (0, i)),
        ],
        out_specs=[rows, whole, whole],
        out_shape=[result, result, result],
        scratch_shapes=[pltpu.VMEM((heads * block, width), f32)],
        cost_estimate=pl.CostEstimate(
            flops=40_000_000_000, bytes_accessed=20 * length * width, transcendentals=0
        ),
        name="attend_back",
    )(bounds, q, grads, k, v, out, log_sum, start)


def partner(x):
    width = x.shape[1]
    lane = lax.broadcasted_iota(jnp.int32, x.shape, 1)
    ahead = pltpu.roll(x, width - HEAD_DIM // 2, 1)
    behind = pltpu.roll(x, HEAD_DIM // 2, 1)
    return jnp.where(lax.rem(lane, HEAD_DIM) < HEAD_DIM // 2, ahead, behind)


def head_sums(x):
    width = x.shape[1]
    row = lax.broadcasted_iota(jnp.int32, (width, width), 0) // HEAD_DIM
    column = lax.broadcasted_iota(jnp.int32, (width, width), 1) // HEAD_DIM
    same = jnp.where(row == column, 1.0, 0.0).astype(bf16)
    high = x.astype(bf16)
    low = (x - high.astype(f32)).astype(bf16)
    return dot_nn(high, same) + dot_nn(low, same)


def widen(table, width):
    return table if table.shape[1] == width else jnp.concatenate([table] * (width // 128), axis=1)


def added(refs):
    total = refs[0][...]
    for ref in refs[1:]:
        total = total + ref[...]
    return total


def project_kernel(count, index_ref, *refs):
    wq_ref, wk_ref, wv_ref, cos_ref, sin_ref, gain_ref = refs[count : count + 6]
    q_ref, k_ref, v_ref, xq_ref, xk_ref = refs[-5:]
    x = added(refs[:count])
    width = q_ref.shape[1]
    cosine = widen(cos_ref[...], width)
    sine = widen(sin_ref[...], width)
    gain = gain_ref[...]
    for w_ref, hat_ref, turned_ref in ((wq_ref, q_ref, xq_ref), (wk_ref, k_ref, xk_ref)):
        raw = dot_nn(x, w_ref[...])
        turned = raw * cosine + partner(raw) * sine
        turned_ref[...] = turned
        hat = turned * lax.rsqrt(head_sums(turned * turned) + norm_eps) * gain
        hat_ref[...] = hat.astype(bf16)
    v_ref[...] = dot_nn(x, wv_ref[...]).astype(bf16)


def project(index, parts, weights, cosine, sine, gain, length, previous):
    rows, model = parts[0].shape
    count = len(parts)
    width = gain.shape[1]
    part = min(256, rows)
    per = rows // part

    def column(m):
        return pl.BlockSpec((model, width), lambda i, at: (0, m))

    table = pl.BlockSpec((part, 128), lambda i, at: (at[0] * per + i, 0))
    out = pl.BlockSpec((part, width), lambda i, at: (at[0] * per + i, 0))
    low = jax.ShapeDtypeStruct((length, width), bf16)
    wide = jax.ShapeDtypeStruct((length, width), f32)
    return pl.pallas_call(
        functools.partial(project_kernel, count),
        grid_spec=pltpu.PrefetchScalarGridSpec(
            num_scalar_prefetch=1,
            grid=(per,),
            in_specs=[pl.BlockSpec((part, model), lambda i, at: (i, 0))] * count
            + [
                column(0),
                column(1),
                column(2),
                table,
                table,
                pl.BlockSpec((1, width), lambda i, at: (0, 0)),
            ]
            + [pl.BlockSpec(memory_space=pl.ANY)] * len(previous),
            out_specs=[out] * 5,
        ),
        out_shape=[low, low, low, wide, wide],
        input_output_aliases={7 + count + i: i for i in range(len(previous))},
        cost_estimate=pl.CostEstimate(
            flops=6 * rows * model * width, bytes_accessed=8 * model * width, transcendentals=0
        ),
        name="project",
    )(index, *parts, weights, weights, weights, cosine, sine, gain, *previous)


def project_back_kernel(groups, index_ref, *refs):
    dq_refs, dk_refs, dv_refs = (refs[m * groups : (m + 1) * groups] for m in range(3))
    (
        xq_ref,
        xk_ref,
        wq_ref,
        wk_ref,
        wv_ref,
        cos_ref,
        sin_ref,
        gain_ref,
        grad_ref,
        gain_grad_ref,
        *piece_refs,
    ) = refs[3 * groups :]

    @pl.when(pl.program_id(0) == 0)
    def _():
        gain_grad_ref[...] = jnp.zeros_like(gain_grad_ref)

    def joined(refs):
        return jnp.concatenate([ref[...] for ref in refs], axis=1) if groups > 1 else refs[0][...]

    width = xq_ref.shape[1]
    cosine = widen(cos_ref[...], width)
    sine = widen(sin_ref[...], width)
    gain = gain_ref[...]
    lows = []
    for d_refs, x_ref in ((dq_refs, xq_ref), (dk_refs, xk_ref)):
        turned = x_ref[...]
        inverse = lax.rsqrt(head_sums(turned * turned) + norm_eps)
        unit = turned * inverse
        hat_grad = joined(d_refs) * scale_factor
        gain_grad_ref[...] += jnp.sum(hat_grad * unit, axis=0, keepdims=True)
        unit_grad = hat_grad * gain
        turned_grad = inverse * (unit_grad - unit * head_sums(unit * unit_grad))
        raw_grad = turned_grad * cosine - partner(turned_grad) * sine
        lows.append(raw_grad.astype(bf16))
    lows.append(joined(dv_refs).astype(bf16))
    piece = jnp.zeros(piece_refs[0].shape, f32)
    for m, w_ref in enumerate((wq_ref, wk_ref, wv_ref)):
        grad_ref[:, m * width : (m + 1) * width] = lows[m]
        piece = piece + dot_nt(lows[m], w_ref[...])
    low = piece.astype(bf16)
    block = pl.program_id(0) // (pl.num_programs(0) // len(piece_refs))
    for d, piece_ref in enumerate(piece_refs):

        @pl.when(block == d)
        def _(piece_ref=piece_ref):
            piece_ref[...] = low


def project_back(index, grads, turned, weights, cosine, sine, gain, rows):
    length, width = turned[0].shape
    groups = len(grads)
    model = weights.shape[0]
    part = min(256, rows)
    per = rows // part
    blocks = length // part

    def column(m):
        return pl.BlockSpec((model, width), lambda i, at: (0, m))

    def turn(i, at):
        return (lax.rem(at[0] * per + i, blocks), 0)

    def piece_block(d):
        return pl.BlockSpec((part, model), lambda i, at: (jnp.clip(i - d * per, 0, per - 1), 0))

    tall = pl.BlockSpec((part, width), turn)
    table = pl.BlockSpec((part, 128), turn)
    return pl.pallas_call(
        functools.partial(project_back_kernel, groups),
        grid_spec=pltpu.PrefetchScalarGridSpec(
            num_scalar_prefetch=1,
            grid=(blocks,),
            in_specs=[pl.BlockSpec((part, width // groups), turn)] * (3 * groups)
            + [tall] * 2
            + [column(0), column(1), column(2), table, table]
            + [pl.BlockSpec((1, width), lambda i, at: (0, 0))],
            out_specs=[
                pl.BlockSpec((part, 3 * width), lambda i, at: (i, 0)),
                pl.BlockSpec((1, width), lambda i, at: (0, 0)),
            ]
            + [piece_block(d) for d in range(length // rows)],
        ),
        out_shape=[
            jax.ShapeDtypeStruct((length, 3 * width), bf16),
            jax.ShapeDtypeStruct((1, width), f32),
        ]
        + [jax.ShapeDtypeStruct((rows, model), bf16)] * (length // rows),
        cost_estimate=pl.CostEstimate(
            flops=length * width, bytes_accessed=length * width, transcendentals=0
        ),
        name="project_back",
    )(index, *[g[m] for m in range(3) for g in grads], *turned, weights, weights, weights, cosine, sine, gain)


def projection_grads_kernel(counts, *refs):
    grad_ref, out_ref = refs[-2:]
    total = None
    for d, count in enumerate(counts):
        hidden = added(refs[:count])
        refs = refs[count:]
        rows = hidden.shape[0]
        part = dot_tn(hidden, grad_ref[d * rows : (d + 1) * rows, :])
        total = part if total is None else total + part
    out_ref[...] = total.astype(bf16)


def projection_grads(hidden, qkv_grad):
    rows, model = hidden[0][0].shape
    length, width = qkv_grad.shape
    counts = tuple(len(parts) for parts in hidden)
    part = 256
    return pl.pallas_call(
        functools.partial(projection_grads_kernel, counts),
        grid=(model // part,),
        in_specs=[pl.BlockSpec((rows, part), lambda i: (0, i))] * sum(counts)
        + [pl.BlockSpec(qkv_grad.shape, lambda i: (0, 0))],
        out_specs=pl.BlockSpec((part, width), lambda i: (i, 0)),
        out_shape=jax.ShapeDtypeStruct((model, width), bf16),
        cost_estimate=pl.CostEstimate(
            flops=2 * length * model * width,
            bytes_accessed=8 * length * model,
            transcendentals=0,
        ),
        name="projection_grads",
    )(*[x for parts in hidden for x in parts], qkv_grad)


def out_grads_kernel(count, *refs):
    attended = refs[:count]
    branch_ref, out_ref = refs[count:]
    width = attended[0].shape[1]
    turned = branch_ref[...].T
    for d in range(count):
        out_ref[:, d * width : (d + 1) * width] = dot_nn(turned, attended[d][...]).astype(bf16)


def out_grads(attended, branch_grad):
    count = len(attended)
    rows, model = branch_grad.shape
    width = attended[0].shape[1]
    part = 256
    return pl.pallas_call(
        functools.partial(out_grads_kernel, count),
        grid=(model // part,),
        in_specs=[pl.BlockSpec(x.shape, lambda i: (0, 0)) for x in attended]
        + [pl.BlockSpec((rows, part), lambda i: (0, i))],
        out_specs=pl.BlockSpec((part, count * width), lambda i: (i, 0)),
        out_shape=jax.ShapeDtypeStruct((model, count * width), bf16),
        cost_estimate=pl.CostEstimate(
            flops=2 * rows * count * model * width,
            bytes_accessed=4 * rows * count * model,
            transcendentals=0,
        ),
        name="out_grads",
    )(*attended, branch_grad)


def assemble_kernel(order, wide_counts, shard, width, *refs):
    out_ref = refs[-1]
    size = len(order)
    hidden_width = out_ref.shape[1]
    wide, low = [], []
    for blocks in (wide, low):
        for count in wide_counts:
            blocks.append(refs[:count])
            refs = refs[count:]
    for p, d in enumerate(order):
        out_ref[2 * p * shard : 2 * (p + 1) * shard, :] = added(wide[d])
    packed = shard * width // hidden_width
    per = hidden_width // width
    for p, d in enumerate(order):
        down = [ref[:shard, :] for ref in low[d]]
        out_ref[(2 * size + p) * shard : (2 * size + p + 1) * shard, :] = sum(down[1:], down[0])
    for d in range(size):
        outs = [ref[shard:, :] for ref in low[d]]
        block = sum(outs[1:], outs[0])
        columns = slice((d % per) * width, (d % per + 1) * width)
        for c in range(per):
            row = (3 * size + d // per) * shard + c * packed
            out_ref[row : row + packed, columns] = block[:, c * width : (c + 1) * width]


def assemble(order, wide, low, shard, width):
    hidden_width = wide[0][0].shape[1]
    counts = tuple(len(parts) for parts in wide)
    blocks = 3 * len(order) + len(order) * width // hidden_width
    return pl.pallas_call(
        functools.partial(assemble_kernel, tuple(order), counts, shard, width),
        out_shape=jax.ShapeDtypeStruct((blocks * shard, hidden_width), bf16),
        name="assemble",
    )(*[x for parts in list(wide) + list(low) for x in parts])


def rms_scale(x):
    return lax.rsqrt(jnp.mean(x * x, axis=-1, keepdims=True) + norm_eps)


def mix_kernel(count, *refs):
    pieces, weights = refs[:count], refs[count : 2 * count]
    hidden_ref, rates_ref, branch_ref, middle_ref, low_ref, turned_ref, out_ref = refs[2 * count :]
    branch = dot_nt(pieces[0][...], block_of(weights[0]))
    for d in range(1, count):
        branch = branch + dot_nt(pieces[d][...], block_of(weights[d]))

    @pl.when(pl.program_id(0) == 0)
    def _():
        width = pieces[0].shape[1]
        for d in range(count):
            out_ref[:, d * width : (d + 1) * width] = block_of(weights[d])

    branch_ref[...] = branch
    hidden = hidden_ref[...].astype(f32)
    mixed = hidden + rates_ref[0:1, :] * (branch * rms_scale(branch) - hidden)
    middle = mixed * rms_scale(mixed)
    middle_ref[...] = middle
    low_ref[...] = middle.astype(bf16)
    turned_ref[...] = middle.T.astype(bf16)


def mix(pieces, weights, hidden, rates):
    count = len(pieces)
    rows, model = hidden.shape
    width = pieces[0].shape[1]
    part = min(128, rows)

    nd, blocks, shard, local_width = weights.shape
    per = local_width // width
    first = blocks - count // per

    def column(d):
        return pl.BlockSpec((nd, 1, shard, width), lambda i: (0, first + d // per, 0, d % per))

    wide = pl.BlockSpec((part, model), lambda i: (i, 0))
    return pl.pallas_call(
        functools.partial(mix_kernel, count),
        grid=(rows // part,),
        in_specs=[pl.BlockSpec((part, width), lambda i: (i, 0))] * count
        + [column(d) for d in range(count)]
        + [wide, pl.BlockSpec((2, model), lambda i: (0, 0))],
        out_specs=[wide, wide, wide, pl.BlockSpec((model, part), lambda i: (0, i))]
        + [pl.BlockSpec((model, count * width), lambda i: (0, 0))],
        out_shape=[
            jax.ShapeDtypeStruct((rows, model), f32),
            jax.ShapeDtypeStruct((rows, model), f32),
            jax.ShapeDtypeStruct((rows, model), bf16),
            jax.ShapeDtypeStruct((model, rows), bf16),
            jax.ShapeDtypeStruct((model, count * width), bf16),
        ],
        cost_estimate=pl.CostEstimate(
            flops=2 * rows * model * model, bytes_accessed=14 * rows * model, transcendentals=0
        ),
        name="mix",
    )(*pieces, *([weights] * count), hidden, rates)


def block_of(w_ref):
    value = w_ref[:, 0]
    return value.reshape(value.shape[0] * value.shape[1], value.shape[2])


def feed_kernel(
    m_ref,
    wu_ref,
    wg_ref,
    wd_ref,
    s_ref,
    middle_ref,
    cot_ref,
    live_ref,
    rates_ref,
    up_ref,
    gate_ref,
    h_ref,
    result_ref,
    direct_ref,
    low_ref,
    turned_ref,
    rate_ref,
    acc,
):
    i = pl.program_id(0)
    tokens = m_ref[...]
    up = dot_nn(tokens, block_of(wu_ref))
    gate = dot_nn(tokens, block_of(wg_ref))
    up_ref[...] = up
    gate_ref[...] = gate
    scaled = gate * s_ref[1:2, :]
    hidden = (up * s_ref[0:1, :] * (scaled * jax.nn.sigmoid(scaled))).astype(bf16)
    h_ref[...] = hidden
    part_out = dot_nt(hidden, block_of(wd_ref))

    @pl.when(i == 0)
    def _():
        acc[...] = part_out

    @pl.when(i > 0)
    def _():
        acc[...] += part_out

    @pl.when(i == pl.num_programs(0) - 1)
    def _():
        rate_ref[...] = jnp.zeros_like(rate_ref)
        rate = rates_ref[1:2, :]
        part = min(128, acc.shape[0])

        def body(at, carry):
            rows = pl.ds(pl.multiple_of(at * part, part), part)
            out = acc[rows, :]
            middle = middle_ref[rows, :]
            out_scale = rms_scale(out)
            unit = out * out_scale
            mixed = middle + rate * (unit - middle)
            scale = rms_scale(mixed)
            final = mixed * scale
            result_ref[rows, :] = final.astype(bf16)
            grad = cot_ref[rows, :].astype(f32) * live_ref[rows, :]
            mixed_grad = scale * (grad - final * jnp.mean(final * grad, axis=-1, keepdims=True))
            direct_ref[rows, :] = mixed_grad * (1.0 - rate)
            rate_ref[...] += jnp.sum(mixed_grad * (unit - middle), axis=0, keepdims=True)
            unit_grad = mixed_grad * rate
            out_grad = out_scale * (
                unit_grad - unit * jnp.mean(unit * unit_grad, axis=-1, keepdims=True)
            )
            low_ref[rows, :] = out_grad.astype(bf16)
            return carry

        lax.fori_loop(0, acc.shape[0] // part, body, 0)
        for at in range(acc.shape[0] // 128):
            rows = slice(at * 128, (at + 1) * 128)
            turned_ref[:, rows] = low_ref[rows, :].T


def weight_specs(weights, step, total, base=0):
    nd, _, shard, local_width = weights.shape
    per = local_width // step

    def spec(m):
        def place(i):
            p = (i + base) // per
            return (0, 2 * p + m if m < 2 else 2 * (total // local_width) + p, 0, (i + base) % per)

        return pl.BlockSpec((nd, 1, shard, step), place)

    return [spec(0), spec(1), spec(2)]


def feed(low, weights, scales, middle, cotangent, live, rates, step):
    rows, model = low.shape
    total = scales.shape[1]
    columns = pl.BlockSpec((rows, step), lambda i: (0, i))
    whole = pl.BlockSpec((rows, model), lambda i: (0, 0))
    return pl.pallas_call(
        feed_kernel,
        grid=(total // step,),
        in_specs=[whole]
        + weight_specs(weights, step, total)
        + [
            pl.BlockSpec((2, step), lambda i: (0, i)),
            whole,
            whole,
            pl.BlockSpec((rows, 1), lambda i: (0, 0)),
            pl.BlockSpec((2, model), lambda i: (0, 0)),
        ],
        out_specs=[columns, columns, columns, whole, whole, whole]
        + [
            pl.BlockSpec((model, rows), lambda i: (0, 0)),
            pl.BlockSpec((1, model), lambda i: (0, 0)),
        ],
        out_shape=[
            jax.ShapeDtypeStruct((rows, total), f32),
            jax.ShapeDtypeStruct((rows, total), f32),
            jax.ShapeDtypeStruct((rows, total), bf16),
            jax.ShapeDtypeStruct((rows, model), bf16),
            jax.ShapeDtypeStruct((rows, model), f32),
            jax.ShapeDtypeStruct((rows, model), bf16),
            jax.ShapeDtypeStruct((model, rows), bf16),
            jax.ShapeDtypeStruct((1, model), f32),
        ],
        scratch_shapes=[pltpu.VMEM((rows, model), f32)],
        cost_estimate=pl.CostEstimate(
            flops=6 * rows * model * total,
            bytes_accessed=6 * model * total + 10 * rows * total,
            transcendentals=0,
        ),
        name="feed",
    )(low, weights, weights, weights, scales, middle, cotangent, live, rates)


def feed_back_step(
    og_ref, ogt_ref, mt_ref, wu_ref, wg_ref, wd_ref, s_ref, up_ref, gate_ref, h_ref, start_ref, grad_ref, sg_ref, acc
):
    i = pl.program_id(0)
    grad_ref[2] = dot_nn(ogt_ref[...], h_ref[...]).astype(bf16)
    hidden_grad = dot_nn(og_ref[...], block_of(wd_ref))
    up = up_ref[...]
    gate = gate_ref[...]
    up_gain = s_ref[0:1, :]
    gate_gain = s_ref[1:2, :]
    scaled = gate * gate_gain
    sig = jax.nn.sigmoid(scaled)
    up_part = hidden_grad * (scaled * sig)
    gate_part = hidden_grad * (up * up_gain) * (sig * (1.0 + scaled * (1.0 - sig)))
    sg_ref[0:1, :] = jnp.sum(up_part * up, axis=0, keepdims=True)
    sg_ref[1:2, :] = jnp.sum(gate_part * gate, axis=0, keepdims=True)
    up_low = (up_part * up_gain).astype(bf16)
    gate_low = (gate_part * gate_gain).astype(bf16)
    tokens_t = mt_ref[...]
    grad_ref[0] = dot_nn(tokens_t, up_low).astype(bf16)
    grad_ref[1] = dot_nn(tokens_t, gate_low).astype(bf16)
    back = dot_nt(up_low, block_of(wu_ref)) + dot_nt(gate_low, block_of(wg_ref))

    @pl.when(i == 0)
    def _():
        acc[...] = start_ref[...] + back

    @pl.when(i > 0)
    def _():
        acc[...] += back


def feed_back_first_kernel(*refs):
    feed_back_step(*refs)


def feed_back_last_kernel(*refs):
    branch_ref, hidden_ref, rates_ref = refs[11:14]
    grad_ref, sg_ref, token_ref, low_ref, rate_ref, acc = refs[14:]
    feed_back_step(*refs[:11], grad_ref, sg_ref, acc)

    @pl.when(pl.program_id(0) == pl.num_programs(0) - 1)
    def _():
        rate_ref[...] = jnp.zeros_like(rate_ref)
        rate = rates_ref[0:1, :]
        part = min(128, acc.shape[0])

        def body(at, carry):
            rows = pl.ds(pl.multiple_of(at * part, part), part)
            grad = acc[rows, :]
            branch = branch_ref[rows, :]
            hidden = hidden_ref[rows, :].astype(f32)
            branch_scale = rms_scale(branch)
            unit = branch * branch_scale
            mixed = hidden + rate * (unit - hidden)
            scale = rms_scale(mixed)
            middle = mixed * scale
            mixed_grad = scale * (grad - middle * jnp.mean(middle * grad, axis=-1, keepdims=True))
            token_ref[rows, :] = mixed_grad * (1.0 - rate)
            rate_ref[...] += jnp.sum(mixed_grad * (unit - hidden), axis=0, keepdims=True)
            unit_grad = mixed_grad * rate
            branch_grad = branch_scale * (
                unit_grad - unit * jnp.mean(unit * unit_grad, axis=-1, keepdims=True)
            )
            low_ref[rows, :] = branch_grad.astype(bf16)
            return carry

        lax.fori_loop(0, acc.shape[0] // part, body, 0)


def feed_back(
    out_grad, out_grad_t, middle_t, weights, scales, up, gate, hidden_units, start, mixing, step, base, count
):
    model, rows = middle_t.shape
    width = count * step
    columns = pl.BlockSpec((rows, step), lambda i: (0, i + base))
    whole = pl.BlockSpec((rows, model), lambda i: (0, 0))
    turned = pl.BlockSpec((model, rows), lambda i: (0, 0))
    wide = jax.ShapeDtypeStruct((rows, model), f32)
    grads_specs = [
        pl.BlockSpec((3, model, step), lambda i: (0, 0, i)),
        pl.BlockSpec((2, step), lambda i: (0, i)),
    ]
    grads_shapes = [
        jax.ShapeDtypeStruct((3, model, width), bf16),
        jax.ShapeDtypeStruct((2, width), f32),
    ]
    last = bool(mixing)
    return pl.pallas_call(
        feed_back_last_kernel if last else feed_back_first_kernel,
        grid=(count,),
        in_specs=[whole, turned, turned]
        + weight_specs(weights, step, scales.shape[1], base)
        + [pl.BlockSpec((2, step), lambda i: (0, i + base)), columns, columns, columns, whole]
        + ([whole, whole, pl.BlockSpec((2, model), lambda i: (0, 0))] if last else []),
        out_specs=grads_specs
        + ([whole, whole, pl.BlockSpec((1, model), lambda i: (0, 0))] if last else [whole]),
        out_shape=grads_shapes
        + (
            [
                wide,
                jax.ShapeDtypeStruct((rows, model), bf16),
                jax.ShapeDtypeStruct((1, model), f32),
            ]
            if last
            else [wide]
        ),
        scratch_shapes=[pltpu.VMEM((rows, model), f32)] if last else [],
        cost_estimate=pl.CostEstimate(
            flops=12 * rows * model * width,
            bytes_accessed=12 * model * width + 10 * rows * width,
            transcendentals=0,
        ),
        name="feed_back_last" if last else "feed_back_first",
    )(
        out_grad,
        out_grad_t,
        middle_t,
        weights,
        weights,
        weights,
        scales,
        up,
        gate,
        hidden_units,
        start,
        *mixing,
    )


def shift(value, axis, distance, size):
    return lax.ppermute(value, axis, [(i, (i + distance) % size) for i in range(size)])


def carry_on(up, down, hop, axis, size):
    up = lax.ppermute(up, axis, [(i, i + 1) for i in range(hop - 1, size - 1)])
    down = lax.ppermute(down, axis, [(i, i - 1) for i in range(1, size - hop + 1)])
    return up, down


def line_sum(pieces, hop, up, down, axis, size):
    ahead, behind = pieces[size - hop], pieces[hop]
    ahead = ahead if up is None else ahead + up
    behind = behind if down is None else behind + down
    up = lax.ppermute(ahead, axis, [(i, i + 1) for i in range(hop)])
    down = lax.ppermute(behind, axis, [(i, i - 1) for i in range(size - hop, size)])
    return up, down


def halving(value, axis, size, step):
    lead, (count, rows, width) = value.shape[:-3], value.shape[-3:]
    bit = (lax.axis_index(axis) // step) % 2
    pairs = value.reshape(lead + (count // 2, 2, rows, width))
    sent = lax.dynamic_index_in_dim(pairs, 1 - bit, len(lead) + 1, False)
    kept = lax.dynamic_index_in_dim(pairs, bit, len(lead) + 1, False)
    other = lax.ppermute(sent, axis, [(i, i ^ step) for i in range(size)])
    value = kept.astype(f32) + other.astype(f32)
    return value.reshape(lead + (rows, width)) if 2 * step == size else value.astype(bf16)


def exchange_add(value, axis, size, step):
    return value + lax.ppermute(value, axis, [(i, i ^ step) for i in range(size)])


def doublings(size):
    return [1 << k for k in range(size.bit_length() - 1)]


def butterfly(value, axis, size):
    for step in doublings(size):
        value = exchange_add(value, axis, size, step)
    return value


def take_block(value, index, size, axis):
    return lax.dynamic_slice_in_dim(value, index * size, size, axis)


def put_block(whole, value, index, axis):
    return lax.dynamic_update_slice_in_dim(whole, value, index * value.shape[axis], axis)


def local(
    nd,
    nt,
    hidden_in,
    cotangent,
    segments,
    attn_weight,
    mlp_weight,
    rates,
    qk_scale,
    mlp_scales,
    attn_moment_one,
    attn_moment_two,
    mlp_moment_one,
    mlp_moment_two,
):
    rows, model = hidden_in.shape
    length = segments.shape[0]
    shard = attn_weight.shape[1]
    heads_width = attn_weight.shape[2]
    hidden_width = mlp_weight.shape[2]
    block = min(512, length)
    step = min(512, hidden_width)
    me = lax.axis_index("tensor")

    def gather(value):
        return [value] + [shift(value, "tensor", d, nt) for d in range(1, nt)]

    def both(ups, downs, d):
        return (ups[0],) if d == 0 else (ups[d], downs[nt - d])

    middle_hop = nt // 2
    order = [d for d in range(nt) if d != middle_hop] + [middle_hop]
    attn_low = attn_weight.astype(bf16)
    qkv_full = lax.all_gather(
        jnp.concatenate([attn_low[0], attn_low[1], attn_low[2]], axis=1), "dp", axis=0, tiled=True
    )
    mlp_low = mlp_weight.astype(bf16)
    splits = hidden_width // heads_width
    packed = jnp.concatenate(jnp.split(attn_low[3], splits, axis=0), axis=1)
    chunks = [
        mlp_low[:2].reshape(2 * shard, hidden_width),
        jnp.concatenate([mlp_low[2], packed], axis=0),
    ]
    lines = [([chunk], [chunk]) for chunk in chunks]
    for hop in range(1, nt):
        for c, (ups, downs) in enumerate(lines):
            if hop == nt - 1 and c == 1:
                ups[-1], downs[-1], hidden_in = lax.optimization_barrier(
                    (ups[-1], downs[-1], hidden_in)
                )
            up, down = carry_on(ups[-1], downs[-1], hop, "tensor", nt)
            ups.append(up)
            downs.append(down)
    wide_blocks, low_blocks = [
        [both(ups, downs, d) for d in range(nt)] for ups, downs in lines
    ]
    operand = assemble(order, wide_blocks, low_blocks, shard, heads_width)
    mlp_full = lax.all_gather(operand, "dp", axis=0, tiled=True)
    mlp_full = mlp_full.reshape(nd, -1, shard, hidden_width)
    scales_parts = gather(mlp_scales)
    scales_row = jnp.concatenate([scales_parts[d] for d in order], axis=1)

    starts = starts_of(segments)
    positions = (jnp.arange(length, dtype=jnp.int32) - starts).astype(f32)
    lane = jnp.arange(128, dtype=jnp.int32)
    half = HEAD_DIM // 2
    frequency = 10000.0 ** (-(lane % half).astype(f32) / half)
    sign = jnp.where(lane % HEAD_DIM < half, -1.0, 1.0)
    angles = positions[:, None] * frequency[None, :]
    cosine = jnp.cos(angles)
    sine = jnp.sin(angles) * sign[None, :]
    gain = qk_scale.reshape(1, heads_width)

    ups, downs, state = [hidden_in], [hidden_in], ()
    hidden_parts = [None] * nt

    def projected(hop, state):
        for d in range(nt):
            if (max(d, nt - d) if d else 0) == hop:
                hidden_parts[d] = both(ups, downs, d)
                index = ((me + nt - d) % nt).reshape(1)
                state = project(index, hidden_parts[d], qkv_full, cosine, sine, gain, length, state)
        return state

    for hop in range(1, nt):
        ups[-1], downs[-1], state = lax.optimization_barrier((ups[-1], downs[-1], state))
        up, down = carry_on(ups[-1], downs[-1], hop, "tensor", nt)
        ups.append(up)
        downs.append(down)
        state = projected(hop - 1, state)
    ups[-1], downs[-1], state = lax.optimization_barrier((ups[-1], downs[-1], state))
    state = projected(nt - 1, state)
    query_hat, key_hat, value_hat, query_turned, key_turned = state
    bounds = key_bounds(starts, block)
    attended_row, attended_f32, log_sum = attend(
        bounds, query_hat, key_hat, value_hat, starts[:, None], block
    )
    attended = [take_block(attended_row, me, rows, 0)] + [
        shift(take_block(attended_row, (me + d) % nt, rows, 0), "tensor", d, nt)
        for d in range(1, nt)
    ]
    branch, middle, middle_low, middle_t, out_full = mix(attended, mlp_full, hidden_in, rates)
    row_segments = take_block(segments, me, rows, 0)
    live = (row_segments < pad_segment).astype(f32)[:, None]
    up, gate, hidden_units, result, middle_direct, mlp_out_low, mlp_out_t, rate_mlp_grad = feed(
        middle_low, mlp_full, scales_row, middle, cotangent, live, rates, step
    )
    def spread(value, places):
        width = value.shape[1] // nt
        whole = jnp.zeros_like(value)
        for p, d in enumerate(places):
            piece = value[:, p * width : (p + 1) * width]
            whole = put_block(whole, piece, (me + nt - d) % nt, 1)
        return whole

    def blocks_of(part, axis, width):
        return [
            lax.slice_in_dim(part, at, at + width, axis=axis)
            for at in range(0, part.shape[axis], width)
        ]

    def to_owners(pieces, places):
        return [shift(piece, "tensor", -d, nt) if d else piece for d, piece in zip(places, pieces)]

    per = hidden_width // step
    near = (nt - 1) * per
    feed_args = (mlp_out_low, mlp_out_t, middle_t, mlp_full, scales_row, up, gate, hidden_units)
    far_grad, far_scales, partial = feed_back(*feed_args, middle_direct, (), step, near, per)
    halvings = doublings(nd)
    far_part = lax.psum_scatter(far_grad, "dp", scatter_dimension=1, tiled=True)
    near_grad, near_scales, token_direct, branch_low, rate_attn_grad = feed_back(
        *feed_args, partial, (branch, hidden_in, rates), step, 0, near
    )
    near_part = lax.psum_scatter(near_grad, "dp", scatter_dimension=1, tiled=True)

    grad_pieces = []
    for d in list(range(1, nt)) + [0]:
        piece = dot_nn(branch_low, out_full[:, d * heads_width : (d + 1) * heads_width])
        piece = piece.astype(bf16)
        grad_pieces.append((d, shift(piece, "tensor", -d, nt) if d else piece))
    grad_row = jnp.zeros((length, heads_width), bf16)
    for d, piece in grad_pieces[-1:] + grad_pieces[:-1]:
        grad_row = put_block(grad_row, piece, (me + d) % nt, 0)
    out_sum = out_grads(attended, branch_low).reshape(nd, shard, -1)
    out_sum = halving(out_sum, "dp", nd, halvings[0])

    scales_grad = spread(jnp.concatenate([near_scales, far_scales], axis=1), order)
    small = jnp.concatenate(
        [rate_attn_grad, rate_mlp_grad, scales_grad.reshape(-1, model)], axis=0
    )
    steps = [("tensor", nt, k) for k in doublings(nt)] + [("dp", nd, k) for k in doublings(nd)]

    def advance(small):
        return exchange_add(small, *steps.pop(0)) if steps else small

    far_part, grad_row, out_sum, small = lax.optimization_barrier(
        (far_part, grad_row, out_sum, small)
    )
    small = advance(small)
    out_sum = halving(out_sum, "dp", nd, halvings[1])
    head_group = max(128, heads_width // 2)
    head_grads = []
    for group in range(heads_width // head_group):
        if group == 1:
            head_grads, grad_row, far_part, small, out_sum = lax.optimization_barrier(
                (head_grads, grad_row, far_part, small, out_sum)
            )
            small = advance(small)
            out_sum = halving(out_sum, "dp", nd, halvings[2])
        head_grads.append(
            attend_back(
                bounds,
                query_hat,
                key_hat,
                value_hat,
                grad_row,
                attended_f32,
                log_sum,
                starts[None, :],
                block,
                group,
                head_group,
            )
        )
    far_first = shift(far_part[:2], "tensor", -middle_hop, nt)
    far_last = far_part[2:]
    head_grads, small, out_sum, far_first, far_last = lax.optimization_barrier(
        (head_grads, small, out_sum, far_first, far_last)
    )
    far_last = shift(far_last, "tensor", -middle_hop, nt)
    small = advance(small)
    for k in halvings[2 if len(head_grads) == 1 else 3 :]:
        out_sum = halving(out_sum, "dp", nd, k)
    out_pieces = to_owners(blocks_of(out_sum.astype(bf16), 1, heads_width), range(nt))
    qkv_grad, gain_grad, *pieces = project_back(
        me.reshape(1),
        head_grads,
        (query_turned, key_turned),
        qkv_full,
        cosine,
        sine,
        gain,
        rows,
    )
    qkv_grad, pieces, small, out_pieces, far_last = lax.optimization_barrier(
        (qkv_grad, pieces, small, out_pieces, far_last)
    )
    far_part = jnp.concatenate([far_first, far_last], axis=0)
    hidden_turn = [hidden_parts[(nt - d) % nt] for d in range(nt)]
    qkv_sum = projection_grads(hidden_turn, qkv_grad)
    qkv_sum = qkv_sum.reshape(nd, shard, -1)

    ahead = behind = None
    for hop in range(1, nt):
        if hop == 2:
            ahead, behind, qkv_sum, gain_grad = lax.optimization_barrier(
                (ahead, behind, qkv_sum, gain_grad)
            )
            gain_parts = gather(gain_grad)
        if hop == max(2, nt - 1):
            ahead, behind, near_part, qkv_sum, gain_parts = lax.optimization_barrier(
                (ahead, behind, near_part, qkv_sum, gain_parts)
            )
            near_pieces = blocks_of(near_part, 2, hidden_width)
            near_pieces, qkv_sum, small = lax.optimization_barrier((near_pieces, qkv_sum, small))
            near_pieces = to_owners(near_pieces, order[:-1])
        ahead, behind = line_sum(pieces, hop, ahead, behind, "tensor", nt)
        if hop == 2:
            for k in halvings[:2]:
                qkv_sum = halving(qkv_sum, "dp", nd, k)
    for k in halvings[2:]:
        qkv_sum = halving(qkv_sum, "dp", nd, k)
    gain_row = spread(jnp.concatenate(gain_parts, axis=1), range(nt))
    while steps:
        small = advance(small)
    out_own = sum(piece.astype(f32) for piece in out_pieces)
    attn_weight_grad = jnp.stack(
        [qkv_sum[:, m * heads_width : (m + 1) * heads_width] for m in range(3)] + [out_own]
    )
    attn_one, attn_two, attn_moved = adam_moved(
        attn_weight, attn_weight_grad, attn_moment_one, attn_moment_two
    )
    attn_square = jnp.sum(attn_moved * attn_moved, axis=1, keepdims=True)
    last = jnp.concatenate([attn_square.reshape(1, -1), gain_row], axis=1)
    last = butterfly(last, "dp", nd)
    near_pieces, last, small = lax.optimization_barrier((near_pieces, last, small))
    rates_grad = small[:2]
    mlp_scales_grad = small[2:].reshape(2, nt * hidden_width)

    attn_square = last[:, : 4 * heads_width].reshape(4, 1, heads_width)
    gain_row = last[:, 4 * heads_width :].reshape(-1)
    attn_new = attn_moved * lax.rsqrt(attn_square + norm_eps)

    mlp_weight_grad = sum(piece.astype(f32) for piece in near_pieces + [far_part])
    mlp_one, mlp_two, mlp_moved = adam_moved(
        mlp_weight, mlp_weight_grad, mlp_moment_one, mlp_moment_two
    )
    mlp_square = jnp.sum(mlp_moved * mlp_moved, axis=1, keepdims=True)
    mlp_square = butterfly(mlp_square.reshape(1, -1), "dp", nd).reshape(mlp_square.shape)
    mlp_square, ahead, behind = lax.optimization_barrier((mlp_square, ahead, behind))
    total = token_direct + pieces[0].astype(f32)
    input_grad = (total + ahead.astype(f32) + behind.astype(f32)).astype(bf16)
    mlp_new = mlp_moved * lax.rsqrt(mlp_square + norm_eps)
    return (
        result.astype(bf16),
        input_grad,
        attn_weight_grad,
        mlp_weight_grad,
        rates_grad,
        gain_row,
        mlp_scales_grad,
        attn_one,
        attn_two,
        mlp_one,
        mlp_two,
        attn_new,
        mlp_new,
    )


def solution(mesh):
    weights = P(None, "dp", "tensor")
    tokens = P(("dp", "tensor"), None)
    return jax.shard_map(
        functools.partial(local, mesh.shape["dp"], mesh.shape["tensor"]),
        mesh=mesh,
        in_specs=(
            tokens,
            tokens,
            P("dp"),
            weights,
            weights,
            P(),
            P("tensor"),
            P(None, "tensor"),
            weights,
            weights,
            weights,
            weights,
        ),
        out_specs=(
            tokens,
            tokens,
            weights,
            weights,
            P(),
            P(),
            P(),
            weights,
            weights,
            weights,
            weights,
            weights,
            weights,
        ),
        check_vma=False,
    )
```
